32 devices in a mesh: wide: 8 (over z, y), narrow: 4 (over x, core).
Axes of the slice: x: 2, y: 2, z: 4, core: 2. Of those that a mesh axis runs over, the one named last changes fastest.
Arguments:
- stream: bfloat16 [1024, 2048], P('wide', 'narrow'), may hold values from -6 to 6
- out_grad: bfloat16 [1024, 2048], P('wide', 'narrow'), may hold values from -6 to 6
- attn_gain: bfloat16 [2048], P('wide'), may hold values from 0.099609375 to 1.8984375
- attn_router: bfloat16 [2048, 4], P('wide'), may hold values from -0.125 to 0.125
- key_value: bfloat16 [2, 2048, 2048], P(None, 'wide', 'narrow'), may hold values from -0.125 to 0.125
- query_proj: bfloat16 [4, 2048, 2048], P(None, 'wide', 'narrow'), may hold values from -0.1875 to 0.1875
- output_proj: bfloat16 [4, 2048, 2048], P(None, 'wide', 'narrow'), may hold values from -0.5 to 0.5
- mlp_gain: bfloat16 [2048], P('wide'), may hold values from 0.099609375 to 1.8984375
- mlp_router: bfloat16 [2048, 4], P('wide'), may hold values from -0.125 to 0.125
- expert_in: bfloat16 [8, 2048, 2, 2816], P('wide', None, None, 'narrow'), may hold values from -0.125 to 0.125
- expert_down: bfloat16 [8, 2816, 2048], P('wide', 'narrow'), may hold values from -0.15625 to 0.15625
- attn_routes: int32 [1024, 2], P('wide'), may hold values from 0 to 3, all different within a row; in each aligned block of 128 rows (0 to 127, 128 to 255, ...) at most 80 rows name the same one
- mlp_routes: int32 [1024, 2], P('wide'), may hold values from 0 to 3, all different within a row; in each aligned block of 128 rows (0 to 127, 128 to 255, ...) at most 80 rows name the same one
- doc_lengths: int32 [8, 4], P('wide'), may hold values from 1 to 96, 128 in all within a row
Outputs:
- layer_out: float32 [1024, 2048], P('wide', 'narrow')
- stream_grad: float32 [1024, 2048], P('wide', 'narrow')
- attn_gain_grad: float32 [2048], P('wide')
- attn_router_grad: float32 [2048, 4], P('wide')
- key_value_grad: float32 [2, 2048, 2048], P(None, 'wide', 'narrow')
- query_grad: float32 [4, 2048, 2048], P(None, 'wide', 'narrow')
- output_grad: float32 [4, 2048, 2048], P(None, 'wide', 'narrow')
- mlp_gain_grad: float32 [2048], P('wide')
- mlp_router_grad: float32 [2048, 4], P('wide')
- expert_in_grad: float32 [8, 2048, 2, 2816], P('wide', None, None, 'narrow')
- expert_down_grad: float32 [8, 2816, 2048], P('wide', 'narrow')
The draws below stay inside these ranges and needn't reach their ends.
Inputs may be any that keep to these rules, and one draw needn't show every extreme that they name: `attn_routes`: the 2 experts of a token differ. Among the 128 tokens of one block no expert is named more than 80 times, a bound that some block reaches. `mlp_routes`: as for attn_routes. `doc_lengths`: row b holds, in order, the lengths of the documents packed into tokens b * 128 to (b + 1) * 128 - 1; each row sums to 128.
All inputs are finite; a program needn't handle non-finite values.
Results may differ from the reference program's by a relative error of at most 0.019.
Values may be sent and summed in bfloat16 or wider, within the bound.
No kernel may reach another device: no remote copies, remote signals or barrier semaphores. Data moves between devices by JAX's collectives and lax.ppermute only.
A program may use at most 256 MiB of HBM per device.

```python
import math
from functools import partial
import jax
import jax.numpy as jnp
import numpy as np
from jax import lax

D = 2048
H = 16
HS = 128
E = 4
TOPK = 2
F = 5632
TOK = 128
DOCS = 4
SLOTS = 80
LONGEST = 96
SUBS = 2
CAP = 576
TOKENS = 1024
N_WIDE = 8


def block_scale(rng, dims, cuts, smallest, high):
    loudness = 1.0
    for axis_at, blocks in cuts:
        steps = jax.random.uniform(jax.random.fold_in(jax.random.fold_in(rng, 6), axis_at), (blocks,), jnp.float32, smallest / len(cuts), high / len(cuts))
        loudness = loudness * jnp.repeat(jnp.exp(steps), dims[axis_at] // blocks).reshape((-1,) + (1,) * (len(dims) - 1 - axis_at))
    return loudness


def profile(count, total, reach, slope):
    loads = [(1 << 20) // math.isqrt(grade ** slope) + 1 for grade in range(2, count + 1)]
    rest, counts = total - reach - (count - 1), [1] * (count - 1)
    while rest > 0:
        free = [i for i in range(count - 1) if counts[i] < reach]
        mass, left = sum([loads[i] for i in free]), rest
        for i in free:
            more = min(reach - counts[i], max(1, left * loads[i] // mass), rest)
            counts[i] = counts[i] + more
            rest = rest - more
    return np.array([reach] + counts)


def ragged(own_key, number_of, total, reach, slope):
    if number_of == 2:
        one = jax.random.randint(own_key, (), max(1, total - reach), min(reach, total - 1) + 1)
        return jnp.stack([one, total - one])
    tallies = jnp.asarray(profile(number_of, total, reach, slope), jnp.int32)
    pairs = (number_of - 1) // 2
    source_of, receiver = tallies[1:1 + 2 * pairs:2], tallies[2:2 + 2 * pairs:2]
    slack = jnp.minimum(source_of - 1, reach - receiver)
    passed = jax.random.randint(jax.random.fold_in(own_key, 1), (pairs,), 0, 1 << 20) % (slack + 1)
    tallies = tallies.at[1:1 + 2 * pairs:2].set(source_of - passed).at[2:2 + 2 * pairs:2].set(receiver + passed)
    return tallies[jax.random.permutation(jax.random.fold_in(own_key, 2), number_of)]


def routed_block(stream_key, own, number, rows, number_of, top, reach, skew):
    sequence = jax.random.permutation(stream_key, number_of)
    heavy_load, usual = load_shares(number_of, rows * top, reach, skew, True), load_shares(number_of, rows * top, reach, skew, False)
    places = jnp.arange(number_of)

    def named(sizes, turn):
        used = int((sizes > 0).sum())
        fixed = max(1, used // 4)
        moved = fixed + (places - fixed + turn * (used - fixed)) % max(1, number_of - fixed)
        return jnp.zeros((number_of,), jnp.int32).at[sequence[jnp.where(places < fixed, places, moved)]].set(jnp.asarray(sizes, jnp.int32))

    sizes = jnp.where(number % 4 == 0, named(heavy_load, number // 4), named(usual, number - number // 4 - 1))
    mixed = jax.random.permutation(jax.random.fold_in(own, 3), number_of)
    donor, sink = mixed[0:number_of // 2 * 2:2], mixed[1:number_of // 2 * 2:2]
    margin = jnp.minimum(sizes[donor] - 1, reach - sizes[sink]) // 2
    margin = jnp.where((donor == sequence[0]) | (sink == sequence[0]) | (sizes[sink] == 0), 0, jnp.maximum(margin, 0))
    moved = jax.random.randint(jax.random.fold_in(own, 4), (number_of // 2,), 0, 1 << 20) % (margin + 1)
    sizes = sizes.at[donor].add(-moved).at[sink].add(moved)
    members = jnp.searchsorted(jnp.cumsum(sizes), jnp.arange(rows * top), side="right").astype(jnp.int32)
    listing = members.reshape(top, rows).T
    listing = listing[jax.random.permutation(jax.random.fold_in(own, 1), rows)]
    turn = jax.random.randint(jax.random.fold_in(own, 2), (rows, 1), 0, top)
    return jnp.take_along_axis(listing, (jnp.arange(top)[None, :] + turn) % top, axis=1)


def load_shares(count, total, limit, skew, full):
    loads = [(1 << 20) // math.isqrt(rank ** skew) + 1 for rank in range(1, count + 1)]
    largest = limit if full else min(limit, max(-(-total // count), total * loads[0] // sum(loads)))
    least = 1 if total - largest >= count - 1 else 0
    counts, surplus = [largest] + [least] * (count - 1), total - largest - least * (count - 1)
    while surplus > 0:
        candidates = [i for i in range(1, count) if counts[i] < largest] or [i for i in range(1, count) if counts[i] < limit]
        whole, budget = sum([loads[i] for i in candidates]), surplus
        for i in candidates:
            more = min(limit - counts[i], max(1, budget * loads[i] // whole), surplus)
            counts[i] = counts[i] + more
            surplus = surplus - more
    return np.array(counts)


def bell_draw(own_key, extent, deviation, most, pieces=(), kind=jnp.bfloat16):
    array = deviation * jax.random.normal(own_key, extent, jnp.float32)
    if pieces:
        array = array * block_scale(own_key, extent, pieces, -0.22, 0.18)
    return jnp.clip(array, -most, most).astype(kind)


def setup_inputs(seed: int = 0) -> dict:
    key_list = jax.random.split(jax.random.key(seed), 15)
    stream = bell_draw(key_list[0], (TOKENS, D), 1.0, 6.0, ((0, 8), (1, 4)))
    out_grad = bell_draw(key_list[1], (TOKENS, D), 1.0, 6.0, ((0, 8), (1, 4)))
    attn_gain = jnp.clip(1.0 + 0.18 * jax.random.normal(key_list[2], (D,), jnp.float32), 0.099609375, 1.8984375).astype(jnp.bfloat16)
    attn_router = bell_draw(key_list[3], (D, E), D ** -0.5, 0.125, ((0, 8),))
    key_value = bell_draw(key_list[4], (2, D, H * HS), D ** -0.5, 0.125, ((1, 8), (2, 4)))
    query_proj = bell_draw(key_list[5], (E, D, H * HS), (D // 2) ** -0.5, 0.1875, ((1, 8), (2, 4)))
    output_proj = bell_draw(key_list[6], (E, D, H * HS), (H * HS // 16) ** -0.5, 0.5, ((1, 8), (2, 4)))
    mlp_gain = jnp.clip(1.0 + 0.18 * jax.random.normal(key_list[7], (D,), jnp.float32), 0.099609375, 1.8984375).astype(jnp.bfloat16)
    mlp_router = bell_draw(key_list[8], (D, E), D ** -0.5, 0.125, ((0, 8),))
    expert_in = bell_draw(key_list[9], (E * SUBS, D, 2, F // SUBS), D ** -0.5, 0.125, ((0, 8), (3, 4)))
    expert_down = bell_draw(key_list[10], (E * SUBS, F // SUBS, D), (F // 4) ** -0.5, 0.15625, ((0, 8), (1, 4)))
    attn_routes_keys = jax.random.split(jax.random.fold_in(key_list[11], 1), TOKENS // TOK)
    attn_routes_turns = jax.random.permutation(jax.random.fold_in(key_list[11], 3), TOKENS // TOK)
    attn_routes = jax.vmap(lambda own, number: routed_block(jax.random.fold_in(key_list[11], 2), own, number, TOK, E, TOPK, SLOTS, 2))(attn_routes_keys, attn_routes_turns).reshape((TOKENS, TOPK))
    mlp_routes_keys = jax.random.split(jax.random.fold_in(key_list[12], 1), TOKENS // TOK)
    mlp_routes_turns = jax.random.permutation(jax.random.fold_in(key_list[12], 3), TOKENS // TOK)
    mlp_routes = jax.vmap(lambda own, number: routed_block(jax.random.fold_in(key_list[12], 2), own, number, TOK, E, TOPK, SLOTS, 2))(mlp_routes_keys, mlp_routes_turns).reshape((TOKENS, TOPK))
    doc_lengths = jax.vmap(lambda own: ragged(own, DOCS, TOK, LONGEST, 1))(jax.random.split(key_list[13], N_WIDE)).reshape((N_WIDE, DOCS)).astype(jnp.int32)
    return dict(stream=stream, out_grad=out_grad, attn_gain=attn_gain, attn_router=attn_router, key_value=key_value, query_proj=query_proj, output_proj=output_proj, mlp_gain=mlp_gain, mlp_router=mlp_router, expert_in=expert_in, expert_down=expert_down, attn_routes=attn_routes, mlp_routes=mlp_routes, doc_lengths=doc_lengths)


EPSILON = 1e-05
NEGATIVE = -1000000000.0
PRECISE = lax.Precision.HIGHEST

@jax.custom_vjp
def low(v):
    return lax.optimization_barrier(v.astype(jnp.bfloat16)).astype(jnp.float32)

@jax.custom_vjp
def low_back(v):
    return v

def low_keep(v):
    return (low(v), None)

def low_pass(kept, grad):
    return (grad,)

def back_keep(v):
    return (v, None)

def back_low(kept, grad):
    return (low(grad),)
low.defvjp(low_keep, low_pass)
low_back.defvjp(back_keep, back_low)

def rms_scale(values):
    return lax.rsqrt(lax.optimization_barrier(jnp.mean(values * values, axis=-1)) + EPSILON)

def expert_hot(routes):
    return (routes[:, :, None] == jnp.arange(E, dtype=jnp.int32)[None, None, :]).astype(jnp.float32)

def route_table(routes):
    flat_routes = routes.reshape(-1)
    one_hot = (flat_routes[:, None] == jnp.arange(E, dtype=jnp.int32)[None, :]).astype(jnp.int32)
    before = jnp.cumsum(one_hot, axis=0) - one_hot
    positions = lax.optimization_barrier(jnp.sum(before * one_hot, axis=1)).astype(jnp.int32)
    return (flat_routes, positions, positions < CAP)

def chosen_gates(logits, routes, keep_mask):
    picked = lax.optimization_barrier(jnp.sum(expert_hot(routes) * logits[:, None, :], axis=-1))
    return jax.nn.softmax(picked, axis=-1) * keep_mask.reshape(picked.shape).astype(jnp.float32)

def doc_mask(lengths):
    doc_ends = jnp.cumsum(lengths).astype(jnp.int32)
    positions = jnp.arange(TOK, dtype=jnp.int32)
    member = lax.optimization_barrier(jnp.sum((positions[:, None] >= doc_ends[None, :]).astype(jnp.int32), axis=1))
    return (member[:, None] == member[None, :]) & (positions[None, :] <= positions[:, None])

def attend_block(inputs, kv_weight, query_weight, out_weight):
    block_rows, block_routes, gate_vals, lengths = inputs
    score_scale = HS ** (-0.5)
    key_val = low(low_back(jnp.einsum('td,kdh->kth', block_rows, kv_weight, precision=PRECISE)))
    key_rows = key_val[0].reshape(TOK, H, HS)
    value_rows = key_val[1].reshape(TOK, H, HS)
    route_mask = expert_hot(block_routes)
    every_query = jnp.einsum('td,edh->teh', block_rows, query_weight, precision=PRECISE)
    query = low(low_back(jnp.einsum('tke,teh->tkh', route_mask, every_query, precision=PRECISE)))
    query_rows = query.reshape(TOK * 2, H, HS)
    allowed = jnp.repeat(doc_mask(lengths), 2, axis=0)
    scores = low_back(jnp.einsum('rhc,jhc->hrj', query_rows, key_rows, precision=PRECISE) * score_scale)
    scores = jnp.where(allowed[None, :, :], scores, NEGATIVE)
    weights = jax.nn.softmax(scores, axis=-1)
    context = low(low_back(jnp.einsum('hrj,jhc->rhc', low(weights), value_rows, precision=PRECISE)))
    context = context.reshape(TOK, 2, H * HS)
    mixed = jnp.einsum('tke,tk,tkh->teh', route_mask, gate_vals, context, precision=PRECISE)
    return jnp.einsum('teh,edh->td', mixed, out_weight, precision=PRECISE)

def reference(stream, out_grad, attn_gain, attn_router, key_value, query_proj, output_proj, mlp_gain, mlp_router, expert_in, expert_down, attn_routes, mlp_routes, doc_lengths):
    attn_flat, attn_place, attn_keep = route_table(attn_routes)
    mlp_flat, mlp_place, mlp_keep = route_table(mlp_routes)
    slot_pair = jnp.full((E, CAP), TOKENS * 2, jnp.int32)
    slot_pair = slot_pair.at[mlp_flat, jnp.where(mlp_keep, mlp_place, CAP)].set(jnp.arange(TOKENS * 2, dtype=jnp.int32), mode='drop')

    def forward(stream_in, gain_one, router_one, kv_weight, query_weight, out_weight, gain_two, router_two, up_weight, down_weight):
        scale_one = rms_scale(stream_in)
        normed_one = stream_in * scale_one[:, None] * gain_one
        gate_one = chosen_gates(jnp.dot(normed_one, router_one, precision=PRECISE), attn_routes, attn_keep)
        block_attend = partial(attend_block, kv_weight=kv_weight, query_weight=query_weight, out_weight=out_weight)
        attention = lax.map(jax.checkpoint(block_attend), (low(normed_one).reshape(N_WIDE, TOK, D), attn_routes.reshape(N_WIDE, TOK, 2), gate_one.reshape(N_WIDE, TOK, 2), doc_lengths))
        hidden = stream_in + low_back(attention.reshape(TOKENS, D))
        scale_two = rms_scale(hidden)
        normed_two = hidden * scale_two[:, None] * gain_two
        gate_two = chosen_gates(jnp.dot(normed_two, router_two, precision=PRECISE), mlp_routes, mlp_keep)
        normed_low = low(normed_two)
        up_all = up_weight.reshape(E, SUBS, D, 2, F // SUBS).transpose(0, 2, 3, 1, 4).reshape(E, D, 2, F)
        down_all = down_weight.reshape(E, F, D)

        def expert(inputs):
            up_expert, down_expert, pair_ids = inputs
            expert_rows = jnp.take(normed_low, pair_ids // 2, axis=0, mode='fill', fill_value=0.0)
            gate_up = low_back(jnp.einsum('cd,dkf->ckf', expert_rows, up_expert, precision=PRECISE))
            activation = low(jax.nn.silu(gate_up[:, 0]) * gate_up[:, 1])
            return low_back(jnp.dot(activation, down_expert, precision=PRECISE))
        expert_out = lax.map(jax.checkpoint(expert), (up_all, down_all, slot_pair))
        slot_gate = jnp.take(gate_two.reshape(-1), slot_pair, mode='fill', fill_value=0.0)
        mixture = jnp.zeros((TOKENS, D), jnp.float32).at[slot_pair // 2].add(expert_out * slot_gate[:, :, None], mode='drop')
        return hidden + mixture
    primals = (stream.astype(jnp.float32), attn_gain.astype(jnp.float32), attn_router.astype(jnp.float32), key_value.astype(jnp.float32), query_proj.astype(jnp.float32), output_proj.astype(jnp.float32), mlp_gain.astype(jnp.float32), mlp_router.astype(jnp.float32), expert_in.astype(jnp.float32), expert_down.astype(jnp.float32))
    layer_out, pullback = jax.vjp(forward, *primals)
    gradients = pullback(out_grad.astype(jnp.float32))
    return (layer_out, gradients[0], gradients[1], gradients[2], gradients[3], gradients[4], gradients[5], gradients[6], gradients[7], gradients[8], gradients[9])
```

```python
import jax
import jax.numpy as jnp
from jax import lax
from jax.sharding import PartitionSpec as P

HS = 128
E = 4
TOPK = 2
TOK = 128
SLOTS = 80

EPSILON = 1e-05
NEGATIVE = -1000000000.0
PRECISE = lax.Precision.HIGHEST
F32 = jnp.float32
BF16 = jnp.bfloat16


def dot(left, right, contract, precision=None):
    return lax.dot_general(
        left, right, ((contract[0], contract[1]), ((), ())), precision=precision, preferred_element_type=F32
    )


def xor_shuffle(values, amount):
    count, bit = values.shape[0], 1
    while bit < count:
        split = values.reshape((count // (2 * bit), 2, bit) + values.shape[1:])
        flipped = split[:, ::-1].reshape(values.shape)
        values = jnp.where((amount & bit) != 0, flipped, values)
        bit *= 2
    return values


def local(
    stream,
    out_grad,
    attn_gain,
    attn_router,
    key_value,
    query_proj,
    output_proj,
    mlp_gain,
    mlp_router,
    expert_in,
    expert_down,
    attn_routes,
    mlp_routes,
    doc_lengths,
):
    wide_count = lax.axis_size("wide")
    narrow_count = lax.axis_size("narrow")
    subs = wide_count // E
    wide = lax.axis_index("wide")
    narrow = lax.axis_index("narrow")
    plane, sub = wide // subs, wide % subs
    capacity = 9 * TOK * wide_count * TOPK // (8 * E)
    slice_width = stream.shape[1]
    shard_rows = attn_gain.shape[0]
    width = slice_width * narrow_count
    local_width = key_value.shape[2]
    head_count = local_width // HS
    hidden_units = expert_down.shape[1]
    score_scale = HS ** (-0.5)

    def by_plane(values, k):
        return lax.ppermute(values, "wide", [(i, i ^ (k * subs)) for i in range(wide_count)])

    def by_sub(values, k):
        return lax.ppermute(values, "wide", [(i, i ^ k) for i in range(wide_count)])

    def by_narrow(values, k):
        return lax.ppermute(values, "narrow", [(i, i ^ k) for i in range(narrow_count)])

    def swap(values):
        pairs = []
        for w in range(wide_count):
            for n in range(narrow_count):
                z, y = w // subs, w % subs
                pairs.append((w * narrow_count + n, (n * subs + y) * narrow_count + z))
        return lax.ppermute(values, ("wide", "narrow"), pairs)

    def gather_planes(values):
        return [values] + [by_plane(values, k) for k in range(1, E)]

    def exchange_planes(parts):
        return [parts[0]] + [by_plane(parts[k], k) for k in range(1, E)]

    def gather_subs(values):
        parts, bit = [values], 1
        while bit < subs:
            parts = parts + [by_sub(one, bit) for one in parts]
            bit *= 2
        return parts

    def reduce_subs(parts):
        bit = subs // 2
        while bit >= 1:
            parts = [parts[j] + by_sub(parts[j + bit].astype(BF16), bit).astype(F32) for j in range(bit)]
            bit //= 2
        return parts[0]

    def gather_narrow(values):
        two = jnp.stack([values, by_narrow(values, 2)])
        one = by_narrow(two, 1)
        return jnp.stack([two[0], one[0], two[1], one[1]])

    def reduce_narrow(parts):
        low = parts.astype(BF16)
        two = jnp.stack([parts[0], parts[1]]) + by_narrow(low[2:4], 2).astype(F32)
        return two[0] + by_narrow(two[1].astype(BF16), 1).astype(F32)

    def sum_narrow(values):
        values = values + by_narrow(values, 2)
        return values + by_narrow(values, 1)

    def sum_planes(values):
        values = values + by_plane(values, 1)
        return values + by_plane(values, 2)

    def sum_subs(values):
        bit = 1
        while bit < subs:
            values = values + by_sub(values, bit)
            bit *= 2
        return values

    own_rows = jnp.concatenate(
        [attn_gain[None, :], attn_router.T, mlp_gain[None, :], mlp_router.T], axis=0
    )
    own_routes = jnp.concatenate([attn_routes.T, mlp_routes.T], axis=0)
    route_rows = own_routes.astype(BF16).reshape(-1, shard_rows)
    packed = jnp.concatenate([own_rows, route_rows], axis=0)
    used = packed.shape[0]
    packed = jnp.pad(packed, ((0, -used % 16), (0, 0)))
    parts = gather_subs(packed)
    by_k = [gather_planes(one) for one in parts]
    table = jnp.stack([by_k[j][k] for k in range(E) for j in range(subs)])
    table = xor_shuffle(table, wide)
    gain_one = table[:, 0].reshape(width).astype(F32)
    router_one = table[:, 1:5].swapaxes(0, 1).reshape(E, width)
    gain_two = table[:, 5].reshape(width).astype(F32)
    router_two = table[:, 6:10].swapaxes(0, 1).reshape(E, width)
    routes = table[:, 10:used].reshape(wide_count, 4, TOK).astype(jnp.int32)

    experts = jnp.arange(E, dtype=jnp.int32)
    hot = (routes[:, :, :, None] == experts).astype(F32)
    hot = hot.reshape(wide_count, 2, 2, TOK, E)
    both = jnp.sum(hot, axis=2).swapaxes(0, 1)
    earlier = (jnp.arange(TOK)[:, None] > jnp.arange(TOK)[None, :]).astype(BF16)
    rank = jnp.einsum("ts,awse->awte", earlier, both.astype(BF16), preferred_element_type=F32)
    counts = jnp.sum(both, axis=2)
    blocks = jnp.arange(wide_count)
    prefix = jnp.sum(
        jnp.where((blocks[:, None] > blocks[None, :])[None, :, :, None], counts[:, None], 0.0), axis=2
    )
    kept = both * ((prefix[:, :, None, :] + rank) < capacity).astype(F32)

    def pick(values, index):
        return lax.dynamic_index_in_dim(values, index, 0, False)

    turned = narrow * subs + sub
    hot_one = pick(hot[:, 0], wide)
    keep_one = jnp.sum(hot_one * pick(kept[0], wide)[None], axis=-1)
    hot_two = pick(hot[:, 1], turned)
    kept_two = pick(kept[1], turned)
    rank_two = pick(rank[1], turned)
    keep_two = jnp.sum(hot_two * kept_two[None], axis=-1)
    slots = jnp.arange(SLOTS, dtype=F32)
    rank_k = xor_shuffle(rank_two.T, plane)
    kept_k = xor_shuffle(kept_two.T, plane)
    select = jnp.where(
        (rank_k[:, None, :] == slots[None, :, None]) & (kept_k[:, None, :] > 0), 1.0, 0.0
    ).astype(BF16)
    own_expert = (experts == plane).astype(F32)
    rank_m = xor_shuffle(jnp.sum(rank[1] * own_expert, axis=-1), turned)
    kept_m = xor_shuffle(jnp.sum(kept[1] * own_expert, axis=-1), turned)
    both_m = xor_shuffle(both[1], turned)
    select_m = jnp.where(
        (rank_m[:, None, :] == slots[None, :, None]) & (kept_m[:, None, :] > 0), 1.0, 0.0
    ).astype(BF16)
    row_hot = jnp.einsum("wst,wte->wse", select_m, both_m.astype(BF16), preferred_element_type=F32)
    row_hot = row_hot.reshape(-1, E)

    hot_k = hot[:, 0].reshape(E, subs, 2, TOK, E)
    hot_k = lax.dynamic_index_in_dim(hot_k, sub, 1, False)
    hot_k = xor_shuffle(hot_k, plane)

    kv_parts = gather_subs(key_value)
    query_parts = gather_subs(query_proj)
    home_stream = stream.astype(F32)
    turned_stream = swap(stream)
    turned_grad = swap(out_grad)

    def widen(values):
        everyone = xor_shuffle(gather_narrow(values), narrow ^ plane)
        pieces = everyone.reshape(E, TOK, subs, shard_rows).transpose(2, 0, 1, 3)
        return xor_shuffle(pieces, sub)

    def own_slice(vector, place):
        return lax.dynamic_slice_in_dim(vector, place * slice_width, slice_width, vector.ndim - 1)

    gain_one_plane = own_slice(gain_one, plane)
    gain_two_plane = own_slice(gain_two, plane)
    router_two_plane = own_slice(router_two, plane).astype(F32)
    gain_one_home = own_slice(gain_one, narrow)
    router_one_home = own_slice(router_one, narrow).astype(F32)

    wide_stream = widen(turned_stream)
    gain_pieces = xor_shuffle(gain_one_plane.reshape(subs, shard_rows), sub)
    gained = (wide_stream.astype(F32) * gain_pieces[:, None, None, :]).astype(BF16)
    gained = gained.reshape(subs, E * TOK, shard_rows)

    def project(rows, weights):
        total = None
        for j in range(subs):
            one = jnp.einsum("td,adc->atc", rows[j], weights[j], preferred_element_type=F32)
            total = one if total is None else total + one
        return total

    def choose(every):
        shaped = every.reshape(E, E, TOK, -1)
        pairs = []
        for k2 in range(TOPK):
            mask = hot_k[:, k2]
            total = jnp.where(mask[:, :, 0:1] > 0, shaped[0], 0.0)
            for e in range(1, E):
                total = jnp.where(mask[:, :, e : e + 1] > 0, shaped[e], total)
            pairs.append(total)
        return jnp.stack(pairs, axis=1)

    def scatter_planes(partial):
        got = exchange_planes([None] + [partial[k].astype(BF16) for k in range(1, E)])
        total = partial[0]
        for k in range(1, E):
            total = total + got[k].astype(F32)
        return total

    kv_partial = project(gained, kv_parts).reshape(2, E, TOK, local_width).swapaxes(0, 1)
    key_val = scatter_planes(kv_partial)
    query_partial = choose(project(gained, query_parts))
    query_raw = scatter_planes(query_partial)

    gained_home = home_stream * gain_one_home
    stats_one = jnp.concatenate(
        [
            jnp.sum(home_stream * home_stream, axis=-1)[None],
            dot(router_one_home, gained_home, ((1,), (1,)), PRECISE),
        ],
        axis=0,
    )
    stats_one = sum_narrow(stats_one)
    scale_one = lax.rsqrt(stats_one[0] / width + EPSILON)
    logits_one = (stats_one[1:] * scale_one).T

    def gates(logits, hots):
        picked = jnp.sum(hots * logits[None], axis=-1)
        gap = picked[0] - picked[1]
        return jnp.stack([jax.nn.sigmoid(gap), jax.nn.sigmoid(-gap)])

    prob_one = gates(logits_one, hot_one)
    gate_one = prob_one * keep_one
    key_val = (key_val * scale_one[None, :, None]).astype(BF16)
    query = (query_raw * scale_one[None, :, None]).astype(BF16)

    doc_ends = jnp.cumsum(doc_lengths[0])
    positions = jnp.arange(TOK, dtype=jnp.int32)
    member = jnp.sum((positions[:, None] >= doc_ends[None, :]).astype(jnp.int32), axis=1)
    allowed = (member[:, None] == member[None, :]) & (positions[None, :] <= positions[:, None])
    allowed = jnp.concatenate([allowed, allowed], axis=0)
    query_rows = query.reshape(TOPK * TOK, head_count, HS)
    key_rows = key_val[0].reshape(TOK, head_count, HS)
    value_rows = key_val[1].reshape(TOK, head_count, HS)
    scores = (
        jnp.einsum("rhc,jhc->hrj", query_rows, key_rows, preferred_element_type=F32) * score_scale
    )
    scores = jnp.where(allowed[None], scores, NEGATIVE)
    exp_scores = jnp.exp(scores - jnp.max(scores, axis=-1, keepdims=True))
    probs = exp_scores / jnp.sum(exp_scores, axis=-1, keepdims=True)
    probs_low = probs.astype(BF16)
    context = jnp.einsum("hrj,jhc->rhc", probs_low, value_rows, preferred_element_type=F32).astype(BF16)
    context = context.reshape(TOPK, TOK, local_width)
    gated = (context.astype(F32) * gate_one[:, :, None]).astype(BF16)

    out_parts = gather_subs(output_proj)

    def spread(pairs):
        result = []
        for e in range(E):
            first = jnp.where(hot_k[:, 0, :, e : e + 1] > 0, pairs[:, 0], jnp.zeros((), BF16))
            one = jnp.where(hot_k[:, 1, :, e : e + 1] > 0, pairs[:, 1], first)
            result.append(one.reshape(E * TOK, -1))
        return result

    def back(rows, weights):
        total = None
        for a in range(len(rows)):
            one = dot(rows[a], weights[a], ((1,), (1,)))
            total = one if total is None else total + one
        return total

    def to_turned(pieces):
        by_block = jnp.stack(pieces).reshape(subs, E, TOK, shard_rows).transpose(1, 0, 2, 3)
        by_block = xor_shuffle(by_block, narrow ^ plane)
        total = xor_shuffle(reduce_narrow(by_block), sub)
        return total.transpose(1, 0, 2).reshape(TOK, slice_width)

    mixed = spread(jnp.stack(gather_planes(gated)))
    attention = to_turned([back(mixed, out_parts[j]) for j in range(subs)])
    hidden = turned_stream.astype(F32) + attention

    def dispatch(rows):
        picked = jnp.einsum("kst,td->ksd", select, rows, preferred_element_type=F32).astype(BF16)
        got = xor_shuffle(jnp.stack(exchange_planes([picked[k] for k in range(E)])), plane)
        full = got.swapaxes(0, 1).reshape(SLOTS, width)
        full = jnp.stack(gather_subs(full))
        return gather_narrow(full).reshape(-1, width)

    grad_rows = dispatch(turned_grad)
    weight_in = expert_in[0]
    weight_down = expert_down[0]
    dact_raw = dot(grad_rows, weight_down, ((1,), (1,)))

    expert_rows = dispatch((hidden * gain_two_plane).astype(BF16))
    stats_two = jnp.concatenate(
        [
            jnp.sum(hidden * hidden, axis=-1)[None],
            dot(router_two_plane, hidden * gain_two_plane, ((1,), (1,)), PRECISE),
        ],
        axis=0,
    )
    stats_two = sum_planes(stats_two)
    scale_two = lax.rsqrt(stats_two[0] / width + EPSILON)
    logits_two = (stats_two[1:] * scale_two).T
    prob_two = gates(logits_two, hot_two)

    rows_float = expert_rows.astype(F32) / gain_two
    row_scale = lax.rsqrt(jnp.sum(rows_float * rows_float, axis=-1, keepdims=True) / width + EPSILON)
    row_logits = dot(expert_rows, router_two, ((1,), (1,)))
    row_gap = jnp.sum((2.0 * own_expert[None, :] - row_hot) * row_logits, axis=-1, keepdims=True)
    row_gate = jax.nn.sigmoid(row_gap * row_scale)
    gate_up = jnp.einsum("rd,dkf->krf", expert_rows, weight_in, preferred_element_type=F32)
    gate_pre = gate_up[0] * row_scale
    up_pre = gate_up[1] * row_scale
    gate_sig = jax.nn.sigmoid(gate_pre)
    silu_gate = gate_pre * gate_sig
    activation = (silu_gate * up_pre).astype(BF16)
    dactiv = dact_raw * row_gate
    dgate_pre = (dactiv * up_pre * gate_sig * (1.0 + gate_pre * (1.0 - gate_sig))).astype(BF16)
    dup_pre = (dactiv * silu_gate).astype(BF16)
    dprob_rows = jnp.sum(activation.astype(F32) * dact_raw, axis=-1)
    inner_rows = jnp.sum(dgate_pre.astype(F32) * gate_pre + dup_pre.astype(F32) * up_pre, axis=-1)
    drows = jnp.einsum(
        "krf,dkf->rd", jnp.stack([dgate_pre, dup_pre]), weight_in, preferred_element_type=F32
    )
    lanes = jnp.arange(128)
    row_stats = jnp.where(
        lanes[None, :] == 0, dprob_rows[:, None], jnp.where(lanes[None, :] == 1, inner_rows[:, None], 0.0)
    )

    def give_back(rows):
        shaped = rows.reshape(narrow_count, subs, SLOTS, -1)
        low = shaped.astype(BF16)
        got = by_narrow(jnp.stack([low[1], low[3]]), 1)
        two = jnp.stack([shaped[0], shaped[2]]) + got.astype(F32)
        one = two[0] + by_narrow(two[1].astype(BF16), 2).astype(F32)
        return reduce_subs([one[j] for j in range(subs)])

    def from_planes(rows, extra=None):
        pieces = rows.astype(BF16).reshape(SLOTS, E, slice_width).swapaxes(0, 1)
        pieces = xor_shuffle(pieces, plane)
        if extra is not None:
            more = jnp.broadcast_to(extra.astype(BF16)[None], (E,) + extra.shape)
            pieces = jnp.concatenate([pieces, more], axis=-1)
        return jnp.stack(exchange_planes([pieces[k] for k in range(E)]))

    returned = give_back(jnp.concatenate([drows, row_stats], axis=1))
    returned = from_planes(returned[:, :width], returned[:, width:])
    combined = jnp.einsum("kst,ksd->ktd", select, returned, preferred_element_type=F32)
    per_expert = xor_shuffle(combined[:, :, slice_width : slice_width + 2], plane)
    dprob_two = keep_two * jnp.sum(hot_two * per_expert[:, :, 0].T[None], axis=-1)
    inner_two = jnp.sum(per_expert[:, :, 1], axis=0)
    dnormed_two = jnp.sum(combined[:, :, :slice_width], axis=0)

    def gate_back(prob, dprob, hots):
        dselect = prob * (dprob - jnp.sum(prob * dprob, axis=0, keepdims=True))
        return jnp.sum(hots * dselect[:, :, None], axis=0)

    dlogit_two = gate_back(prob_two, dprob_two, hot_two)
    dnormed_two = dnormed_two + dot(dlogit_two, router_two_plane, ((1,), (0,)), PRECISE)
    inner_two = inner_two + jnp.sum(dlogit_two * logits_two, axis=-1)
    dhidden = (
        turned_grad.astype(F32)
        + scale_two[:, None] * (dnormed_two * gain_two_plane)
        - hidden * (scale_two * scale_two * inner_two / width)[:, None]
    )
    scaled_hidden = hidden * scale_two[:, None]
    mlp_terms = jnp.concatenate(
        [
            jnp.sum(dnormed_two * scaled_hidden, axis=0)[None],
            dot(dlogit_two, scaled_hidden * gain_two_plane, ((0,), (0,)), PRECISE),
        ],
        axis=0,
    )

    wide_grad = widen(dhidden.astype(BF16)).reshape(subs, E * TOK, shard_rows)
    dcontext_raw = scatter_planes(choose(project(wide_grad, out_parts)))
    output_grad = reduce_subs(
        [jnp.stack([dot(wide_grad[j], mixed[e], ((0,), (0,))) for e in range(E)]) for j in range(subs)]
    )
    dcontext = (dcontext_raw * gate_one[:, :, None]).astype(BF16)
    dcontext_rows = dcontext.reshape(TOPK * TOK, head_count, HS)
    dweights = jnp.einsum("rhc,jhc->hrj", dcontext_rows, value_rows, preferred_element_type=F32)
    dscores = (probs * (dweights - jnp.sum(probs * dweights, axis=-1, keepdims=True))).astype(BF16)
    dquery = (
        jnp.einsum("hrj,jhc->rhc", dscores, key_rows, preferred_element_type=F32) * score_scale
    ).reshape(TOPK, TOK, local_width)
    dkeys = (
        jnp.einsum("hrj,rhc->jhc", dscores, query_rows, preferred_element_type=F32) * score_scale
    ).reshape(TOK, local_width)
    dvalues = jnp.einsum(
        "hrj,rhc->jhc", probs_low, dcontext_rows, preferred_element_type=F32
    ).reshape(TOK, local_width)
    dkey_val = jnp.stack([dkeys, dvalues])
    home_sums = jnp.concatenate(
        [
            jnp.sum(context.astype(F32) * dcontext_raw, axis=-1),
            (
                jnp.sum(dquery * query.astype(F32), axis=(0, 2))
                + jnp.sum(dkey_val * key_val.astype(F32), axis=(0, 2))
            )[None],
        ],
        axis=0,
    )
    home_sums = sum_narrow(home_sums)
    dprob_one = keep_one * home_sums[:2]
    dlogit_one = gate_back(prob_one, dprob_one, hot_one)
    inner_one = home_sums[2] + jnp.sum(dlogit_one * logits_one, axis=-1)
    dlogit_scaled = dlogit_one * scale_one[:, None]

    dkv_low = (dkey_val * scale_one[None, :, None]).astype(BF16)
    dkv_all = jnp.stack(gather_planes(dkv_low), axis=1).reshape(2, E * TOK, local_width)
    dlogit_low = dlogit_scaled.T.astype(BF16)
    dlogit_rest = (dlogit_scaled.T - dlogit_low.astype(F32)).astype(BF16)
    dlogit_rows = jnp.concatenate([dlogit_low.reshape(1, -1), dlogit_rest.reshape(1, -1)], axis=0)
    dquery_low = (dquery * scale_one[None, :, None]).astype(BF16).reshape(TOPK * TOK, local_width)
    dquery_sent = jnp.concatenate([dquery_low, jnp.pad(dlogit_rows, ((0, 14), (0, 0)))], axis=0)
    dquery_all = jnp.stack(gather_planes(dquery_sent))
    dlogit_all = jnp.sum(dquery_all[:, TOPK * TOK : TOPK * TOK + 2].astype(F32), axis=1)
    dlogit_all = dlogit_all.reshape(E, E, TOK).swapaxes(1, 2).reshape(E * TOK, E)
    dquery_all = dquery_all[:, : TOPK * TOK].reshape(E, TOPK, TOK, local_width)
    dmixed = spread(dquery_all)

    kv_grad = reduce_subs(
        [jnp.stack([dot(gained[j], dkv_all[a], ((0,), (0,))) for a in range(2)]) for j in range(subs)]
    )
    query_grad = reduce_subs(
        [jnp.stack([dot(gained[j], dmixed[e], ((0,), (0,))) for e in range(E)]) for j in range(subs)]
    )
    dnormed_one = to_turned(
        [
            back([dkv_all[0], dkv_all[1]], kv_parts[j]) + back(dmixed, query_parts[j])
            for j in range(subs)
        ]
    )
    turned_out = dhidden + dnormed_one * gain_one_plane
    home_out = swap(turned_out.astype(BF16)).astype(F32)
    stream_grad = (
        home_out
        + gain_one_home * dot(dlogit_scaled, router_one_home, ((1,), (0,)), PRECISE)
        - home_stream * (scale_one * scale_one * inner_one / width)[:, None]
    )

    gain_term = jnp.sum(dnormed_one * turned_stream.astype(F32), axis=0)
    small = jnp.concatenate([mlp_terms, gain_term[None]], axis=0)
    small = sum_narrow(small)
    gained_plane = xor_shuffle(gained, sub).transpose(1, 0, 2).reshape(E * TOK, slice_width)
    router_term = dot(dlogit_all, gained_plane.astype(F32), ((0,), (0,)), PRECISE)
    small = sum_subs(jnp.concatenate([small, router_term], axis=0))
    mine = lax.dynamic_slice_in_dim(small, sub * shard_rows, shard_rows, 1)
    router_one_grad = mine[6:10]
    gain_one_grad = mine[5] + jnp.sum(
        router_one_grad * attn_router.T.astype(F32), axis=0
    ) / attn_gain.astype(F32)

    expert_out = dot(activation, weight_down, ((1,), (0,))) * row_gate
    mixture = from_planes(give_back(expert_out))
    mixture = jnp.einsum("kst,ksd->td", select, mixture, preferred_element_type=F32)
    layer_out = swap((hidden + mixture).astype(BF16)).astype(F32)
    gated_act = (activation.astype(F32) * row_gate).astype(BF16)
    down_grad = dot(gated_act, grad_rows, ((0,), (0,)))
    dboth = jnp.stack(
        [
            (dgate_pre.astype(F32) * row_scale).astype(BF16),
            (dup_pre.astype(F32) * row_scale).astype(BF16),
        ],
        axis=1,
    )
    up_grad = jnp.einsum("rd,rkf->dkf", expert_rows, dboth, preferred_element_type=F32)

    return (
        layer_out,
        stream_grad,
        gain_one_grad,
        router_one_grad.T,
        kv_grad,
        query_grad,
        output_grad,
        mine[0],
        mine[1:5].T,
        up_grad[None],
        down_grad[None],
    )


def solution(mesh):
    in_specs = (
        P("wide", "narrow"),
        P("wide", "narrow"),
        P("wide"),
        P("wide", None),
        P(None, "wide", "narrow"),
        P(None, "wide", "narrow"),
        P(None, "wide", "narrow"),
        P("wide"),
        P("wide", None),
        P("wide", None, None, "narrow"),
        P("wide", "narrow", None),
        P("wide", None),
        P("wide", None),
        P("wide", None),
    )
    out_specs = (
        P("wide", "narrow"),
        P("wide", "narrow"),
        P("wide"),
        P("wide", None),
        P(None, "wide", "narrow"),
        P(None, "wide", "narrow"),
        P(None, "wide", "narrow"),
        P("wide"),
        P("wide", None),
        P("wide", None, None, "narrow"),
        P("wide", "narrow", None),
    )
    return jax.shard_map(local, mesh=mesh, in_specs=in_specs, out_specs=out_specs, check_vma=False)
```

```python
import jax
import jax.numpy as jnp
from jax import lax
from jax.experimental import pallas as pl
from jax.experimental.pallas import tpu as pltpu
from jax.sharding import PartitionSpec as P

HS = 128
E = 4
TOPK = 2
TOK = 128
SLOTS = 80

EPSILON = 1e-05
NEGATIVE = -1000000000.0
PRECISE = lax.Precision.HIGHEST
F32 = jnp.float32
BF16 = jnp.bfloat16


def dot(left, right, contract, precision=None):
    return lax.dot_general(
        left, right, ((contract[0], contract[1]), ((), ())), precision=precision, preferred_element_type=F32
    )


def xor_shuffle(values, amount):
    count, bit = values.shape[0], 1
    while bit < count:
        split = values.reshape((count // (2 * bit), 2, bit) + values.shape[1:])
        flipped = split[:, ::-1].reshape(values.shape)
        values = jnp.where((amount & bit) != 0, flipped, values)
        bit *= 2
    return values


NN = (((1,), (0,)), ((), ()))
NT = (((1,), (1,)), ((), ()))
TN = (((0,), (0,)), ((), ()))


def mul(left, right, form):
    return lax.dot_general(left, right, form, preferred_element_type=F32)


def shape(dims, dtype):
    return jax.ShapeDtypeStruct(tuple(dims), dtype)


def run(name, body, outs, args, scratch=()):
    vector = pl.BlockSpec(memory_space=pltpu.VMEM)
    return pl.pallas_call(
        body,
        out_shape=tuple(outs),
        in_specs=[pl.BlockSpec(memory_space=pltpu.SMEM)] + [vector] * (len(args) - 1),
        out_specs=tuple(vector for _ in outs),
        scratch_shapes=list(scratch),
        name=name,
    )(*args)


def place(store, parts, sub, first=0):
    for j, part in enumerate(parts):
        rows = part.shape[1]
        start = pl.multiple_of((sub ^ j) * rows, rows)
        for a in range(part.shape[0]):
            store[first + a, pl.ds(start, rows), :] = part[a]


def block(index):
    return pl.ds(pl.multiple_of(index * TOK, TOK), TOK)


def send_blocks(total, outs, order):
    for k in range(E):
        for a in range(total.shape[0]):
            outs[k][a] = total[a, block(order ^ k), :].astype(outs[k].dtype)


def key_value_body(subs):
    def body(at, *refs):
        rows, gain, parts = refs[:E], refs[E], refs[E + 1 : E + 1 + subs]
        gained, *outs = refs[E + 1 + subs : E + 2 + subs + E]
        weights, total = refs[E + 2 + subs + E :]
        place(weights, parts, at[1])
        for q in range(E):
            gained[q * TOK : (q + 1) * TOK, :] = (rows[q][...].astype(F32) * gain[...]).astype(BF16)
        for a in range(2):
            total[a] = mul(gained[...], weights[a], NN)
        send_blocks(total, outs, at[0])

    return body


def routed_body(subs, joined):
    count = 1 if joined else E

    def body(at, *refs):
        rows, hot, parts = refs[:count], refs[count], refs[count + 1 : count + 1 + subs]
        rest = refs[count + 1 + subs :]
        if joined:
            wide = rows[0]
        else:
            wide, rest = rest[0], rest[1:]
            for q in range(E):
                wide[q * TOK : (q + 1) * TOK, :] = rows[q][...]
        outs, weights, total = rest[:E], rest[E], rest[E + 1]
        place(weights, parts, at[1])
        for e in range(E):
            every = mul(wide[...], weights[e], NN)
            for i in range(TOPK):
                mine = every * hot[:, i * E + e : i * E + e + 1]
                total[i] = mine if e == 0 else total[i] + mine
        send_blocks(total, outs, at[0])

    return body


def spread_pairs(at, rows, hot, out):
    for k in range(E):
        where = block(at[0] ^ k)
        mask = hot[where, :].astype(BF16)
        for e in range(E):
            out[e, where, :] = (
                rows[k][0] * mask[:, e : e + 1] + rows[k][1] * mask[:, E + e : E + e + 1]
            )


def fold_out(total, keep_0, keep_2, send):
    keep_0[...] = total[0:TOK]
    keep_2[...] = total[2 * TOK : 3 * TOK]
    send[0] = total[TOK : 2 * TOK].astype(BF16)
    send[1] = total[3 * TOK : 4 * TOK].astype(BF16)


def output_body(subs):
    def body(at, *refs):
        rows, hot, parts = refs[:E], refs[E], refs[E + 1 : E + 1 + subs]
        mixed, keep_0, keep_2, send, weights = refs[E + 1 + subs :]
        place(weights, parts, at[1])
        spread_pairs(at, rows, hot, mixed)
        total = mul(mixed[0], weights[0], NT)
        for e in range(1, E):
            total = total + mul(mixed[e], weights[e], NT)
        fold_out(total, keep_0, keep_2, send)

    return body


def spread_body(at, *refs):
    spread_pairs(at, refs[:E], refs[E], refs[E + 1])


def input_body(subs):
    def body(at, *refs):
        rows, dmixed = refs[:E], refs[E]
        kv_parts = refs[E + 1 : E + 1 + subs]
        query_parts = refs[E + 1 + subs : E + 1 + 2 * subs]
        dkv_all, keep_0, keep_2, send, weights = refs[E + 1 + 2 * subs :]
        place(weights, kv_parts, at[1])
        place(weights, query_parts, at[1], 2)
        for k in range(E):
            for a in range(2):
                dkv_all[a, block(at[0] ^ k), :] = rows[k][a]
        total = mul(dkv_all[0], weights[0], NT) + mul(dkv_all[1], weights[1], NT)
        for e in range(E):
            total = total + mul(dmixed[e], weights[2 + e], NT)
        fold_out(total, keep_0, keep_2, send)

    return body


def weight_grad_body(at, rows, other, *refs):
    parts, total = refs[:-1], refs[-1]
    for a in range(other.shape[0]):
        total[...] = mul(rows[...], other[a], TN)
        for j, part in enumerate(parts):
            count = part.shape[1]
            start = pl.multiple_of((at[1] ^ j) * count, count)
            part[a] = total[pl.ds(start, count), :].astype(part.dtype)


def attention_mask(at):
    row = lax.broadcasted_iota(jnp.int32, (TOK, TOK), 0)
    col = lax.broadcasted_iota(jnp.int32, (TOK, TOK), 1)
    row_doc, col_doc, end = jnp.zeros_like(row), jnp.zeros_like(row), 0
    for d in range(4):
        end = end + at[d]
        row_doc = row_doc + (row >= end).astype(jnp.int32)
        col_doc = col_doc + (col >= end).astype(jnp.int32)
    return (row_doc == col_doc) & (col <= row)


def attention_body(at, own_kv, *refs):
    got_kv, own_query, got_query = refs[: E - 1], refs[E - 1], refs[E : 2 * E - 1]
    cols, low, probs, context, gated = refs[2 * E - 1 :]
    scale = cols[:, 0:1]
    for a in range(4):
        own, got = (own_kv, got_kv) if a < 2 else (own_query, got_query)
        total = own[a % 2]
        for one in got:
            total = total + one[a % 2].astype(F32)
        low[a] = (total * scale).astype(BF16)
    allowed = attention_mask(at)
    for h in range(low.shape[2] // HS):
        head = slice(h * HS, (h + 1) * HS)
        for i in range(TOPK):
            scores = mul(low[2 + i, :, head], low[0, :, head], NT) * HS ** (-0.5)
            scores = jnp.where(allowed, scores, NEGATIVE)
            top = jnp.exp(scores - jnp.max(scores, axis=-1, keepdims=True))
            prob = top / jnp.sum(top, axis=-1, keepdims=True)
            probs[h, i * TOK : (i + 1) * TOK, :] = prob
            mixed = mul(prob.astype(BF16), low[1, :, head], NN).astype(BF16)
            context[i, :, head] = mixed
            gated[i, :, head] = (mixed.astype(F32) * cols[:, 1 + i : 2 + i]).astype(BF16)


def attention_back_body(at, own, *refs):
    got = refs[: E - 1]
    cols, low, probs, context, dquery, dkey_val, sums = refs[E - 1 :]
    scale = cols[:, 0:1]
    inner = jnp.zeros((TOK, 1), F32)
    dprob = []
    dcontext = []
    for i in range(TOPK):
        raw = own[i]
        for one in got:
            raw = raw + one[i].astype(F32)
        dprob.append(jnp.sum(context[i].astype(F32) * raw, axis=-1, keepdims=True))
        dcontext.append((raw * cols[:, 1 + i : 2 + i]).astype(BF16))
    for h in range(low.shape[2] // HS):
        head = slice(h * HS, (h + 1) * HS)
        key, value = low[0, :, head], low[1, :, head]
        dkey = jnp.zeros((TOK, HS), F32)
        dvalue = jnp.zeros((TOK, HS), F32)
        for i in range(TOPK):
            query = low[2 + i, :, head]
            grad = dcontext[i][:, head]
            prob = probs[h, i * TOK : (i + 1) * TOK, :]
            dweight = mul(grad, value, NT)
            dscore = prob * (dweight - jnp.sum(prob * dweight, axis=-1, keepdims=True))
            dscore = dscore.astype(BF16)
            done = mul(dscore, key, NN) * HS ** (-0.5)
            dkey = dkey + mul(dscore, query, TN)
            dvalue = dvalue + mul(prob.astype(BF16), grad, TN)
            inner = inner + jnp.sum(done * query.astype(F32), axis=-1, keepdims=True)
            dquery[i, :, head] = (done * scale).astype(BF16)
        dkey = dkey * HS ** (-0.5)
        inner = inner + jnp.sum(
            dkey * key.astype(F32) + dvalue * value.astype(F32), axis=-1, keepdims=True
        )
        dkey_val[0, :, head] = (dkey * scale).astype(BF16)
        dkey_val[1, :, head] = (dvalue * scale).astype(BF16)
    lane = lax.broadcasted_iota(jnp.int32, (TOK, TOK), 1)
    table = jnp.where(lane == 0, dprob[0], jnp.where(lane == 1, dprob[1], jnp.where(lane == 2, inner, 0.0)))
    sums[...] = jnp.transpose(table)[0:8]


def join_body(at, *refs):
    pieces, out = refs[:E], refs[E]
    size = pieces[0].shape[1]
    for k in range(E):
        for p in range(E):

            @pl.when((at[2] ^ k) == p)
            def _(k=k, p=p):
                out[:, p * size : (p + 1) * size] = pieces[k][...]


def split_body(extra):
    def body(at, own, got, *refs):
        outs, store = refs[:E], refs[E]
        store[...] = (own[...] + got[...].astype(F32)).astype(BF16)
        size = outs[0].shape[1] - extra
        for k in range(E):
            for p in range(E):

                @pl.when((at[2] ^ k) == p)
                def _(k=k, p=p):
                    outs[k][:, :size] = store[:, p * size : (p + 1) * size]

            if extra:
                outs[k][:, size:] = store[:, E * size :]

    return body


def local(
    stream,
    out_grad,
    attn_gain,
    attn_router,
    key_value,
    query_proj,
    output_proj,
    mlp_gain,
    mlp_router,
    expert_in,
    expert_down,
    attn_routes,
    mlp_routes,
    doc_lengths,
):
    wide_count = lax.axis_size("wide")
    narrow_count = lax.axis_size("narrow")
    subs = wide_count // E
    wide = lax.axis_index("wide")
    narrow = lax.axis_index("narrow")
    plane, sub = wide // subs, wide % subs
    capacity = 9 * TOK * wide_count * TOPK // (8 * E)
    slice_width = stream.shape[1]
    shard_rows = attn_gain.shape[0]
    width = slice_width * narrow_count
    local_width = key_value.shape[2]
    head_count = local_width // HS
    hidden_units = expert_down.shape[1]
    score_scale = HS ** (-0.5)

    def by_plane(values, k):
        return lax.ppermute(values, "wide", [(i, i ^ (k * subs)) for i in range(wide_count)])

    def by_sub(values, k):
        return lax.ppermute(values, "wide", [(i, i ^ k) for i in range(wide_count)])

    def by_narrow(values, k):
        return lax.ppermute(values, "narrow", [(i, i ^ k) for i in range(narrow_count)])

    def swap(values):
        pairs = []
        for w in range(wide_count):
            for n in range(narrow_count):
                z, y = w // subs, w % subs
                pairs.append((w * narrow_count + n, (n * subs + y) * narrow_count + z))
        return lax.ppermute(values, ("wide", "narrow"), pairs)

    def gather_planes(values):
        return [values] + [by_plane(values, k) for k in range(1, E)]

    def exchange_planes(parts):
        return [parts[0]] + [by_plane(parts[k], k) for k in range(1, E)]

    def gather_subs(values):
        parts, bit = [values], 1
        while bit < subs:
            parts = parts + [by_sub(one, bit) for one in parts]
            bit *= 2
        return parts

    def reduce_subs(parts):
        bit = len(parts) // 2
        while bit >= 1:
            parts = [parts[j] + by_sub(parts[j + bit].astype(BF16), bit).astype(F32) for j in range(bit)]
            bit //= 2
        return parts[0]

    def gather_narrow(values):
        other = by_narrow(values, 2)
        return [values, by_narrow(values, 1), other, by_narrow(other, 1)]

    def reduce_narrow(keep_0, keep_2, send):
        got = by_narrow(send, 1)
        other = by_narrow((keep_2 + got[1].astype(F32)).astype(BF16), 2)
        return keep_0 + got[0].astype(F32) + other.astype(F32)

    def finish_subs(keep, send):
        bit = len(keep)
        keep = [keep[j] + by_sub(send[j], bit).astype(F32) for j in range(bit)]
        return reduce_subs(keep)

    def sum_narrow(values):
        values = values + by_narrow(values, 2)
        return values + by_narrow(values, 1)

    def sum_planes(values):
        values = values + by_plane(values, 1)
        return values + by_plane(values, 2)

    def sum_subs(values):
        bit = 1
        while bit < subs:
            values = values + by_sub(values, bit)
            bit *= 2
        return values

    own_rows = jnp.concatenate(
        [attn_gain[None, :], attn_router.T, mlp_gain[None, :], mlp_router.T], axis=0
    )
    own_routes = jnp.concatenate([attn_routes.T, mlp_routes.T], axis=0)
    route_rows = own_routes.astype(BF16).reshape(-1, shard_rows)
    packed = jnp.concatenate([own_rows, route_rows], axis=0)
    used = packed.shape[0]
    packed = jnp.pad(packed, ((0, -used % 16), (0, 0)))
    parts = gather_subs(packed)
    table = jnp.stack(gather_planes(jnp.stack(parts)))
    table = table.reshape((wide_count,) + packed.shape)
    table = xor_shuffle(table, wide)
    near = xor_shuffle(jnp.stack(parts), sub)
    gain_one_plane = near[:, 0].reshape(slice_width).astype(F32)
    gain_two_plane = near[:, 5].reshape(slice_width).astype(F32)
    router_two_plane = near[:, 6:10].swapaxes(0, 1).reshape(E, slice_width).astype(F32)
    gain_one = table[:, 0].reshape(width).astype(F32)
    router_one = table[:, 1:5].swapaxes(0, 1).reshape(E, width)
    gain_two = table[:, 5].reshape(width).astype(F32)
    router_two = table[:, 6:10].swapaxes(0, 1).reshape(E, width)
    routes = table[:, 10:used].reshape(wide_count, 4, TOK).astype(jnp.int32)

    experts = jnp.arange(E, dtype=jnp.int32)
    hot = (routes[:, :, :, None] == experts).astype(F32)
    hot = hot.reshape(wide_count, 2, 2, TOK, E)
    both = jnp.sum(hot, axis=2).swapaxes(0, 1)
    earlier = (jnp.arange(TOK)[:, None] > jnp.arange(TOK)[None, :]).astype(BF16)
    rank = jnp.einsum("ts,awse->awte", earlier, both.astype(BF16), preferred_element_type=F32)
    counts = jnp.sum(both, axis=2)
    blocks = jnp.arange(wide_count)
    prefix = jnp.sum(
        jnp.where((blocks[:, None] > blocks[None, :])[None, :, :, None], counts[:, None], 0.0), axis=2
    )
    kept = both * ((prefix[:, :, None, :] + rank) < capacity).astype(F32)

    def pick(values, index):
        return lax.dynamic_index_in_dim(values, index, 0, False)

    turned = narrow * subs + sub
    hot_one = pick(hot[:, 0], wide)
    keep_one = jnp.sum(hot_one * pick(kept[0], wide)[None], axis=-1)
    hot_two = pick(hot[:, 1], turned)
    kept_two = pick(kept[1], turned)
    rank_two = pick(rank[1], turned)
    keep_two = jnp.sum(hot_two * kept_two[None], axis=-1)
    slots = jnp.arange(SLOTS, dtype=F32)
    rank_k = xor_shuffle(rank_two.T, plane)
    kept_k = xor_shuffle(kept_two.T, plane)
    select = jnp.where(
        (rank_k[:, None, :] == slots[None, :, None]) & (kept_k[:, None, :] > 0), 1.0, 0.0
    ).astype(BF16)
    own_expert = (experts == plane).astype(F32)
    rank_m = xor_shuffle(jnp.sum(rank[1] * own_expert, axis=-1), turned)
    kept_m = xor_shuffle(jnp.sum(kept[1] * own_expert, axis=-1), turned)
    both_m = xor_shuffle(both[1], turned)
    select_m = jnp.where(
        (rank_m[:, None, :] == slots[None, :, None]) & (kept_m[:, None, :] > 0), 1.0, 0.0
    ).astype(BF16)
    row_hot = jnp.einsum("wst,wte->wse", select_m, both_m.astype(BF16), preferred_element_type=F32)
    row_hot = row_hot.reshape(-1, E)

    hot_k = hot[:, 0].reshape(E, subs, 2, TOK, E)
    hot_k = lax.dynamic_index_in_dim(hot_k, sub, 1, False)
    hot_q = xor_shuffle(hot_k, narrow)
    hot_cols = hot_q.transpose(0, 2, 1, 3).reshape(E * TOK, TOPK * E)
    hot_two_k = xor_shuffle(jnp.moveaxis(hot_two, -1, 0), plane)
    at = jnp.stack([narrow ^ plane, sub, plane, narrow]).astype(jnp.int32)

    kv_parts = gather_subs(key_value)
    query_parts = gather_subs(query_proj)
    home_stream = stream.astype(F32)
    turned_stream = swap(stream)
    turned_grad = swap(out_grad)

    def own_slice(vector, place):
        return lax.dynamic_slice_in_dim(vector, place * slice_width, slice_width, vector.ndim - 1)

    gain_one_home = own_slice(gain_one, narrow)
    router_one_home = own_slice(router_one, narrow).astype(F32)

    rows_all = E * TOK
    sent = shape((2, TOK, local_width), BF16)
    kept_own = shape((2, TOK, local_width), F32)
    gained, *kv_blocks = run(
        "key_value",
        key_value_body(subs),
        [shape((rows_all, slice_width), BF16), kept_own] + [sent] * (E - 1),
        [at, *gather_narrow(turned_stream), gain_one_plane[None], *kv_parts],
        [
            pltpu.VMEM((2, slice_width, local_width), BF16),
            pltpu.VMEM((2, rows_all, local_width), F32),
        ],
    )
    kv_blocks = exchange_planes(kv_blocks)
    routed_scratch = [
        pltpu.VMEM((E, slice_width, local_width), BF16),
        pltpu.VMEM((TOPK, rows_all, local_width), F32),
    ]
    query_blocks = run(
        "query",
        routed_body(subs, True),
        [kept_own] + [sent] * (E - 1),
        [at, gained, hot_cols, *query_parts],
        routed_scratch,
    )
    query_blocks = exchange_planes(query_blocks)

    gained_home = home_stream * gain_one_home
    stats_one = jnp.concatenate(
        [
            jnp.sum(home_stream * home_stream, axis=-1)[None],
            dot(router_one_home, gained_home, ((1,), (1,)), PRECISE),
        ],
        axis=0,
    )
    stats_one = sum_narrow(stats_one)
    scale_one = lax.rsqrt(stats_one[0] / width + EPSILON)
    logits_one = (stats_one[1:] * scale_one).T

    def gates(logits, hots):
        picked = jnp.sum(hots * logits[None], axis=-1)
        gap = picked[0] - picked[1]
        return jnp.stack([jax.nn.sigmoid(gap), jax.nn.sigmoid(-gap)])

    prob_one = gates(logits_one, hot_one)
    gate_one = prob_one * keep_one

    token_cols = jnp.stack([scale_one, gate_one[0], gate_one[1]] + [scale_one] * 5, axis=1)
    low, probs, context, gated = run(
        "attention",
        attention_body,
        [
            shape((4, TOK, local_width), BF16),
            shape((head_count, TOPK * TOK, TOK), F32),
            sent,
            sent,
        ],
        [doc_lengths[0], *kv_blocks, *query_blocks, token_cols],
    )

    out_parts = gather_subs(output_proj)

    folded = [shape((TOK, slice_width), F32), shape((TOK, slice_width), F32), shape((2, TOK, slice_width), BF16)]
    mixed, *attention = run(
        "output",
        output_body(subs),
        [shape((E, rows_all, local_width), BF16)] + folded,
        [at, *gather_planes(gated), hot_cols, *out_parts],
        [pltpu.VMEM((E, slice_width, local_width), BF16)],
    )
    hidden = turned_stream.astype(F32) + reduce_narrow(*attention)

    def dispatch(rows):
        picked = jnp.einsum("kst,td->ksd", select, rows, preferred_element_type=F32).astype(BF16)
        (full,) = run(
            "join",
            join_body,
            [shape((SLOTS, width), BF16)],
            [at, *exchange_planes([picked[k] for k in range(E)])],
        )
        full = jnp.stack(gather_subs(full))
        two = jnp.stack([full, by_narrow(full, 2)])
        one = by_narrow(two, 1)
        return jnp.stack([two[0], one[0], two[1], one[1]]).reshape(-1, width)

    grad_rows = dispatch(turned_grad)
    weight_in = expert_in[0]
    weight_down = expert_down[0]
    dact_raw = dot(grad_rows, weight_down, ((1,), (1,)))

    expert_rows = dispatch((hidden * gain_two_plane).astype(BF16))
    stats_two = jnp.concatenate(
        [
            jnp.sum(hidden * hidden, axis=-1)[None],
            dot(router_two_plane, hidden * gain_two_plane, ((1,), (1,)), PRECISE),
        ],
        axis=0,
    )
    stats_two = sum_planes(stats_two)
    scale_two = lax.rsqrt(stats_two[0] / width + EPSILON)
    logits_two = (stats_two[1:] * scale_two).T
    prob_two = gates(logits_two, hot_two)

    rows_float = expert_rows.astype(F32) / gain_two
    row_scale = lax.rsqrt(jnp.sum(rows_float * rows_float, axis=-1, keepdims=True) / width + EPSILON)
    row_logits = dot(expert_rows, router_two, ((1,), (1,)))
    row_gap = jnp.sum((2.0 * own_expert[None, :] - row_hot) * row_logits, axis=-1, keepdims=True)
    row_gate = jax.nn.sigmoid(row_gap * row_scale)
    gate_up = jnp.einsum("rd,dkf->krf", expert_rows, weight_in, preferred_element_type=F32)
    gate_pre = gate_up[0] * row_scale
    up_pre = gate_up[1] * row_scale
    gate_sig = jax.nn.sigmoid(gate_pre)
    silu_gate = gate_pre * gate_sig
    activation = (silu_gate * up_pre).astype(BF16)
    dactiv = dact_raw * row_gate
    dgate_pre = (dactiv * up_pre * gate_sig * (1.0 + gate_pre * (1.0 - gate_sig))).astype(BF16)
    dup_pre = (dactiv * silu_gate).astype(BF16)
    dprob_rows = jnp.sum(activation.astype(F32) * dact_raw, axis=-1)
    inner_rows = jnp.sum(dgate_pre.astype(F32) * gate_pre + dup_pre.astype(F32) * up_pre, axis=-1)
    drows = jnp.einsum(
        "krf,dkf->rd", jnp.stack([dgate_pre, dup_pre]), weight_in, preferred_element_type=F32
    )
    lanes = jnp.arange(128)
    row_stats = jnp.where(
        lanes[None, :] == 0, dprob_rows[:, None], jnp.where(lanes[None, :] == 1, inner_rows[:, None], 0.0)
    )

    def give_back(rows):
        shaped = rows.reshape(narrow_count, subs, SLOTS, -1)
        low = shaped.astype(BF16)
        got = by_narrow(jnp.stack([low[1], low[3]]), 1)
        two = jnp.stack([shaped[0], shaped[2]]) + got.astype(F32)
        one = two[0] + by_narrow(two[1].astype(BF16), 2).astype(F32)
        parts, bit = [one[j] for j in range(subs)], subs // 2
        while bit > 1:
            parts = [parts[j] + by_sub(parts[j + bit].astype(BF16), bit).astype(F32) for j in range(bit)]
            bit //= 2
        return parts[0], by_sub(parts[1].astype(BF16), 1)

    def from_planes(own, got, extra):
        pieces = run(
            "split",
            split_body(extra),
            [shape((SLOTS, slice_width + extra), BF16)] * E,
            [at, own, got],
            [pltpu.VMEM(own.shape, BF16)],
        )
        return jnp.stack(exchange_planes(pieces))

    returned = give_back(jnp.concatenate([drows, row_stats], axis=1))
    returned = from_planes(*returned, row_stats.shape[1])
    combined = jnp.einsum("kst,ksd->ktd", select, returned, preferred_element_type=F32)
    per_expert = combined[:, :, slice_width : slice_width + 2]
    dprob_two = keep_two * jnp.sum(hot_two_k * per_expert[:, None, :, 0], axis=0)
    inner_two = jnp.sum(per_expert[:, :, 1], axis=0)
    dnormed_two = jnp.sum(combined[:, :, :slice_width], axis=0)

    def gate_back(prob, dprob, hots):
        dselect = prob * (dprob - jnp.sum(prob * dprob, axis=0, keepdims=True))
        return jnp.sum(hots * dselect[:, :, None], axis=0)

    dlogit_two = gate_back(prob_two, dprob_two, hot_two)
    dnormed_two = dnormed_two + dot(dlogit_two, router_two_plane, ((1,), (0,)), PRECISE)
    inner_two = inner_two + jnp.sum(dlogit_two * logits_two, axis=-1)
    dhidden = (
        turned_grad.astype(F32)
        + scale_two[:, None] * (dnormed_two * gain_two_plane)
        - hidden * (scale_two * scale_two * inner_two / width)[:, None]
    )
    scaled_hidden = hidden * scale_two[:, None]
    mlp_terms = jnp.concatenate(
        [
            jnp.sum(dnormed_two * scaled_hidden, axis=0)[None],
            dot(dlogit_two, scaled_hidden * gain_two_plane, ((0,), (0,)), PRECISE),
        ],
        axis=0,
    )

    wide_grad, *dcontext_blocks = run(
        "dcontext",
        routed_body(subs, False),
        [shape((rows_all, slice_width), BF16), kept_own] + [sent] * (E - 1),
        [at, *gather_narrow(dhidden.astype(BF16)), hot_cols, *out_parts],
        routed_scratch,
    )
    dcontext_blocks = exchange_planes(dcontext_blocks)

    def weight_grad(name, rows, other):
        count, half = other.shape[0], subs // 2
        parts = run(
            name,
            weight_grad_body,
            [shape((count, shard_rows, local_width), F32 if j < half else BF16) for j in range(subs)],
            [at, rows, other],
            [pltpu.VMEM((slice_width, local_width), F32)],
        )
        return finish_subs(parts[:half], parts[half:])

    output_grad = weight_grad("output_grad", wide_grad, mixed)
    dquery_low, dkv_low, home_sums = run(
        "attention_back",
        attention_back_body,
        [sent, sent, shape((8, TOK), F32)],
        [at, *dcontext_blocks, token_cols, low, probs, context],
    )
    (dmixed,) = run(
        "spread",
        spread_body,
        [shape((E, rows_all, local_width), BF16)],
        [at, *gather_planes(dquery_low), hot_cols],
    )
    query_grad = weight_grad("query_grad", gained, dmixed)
    home_sums = sum_narrow(home_sums)
    dprob_one = keep_one * home_sums[:2]
    dlogit_one = gate_back(prob_one, dprob_one, hot_one)
    inner_one = home_sums[2] + jnp.sum(dlogit_one * logits_one, axis=-1)
    dlogit_scaled = dlogit_one * scale_one[:, None]

    dkv_all, *dnormed_one = run(
        "input",
        input_body(subs),
        [shape((2, rows_all, local_width), BF16)] + folded,
        [at, *gather_planes(dkv_low), dmixed, *kv_parts, *query_parts],
        [pltpu.VMEM((2 + E, slice_width, local_width), BF16)],
    )
    kv_grad = weight_grad("key_value_grad", gained, dkv_all)
    dnormed_one = reduce_narrow(*dnormed_one)
    turned_out = dhidden + dnormed_one * gain_one_plane
    home_out = swap(turned_out.astype(BF16)).astype(F32)
    stream_grad = (
        home_out
        + gain_one_home * dot(dlogit_scaled, router_one_home, ((1,), (0,)), PRECISE)
        - home_stream * (scale_one * scale_one * inner_one / width)[:, None]
    )

    gain_term = jnp.sum(dnormed_one * turned_stream.astype(F32), axis=0)
    router_term = swap(dot(dlogit_scaled, gained_home, ((0,), (0,)), PRECISE))
    small = jnp.concatenate([mlp_terms, gain_term[None], router_term], axis=0)
    small = sum_subs(sum_narrow(small))
    mine = lax.dynamic_slice_in_dim(small, sub * shard_rows, shard_rows, 1)
    router_one_grad = mine[6:10]
    gain_one_grad = mine[5] + jnp.sum(
        router_one_grad * attn_router.T.astype(F32), axis=0
    ) / attn_gain.astype(F32)

    expert_out = dot(activation, weight_down, ((1,), (0,))) * row_gate
    mixture = from_planes(*give_back(expert_out), 0)
    mixture = jnp.einsum("kst,ksd->td", select, mixture, preferred_element_type=F32)
    layer_out = swap((hidden + mixture).astype(BF16)).astype(F32)
    gated_act = (activation.astype(F32) * row_gate).astype(BF16)
    down_grad = dot(gated_act, grad_rows, ((0,), (0,)))
    dboth = jnp.stack(
        [
            (dgate_pre.astype(F32) * row_scale).astype(BF16),
            (dup_pre.astype(F32) * row_scale).astype(BF16),
        ],
        axis=1,
    )
    up_grad = jnp.einsum("rd,rkf->dkf", expert_rows, dboth, preferred_element_type=F32)

    return (
        layer_out,
        stream_grad,
        gain_one_grad,
        router_one_grad.T,
        kv_grad,
        query_grad,
        output_grad,
        mine[0],
        mine[1:5].T,
        up_grad[None],
        down_grad[None],
    )


def solution(mesh):
    in_specs = (
        P("wide", "narrow"),
        P("wide", "narrow"),
        P("wide"),
        P("wide", None),
        P(None, "wide", "narrow"),
        P(None, "wide", "narrow"),
        P(None, "wide", "narrow"),
        P("wide"),
        P("wide", None),
        P("wide", None, None, "narrow"),
        P("wide", "narrow", None),
        P("wide", None),
        P("wide", None),
        P("wide", None),
    )
    out_specs = (
        P("wide", "narrow"),
        P("wide", "narrow"),
        P("wide"),
        P("wide", None),
        P(None, "wide", "narrow"),
        P(None, "wide", "narrow"),
        P(None, "wide", "narrow"),
        P("wide"),
        P("wide", None),
        P("wide", None, None, "narrow"),
        P("wide", "narrow", None),
    )
    return jax.shard_map(local, mesh=mesh, in_specs=in_specs, out_specs=out_specs, check_vma=False)
```

```python
import jax
import jax.numpy as jnp
from jax import lax
from jax.experimental import pallas as pl
from jax.experimental.pallas import tpu as pltpu
from jax.sharding import PartitionSpec as P

HS = 128
E = 4
TOPK = 2
TOK = 128
SLOTS = 80

EPSILON = 1e-05
NEGATIVE = -1000000000.0
PRECISE = lax.Precision.HIGHEST
F32 = jnp.float32
BF16 = jnp.bfloat16


def dot(left, right, contract, precision=None):
    return lax.dot_general(
        left, right, ((contract[0], contract[1]), ((), ())), precision=precision, preferred_element_type=F32
    )


def xor_shuffle(values, amount):
    count, bit = values.shape[0], 1
    while bit < count:
        split = values.reshape((count // (2 * bit), 2, bit) + values.shape[1:])
        flipped = split[:, ::-1].reshape(values.shape)
        values = jnp.where((amount & bit) != 0, flipped, values)
        bit *= 2
    return values


NN = (((1,), (0,)), ((), ()))
NT = (((1,), (1,)), ((), ()))
TN = (((0,), (0,)), ((), ()))


def mul(left, right, form):
    return lax.dot_general(left, right, form, preferred_element_type=F32)


def shape(dims, dtype):
    return jax.ShapeDtypeStruct(tuple(dims), dtype)


def run(name, body, outs, args, scratch=()):
    vector = pl.BlockSpec(memory_space=pltpu.VMEM)
    return pl.pallas_call(
        body,
        out_shape=tuple(outs),
        in_specs=[pl.BlockSpec(memory_space=pltpu.SMEM)] + [vector] * (len(args) - 1),
        out_specs=tuple(vector for _ in outs),
        scratch_shapes=list(scratch),
        cost_estimate=pl.CostEstimate(flops=1, transcendentals=0, bytes_accessed=1),
        name=name,
    )(*args)


def place(store, parts, sub, first=0):
    for j, part in enumerate(parts):
        rows = part.shape[1]
        start = pl.multiple_of((sub ^ j) * rows, rows)
        for a in range(part.shape[0]):
            store[first + a, pl.ds(start, rows), :] = part[a]


def block(index):
    return pl.ds(pl.multiple_of(index * TOK, TOK), TOK)


def send_blocks(total, outs, order):
    for k in range(E):
        for a in range(total.shape[0]):
            outs[k][a] = total[a, block(order ^ k), :].astype(outs[k].dtype)


def key_value_body(subs):
    def body(at, *refs):
        rows, gain, parts = refs[:E], refs[E], refs[E + 1 : E + 1 + subs]
        gained, *outs = refs[E + 1 + subs : E + 2 + subs + E]
        weights, total = refs[E + 2 + subs + E :]
        place(weights, parts, at[1])
        for q in range(E):
            gained[q * TOK : (q + 1) * TOK, :] = (rows[q][...].astype(F32) * gain[...]).astype(BF16)
        for a in range(2):
            total[a] = mul(gained[...], weights[a], NN)
        send_blocks(total, outs, at[0])

    return body


def routed_body(subs, joined):
    count = 1 if joined else E

    def body(at, *refs):
        rows, hot, parts = refs[:count], refs[count], refs[count + 1 : count + 1 + subs]
        rest = refs[count + 1 + subs :]
        if joined:
            wide = rows[0]
        else:
            wide, rest = rest[0], rest[1:]
            for q in range(E):
                wide[q * TOK : (q + 1) * TOK, :] = rows[q][...]
        outs, weights, total = rest[:E], rest[E], rest[E + 1]
        place(weights, parts, at[1])
        for e in range(E):
            every = mul(wide[...], weights[e], NN)
            for i in range(TOPK):
                mine = every * hot[:, i * E + e : i * E + e + 1]
                total[i] = mine if e == 0 else total[i] + mine
        send_blocks(total, outs, at[0])

    return body


def spread_pairs(at, rows, hot, out, first=0):
    for k in range(E):
        where = block(at[0] ^ k)
        mask = hot[where, :].astype(BF16)
        for e in range(E):
            out[e, where, :] = (
                rows[k][first] * mask[:, e : e + 1]
                + rows[k][first + 1] * mask[:, E + e : E + e + 1]
            )


def fold_out(total, keep_0, keep_2, send):
    keep_0[...] = total[0:TOK]
    keep_2[...] = total[2 * TOK : 3 * TOK]
    send[0] = total[TOK : 2 * TOK].astype(BF16)
    send[1] = total[3 * TOK : 4 * TOK].astype(BF16)


def output_body(subs):
    def body(at, *refs):
        rows, hot, parts = refs[:E], refs[E], refs[E + 1 : E + 1 + subs]
        mixed, keep_0, keep_2, send, weights = refs[E + 1 + subs :]
        place(weights, parts, at[1])
        spread_pairs(at, rows, hot, mixed)
        total = mul(mixed[0], weights[0], NT)
        for e in range(1, E):
            total = total + mul(mixed[e], weights[e], NT)
        fold_out(total, keep_0, keep_2, send)

    return body


def input_body(subs):
    def body(at, *refs):
        rows, dmixed = refs[:E], refs[E]
        kv_parts = refs[E + 1 : E + 1 + subs]
        query_parts = refs[E + 1 + subs : E + 1 + 2 * subs]
        dkv_all, keep_0, keep_2, send, weights = refs[E + 1 + 2 * subs :]
        place(weights, kv_parts, at[1])
        place(weights, query_parts, at[1], 2)
        for k in range(E):
            for a in range(2):
                dkv_all[a, block(at[0] ^ k), :] = rows[k][a]
        total = mul(dkv_all[0], weights[0], NT) + mul(dkv_all[1], weights[1], NT)
        for e in range(E):
            total = total + mul(dmixed[e], weights[2 + e], NT)
        fold_out(total, keep_0, keep_2, send)

    return body


def split_rows(at, rows, other, parts, total):
    for a in range(other.shape[0]):
        total[...] = mul(rows[...], other[a], TN)
        for j, part in enumerate(parts):
            count = part.shape[1]
            start = pl.multiple_of((at[1] ^ j) * count, count)
            part[a] = total[pl.ds(start, count), :].astype(part.dtype)


def weight_grad_body(at, rows, other, *refs):
    split_rows(at, rows, other, refs[:-1], refs[-1])


def query_grad_body(at, rows, hot, *refs):
    dmixed = refs[E]
    spread_pairs(at, refs[:E], hot, dmixed, 2)
    split_rows(at, rows, dmixed, refs[E + 1 : -1], refs[-1])


def attention_mask(at):
    row = lax.broadcasted_iota(jnp.int32, (TOK, TOK), 0)
    col = lax.broadcasted_iota(jnp.int32, (TOK, TOK), 1)
    row_doc, col_doc, end = jnp.zeros_like(row), jnp.zeros_like(row), 0
    for d in range(4):
        end = end + at[d]
        row_doc = row_doc + (row >= end).astype(jnp.int32)
        col_doc = col_doc + (col >= end).astype(jnp.int32)
    return (row_doc == col_doc) & (col <= row)


def attention_body(at, own_kv, *refs):
    got_kv, own_query, got_query = refs[: E - 1], refs[E - 1], refs[E : 2 * E - 1]
    cols, low, probs, context, gated = refs[2 * E - 1 :]
    scale = cols[:, 0:1]
    for a in range(4):
        own, got = (own_kv, got_kv) if a < 2 else (own_query, got_query)
        total = own[a % 2]
        for one in got:
            total = total + one[a % 2].astype(F32)
        low[a] = (total * scale).astype(BF16)
    allowed = attention_mask(at)
    for h in range(low.shape[2] // HS):
        head = slice(h * HS, (h + 1) * HS)
        for i in range(TOPK):
            scores = mul(low[2 + i, :, head], low[0, :, head], NT) * HS ** (-0.5)
            scores = jnp.where(allowed, scores, NEGATIVE)
            top = jnp.exp(scores - jnp.max(scores, axis=-1, keepdims=True))
            prob = top / jnp.sum(top, axis=-1, keepdims=True)
            probs[h, i * TOK : (i + 1) * TOK, :] = prob
            mixed = mul(prob.astype(BF16), low[1, :, head], NN).astype(BF16)
            context[i, :, head] = mixed
            gated[i, :, head] = (mixed.astype(F32) * cols[:, 1 + i : 2 + i]).astype(BF16)


def attention_back_body(at, own, *refs):
    got = refs[: E - 1]
    cols, low, probs, context, grads, sums = refs[E - 1 :]
    scale = cols[:, 0:1]
    inner = jnp.zeros((TOK, 1), F32)
    dprob = []
    dcontext = []
    for i in range(TOPK):
        raw = own[i]
        for one in got:
            raw = raw + one[i].astype(F32)
        dprob.append(jnp.sum(context[i].astype(F32) * raw, axis=-1, keepdims=True))
        dcontext.append((raw * cols[:, 1 + i : 2 + i]).astype(BF16))
    for h in range(low.shape[2] // HS):
        head = slice(h * HS, (h + 1) * HS)
        key, value = low[0, :, head], low[1, :, head]
        dkey = jnp.zeros((TOK, HS), F32)
        dvalue = jnp.zeros((TOK, HS), F32)
        for i in range(TOPK):
            query = low[2 + i, :, head]
            grad = dcontext[i][:, head]
            prob = probs[h, i * TOK : (i + 1) * TOK, :]
            dweight = mul(grad, value, NT)
            dscore = prob * (dweight - jnp.sum(prob * dweight, axis=-1, keepdims=True))
            dscore = dscore.astype(BF16)
            done = mul(dscore, key, NN) * HS ** (-0.5)
            dkey = dkey + mul(dscore, query, TN)
            dvalue = dvalue + mul(prob.astype(BF16), grad, TN)
            inner = inner + jnp.sum(done * query.astype(F32), axis=-1, keepdims=True)
            grads[2 + i, :, head] = (done * scale).astype(BF16)
        dkey = dkey * HS ** (-0.5)
        inner = inner + jnp.sum(
            dkey * key.astype(F32) + dvalue * value.astype(F32), axis=-1, keepdims=True
        )
        grads[0, :, head] = (dkey * scale).astype(BF16)
        grads[1, :, head] = (dvalue * scale).astype(BF16)
    lane = lax.broadcasted_iota(jnp.int32, (TOK, TOK), 1)
    table = jnp.where(lane == 0, dprob[0], jnp.where(lane == 1, dprob[1], jnp.where(lane == 2, inner, 0.0)))
    sums[...] = jnp.transpose(table)[0:8]


def join_body(at, *refs):
    pieces, out = refs[:E], refs[E]
    size = pieces[0].shape[1]
    for k in range(E):
        for p in range(E):

            @pl.when((at[2] ^ k) == p)
            def _(k=k, p=p):
                out[:, p * size : (p + 1) * size] = pieces[k][...]


def split_body(extra):
    def body(at, own, got, *refs):
        outs, store = refs[:E], refs[E]
        store[...] = (own[...] + got[...].astype(F32)).astype(BF16)
        size = outs[0].shape[1] - extra
        for k in range(E):
            for p in range(E):

                @pl.when((at[2] ^ k) == p)
                def _(k=k, p=p):
                    outs[k][:, :size] = store[:, p * size : (p + 1) * size]

            if extra:
                outs[k][:, size:] = store[:, E * size :]

    return body


def local(
    stream,
    out_grad,
    attn_gain,
    attn_router,
    key_value,
    query_proj,
    output_proj,
    mlp_gain,
    mlp_router,
    expert_in,
    expert_down,
    attn_routes,
    mlp_routes,
    doc_lengths,
):
    wide_count = lax.axis_size("wide")
    narrow_count = lax.axis_size("narrow")
    subs = wide_count // E
    wide = lax.axis_index("wide")
    narrow = lax.axis_index("narrow")
    plane, sub = wide // subs, wide % subs
    capacity = 9 * TOK * wide_count * TOPK // (8 * E)
    slice_width = stream.shape[1]
    shard_rows = attn_gain.shape[0]
    width = slice_width * narrow_count
    local_width = key_value.shape[2]
    head_count = local_width // HS
    hidden_units = expert_down.shape[1]
    score_scale = HS ** (-0.5)

    def after(values, *others):
        return lax.optimization_barrier((values, others))[0]

    def by_plane(values, k):
        return lax.ppermute(values, "wide", [(i, i ^ (k * subs)) for i in range(wide_count)])

    def by_sub(values, k):
        return lax.ppermute(values, "wide", [(i, i ^ k) for i in range(wide_count)])

    def by_narrow(values, k):
        return lax.ppermute(values, "narrow", [(i, i ^ k) for i in range(narrow_count)])

    def swap(values):
        pairs = []
        for w in range(wide_count):
            for n in range(narrow_count):
                z, y = w // subs, w % subs
                pairs.append((w * narrow_count + n, (n * subs + y) * narrow_count + z))
        return lax.ppermute(values, ("wide", "narrow"), pairs)

    def gather_planes(values):
        return [values] + [by_plane(values, k) for k in range(1, E)]

    def exchange_planes(parts):
        return [parts[0]] + [by_plane(parts[k], k) for k in range(1, E)]

    def gather_subs(values):
        parts, bit = [values], 1
        while bit < subs:
            parts = parts + [by_sub(one, bit) for one in parts]
            bit *= 2
        return parts

    def reduce_subs(parts):
        bit = len(parts) // 2
        while bit >= 1:
            parts = [parts[j] + by_sub(parts[j + bit].astype(BF16), bit).astype(F32) for j in range(bit)]
            bit //= 2
        return parts[0]

    def gather_narrow(values):
        other = by_narrow(values, 2)
        return [values, by_narrow(values, 1), other, by_narrow(other, 1)]

    def reduce_narrow(keep_0, keep_2, send):
        got = by_narrow(send, 1)
        other = by_narrow((keep_2 + got[1].astype(F32)).astype(BF16), 2)
        return keep_0 + got[0].astype(F32) + other.astype(F32)

    def finish_subs(keep, send):
        bit = len(keep)
        keep = [keep[j] + by_sub(send[j], bit).astype(F32) for j in range(bit)]
        return reduce_subs(keep)

    def sum_narrow(values):
        values = values + by_narrow(values, 2)
        return values + by_narrow(values, 1)

    def sum_planes(values):
        values = values + by_plane(values, 1)
        return values + by_plane(values, 2)

    def sum_subs(values):
        bit = 1
        while bit < subs:
            values = values + by_sub(values, bit)
            bit *= 2
        return values

    own_rows = jnp.concatenate(
        [attn_gain[None, :], attn_router.T, mlp_gain[None, :], mlp_router.T], axis=0
    )
    own_routes = jnp.concatenate([attn_routes.T, mlp_routes.T], axis=0)
    route_rows = own_routes.astype(BF16).reshape(-1, shard_rows)
    packed = jnp.concatenate([own_rows, route_rows], axis=0)
    used = packed.shape[0]
    packed = jnp.pad(packed, ((0, -used % 16), (0, 0)))
    parts = gather_subs(packed)
    table = jnp.stack(gather_planes(jnp.stack(parts)))
    table = table.reshape((wide_count,) + packed.shape)
    table = xor_shuffle(table, wide)
    near = xor_shuffle(jnp.stack(parts), sub)
    gain_one_plane = near[:, 0].reshape(slice_width).astype(F32)
    gain_two_plane = near[:, 5].reshape(slice_width).astype(F32)
    router_two_plane = near[:, 6:10].swapaxes(0, 1).reshape(E, slice_width).astype(F32)
    gain_one = table[:, 0].reshape(width).astype(F32)
    router_one = table[:, 1:5].swapaxes(0, 1).reshape(E, width)
    gain_two = table[:, 5].reshape(width).astype(F32)
    router_two = table[:, 6:10].swapaxes(0, 1).reshape(E, width)
    routes = table[:, 10:used].reshape(wide_count, 4, TOK).astype(jnp.int32)

    experts = jnp.arange(E, dtype=jnp.int32)
    hot = (routes[:, :, :, None] == experts).astype(F32)
    hot = hot.reshape(wide_count, 2, 2, TOK, E)
    both = jnp.sum(hot, axis=2).swapaxes(0, 1)
    earlier = (jnp.arange(TOK)[:, None] > jnp.arange(TOK)[None, :]).astype(BF16)
    rank = jnp.einsum("ts,awse->awte", earlier, both.astype(BF16), preferred_element_type=F32)
    counts = jnp.sum(both, axis=2)
    blocks = jnp.arange(wide_count)
    prefix = jnp.sum(
        jnp.where((blocks[:, None] > blocks[None, :])[None, :, :, None], counts[:, None], 0.0), axis=2
    )
    kept = both * ((prefix[:, :, None, :] + rank) < capacity).astype(F32)

    def pick(values, index):
        return lax.dynamic_index_in_dim(values, index, 0, False)

    turned = narrow * subs + sub
    hot_one = pick(hot[:, 0], wide)
    keep_one = jnp.sum(hot_one * pick(kept[0], wide)[None], axis=-1)
    hot_two = pick(hot[:, 1], turned)
    kept_two = pick(kept[1], turned)
    rank_two = pick(rank[1], turned)
    keep_two = jnp.sum(hot_two * kept_two[None], axis=-1)
    slots = jnp.arange(SLOTS, dtype=F32)
    rank_k = xor_shuffle(rank_two.T, plane)
    kept_k = xor_shuffle(kept_two.T, plane)
    select = jnp.where(
        (rank_k[:, None, :] == slots[None, :, None]) & (kept_k[:, None, :] > 0), 1.0, 0.0
    ).astype(BF16)
    own_expert = (experts == plane).astype(F32)
    rank_m = xor_shuffle(jnp.sum(rank[1] * own_expert, axis=-1), turned)
    kept_m = xor_shuffle(jnp.sum(kept[1] * own_expert, axis=-1), turned)
    both_m = xor_shuffle(both[1], turned)
    select_m = jnp.where(
        (rank_m[:, None, :] == slots[None, :, None]) & (kept_m[:, None, :] > 0), 1.0, 0.0
    ).astype(BF16)
    row_hot = jnp.einsum("wst,wte->wse", select_m, both_m.astype(BF16), preferred_element_type=F32)
    row_hot = row_hot.reshape(-1, E)

    hot_k = hot[:, 0].reshape(E, subs, 2, TOK, E)
    hot_k = lax.dynamic_index_in_dim(hot_k, sub, 1, False)
    hot_q = xor_shuffle(hot_k, narrow)
    hot_cols = hot_q.transpose(0, 2, 1, 3).reshape(E * TOK, TOPK * E)
    hot_two_k = xor_shuffle(jnp.moveaxis(hot_two, -1, 0), plane)
    at = jnp.stack([narrow ^ plane, sub, plane, narrow]).astype(jnp.int32)

    kv_parts = gather_subs(key_value)
    query_parts = gather_subs(query_proj)
    home_stream = stream.astype(F32)
    turned_stream = swap(stream)
    turned_grad = swap(out_grad)

    def own_slice(vector, place):
        return lax.dynamic_slice_in_dim(vector, place * slice_width, slice_width, vector.ndim - 1)

    gain_one_home = own_slice(gain_one, narrow)
    router_one_home = own_slice(router_one, narrow).astype(F32)

    rows_all = E * TOK
    sent = shape((2, TOK, local_width), BF16)
    kept_own = shape((2, TOK, local_width), F32)
    gained, *kv_blocks = run(
        "key_value",
        key_value_body(subs),
        [shape((rows_all, slice_width), BF16), kept_own] + [sent] * (E - 1),
        [at, *gather_narrow(turned_stream), gain_one_plane[None], *kv_parts],
        [
            pltpu.VMEM((2, slice_width, local_width), BF16),
            pltpu.VMEM((2, rows_all, local_width), F32),
        ],
    )
    kv_blocks = exchange_planes(kv_blocks)
    routed_scratch = [
        pltpu.VMEM((E, slice_width, local_width), BF16),
        pltpu.VMEM((TOPK, rows_all, local_width), F32),
    ]
    query_blocks = run(
        "query",
        routed_body(subs, True),
        [kept_own] + [sent] * (E - 1),
        [at, gained, hot_cols, *query_parts],
        routed_scratch,
    )
    query_blocks = exchange_planes(query_blocks)

    gained_home = home_stream * gain_one_home
    stats_one = jnp.concatenate(
        [
            jnp.sum(home_stream * home_stream, axis=-1)[None],
            dot(router_one_home, gained_home, ((1,), (1,)), PRECISE),
        ],
        axis=0,
    )
    stats_one = sum_narrow(stats_one)
    scale_one = lax.rsqrt(stats_one[0] / width + EPSILON)
    logits_one = (stats_one[1:] * scale_one).T

    def gates(logits, hots):
        picked = jnp.sum(hots * logits[None], axis=-1)
        gap = picked[0] - picked[1]
        return jnp.stack([jax.nn.sigmoid(gap), jax.nn.sigmoid(-gap)])

    prob_one = gates(logits_one, hot_one)
    gate_one = prob_one * keep_one

    token_cols = jnp.stack([scale_one, gate_one[0], gate_one[1]] + [scale_one] * 5, axis=1)
    low, probs, context, gated = run(
        "attention",
        attention_body,
        [
            shape((4, TOK, local_width), BF16),
            shape((head_count, TOPK * TOK, TOK), F32),
            sent,
            sent,
        ],
        [doc_lengths[0], *kv_blocks, *query_blocks, token_cols],
    )

    out_parts = gather_subs(output_proj)

    folded = [shape((TOK, slice_width), F32), shape((TOK, slice_width), F32), shape((2, TOK, slice_width), BF16)]
    mixed, *attention = run(
        "output",
        output_body(subs),
        [shape((E, rows_all, local_width), BF16)] + folded,
        [at, *gather_planes(gated), hot_cols, *out_parts],
        [pltpu.VMEM((E, slice_width, local_width), BF16)],
    )
    hidden = turned_stream.astype(F32) + reduce_narrow(*attention)

    def dispatch(rows):
        picked = jnp.einsum("kst,td->ksd", select, rows, preferred_element_type=F32).astype(BF16)
        (full,) = run(
            "join",
            join_body,
            [shape((SLOTS, width), BF16)],
            [at, *exchange_planes([picked[k] for k in range(E)])],
        )
        full = jnp.stack(gather_subs(full))
        two = jnp.stack([full, by_narrow(full, 2)])
        one = by_narrow(two, 1)
        return jnp.stack([two[0], one[0], two[1], one[1]]).reshape(-1, width)

    grad_rows = dispatch(turned_grad)
    weight_in = expert_in[0]
    weight_down = expert_down[0]
    dact_raw = dot(grad_rows, weight_down, ((1,), (1,)))

    expert_rows = dispatch((hidden * gain_two_plane).astype(BF16))
    stats_two = jnp.concatenate(
        [
            jnp.sum(hidden * hidden, axis=-1)[None],
            dot(router_two_plane, hidden * gain_two_plane, ((1,), (1,)), PRECISE),
        ],
        axis=0,
    )
    stats_two = sum_planes(stats_two)
    scale_two = lax.rsqrt(stats_two[0] / width + EPSILON)
    logits_two = (stats_two[1:] * scale_two).T
    prob_two = gates(logits_two, hot_two)

    rows_float = expert_rows.astype(F32) / gain_two
    row_scale = lax.rsqrt(jnp.sum(rows_float * rows_float, axis=-1, keepdims=True) / width + EPSILON)
    row_logits = dot(expert_rows, router_two, ((1,), (1,)))
    row_gap = jnp.sum((2.0 * own_expert[None, :] - row_hot) * row_logits, axis=-1, keepdims=True)
    row_gate = jax.nn.sigmoid(row_gap * row_scale)
    gate_up = jnp.einsum("rd,dkf->krf", expert_rows, weight_in, preferred_element_type=F32)
    gate_pre = gate_up[0] * row_scale
    up_pre = gate_up[1] * row_scale
    gate_sig = jax.nn.sigmoid(gate_pre)
    silu_gate = gate_pre * gate_sig
    activation = (silu_gate * up_pre).astype(BF16)
    dactiv = dact_raw * row_gate
    dgate_pre = (dactiv * up_pre * gate_sig * (1.0 + gate_pre * (1.0 - gate_sig))).astype(BF16)
    dup_pre = (dactiv * silu_gate).astype(BF16)
    dprob_rows = jnp.sum(activation.astype(F32) * dact_raw, axis=-1)
    inner_rows = jnp.sum(dgate_pre.astype(F32) * gate_pre + dup_pre.astype(F32) * up_pre, axis=-1)
    drows = jnp.einsum(
        "krf,dkf->rd", jnp.stack([dgate_pre, dup_pre]), weight_in, preferred_element_type=F32
    )
    lanes = jnp.arange(128)
    row_stats = jnp.where(
        lanes[None, :] == 0, dprob_rows[:, None], jnp.where(lanes[None, :] == 1, inner_rows[:, None], 0.0)
    )

    def give_back(rows):
        shaped = rows.reshape(narrow_count, subs, SLOTS, -1)
        low = shaped.astype(BF16)
        got = by_narrow(jnp.stack([low[1], low[3]]), 1)
        two = jnp.stack([shaped[0], shaped[2]]) + got.astype(F32)
        one = two[0] + by_narrow(two[1].astype(BF16), 2).astype(F32)
        parts, bit = [one[j] for j in range(subs)], subs // 2
        while bit > 1:
            parts = [parts[j] + by_sub(parts[j + bit].astype(BF16), bit).astype(F32) for j in range(bit)]
            bit //= 2
        return parts[0], by_sub(parts[1].astype(BF16), 1)

    def from_planes(own, got, extra, last=None):
        pieces = run(
            "split",
            split_body(extra),
            [shape((SLOTS, slice_width + extra), BF16)] * E,
            [at, own, got],
            [pltpu.VMEM(own.shape, BF16)],
        )
        if last is not None:
            pieces = after(pieces, last)
        return jnp.stack(exchange_planes(pieces))

    returned = give_back(jnp.concatenate([drows, row_stats], axis=1))
    returned = from_planes(*returned, row_stats.shape[1])
    combined = jnp.einsum("kst,ksd->ktd", select, returned, preferred_element_type=F32)
    per_expert = combined[:, :, slice_width : slice_width + 2]
    dprob_two = keep_two * jnp.sum(hot_two_k * per_expert[:, None, :, 0], axis=0)
    inner_two = jnp.sum(per_expert[:, :, 1], axis=0)
    dnormed_two = jnp.sum(combined[:, :, :slice_width], axis=0)

    def gate_back(prob, dprob, hots):
        dselect = prob * (dprob - jnp.sum(prob * dprob, axis=0, keepdims=True))
        return jnp.sum(hots * dselect[:, :, None], axis=0)

    dlogit_two = gate_back(prob_two, dprob_two, hot_two)
    dnormed_two = dnormed_two + dot(dlogit_two, router_two_plane, ((1,), (0,)), PRECISE)
    inner_two = inner_two + jnp.sum(dlogit_two * logits_two, axis=-1)
    dhidden = (
        turned_grad.astype(F32)
        + scale_two[:, None] * (dnormed_two * gain_two_plane)
        - hidden * (scale_two * scale_two * inner_two / width)[:, None]
    )
    scaled_hidden = hidden * scale_two[:, None]
    mlp_terms = jnp.concatenate(
        [
            jnp.sum(dnormed_two * scaled_hidden, axis=0)[None],
            dot(dlogit_two, scaled_hidden * gain_two_plane, ((0,), (0,)), PRECISE),
        ],
        axis=0,
    )

    wide_grad, *dcontext_blocks = run(
        "dcontext",
        routed_body(subs, False),
        [shape((rows_all, slice_width), BF16), kept_own] + [sent] * (E - 1),
        [at, *gather_narrow(dhidden.astype(BF16)), hot_cols, *out_parts],
        routed_scratch,
    )
    dcontext_blocks = exchange_planes(dcontext_blocks)

    def weight_parts(count):
        return [
            shape((count, shard_rows, local_width), F32 if j < subs // 2 else BF16)
            for j in range(subs)
        ]

    def weight_sum(parts):
        return finish_subs(parts[: subs // 2], parts[subs // 2 :])

    weight_scratch = [pltpu.VMEM((slice_width, local_width), F32)]
    output_parts = run(
        "output_grad", weight_grad_body, weight_parts(E), [at, wide_grad, mixed], weight_scratch
    )
    output_grad = weight_sum(output_parts)
    gated_act = (activation.astype(F32) * row_gate).astype(BF16)
    down_grad = dot(after(gated_act, dcontext_blocks[1]), grad_rows, ((0,), (0,)))
    grads_low, home_sums = run(
        "attention_back",
        attention_back_body,
        [shape((4, TOK, local_width), BF16), shape((8, TOK), F32)],
        [
            at,
            *after(dcontext_blocks, output_parts[-1], down_grad),
            token_cols,
            low,
            probs,
            context,
        ],
    )
    grad_planes = gather_planes(grads_low)
    dmixed, *query_grad_parts = run(
        "query_grad",
        query_grad_body,
        [shape((E, rows_all, local_width), BF16)] + weight_parts(E),
        [at, gained, hot_cols, *after(grad_planes, output_grad)],
        weight_scratch,
    )
    query_grad = weight_sum(query_grad_parts)
    home_sums = sum_narrow(home_sums)
    dprob_one = keep_one * home_sums[:2]
    dlogit_one = gate_back(prob_one, dprob_one, hot_one)
    inner_one = home_sums[2] + jnp.sum(dlogit_one * logits_one, axis=-1)
    dlogit_scaled = dlogit_one * scale_one[:, None]

    dkv_all, *dnormed_one = run(
        "input",
        input_body(subs),
        [shape((2, rows_all, local_width), BF16)] + folded,
        [at, *after(grad_planes, query_grad_parts[-1]), dmixed, *kv_parts, *query_parts],
        [pltpu.VMEM((2 + E, slice_width, local_width), BF16)],
    )
    kv_grad_parts = run(
        "key_value_grad", weight_grad_body, weight_parts(2), [at, gained, dkv_all], weight_scratch
    )
    kv_grad = weight_sum(after(kv_grad_parts, query_grad))
    dnormed_one = after(reduce_narrow(*dnormed_one), kv_grad_parts[-1], query_grad)
    turned_out = dhidden + dnormed_one * gain_one_plane
    home_out = swap(turned_out.astype(BF16)).astype(F32)
    stream_grad = (
        home_out
        + gain_one_home * dot(dlogit_scaled, router_one_home, ((1,), (0,)), PRECISE)
        - home_stream * (scale_one * scale_one * inner_one / width)[:, None]
    )

    gain_term = jnp.sum(dnormed_one * turned_stream.astype(F32), axis=0)
    router_term = swap(dot(dlogit_scaled, gained_home, ((0,), (0,)), PRECISE))
    small = jnp.concatenate([mlp_terms, gain_term[None], router_term], axis=0)
    small = sum_subs(sum_narrow(small))
    mine = lax.dynamic_slice_in_dim(small, sub * shard_rows, shard_rows, 1)
    router_one_grad = mine[6:10]
    gain_one_grad = mine[5] + jnp.sum(
        router_one_grad * attn_router.T.astype(F32), axis=0
    ) / attn_gain.astype(F32)

    expert_out = dot(activation, weight_down, ((1,), (0,))) * row_gate
    mixture = from_planes(*give_back(expert_out), 0, grad_planes[E - 1])
    mixture = jnp.einsum("kst,ksd->td", select, after(mixture, turned_out), preferred_element_type=F32)
    layer_out = swap((hidden + mixture).astype(BF16)).astype(F32)
    dboth = jnp.stack(
        [
            (dgate_pre.astype(F32) * row_scale).astype(BF16),
            (dup_pre.astype(F32) * row_scale).astype(BF16),
        ],
        axis=1,
    )
    up_grad = jnp.einsum(
        "rd,rkf->dkf", expert_rows, after(dboth, turned_out), preferred_element_type=F32
    )

    return (
        layer_out,
        stream_grad,
        gain_one_grad,
        router_one_grad.T,
        kv_grad,
        query_grad,
        output_grad,
        mine[0],
        mine[1:5].T,
        up_grad[None],
        down_grad[None],
    )


def solution(mesh):
    in_specs = (
        P("wide", "narrow"),
        P("wide", "narrow"),
        P("wide"),
        P("wide", None),
        P(None, "wide", "narrow"),
        P(None, "wide", "narrow"),
        P(None, "wide", "narrow"),
        P("wide"),
        P("wide", None),
        P("wide", None, None, "narrow"),
        P("wide", "narrow", None),
        P("wide", None),
        P("wide", None),
        P("wide", None),
    )
    out_specs = (
        P("wide", "narrow"),
        P("wide", "narrow"),
        P("wide"),
        P("wide", None),
        P(None, "wide", "narrow"),
        P(None, "wide", "narrow"),
        P(None, "wide", "narrow"),
        P("wide"),
        P("wide", None),
        P("wide", None, None, "narrow"),
        P("wide", "narrow", None),
    )
    return jax.shard_map(local, mesh=mesh, in_specs=in_specs, out_specs=out_specs, check_vma=False)
```

```python
import jax
import jax.numpy as jnp
from jax import lax
from jax.experimental import pallas as pl
from jax.experimental.pallas import tpu as pltpu
from jax.sharding import PartitionSpec as P

HS = 128
E = 4
TOPK = 2
TOK = 128
SLOTS = 80

EPSILON = 1e-05
NEGATIVE = -1000000000.0
PRECISE = lax.Precision.HIGHEST
F32 = jnp.float32
BF16 = jnp.bfloat16


def dot(left, right, contract, precision=None):
    return lax.dot_general(
        left, right, ((contract[0], contract[1]), ((), ())), precision=precision, preferred_element_type=F32
    )


def xor_shuffle(values, amount):
    count, bit = values.shape[0], 1
    while bit < count:
        split = values.reshape((count // (2 * bit), 2, bit) + values.shape[1:])
        flipped = split[:, ::-1].reshape(values.shape)
        values = jnp.where((amount & bit) != 0, flipped, values)
        bit *= 2
    return values


NN = (((1,), (0,)), ((), ()))
NT = (((1,), (1,)), ((), ()))
TN = (((0,), (0,)), ((), ()))


def mul(left, right, form):
    return lax.dot_general(left, right, form, preferred_element_type=F32)


def shape(dims, dtype):
    return jax.ShapeDtypeStruct(tuple(dims), dtype)


def run(name, body, outs, args, scratch=()):
    vector = pl.BlockSpec(memory_space=pltpu.VMEM)
    return pl.pallas_call(
        body,
        out_shape=tuple(outs),
        in_specs=[pl.BlockSpec(memory_space=pltpu.SMEM)] + [vector] * (len(args) - 1),
        out_specs=tuple(vector for _ in outs),
        scratch_shapes=list(scratch),
        cost_estimate=pl.CostEstimate(flops=1, transcendentals=0, bytes_accessed=1),
        name=name,
    )(*args)


def place(store, parts, sub, first=0):
    for j, part in enumerate(parts):
        rows = part.shape[1]
        start = pl.multiple_of((sub ^ j) * rows, rows)
        for a in range(part.shape[0]):
            store[first + a, pl.ds(start, rows), :] = part[a]


def block(index):
    return pl.ds(pl.multiple_of(index * TOK, TOK), TOK)


def send_blocks(total, outs, order):
    for k in range(E):
        for a in range(total.shape[0]):
            outs[k][a] = total[a, block(order ^ k), :].astype(outs[k].dtype)


def key_value_body(subs):
    def body(at, *refs):
        rows, gain, parts = refs[:E], refs[E], refs[E + 1 : E + 1 + subs]
        gained, *outs = refs[E + 1 + subs : E + 2 + subs + E]
        weights, total = refs[E + 2 + subs + E :]
        place(weights, parts, at[1])
        for q in range(E):
            gained[q * TOK : (q + 1) * TOK, :] = (rows[q][...].astype(F32) * gain[...]).astype(BF16)
        for a in range(2):
            total[a] = mul(gained[...], weights[a], NN)
        send_blocks(total, outs, at[0])

    return body


def routed_body(subs, joined):
    count = 1 if joined else E

    def body(at, *refs):
        rows, hot, parts = refs[:count], refs[count], refs[count + 1 : count + 1 + subs]
        rest = refs[count + 1 + subs :]
        if joined:
            wide = rows[0]
        else:
            wide, rest = rest[0], rest[1:]
            for q in range(E):
                wide[q * TOK : (q + 1) * TOK, :] = rows[q][...]
        outs, weights, total = rest[:E], rest[E], rest[E + 1]
        place(weights, parts, at[1])
        for e in range(E):
            every = mul(wide[...], weights[e], NN)
            for i in range(TOPK):
                mine = every * hot[:, i * E + e : i * E + e + 1]
                total[i] = mine if e == 0 else total[i] + mine
        send_blocks(total, outs, at[0])

    return body


def spread_pairs(at, rows, hot, out, first=0):
    for k in range(E):
        where = block(at[0] ^ k)
        mask = hot[where, :].astype(BF16)
        for e in range(E):
            out[e, where, :] = (
                rows[k][first] * mask[:, e : e + 1]
                + rows[k][first + 1] * mask[:, E + e : E + e + 1]
            )


def fold_out(total, keep_0, keep_2, send):
    keep_0[...] = total[0:TOK]
    keep_2[...] = total[2 * TOK : 3 * TOK]
    send[0] = total[TOK : 2 * TOK].astype(BF16)
    send[1] = total[3 * TOK : 4 * TOK].astype(BF16)


def output_body(subs):
    def body(at, *refs):
        rows, hot, parts = refs[:E], refs[E], refs[E + 1 : E + 1 + subs]
        mixed, keep_0, keep_2, send, weights = refs[E + 1 + subs :]
        place(weights, parts, at[1])
        spread_pairs(at, rows, hot, mixed)
        total = mul(mixed[0], weights[0], NT)
        for e in range(1, E):
            total = total + mul(mixed[e], weights[e], NT)
        fold_out(total, keep_0, keep_2, send)

    return body


def input_body(subs):
    def body(at, *refs):
        rows, dmixed = refs[:E], refs[E]
        kv_parts = refs[E + 1 : E + 1 + subs]
        query_parts = refs[E + 1 + subs : E + 1 + 2 * subs]
        dkv_all, keep_0, keep_2, send, weights = refs[E + 1 + 2 * subs :]
        place(weights, kv_parts, at[1])
        place(weights, query_parts, at[1], 2)
        for k in range(E):
            for a in range(2):
                dkv_all[a, block(at[0] ^ k), :] = rows[k][a]
        total = mul(dkv_all[0], weights[0], NT) + mul(dkv_all[1], weights[1], NT)
        for e in range(E):
            total = total + mul(dmixed[e], weights[2 + e], NT)
        fold_out(total, keep_0, keep_2, send)

    return body


def split_rows(at, rows, other, parts, total):
    for a in range(other.shape[0]):
        total[...] = mul(rows[...], other[a], TN)
        for j, part in enumerate(parts):
            count = part.shape[1]
            start = pl.multiple_of((at[1] ^ j) * count, count)
            part[a] = total[pl.ds(start, count), :].astype(part.dtype)


def weight_grad_body(at, rows, other, *refs):
    split_rows(at, rows, other, refs[:-1], refs[-1])


def query_grad_body(at, rows, hot, *refs):
    dmixed = refs[E]
    spread_pairs(at, refs[:E], hot, dmixed, 2)
    split_rows(at, rows, dmixed, refs[E + 1 : -1], refs[-1])


def attention_mask(at):
    row = lax.broadcasted_iota(jnp.int32, (TOK, TOK), 0)
    col = lax.broadcasted_iota(jnp.int32, (TOK, TOK), 1)
    row_doc, col_doc, end = jnp.zeros_like(row), jnp.zeros_like(row), 0
    for d in range(4):
        end = end + at[d]
        row_doc = row_doc + (row >= end).astype(jnp.int32)
        col_doc = col_doc + (col >= end).astype(jnp.int32)
    return (row_doc == col_doc) & (col <= row)


def attention_body(at, own_kv, *refs):
    got_kv, own_query, got_query = refs[: E - 1], refs[E - 1], refs[E : 2 * E - 1]
    rows, low, probs, context, gated = refs[2 * E - 1 :]
    cols = columns(rows[...])
    scale = cols[:, 0:1]
    for a in range(4):
        own, got = (own_kv, got_kv) if a < 2 else (own_query, got_query)
        total = own[a % 2]
        for one in got:
            total = total + one[a % 2].astype(F32)
        low[a] = (total * scale).astype(BF16)
    allowed = attention_mask(at)
    for h in range(low.shape[2] // HS):
        head = slice(h * HS, (h + 1) * HS)
        for i in range(TOPK):
            scores = mul(low[2 + i, :, head], low[0, :, head], NT) * HS ** (-0.5)
            scores = jnp.where(allowed, scores, NEGATIVE)
            top = jnp.exp(scores - jnp.max(scores, axis=-1, keepdims=True))
            prob = top / jnp.sum(top, axis=-1, keepdims=True)
            probs[h, i * TOK : (i + 1) * TOK, :] = prob
            mixed = mul(prob.astype(BF16), low[1, :, head], NN).astype(BF16)
            context[i, :, head] = mixed
            gated[i, :, head] = (mixed.astype(F32) * cols[:, 1 + i : 2 + i]).astype(BF16)


def attention_back_body(at, own, *refs):
    got = refs[: E - 1]
    rows, low, probs, context, grads, sums = refs[E - 1 :]
    cols = columns(rows[...])
    scale = cols[:, 0:1]
    inner = jnp.zeros((TOK, 1), F32)
    dprob = []
    dcontext = []
    for i in range(TOPK):
        raw = own[i]
        for one in got:
            raw = raw + one[i].astype(F32)
        dprob.append(jnp.sum(context[i].astype(F32) * raw, axis=-1, keepdims=True))
        dcontext.append((raw * cols[:, 1 + i : 2 + i]).astype(BF16))
    for h in range(low.shape[2] // HS):
        head = slice(h * HS, (h + 1) * HS)
        key, value = low[0, :, head], low[1, :, head]
        dkey = jnp.zeros((TOK, HS), F32)
        dvalue = jnp.zeros((TOK, HS), F32)
        for i in range(TOPK):
            query = low[2 + i, :, head]
            grad = dcontext[i][:, head]
            prob = probs[h, i * TOK : (i + 1) * TOK, :]
            dweight = mul(grad, value, NT)
            dscore = prob * (dweight - jnp.sum(prob * dweight, axis=-1, keepdims=True))
            dscore = dscore.astype(BF16)
            done = mul(dscore, key, NN) * HS ** (-0.5)
            dkey = dkey + mul(dscore, query, TN)
            dvalue = dvalue + mul(prob.astype(BF16), grad, TN)
            inner = inner + jnp.sum(done * query.astype(F32), axis=-1, keepdims=True)
            grads[2 + i, :, head] = (done * scale).astype(BF16)
        dkey = dkey * HS ** (-0.5)
        inner = inner + jnp.sum(
            dkey * key.astype(F32) + dvalue * value.astype(F32), axis=-1, keepdims=True
        )
        grads[0, :, head] = (dkey * scale).astype(BF16)
        grads[1, :, head] = (dvalue * scale).astype(BF16)
    lane = lax.broadcasted_iota(jnp.int32, (TOK, TOK), 1)
    table = jnp.where(lane == 0, dprob[0], jnp.where(lane == 1, dprob[1], jnp.where(lane == 2, inner, 0.0)))
    sums[...] = jnp.transpose(table)[0:8]


def columns(rows):
    return jnp.transpose(jnp.concatenate([rows] * (TOK // rows.shape[0]), axis=0))


def pick_row(values, index):
    line = lax.broadcasted_iota(jnp.int32, values.shape, 0)
    return jnp.sum(jnp.where(line == index, values, 0.0), axis=0, keepdims=True)


def route_body(subs, capacity):
    count = E * subs * 8

    def body(at, *refs):
        tables = refs[:E]
        hot_cols, home, turned, mlp_cols, expert_rows, select = refs[E : E + 6]
        both, rank, kept, hot, mlp_hot = refs[E + 6 :]
        expert = lax.broadcasted_iota(jnp.int32, (E, TOK), 0).astype(F32)
        for k in range(E):
            for j in range(subs):
                line = tables[k][j].astype(F32)
                ones = [(line[r : r + 1] == expert).astype(F32) for r in range(4)]
                start = (k * subs + j) * 8
                both[start : start + 4, :] = ones[0] + ones[1]
                both[start + 4 : start + 8, :] = ones[2] + ones[3]
                if j == 0:
                    hot[k, 0:4, :], hot[k, 4:8, :] = ones[0], ones[1]
                    mlp_hot[k, 0:4, :], mlp_hot[k, 4:8, :] = ones[2], ones[3]
        low = both[...].astype(BF16)
        row = lax.broadcasted_iota(jnp.int32, (TOK, TOK), 0)
        col = lax.broadcasted_iota(jnp.int32, (TOK, TOK), 1)
        rank[...] = mul(low, (row < col).astype(F32).astype(BF16), NN)
        row = lax.broadcasted_iota(jnp.int32, (count, count), 0)
        col = lax.broadcasted_iota(jnp.int32, (count, count), 1)
        own = at[2] * subs + at[1]
        ahead = (((col >> 3) ^ own) < ((row >> 3) ^ own)) & ((col & 7) == (row & 7))
        before = mul(ahead.astype(F32).astype(BF16), low, NN)
        place_of = jnp.sum(before, axis=-1, keepdims=True) + rank[...]
        kept[...] = both[...] * (place_of < capacity).astype(F32)

        for k in range(E):
            hot_cols[block(at[0] ^ k), :] = columns(hot[k])[:, 0:8]
        pad = jnp.zeros((6, TOK), F32)
        home[0:8, :] = hot[0]
        for i in range(TOPK):
            home[8 + i : 9 + i, :] = jnp.sum(
                hot[0, i * E : (i + 1) * E, :] * kept[0:E, :], axis=0, keepdims=True
            )
        home[10:16, :] = pad
        mine = mlp_hot[at[0]]
        start = pl.multiple_of(at[0] * (subs * 8), 8)
        kept_mine = kept[pl.ds(start, 8), :][4:8]
        rank_mine = rank[pl.ds(start, 8), :][4:8]
        turned[0:8, :] = mine
        for i in range(TOPK):
            turned[8 + i : 9 + i, :] = jnp.sum(
                mine[i * E : (i + 1) * E] * kept_mine, axis=0, keepdims=True
            )
        turned[10:16, :] = pad
        mlp_cols[...] = columns(mine)[:, 0:8]
        slot = lax.broadcasted_iota(jnp.int32, (SLOTS, TOK), 0).astype(F32)
        for k in range(E):
            e = at[2] ^ k
            for i in range(TOPK):
                expert_rows[2 * k + i : 2 * k + i + 1, :] = pick_row(mine[i * E : (i + 1) * E], e)
            taken = (slot == pick_row(rank_mine, e)) & (pick_row(kept_mine, e) > 0)
            select[k] = taken.astype(F32).astype(BF16)

    return body


def two_halves(values):
    lane = lax.broadcasted_iota(jnp.int32, (values[0].shape[0], 128), 1)
    table = jnp.zeros((values[0].shape[0], 128), F32)
    for i, one in enumerate(values):
        high = one.astype(BF16).astype(F32)
        table = jnp.where(lane == 2 * i, high, table)
        table = jnp.where(lane == 2 * i + 1, one - high, table)
    return table.astype(BF16)


def pick_body(at, stream, keep, got, other, gain, router, mlp_cols, select, *refs):
    hidden, stats, outs = refs[0], refs[1], refs[2:]
    size = hidden.shape[1]
    total = stream[...].astype(F32) + (keep[...] + got[0].astype(F32) + other[...].astype(F32))
    hidden[...] = total
    gained = total * gain[...]
    square = jnp.sum(total * total, axis=-1, keepdims=True)
    logits = lax.dot_general(
        gained, router[...], NT, precision=lax.Precision.HIGHEST, preferred_element_type=F32
    )
    lane = lax.broadcasted_iota(jnp.int32, logits.shape, 1)
    chosen = jnp.zeros_like(square)
    for e in range(E):
        one = mlp_cols[:, e : e + 1] + mlp_cols[:, E + e : E + e + 1]
        chosen = chosen + one * logits[:, e : e + 1]
    low = gained.astype(BF16)
    for k in range(E):
        own = jnp.sum(jnp.where(lane == (at[2] ^ k), logits, 0.0), axis=-1, keepdims=True)
        extra = two_halves([square, 2.0 * own - chosen])
        outs[k][:, :size] = mul(select[k], low, NN).astype(BF16)
        outs[k][:, size:] = mul(select[k], extra, NN).astype(BF16)
    lane = lax.broadcasted_iota(jnp.int32, (TOK, TOK), 1)
    table = jnp.where(lane == E, square, 0.0)
    for e in range(E):
        table = jnp.where(lane == e, logits[:, e : e + 1], table)
    stats[...] = jnp.transpose(table)[0:8]


def join_rows_body(at, *refs):
    pieces, out = refs[:E], refs[E]
    size = pieces[0].shape[1] - 128
    join_pieces(at, pieces, out, size)
    total = pieces[0][:, size:].astype(F32)
    for k in range(1, E):
        total = total + pieces[k][:, size:].astype(F32)
    square, gap = total[:, 0:1] + total[:, 1:2], total[:, 2:3] + total[:, 3:4]
    scale = lax.rsqrt(square / (E * size) + EPSILON)
    small = jnp.exp(-jnp.abs(gap * scale))
    gate = jnp.where(gap < 0.0, small, 1.0) / (1.0 + small)
    out[:, E * size :] = two_halves([scale, gate])


def join_pieces(at, pieces, out, size):
    for k in range(E):
        for p in range(E):

            @pl.when((at[2] ^ k) == p)
            def _(k=k, p=p):
                out[:, p * size : (p + 1) * size] = pieces[k][:, :size]


def join_body(at, *refs):
    join_pieces(at, refs[:E], refs[E], refs[0].shape[1])


def split_body(extra):
    def body(at, own, got, *refs):
        outs, store = refs[:E], refs[E]
        store[...] = (own[...] + got[...].astype(F32)).astype(BF16)
        size = outs[0].shape[1] - extra
        for k in range(E):
            for p in range(E):

                @pl.when((at[2] ^ k) == p)
                def _(k=k, p=p):
                    outs[k][:, :size] = store[:, p * size : (p + 1) * size]

            if extra:
                outs[k][:, size:] = store[:, E * size :]

    return body


def local(
    stream,
    out_grad,
    attn_gain,
    attn_router,
    key_value,
    query_proj,
    output_proj,
    mlp_gain,
    mlp_router,
    expert_in,
    expert_down,
    attn_routes,
    mlp_routes,
    doc_lengths,
):
    wide_count = lax.axis_size("wide")
    narrow_count = lax.axis_size("narrow")
    subs = wide_count // E
    wide = lax.axis_index("wide")
    narrow = lax.axis_index("narrow")
    plane, sub = wide // subs, wide % subs
    capacity = 9 * TOK * wide_count * TOPK // (8 * E)
    slice_width = stream.shape[1]
    shard_rows = attn_gain.shape[0]
    width = slice_width * narrow_count
    local_width = key_value.shape[2]
    head_count = local_width // HS
    hidden_units = expert_down.shape[1]
    score_scale = HS ** (-0.5)

    def after(values, *others):
        return lax.optimization_barrier((values, others))[0]

    def by_plane(values, k):
        return lax.ppermute(values, "wide", [(i, i ^ (k * subs)) for i in range(wide_count)])

    def by_sub(values, k):
        return lax.ppermute(values, "wide", [(i, i ^ k) for i in range(wide_count)])

    def by_narrow(values, k):
        return lax.ppermute(values, "narrow", [(i, i ^ k) for i in range(narrow_count)])

    def swap(values):
        pairs = []
        for w in range(wide_count):
            for n in range(narrow_count):
                z, y = w // subs, w % subs
                pairs.append((w * narrow_count + n, (n * subs + y) * narrow_count + z))
        return lax.ppermute(values, ("wide", "narrow"), pairs)

    def gather_planes(values):
        return [values] + [by_plane(values, k) for k in range(1, E)]

    def exchange_planes(parts):
        return [parts[0]] + [by_plane(parts[k], k) for k in range(1, E)]

    def gather_subs(values):
        parts, bit = [values], 1
        while bit < subs:
            parts = parts + [by_sub(one, bit) for one in parts]
            bit *= 2
        return parts

    def reduce_subs(parts):
        bit = len(parts) // 2
        while bit >= 1:
            parts = [parts[j] + by_sub(parts[j + bit].astype(BF16), bit).astype(F32) for j in range(bit)]
            bit //= 2
        return parts[0]

    def gather_narrow(values):
        other = by_narrow(values, 2)
        return [values, by_narrow(values, 1), other, by_narrow(other, 1)]

    def reduce_narrow(keep_0, keep_2, send):
        got = by_narrow(send, 1)
        other = by_narrow((keep_2 + got[1].astype(F32)).astype(BF16), 2)
        return keep_0, got, other

    def finish_subs(keep, send):
        bit = len(keep)
        keep = [keep[j] + by_sub(send[j], bit).astype(F32) for j in range(bit)]
        return reduce_subs(keep)

    def sum_narrow(values):
        values = values + by_narrow(values, 2)
        return values + by_narrow(values, 1)

    def sum_planes(values):
        values = values + by_plane(values, 1)
        return values + by_plane(values, 2)

    def sum_subs(values):
        bit = 1
        while bit < subs:
            values = values + by_sub(values, bit)
            bit *= 2
        return values

    own_rows = jnp.concatenate(
        [attn_gain[None, :], attn_router.T, mlp_gain[None, :], mlp_router.T], axis=0
    )
    parts = gather_subs(jnp.pad(own_rows, ((0, 16 - own_rows.shape[0]), (0, 0))))
    near = xor_shuffle(jnp.stack(parts), sub).swapaxes(0, 1).reshape(16, slice_width)
    gain_one_plane = near[0].astype(F32)
    gain_two_plane = near[5].astype(F32)
    router_two_plane = near[6:10].astype(F32)
    home_rows = swap(near)
    gain_one_home = home_rows[0].astype(F32)
    router_one_home = home_rows[1:5].astype(F32)

    own_routes = jnp.concatenate([attn_routes.T, mlp_routes.T], axis=0).astype(BF16)
    route_parts = gather_subs(jnp.pad(own_routes, ((0, 4), (0, 0))))
    at = jnp.stack([narrow ^ plane, sub, plane, narrow]).astype(jnp.int32)
    line_count = wide_count * 8
    hot_cols, home_hot, turned_hot, mlp_cols, expert_hot, select = run(
        "route",
        route_body(subs, capacity),
        [
            shape((E * TOK, 8), F32),
            shape((16, TOK), F32),
            shape((16, TOK), F32),
            shape((TOK, 8), F32),
            shape((8, TOK), F32),
            shape((E, SLOTS, TOK), BF16),
        ],
        [at, *gather_planes(jnp.stack(route_parts))],
        [pltpu.VMEM((line_count, TOK), F32)] * 3 + [pltpu.VMEM((E, 8, TOK), F32)] * 2,
    )
    hot_one, keep_one = home_hot[0:8].reshape(TOPK, E, TOK), home_hot[8:10]
    hot_two, keep_two = turned_hot[0:8].reshape(TOPK, E, TOK), turned_hot[8:10]
    hot_two_k = expert_hot.reshape(E, TOPK, TOK)

    kv_parts = gather_subs(key_value)
    query_parts = gather_subs(query_proj)
    home_stream = stream.astype(F32)
    turned_stream = swap(stream)
    turned_grad = swap(out_grad)

    rows_all = E * TOK
    sent = shape((2, TOK, local_width), BF16)
    kept_own = shape((2, TOK, local_width), F32)
    gained, *kv_blocks = run(
        "key_value",
        key_value_body(subs),
        [shape((rows_all, slice_width), BF16), kept_own] + [sent] * (E - 1),
        [at, *gather_narrow(turned_stream), gain_one_plane[None], *kv_parts],
        [
            pltpu.VMEM((2, slice_width, local_width), BF16),
            pltpu.VMEM((2, rows_all, local_width), F32),
        ],
    )
    kv_blocks = exchange_planes(kv_blocks)
    routed_scratch = [
        pltpu.VMEM((E, slice_width, local_width), BF16),
        pltpu.VMEM((TOPK, rows_all, local_width), F32),
    ]
    query_blocks = run(
        "query",
        routed_body(subs, True),
        [kept_own] + [sent] * (E - 1),
        [at, gained, hot_cols, *query_parts],
        routed_scratch,
    )
    query_blocks = exchange_planes(query_blocks)

    gained_home = home_stream * gain_one_home
    stats_one = jnp.concatenate(
        [
            jnp.sum(home_stream * home_stream, axis=-1)[None],
            dot(router_one_home, gained_home, ((1,), (1,)), PRECISE),
        ],
        axis=0,
    )
    stats_one = sum_narrow(stats_one)
    scale_one = lax.rsqrt(stats_one[0] / width + EPSILON)
    logits_one = stats_one[1:] * scale_one

    def gates(logits, hots):
        picked = jnp.sum(hots * logits[None], axis=1)
        gap = picked[0] - picked[1]
        return jnp.stack([jax.nn.sigmoid(gap), jax.nn.sigmoid(-gap)])

    prob_one = gates(logits_one, hot_one)
    gate_one = prob_one * keep_one

    token_rows = jnp.stack([scale_one, gate_one[0], gate_one[1]] + [scale_one] * 5)
    low, probs, context, gated = run(
        "attention",
        attention_body,
        [
            shape((4, TOK, local_width), BF16),
            shape((head_count, TOPK * TOK, TOK), F32),
            sent,
            sent,
        ],
        [doc_lengths[0], *kv_blocks, *query_blocks, token_rows],
    )

    out_parts = gather_subs(output_proj)

    folded = [shape((TOK, slice_width), F32), shape((TOK, slice_width), F32), shape((2, TOK, slice_width), BF16)]
    mixed, *attention = run(
        "output",
        output_body(subs),
        [shape((E, rows_all, local_width), BF16)] + folded,
        [at, *gather_planes(gated), hot_cols, *out_parts],
        [pltpu.VMEM((E, slice_width, local_width), BF16)],
    )
    def share(full):
        full = jnp.stack(gather_subs(full))
        two = jnp.stack([full, by_narrow(full, 2)])
        one = by_narrow(two, 1)
        return jnp.stack([two[0], one[0], two[1], one[1]]).reshape(-1, full.shape[-1])

    picked = jnp.einsum("kst,td->ksd", select, turned_grad, preferred_element_type=F32).astype(BF16)
    (full,) = run(
        "join",
        join_body,
        [shape((SLOTS, width), BF16)],
        [at, *exchange_planes([picked[k] for k in range(E)])],
    )
    grad_rows = share(full)
    weight_in = expert_in[0]
    weight_down = expert_down[0]
    dact_raw = dot(grad_rows, weight_down, ((1,), (1,)))

    hidden, stats_two, *picked = run(
        "pick",
        pick_body,
        [shape((TOK, slice_width), F32), shape((8, TOK), F32)]
        + [shape((SLOTS, slice_width + 128), BF16)] * E,
        [
            at,
            turned_stream,
            *reduce_narrow(*attention),
            gain_two_plane[None],
            jnp.pad(router_two_plane, ((0, 4), (0, 0))),
            mlp_cols,
            select,
        ],
    )
    (full,) = run(
        "join_rows",
        join_rows_body,
        [shape((SLOTS, width + 128), BF16)],
        [at, *exchange_planes(picked)],
    )
    full = share(full)
    expert_rows = full[:, :width]
    row_pairs = full[:, width : width + 4].astype(F32)
    row_scale = row_pairs[:, 0:1] + row_pairs[:, 1:2]
    row_gate = row_pairs[:, 2:3] + row_pairs[:, 3:4]
    stats_two = sum_planes(stats_two)
    scale_two = lax.rsqrt(stats_two[E] / width + EPSILON)
    logits_two = stats_two[:E] * scale_two
    prob_two = gates(logits_two, hot_two)

    gate_up = jnp.einsum("rd,dkf->krf", expert_rows, weight_in, preferred_element_type=F32)
    gate_pre = gate_up[0] * row_scale
    up_pre = gate_up[1] * row_scale
    gate_sig = jax.nn.sigmoid(gate_pre)
    silu_gate = gate_pre * gate_sig
    activation = (silu_gate * up_pre).astype(BF16)
    dactiv = dact_raw * row_gate
    dgate_pre = (dactiv * up_pre * gate_sig * (1.0 + gate_pre * (1.0 - gate_sig))).astype(BF16)
    dup_pre = (dactiv * silu_gate).astype(BF16)
    dprob_rows = jnp.sum(activation.astype(F32) * dact_raw, axis=-1)
    inner_rows = jnp.sum(dgate_pre.astype(F32) * gate_pre + dup_pre.astype(F32) * up_pre, axis=-1)
    drows = jnp.einsum(
        "krf,dkf->rd", jnp.stack([dgate_pre, dup_pre]), weight_in, preferred_element_type=F32
    )
    lanes = jnp.arange(128)
    row_stats = jnp.where(
        lanes[None, :] == 0, dprob_rows[:, None], jnp.where(lanes[None, :] == 1, inner_rows[:, None], 0.0)
    )

    def give_back(rows):
        shaped = rows.reshape(narrow_count, subs, SLOTS, -1)
        low = shaped.astype(BF16)
        got = by_narrow(jnp.stack([low[1], low[3]]), 1)
        two = jnp.stack([shaped[0], shaped[2]]) + got.astype(F32)
        one = two[0] + by_narrow(two[1].astype(BF16), 2).astype(F32)
        parts, bit = [one[j] for j in range(subs)], subs // 2
        while bit > 1:
            parts = [parts[j] + by_sub(parts[j + bit].astype(BF16), bit).astype(F32) for j in range(bit)]
            bit //= 2
        return parts[0], by_sub(parts[1].astype(BF16), 1)

    def from_planes(own, got, extra, last=None):
        pieces = run(
            "split",
            split_body(extra),
            [shape((SLOTS, slice_width + extra), BF16)] * E,
            [at, own, got],
            [pltpu.VMEM(own.shape, BF16)],
        )
        if last is not None:
            pieces = after(pieces, last)
        return jnp.stack(exchange_planes(pieces))

    returned = give_back(jnp.concatenate([drows, row_stats], axis=1))
    returned = from_planes(*returned, row_stats.shape[1])
    combined = jnp.einsum("kst,ksd->ktd", select, returned, preferred_element_type=F32)
    per_expert = combined[:, :, slice_width : slice_width + 2]
    dprob_two = keep_two * jnp.sum(hot_two_k * per_expert[:, None, :, 0], axis=0)
    inner_two = jnp.sum(per_expert[:, :, 1], axis=0)
    dnormed_two = jnp.sum(combined[:, :, :slice_width], axis=0)

    def gate_back(prob, dprob, hots):
        dselect = prob * (dprob - jnp.sum(prob * dprob, axis=0, keepdims=True))
        return jnp.sum(hots * dselect[:, None, :], axis=0)

    dlogit_two = gate_back(prob_two, dprob_two, hot_two)
    dnormed_two = dnormed_two + dot(dlogit_two, router_two_plane, ((0,), (0,)), PRECISE)
    inner_two = inner_two + jnp.sum(dlogit_two * logits_two, axis=0)
    dhidden = (
        turned_grad.astype(F32)
        + scale_two[:, None] * (dnormed_two * gain_two_plane)
        - hidden * (scale_two * scale_two * inner_two / width)[:, None]
    )
    scaled_hidden = hidden * scale_two[:, None]
    mlp_terms = jnp.concatenate(
        [
            jnp.sum(dnormed_two * scaled_hidden, axis=0)[None],
            dot(dlogit_two, scaled_hidden * gain_two_plane, ((1,), (0,)), PRECISE),
        ],
        axis=0,
    )

    wide_grad, *dcontext_blocks = run(
        "dcontext",
        routed_body(subs, False),
        [shape((rows_all, slice_width), BF16), kept_own] + [sent] * (E - 1),
        [at, *gather_narrow(dhidden.astype(BF16)), hot_cols, *out_parts],
        routed_scratch,
    )
    dcontext_blocks = exchange_planes(dcontext_blocks)

    def weight_parts(count):
        return [
            shape((count, shard_rows, local_width), F32 if j < subs // 2 else BF16)
            for j in range(subs)
        ]

    def weight_sum(parts):
        return finish_subs(parts[: subs // 2], parts[subs // 2 :])

    weight_scratch = [pltpu.VMEM((slice_width, local_width), F32)]
    output_parts = run(
        "output_grad", weight_grad_body, weight_parts(E), [at, wide_grad, mixed], weight_scratch
    )
    output_grad = weight_sum(output_parts)
    gated_act = (activation.astype(F32) * row_gate).astype(BF16)
    down_grad = dot(after(gated_act, dcontext_blocks[1]), grad_rows, ((0,), (0,)))
    grads_low, home_sums = run(
        "attention_back",
        attention_back_body,
        [shape((4, TOK, local_width), BF16), shape((8, TOK), F32)],
        [
            at,
            *after(dcontext_blocks, output_parts[-1], down_grad),
            token_rows,
            low,
            probs,
            context,
        ],
    )
    grad_planes = gather_planes(grads_low)
    home_sums = sum_narrow(home_sums)
    dprob_one = keep_one * home_sums[:2]
    dlogit_one = gate_back(prob_one, dprob_one, hot_one)
    inner_one = home_sums[2] + jnp.sum(dlogit_one * logits_one, axis=0)
    dlogit_scaled = dlogit_one * scale_one
    router_term = swap(dot(dlogit_scaled, gained_home, ((1,), (0,)), PRECISE))
    dmixed, *query_grad_parts = run(
        "query_grad",
        query_grad_body,
        [shape((E, rows_all, local_width), BF16)] + weight_parts(E),
        [at, gained, hot_cols, *after(grad_planes, output_grad, router_term)],
        weight_scratch,
    )
    query_grad = weight_sum(query_grad_parts)
    dkv_all, *dnormed_one = run(
        "input",
        input_body(subs),
        [shape((2, rows_all, local_width), BF16)] + folded,
        [at, *after(grad_planes, query_grad_parts[-1]), dmixed, *kv_parts, *query_parts],
        [pltpu.VMEM((2 + E, slice_width, local_width), BF16)],
    )
    kv_grad_parts = run(
        "key_value_grad", weight_grad_body, weight_parts(2), [at, gained, dkv_all], weight_scratch
    )
    kv_grad = weight_sum(after(kv_grad_parts, query_grad))
    keep, got, other = after(reduce_narrow(*dnormed_one), kv_grad_parts[-1], query_grad)
    dnormed_one = keep + got[0].astype(F32) + other.astype(F32)
    turned_out = dhidden + dnormed_one * gain_one_plane
    home_out = swap(turned_out.astype(BF16)).astype(F32)
    stream_grad = (
        home_out
        + gain_one_home * dot(dlogit_scaled, router_one_home, ((0,), (0,)), PRECISE)
        - home_stream * (scale_one * scale_one * inner_one / width)[:, None]
    )

    gain_term = jnp.sum(dnormed_one * turned_stream.astype(F32), axis=0)
    small = jnp.concatenate([mlp_terms, gain_term[None], router_term], axis=0)
    small = sum_subs(sum_narrow(small))
    mine = lax.dynamic_slice_in_dim(small, sub * shard_rows, shard_rows, 1)
    router_one_grad = mine[6:10]
    gain_one_grad = mine[5] + jnp.sum(
        router_one_grad * attn_router.T.astype(F32), axis=0
    ) / attn_gain.astype(F32)

    expert_out = dot(activation, weight_down, ((1,), (0,))) * row_gate
    mixture = from_planes(*give_back(expert_out), 0, grad_planes[E - 1])
    mixture = jnp.einsum("kst,ksd->td", select, after(mixture, turned_out), preferred_element_type=F32)
    layer_out = swap((hidden + mixture).astype(BF16)).astype(F32)
    dboth = jnp.stack(
        [
            (dgate_pre.astype(F32) * row_scale).astype(BF16),
            (dup_pre.astype(F32) * row_scale).astype(BF16),
        ],
        axis=1,
    )
    up_grad = jnp.einsum(
        "rd,rkf->dkf", expert_rows, after(dboth, turned_out), preferred_element_type=F32
    )

    return (
        layer_out,
        stream_grad,
        gain_one_grad,
        router_one_grad.T,
        kv_grad,
        query_grad,
        output_grad,
        mine[0],
        mine[1:5].T,
        up_grad[None],
        down_grad[None],
    )


def solution(mesh):
    in_specs = (
        P("wide", "narrow"),
        P("wide", "narrow"),
        P("wide"),
        P("wide", None),
        P(None, "wide", "narrow"),
        P(None, "wide", "narrow"),
        P(None, "wide", "narrow"),
        P("wide"),
        P("wide", None),
        P("wide", None, None, "narrow"),
        P("wide", "narrow", None),
        P("wide", None),
        P("wide", None),
        P("wide", None),
    )
    out_specs = (
        P("wide", "narrow"),
        P("wide", "narrow"),
        P("wide"),
        P("wide", None),
        P(None, "wide", "narrow"),
        P(None, "wide", "narrow"),
        P(None, "wide", "narrow"),
        P("wide"),
        P("wide", None),
        P("wide", None, None, "narrow"),
        P("wide", "narrow", None),
    )
    return jax.shard_map(local, mesh=mesh, in_specs=in_specs, out_specs=out_specs, check_vma=False)
```

```python
import jax
import jax.numpy as jnp
from jax import lax
from jax.experimental import pallas as pl
from jax.experimental.pallas import tpu as pltpu
from jax.sharding import PartitionSpec as P

HS = 128
E = 4
TOPK = 2
TOK = 128
SLOTS = 80

EPSILON = 1e-05
NEGATIVE = -1000000000.0
PRECISE = lax.Precision.HIGHEST
F32 = jnp.float32
BF16 = jnp.bfloat16


def dot(left, right, contract, precision=None):
    return lax.dot_general(
        left, right, ((contract[0], contract[1]), ((), ())), precision=precision, preferred_element_type=F32
    )


def xor_shuffle(values, amount):
    count, bit = values.shape[0], 1
    while bit < count:
        split = values.reshape((count // (2 * bit), 2, bit) + values.shape[1:])
        flipped = split[:, ::-1].reshape(values.shape)
        values = jnp.where((amount & bit) != 0, flipped, values)
        bit *= 2
    return values


NN = (((1,), (0,)), ((), ()))
NT = (((1,), (1,)), ((), ()))
TN = (((0,), (0,)), ((), ()))


def mul(left, right, form):
    return lax.dot_general(left, right, form, preferred_element_type=F32)


def shape(dims, dtype):
    return jax.ShapeDtypeStruct(tuple(dims), dtype)


def run(name, body, outs, args, scratch=()):
    vector = pl.BlockSpec(memory_space=pltpu.VMEM)
    return pl.pallas_call(
        body,
        out_shape=tuple(outs),
        in_specs=[pl.BlockSpec(memory_space=pltpu.SMEM)] + [vector] * (len(args) - 1),
        out_specs=tuple(vector for _ in outs),
        scratch_shapes=list(scratch),
        cost_estimate=pl.CostEstimate(flops=1, transcendentals=0, bytes_accessed=1),
        name=name,
    )(*args)


def place(store, parts, sub, first=0):
    for j, part in enumerate(parts):
        rows = part.shape[1]
        start = pl.multiple_of((sub ^ j) * rows, rows)
        for a in range(part.shape[0]):
            store[first + a, pl.ds(start, rows), :] = part[a]


def block(index):
    return pl.ds(pl.multiple_of(index * TOK, TOK), TOK)


def send_blocks(total, outs, order):
    for k in range(E):
        for a in range(total.shape[0]):
            outs[k][a] = total[a, block(order ^ k), :].astype(outs[k].dtype)


def key_value_body(subs):
    def body(at, *refs):
        rows, gain, parts = refs[:E], refs[E], refs[E + 1 : E + 1 + subs]
        gained, *outs = refs[E + 1 + subs : E + 2 + subs + E]
        weights, total = refs[E + 2 + subs + E :]
        place(weights, parts, at[1])
        for q in range(E):
            gained[q * TOK : (q + 1) * TOK, :] = (rows[q][...].astype(F32) * gain[...]).astype(BF16)
        for a in range(2):
            total[a] = mul(gained[...], weights[a], NN)
        send_blocks(total, outs, at[0])

    return body


def routed_body(subs, joined):
    count = 1 if joined else E

    def body(at, *refs):
        rows, hot, parts = refs[:count], refs[count], refs[count + 1 : count + 1 + subs]
        rest = refs[count + 1 + subs :]
        if joined:
            wide = rows[0]
        else:
            wide, rest = rest[0], rest[1:]
            for q in range(E):
                wide[q * TOK : (q + 1) * TOK, :] = rows[q][...]
        outs, weights, total = rest[:E], rest[E], rest[E + 1]
        place(weights, parts, at[1])
        for e in range(E):
            every = mul(wide[...], weights[e], NN)
            for i in range(TOPK):
                mine = every * hot[:, i * E + e : i * E + e + 1]
                total[i] = mine if e == 0 else total[i] + mine
        send_blocks(total, outs, at[0])

    return body


def spread_pairs(at, rows, hot, out, first=0):
    for k in range(E):
        where = block(at[0] ^ k)
        mask = hot[where, :].astype(BF16)
        for e in range(E):
            out[e, where, :] = (
                rows[k][first] * mask[:, e : e + 1]
                + rows[k][first + 1] * mask[:, E + e : E + e + 1]
            )


def fold_out(total, keep_0, keep_2, send):
    keep_0[...] = total[0:TOK]
    keep_2[...] = total[2 * TOK : 3 * TOK]
    send[0] = total[TOK : 2 * TOK].astype(BF16)
    send[1] = total[3 * TOK : 4 * TOK].astype(BF16)


def output_body(subs):
    def body(at, *refs):
        rows, hot, parts = refs[:E], refs[E], refs[E + 1 : E + 1 + subs]
        mixed, keep_0, keep_2, send, weights = refs[E + 1 + subs :]
        place(weights, parts, at[1])
        spread_pairs(at, rows, hot, mixed)
        total = mul(mixed[0], weights[0], NT)
        for e in range(1, E):
            total = total + mul(mixed[e], weights[e], NT)
        fold_out(total, keep_0, keep_2, send)

    return body


def input_body(subs):
    def body(at, *refs):
        rows, dmixed = refs[:E], refs[E]
        kv_parts = refs[E + 1 : E + 1 + subs]
        query_parts = refs[E + 1 + subs : E + 1 + 2 * subs]
        streams = refs[E + 1 + 2 * subs : 2 * E + 1 + 2 * subs]
        dkv_all, gain_row, keep_0, keep_2, send, weights = refs[2 * E + 1 + 2 * subs :]
        place(weights, kv_parts, at[1])
        place(weights, query_parts, at[1], 2)
        for k in range(E):
            for a in range(2):
                dkv_all[a, block(at[0] ^ k), :] = rows[k][a]
        total = mul(dkv_all[0], weights[0], NT) + mul(dkv_all[1], weights[1], NT)
        for e in range(E):
            total = total + mul(dmixed[e], weights[2 + e], NT)
        gain = jnp.zeros((1, total.shape[1]), F32)
        for q in range(E):
            part = total[q * TOK : (q + 1) * TOK] * streams[q][...].astype(F32)
            gain = gain + jnp.sum(part, axis=0, keepdims=True)
        gain_row[...] = gain
        fold_out(total, keep_0, keep_2, send)

    return body


def split_rows(at, rows, other, parts, total):
    for a in range(other.shape[0]):
        total[...] = mul(rows[...], other[a], TN)
        for j, part in enumerate(parts):
            count = part.shape[1]
            start = pl.multiple_of((at[1] ^ j) * count, count)
            part[a] = total[pl.ds(start, count), :].astype(part.dtype)


def weight_grad_body(at, rows, other, *refs):
    split_rows(at, rows, other, refs[:-1], refs[-1])


def query_grad_body(at, rows, hot, *refs):
    dmixed = refs[E]
    spread_pairs(at, refs[:E], hot, dmixed, 2)
    split_rows(at, rows, dmixed, refs[E + 1 : -1], refs[-1])


def attention_mask(at):
    row = lax.broadcasted_iota(jnp.int32, (TOK, TOK), 0)
    col = lax.broadcasted_iota(jnp.int32, (TOK, TOK), 1)
    row_doc, col_doc, end = jnp.zeros_like(row), jnp.zeros_like(row), 0
    for d in range(4):
        end = end + at[d]
        row_doc = row_doc + (row >= end).astype(jnp.int32)
        col_doc = col_doc + (col >= end).astype(jnp.int32)
    return (row_doc == col_doc) & (col <= row)


def attention_body(at, own_kv, *refs):
    got_kv, own_query, got_query = refs[: E - 1], refs[E - 1], refs[E : 2 * E - 1]
    rows, low, probs, context, gated = refs[2 * E - 1 :]
    cols = columns(rows[...])
    scale = cols[:, 0:1]
    for a in range(4):
        own, got = (own_kv, got_kv) if a < 2 else (own_query, got_query)
        total = own[a % 2]
        for one in got:
            total = total + one[a % 2].astype(F32)
        low[a] = (total * scale).astype(BF16)
    allowed = attention_mask(at)
    for h in range(low.shape[2] // HS):
        head = slice(h * HS, (h + 1) * HS)
        for i in range(TOPK):
            scores = mul(low[2 + i, :, head], low[0, :, head], NT) * HS ** (-0.5)
            scores = jnp.where(allowed, scores, NEGATIVE)
            top = jnp.exp(scores - jnp.max(scores, axis=-1, keepdims=True))
            prob = top / jnp.sum(top, axis=-1, keepdims=True)
            probs[h, i * TOK : (i + 1) * TOK, :] = prob
            mixed = mul(prob.astype(BF16), low[1, :, head], NN).astype(BF16)
            context[i, :, head] = mixed
            gated[i, :, head] = (mixed.astype(F32) * cols[:, 1 + i : 2 + i]).astype(BF16)


def attention_back_body(at, own, *refs):
    got = refs[: E - 1]
    rows, low, probs, context, grads, sums = refs[E - 1 :]
    cols = columns(rows[...])
    scale = cols[:, 0:1]
    inner = jnp.zeros((TOK, 1), F32)
    dprob = []
    dcontext = []
    for i in range(TOPK):
        raw = own[i]
        for one in got:
            raw = raw + one[i].astype(F32)
        dprob.append(jnp.sum(context[i].astype(F32) * raw, axis=-1, keepdims=True))
        dcontext.append((raw * cols[:, 1 + i : 2 + i]).astype(BF16))
    for h in range(low.shape[2] // HS):
        head = slice(h * HS, (h + 1) * HS)
        key, value = low[0, :, head], low[1, :, head]
        dkey = jnp.zeros((TOK, HS), F32)
        dvalue = jnp.zeros((TOK, HS), F32)
        for i in range(TOPK):
            query = low[2 + i, :, head]
            grad = dcontext[i][:, head]
            prob = probs[h, i * TOK : (i + 1) * TOK, :]
            dweight = mul(grad, value, NT)
            dscore = prob * (dweight - jnp.sum(prob * dweight, axis=-1, keepdims=True))
            dscore = dscore.astype(BF16)
            done = mul(dscore, key, NN) * HS ** (-0.5)
            dkey = dkey + mul(dscore, query, TN)
            dvalue = dvalue + mul(prob.astype(BF16), grad, TN)
            inner = inner + jnp.sum(done * query.astype(F32), axis=-1, keepdims=True)
            grads[2 + i, :, head] = (done * scale).astype(BF16)
        dkey = dkey * HS ** (-0.5)
        inner = inner + jnp.sum(
            dkey * key.astype(F32) + dvalue * value.astype(F32), axis=-1, keepdims=True
        )
        grads[0, :, head] = (dkey * scale).astype(BF16)
        grads[1, :, head] = (dvalue * scale).astype(BF16)
    lane = lax.broadcasted_iota(jnp.int32, (TOK, TOK), 1)
    table = jnp.where(lane == 0, dprob[0], jnp.where(lane == 1, dprob[1], jnp.where(lane == 2, inner, 0.0)))
    sums[...] = jnp.transpose(table)[0:8]


def columns(rows):
    return jnp.transpose(jnp.concatenate([rows] * (TOK // rows.shape[0]), axis=0))


def pick_row(values, index):
    line = lax.broadcasted_iota(jnp.int32, values.shape, 0)
    return jnp.sum(jnp.where(line == index, values, 0.0), axis=0, keepdims=True)


def route_body(subs, capacity):
    count = E * subs * 8

    def body(at, *refs):
        tables = refs[:E]
        hot_cols, home, turned, mlp_cols, expert_rows, select = refs[E : E + 6]
        both, rank, kept, hot, mlp_hot = refs[E + 6 :]
        expert = lax.broadcasted_iota(jnp.int32, (E, TOK), 0).astype(F32)
        for k in range(E):
            for j in range(subs):
                line = tables[k][j].astype(F32)
                ones = [(line[r : r + 1] == expert).astype(F32) for r in range(4)]
                start = (k * subs + j) * 8
                both[start : start + 4, :] = ones[0] + ones[1]
                both[start + 4 : start + 8, :] = ones[2] + ones[3]
                if j == 0:
                    hot[k, 0:4, :], hot[k, 4:8, :] = ones[0], ones[1]
                    mlp_hot[k, 0:4, :], mlp_hot[k, 4:8, :] = ones[2], ones[3]
        low = both[...].astype(BF16)
        row = lax.broadcasted_iota(jnp.int32, (TOK, TOK), 0)
        col = lax.broadcasted_iota(jnp.int32, (TOK, TOK), 1)
        rank[...] = mul(low, (row < col).astype(F32).astype(BF16), NN)
        row = lax.broadcasted_iota(jnp.int32, (count, count), 0)
        col = lax.broadcasted_iota(jnp.int32, (count, count), 1)
        own = at[2] * subs + at[1]
        ahead = (((col >> 3) ^ own) < ((row >> 3) ^ own)) & ((col & 7) == (row & 7))
        before = mul(ahead.astype(F32).astype(BF16), low, NN)
        place_of = jnp.sum(before, axis=-1, keepdims=True) + rank[...]
        kept[...] = both[...] * (place_of < capacity).astype(F32)

        for k in range(E):
            hot_cols[block(at[0] ^ k), :] = columns(hot[k])[:, 0:8]
        pad = jnp.zeros((6, TOK), F32)
        home[0:8, :] = hot[0]
        for i in range(TOPK):
            home[8 + i : 9 + i, :] = jnp.sum(
                hot[0, i * E : (i + 1) * E, :] * kept[0:E, :], axis=0, keepdims=True
            )
        home[10:16, :] = pad
        mine = mlp_hot[at[0]]
        start = pl.multiple_of(at[0] * (subs * 8), 8)
        kept_mine = kept[pl.ds(start, 8), :][4:8]
        rank_mine = rank[pl.ds(start, 8), :][4:8]
        turned[0:8, :] = mine
        for i in range(TOPK):
            turned[8 + i : 9 + i, :] = jnp.sum(
                mine[i * E : (i + 1) * E] * kept_mine, axis=0, keepdims=True
            )
        turned[10:16, :] = pad
        mlp_cols[...] = columns(mine)[:, 0:8]
        slot = lax.broadcasted_iota(jnp.int32, (SLOTS, TOK), 0).astype(F32)
        for k in range(E):
            e = at[2] ^ k
            for i in range(TOPK):
                expert_rows[2 * k + i : 2 * k + i + 1, :] = pick_row(mine[i * E : (i + 1) * E], e)
            taken = (slot == pick_row(rank_mine, e)) & (pick_row(kept_mine, e) > 0)
            select[k] = taken.astype(F32).astype(BF16)

    return body


def two_halves(values):
    lane = lax.broadcasted_iota(jnp.int32, (values[0].shape[0], 128), 1)
    table = jnp.zeros((values[0].shape[0], 128), F32)
    for i, one in enumerate(values):
        high = one.astype(BF16).astype(F32)
        table = jnp.where(lane == 2 * i, high, table)
        table = jnp.where(lane == 2 * i + 1, one - high, table)
    return table.astype(BF16)


def pick_body(at, stream, keep, got, other, gain, router, mlp_cols, select, *refs):
    hidden, stats, outs = refs[0], refs[1], refs[2:]
    size = hidden.shape[1]
    total = stream[...].astype(F32) + (keep[...] + got[0].astype(F32) + other[...].astype(F32))
    hidden[...] = total
    gained = total * gain[...]
    square = jnp.sum(total * total, axis=-1, keepdims=True)
    logits = lax.dot_general(
        gained, router[...], NT, precision=lax.Precision.HIGHEST, preferred_element_type=F32
    )
    lane = lax.broadcasted_iota(jnp.int32, logits.shape, 1)
    chosen = jnp.zeros_like(square)
    for e in range(E):
        one = mlp_cols[:, e : e + 1] + mlp_cols[:, E + e : E + e + 1]
        chosen = chosen + one * logits[:, e : e + 1]
    low = gained.astype(BF16)
    for k in range(E):
        own = jnp.sum(jnp.where(lane == (at[2] ^ k), logits, 0.0), axis=-1, keepdims=True)
        extra = two_halves([square, 2.0 * own - chosen])
        outs[k][:, :size] = mul(select[k], low, NN).astype(BF16)
        outs[k][:, size:] = mul(select[k], extra, NN).astype(BF16)
    lane = lax.broadcasted_iota(jnp.int32, (TOK, TOK), 1)
    table = jnp.where(lane == E, square, 0.0)
    for e in range(E):
        table = jnp.where(lane == e, logits[:, e : e + 1], table)
    stats[...] = jnp.transpose(table)[0:8]


def join_rows_body(at, *refs):
    pieces, out = refs[:E], refs[E]
    size = pieces[0].shape[1] - 128
    join_pieces(at, pieces, out, size)
    total = pieces[0][:, size:].astype(F32)
    for k in range(1, E):
        total = total + pieces[k][:, size:].astype(F32)
    square, gap = total[:, 0:1] + total[:, 1:2], total[:, 2:3] + total[:, 3:4]
    scale = lax.rsqrt(square / (E * size) + EPSILON)
    small = jnp.exp(-jnp.abs(gap * scale))
    gate = jnp.where(gap < 0.0, small, 1.0) / (1.0 + small)
    out[:, E * size :] = two_halves([scale, gate])


def join_pieces(at, pieces, out, size):
    for k in range(E):
        for p in range(E):

            @pl.when((at[2] ^ k) == p)
            def _(k=k, p=p):
                out[:, p * size : (p + 1) * size] = pieces[k][:, :size]


def join_body(at, *refs):
    join_pieces(at, refs[:E], refs[E], refs[0].shape[1])


def split_body(extra):
    def body(at, own, got, *refs):
        outs, store = refs[:E], refs[E]
        store[...] = (own[...] + got[...].astype(F32)).astype(BF16)
        size = outs[0].shape[1] - extra
        for k in range(E):
            for p in range(E):

                @pl.when((at[2] ^ k) == p)
                def _(k=k, p=p):
                    outs[k][:, :size] = store[:, p * size : (p + 1) * size]

            if extra:
                outs[k][:, size:] = store[:, E * size :]

    return body


def local(
    stream,
    out_grad,
    attn_gain,
    attn_router,
    key_value,
    query_proj,
    output_proj,
    mlp_gain,
    mlp_router,
    expert_in,
    expert_down,
    attn_routes,
    mlp_routes,
    doc_lengths,
):
    wide_count = lax.axis_size("wide")
    narrow_count = lax.axis_size("narrow")
    subs = wide_count // E
    wide = lax.axis_index("wide")
    narrow = lax.axis_index("narrow")
    plane, sub = wide // subs, wide % subs
    capacity = 9 * TOK * wide_count * TOPK // (8 * E)
    slice_width = stream.shape[1]
    shard_rows = attn_gain.shape[0]
    width = slice_width * narrow_count
    local_width = key_value.shape[2]
    head_count = local_width // HS
    hidden_units = expert_down.shape[1]
    score_scale = HS ** (-0.5)

    def after(values, *others):
        return lax.optimization_barrier((values, others))[0]

    def by_plane(values, k):
        return lax.ppermute(values, "wide", [(i, i ^ (k * subs)) for i in range(wide_count)])

    def by_sub(values, k):
        return lax.ppermute(values, "wide", [(i, i ^ k) for i in range(wide_count)])

    def by_narrow(values, k):
        return lax.ppermute(values, "narrow", [(i, i ^ k) for i in range(narrow_count)])

    def swap(values):
        pairs = []
        for w in range(wide_count):
            for n in range(narrow_count):
                z, y = w // subs, w % subs
                pairs.append((w * narrow_count + n, (n * subs + y) * narrow_count + z))
        return lax.ppermute(values, ("wide", "narrow"), pairs)

    def by_side(values, side):
        pairs = []
        for w in range(wide_count):
            for n in range(narrow_count):
                other = (w ^ 1, n) if (n & 1) == side else (w, n ^ 2)
                pairs.append((w * narrow_count + n, other[0] * narrow_count + other[1]))
        return lax.ppermute(values, ("wide", "narrow"), pairs)

    def gather_planes(values):
        return [values] + [by_plane(values, k) for k in range(1, E)]

    def exchange_planes(parts):
        return [parts[0]] + [by_plane(parts[k], k) for k in range(1, E)]

    def gather_subs(values, *others):
        parts, bit = [values], 1
        while bit < subs:
            parts = parts + [by_sub(after(one, *others) if others else one, bit) for one in parts]
            bit *= 2
        return parts

    def reduce_subs(parts):
        bit = len(parts) // 2
        while bit >= 1:
            parts = [parts[j] + by_sub(parts[j + bit].astype(BF16), bit).astype(F32) for j in range(bit)]
            bit //= 2
        return parts[0]

    def gather_narrow(values):
        other = by_narrow(values, 2)
        return [values, by_narrow(values, 1), other, by_narrow(other, 1)]

    def reduce_narrow(keep_0, keep_2, send):
        got = by_narrow(send, 1)
        other = by_narrow((keep_2 + got[1].astype(F32)).astype(BF16), 2)
        return keep_0, got, other

    def finish_subs(keep, send):
        bit = len(keep)
        got = [by_sub(send[j], bit) for j in range(bit)]
        return reduce_subs([keep[j] + got[j].astype(F32) for j in range(bit)]), got

    def sum_narrow(values):
        values = values + by_narrow(values, 2)
        return values + by_narrow(values, 1)

    def sum_planes(values):
        values = values + by_plane(values, 1)
        return values + by_plane(values, 2)

    def sum_subs(values):
        bit = 1
        while bit < subs:
            values = values + by_sub(values, bit)
            bit *= 2
        return values

    turned_stream = swap(stream)

    own_rows = jnp.concatenate(
        [attn_gain[None, :], attn_router.T, mlp_gain[None, :], mlp_router.T], axis=0
    )
    parts = gather_subs(jnp.pad(own_rows, ((0, 16 - own_rows.shape[0]), (0, 0))))
    near = xor_shuffle(jnp.stack(parts), sub).swapaxes(0, 1).reshape(16, slice_width)
    gain_one_plane = near[0].astype(F32)
    gain_two_plane = near[5].astype(F32)
    router_two_plane = near[6:10].astype(F32)
    home_rows = swap(near)
    gain_one_home = home_rows[0].astype(F32)
    router_one_home = home_rows[1:5].astype(F32)

    own_routes = jnp.concatenate([attn_routes.T, mlp_routes.T], axis=0).astype(BF16)
    route_parts = gather_subs(jnp.pad(own_routes, ((0, 4), (0, 0))))
    at = jnp.stack([narrow ^ plane, sub, plane, narrow]).astype(jnp.int32)
    line_count = wide_count * 8
    hot_cols, home_hot, turned_hot, mlp_cols, expert_hot, select = run(
        "route",
        route_body(subs, capacity),
        [
            shape((E * TOK, 8), F32),
            shape((16, TOK), F32),
            shape((16, TOK), F32),
            shape((TOK, 8), F32),
            shape((8, TOK), F32),
            shape((E, SLOTS, TOK), BF16),
        ],
        [at, *after(gather_planes(jnp.stack(route_parts)), turned_stream)],
        [pltpu.VMEM((line_count, TOK), F32)] * 3 + [pltpu.VMEM((E, 8, TOK), F32)] * 2,
    )
    hot_one, keep_one = home_hot[0:8].reshape(TOPK, E, TOK), home_hot[8:10]
    hot_two, keep_two = turned_hot[0:8].reshape(TOPK, E, TOK), turned_hot[8:10]
    hot_two_k = expert_hot.reshape(E, TOPK, TOK)

    kv_parts = gather_subs(key_value)
    query_parts = gather_subs(query_proj, kv_parts[-1])
    out_parts = gather_subs(output_proj, query_parts[-1])
    home_stream = stream.astype(F32)
    turned_grad = swap(out_grad)

    rows_all = E * TOK
    sent = shape((2, TOK, local_width), BF16)
    kept_own = shape((2, TOK, local_width), F32)
    all_streams = gather_narrow(turned_stream)
    gained, *kv_blocks = run(
        "key_value",
        key_value_body(subs),
        [shape((rows_all, slice_width), BF16), kept_own] + [sent] * (E - 1),
        [at, *all_streams, gain_one_plane[None], *kv_parts],
        [
            pltpu.VMEM((2, slice_width, local_width), BF16),
            pltpu.VMEM((2, rows_all, local_width), F32),
        ],
    )
    kv_blocks = exchange_planes(kv_blocks)
    routed_scratch = [
        pltpu.VMEM((E, slice_width, local_width), BF16),
        pltpu.VMEM((TOPK, rows_all, local_width), F32),
    ]
    gained_home = home_stream * gain_one_home
    stats_one = jnp.concatenate(
        [
            jnp.sum(home_stream * home_stream, axis=-1)[None],
            dot(router_one_home, gained_home, ((1,), (1,)), PRECISE),
        ],
        axis=0,
    )
    stats_one = sum_narrow(stats_one)
    query_blocks = run(
        "query",
        routed_body(subs, True),
        [kept_own] + [sent] * (E - 1),
        [at, after(gained, *kv_blocks[1:], stats_one), hot_cols, *query_parts],
        routed_scratch,
    )
    query_blocks = exchange_planes(query_blocks)

    scale_one = lax.rsqrt(stats_one[0] / width + EPSILON)
    logits_one = stats_one[1:] * scale_one

    def gates(logits, hots):
        picked = jnp.sum(hots * logits[None], axis=1)
        gap = picked[0] - picked[1]
        return jnp.stack([jax.nn.sigmoid(gap), jax.nn.sigmoid(-gap)])

    prob_one = gates(logits_one, hot_one)
    gate_one = prob_one * keep_one

    def share(full):
        size = full.shape[-1]
        full = jnp.concatenate([full, by_side(full, 0)], axis=0)
        got = by_side(full, 1)
        full = jnp.concatenate([full, got], axis=0)
        bit = 2
        while bit < subs:
            full = jnp.concatenate([full, by_sub(full, bit)], axis=0)
            bit *= 2
        return jnp.concatenate([full, by_narrow(full, 1)], axis=0).reshape(-1, size), got

    picked = jnp.einsum("kst,td->ksd", select, turned_grad, preferred_element_type=F32).astype(BF16)
    token_rows = jnp.stack([scale_one, gate_one[0], gate_one[1]] + [scale_one] * 5)
    low, probs, context, gated = run(
        "attention",
        attention_body,
        [
            shape((4, TOK, local_width), BF16),
            shape((head_count, TOPK * TOK, TOK), F32),
            sent,
            sent,
        ],
        [doc_lengths[0], *kv_blocks, *query_blocks, token_rows],
    )

    (full,) = run(
        "join",
        join_body,
        [shape((SLOTS, width), BF16)],
        [at, *after(exchange_planes([picked[k] for k in range(E)]), gated)],
    )
    grad_rows, grad_got = share(full)
    folded = [shape((TOK, slice_width), F32), shape((TOK, slice_width), F32), shape((2, TOK, slice_width), BF16)]
    mixed, *attention = run(
        "output",
        output_body(subs),
        [shape((E, rows_all, local_width), BF16)] + folded,
        [at, *gather_planes(gated), hot_cols, *out_parts],
        [pltpu.VMEM((E, slice_width, local_width), BF16)],
    )
    weight_in = expert_in[0]
    weight_down = expert_down[0]
    dact_raw = dot(grad_rows, weight_down, ((1,), (1,)))

    hidden, stats_two, *picked = run(
        "pick",
        pick_body,
        [shape((TOK, slice_width), F32), shape((8, TOK), F32)]
        + [shape((SLOTS, slice_width + 128), BF16)] * E,
        [
            at,
            turned_stream,
            *after(reduce_narrow(*attention), grad_got),
            gain_two_plane[None],
            jnp.pad(router_two_plane, ((0, 4), (0, 0))),
            mlp_cols,
            select,
        ],
    )
    (full,) = run(
        "join_rows",
        join_rows_body,
        [shape((SLOTS, width + 128), BF16)],
        [at, *exchange_planes(picked)],
    )
    stats_two = sum_planes(stats_two)
    full, _ = share(full)
    full = after(full, stats_two)
    expert_rows = full[:, :width]
    row_pairs = full[:, width : width + 4].astype(F32)
    row_scale = row_pairs[:, 0:1] + row_pairs[:, 1:2]
    row_gate = row_pairs[:, 2:3] + row_pairs[:, 3:4]
    scale_two = lax.rsqrt(stats_two[E] / width + EPSILON)
    logits_two = stats_two[:E] * scale_two
    prob_two = gates(logits_two, hot_two)

    gate_up = jnp.einsum("rd,dkf->krf", expert_rows, weight_in, preferred_element_type=F32)
    gate_pre = gate_up[0] * row_scale
    up_pre = gate_up[1] * row_scale
    gate_sig = jax.nn.sigmoid(gate_pre)
    silu_gate = gate_pre * gate_sig
    activation = (silu_gate * up_pre).astype(BF16)
    dactiv = dact_raw * row_gate
    dgate_pre = (dactiv * up_pre * gate_sig * (1.0 + gate_pre * (1.0 - gate_sig))).astype(BF16)
    dup_pre = (dactiv * silu_gate).astype(BF16)
    dprob_rows = jnp.sum(activation.astype(F32) * dact_raw, axis=-1)
    inner_rows = jnp.sum(dgate_pre.astype(F32) * gate_pre + dup_pre.astype(F32) * up_pre, axis=-1)
    drows = jnp.einsum(
        "krf,dkf->rd", jnp.stack([dgate_pre, dup_pre]), weight_in, preferred_element_type=F32
    )
    lanes = jnp.arange(128)
    row_stats = jnp.where(
        lanes[None, :] == 0, dprob_rows[:, None], jnp.where(lanes[None, :] == 1, inner_rows[:, None], 0.0)
    )

    def give_back(rows):
        half = rows.shape[0] // 2
        rows = rows[:half] + by_narrow(rows[half:].astype(BF16), 1).astype(F32)
        bit = subs // 2
        while bit > 1:
            half = rows.shape[0] // 2
            rows = rows[:half] + by_sub(rows[half:].astype(BF16), bit).astype(F32)
            bit //= 2
        half = rows.shape[0] // 2
        rows = rows[:half] + by_side(rows[half:].astype(BF16), 1).astype(F32)
        return rows[:SLOTS], by_side(rows[SLOTS:].astype(BF16), 0)

    def from_planes(own, got, extra, last=None):
        if last is not None:
            own = after(own, last)
        pieces = run(
            "split",
            split_body(extra),
            [shape((SLOTS, slice_width + extra), BF16)] * E,
            [at, own, got],
            [pltpu.VMEM(own.shape, BF16)],
        )
        return jnp.stack(exchange_planes(pieces))

    returned = give_back(jnp.concatenate([drows, row_stats], axis=1))
    returned = from_planes(*returned, row_stats.shape[1])
    combined = jnp.einsum("kst,ksd->ktd", select, returned, preferred_element_type=F32)
    per_expert = combined[:, :, slice_width : slice_width + 2]
    dprob_two = keep_two * jnp.sum(hot_two_k * per_expert[:, None, :, 0], axis=0)
    inner_two = jnp.sum(per_expert[:, :, 1], axis=0)
    dnormed_two = jnp.sum(combined[:, :, :slice_width], axis=0)

    def gate_back(prob, dprob, hots):
        dselect = prob * (dprob - jnp.sum(prob * dprob, axis=0, keepdims=True))
        return jnp.sum(hots * dselect[:, None, :], axis=0)

    dlogit_two = gate_back(prob_two, dprob_two, hot_two)
    dnormed_two = dnormed_two + dot(dlogit_two, router_two_plane, ((0,), (0,)), PRECISE)
    inner_two = inner_two + jnp.sum(dlogit_two * logits_two, axis=0)
    dhidden = (
        turned_grad.astype(F32)
        + scale_two[:, None] * (dnormed_two * gain_two_plane)
        - hidden * (scale_two * scale_two * inner_two / width)[:, None]
    )
    scaled_hidden = hidden * scale_two[:, None]
    mlp_terms = jnp.concatenate(
        [
            jnp.sum(dnormed_two * scaled_hidden, axis=0)[None],
            dot(dlogit_two, scaled_hidden * gain_two_plane, ((1,), (0,)), PRECISE),
        ],
        axis=0,
    )

    wide_grad, *dcontext_blocks = run(
        "dcontext",
        routed_body(subs, False),
        [shape((rows_all, slice_width), BF16), kept_own] + [sent] * (E - 1),
        [at, *gather_narrow(dhidden.astype(BF16)), hot_cols, *out_parts],
        routed_scratch,
    )
    dcontext_blocks = exchange_planes(dcontext_blocks)

    def weight_parts(count):
        return [
            shape((count, shard_rows, local_width), F32 if j < subs // 2 else BF16)
            for j in range(subs)
        ]

    def weight_sum(parts):
        return finish_subs(parts[: subs // 2], parts[subs // 2 :])

    weight_scratch = [pltpu.VMEM((slice_width, local_width), F32)]
    output_parts = run(
        "output_grad", weight_grad_body, weight_parts(E), [at, wide_grad, mixed], weight_scratch
    )
    expert_out = dot(activation, weight_down, ((1,), (0,))) * row_gate
    mixture = give_back(expert_out)
    output_grad, output_got = weight_sum(output_parts)
    gated_act = (activation.astype(F32) * row_gate).astype(BF16)
    down_grad = dot(after(gated_act, dcontext_blocks[0]), grad_rows, ((0,), (0,)))
    grads_low, home_sums = run(
        "attention_back",
        attention_back_body,
        [shape((4, TOK, local_width), BF16), shape((8, TOK), F32)],
        [
            at,
            *after(dcontext_blocks, output_parts[-1], down_grad),
            token_rows,
            low,
            probs,
            context,
        ],
    )
    grad_planes = gather_planes(grads_low)
    dmixed, *query_grad_parts = run(
        "query_grad",
        query_grad_body,
        [shape((E, rows_all, local_width), BF16)] + weight_parts(E),
        [at, gained, hot_cols, *after(grad_planes, output_got)],
        weight_scratch,
    )
    query_grad, query_got = weight_sum(query_grad_parts)
    dkv_all, gain_row, *dnormed_one = run(
        "input",
        input_body(subs),
        [shape((2, rows_all, local_width), BF16), shape((1, slice_width), F32)] + folded,
        [
            at,
            *after(grad_planes, query_grad_parts[-1]),
            dmixed,
            *kv_parts,
            *query_parts,
            *all_streams,
        ],
        [pltpu.VMEM((2 + E, slice_width, local_width), BF16)],
    )
    home_sums = sum_narrow(after(home_sums, gain_row))
    dprob_one = keep_one * home_sums[:2]
    dlogit_one = gate_back(prob_one, dprob_one, hot_one)
    inner_one = home_sums[2] + jnp.sum(dlogit_one * logits_one, axis=0)
    dlogit_scaled = dlogit_one * scale_one
    router_term = swap(dot(dlogit_scaled, gained_home, ((1,), (0,)), PRECISE))
    kv_grad_parts = run(
        "key_value_grad", weight_grad_body, weight_parts(2), [at, gained, dkv_all], weight_scratch
    )
    kv_grad, _ = weight_sum(after(kv_grad_parts, query_got))
    keep, got, other = after(reduce_narrow(*dnormed_one), kv_grad_parts[-1], query_got)
    dnormed_one = keep + got[0].astype(F32) + other.astype(F32)
    turned_out = dhidden + dnormed_one * gain_one_plane
    home_out = swap(turned_out.astype(BF16)).astype(F32)
    stream_grad = (
        home_out
        + gain_one_home * dot(dlogit_scaled, router_one_home, ((0,), (0,)), PRECISE)
        - home_stream * (scale_one * scale_one * inner_one / width)[:, None]
    )

    small = jnp.concatenate([mlp_terms, gain_row, router_term], axis=0)
    small = sum_subs(sum_narrow(after(small, query_got)))
    mine = lax.dynamic_slice_in_dim(small, sub * shard_rows, shard_rows, 1)
    router_one_grad = mine[6:10]
    gain_one_grad = mine[5] + jnp.sum(
        router_one_grad * attn_router.T.astype(F32), axis=0
    ) / attn_gain.astype(F32)

    mixture = from_planes(*mixture, 0, gain_row)
    mixture = jnp.einsum("kst,ksd->td", select, after(mixture, turned_out), preferred_element_type=F32)
    layer_out = swap((hidden + mixture).astype(BF16)).astype(F32)
    dboth = jnp.stack(
        [
            (dgate_pre.astype(F32) * row_scale).astype(BF16),
            (dup_pre.astype(F32) * row_scale).astype(BF16),
        ],
        axis=1,
    )
    up_grad = jnp.einsum(
        "rd,rkf->dkf", expert_rows, after(dboth, turned_out), preferred_element_type=F32
    )

    return (
        layer_out,
        stream_grad,
        gain_one_grad,
        router_one_grad.T,
        kv_grad,
        query_grad,
        output_grad,
        mine[0],
        mine[1:5].T,
        up_grad[None],
        down_grad[None],
    )


def solution(mesh):
    in_specs = (
        P("wide", "narrow"),
        P("wide", "narrow"),
        P("wide"),
        P("wide", None),
        P(None, "wide", "narrow"),
        P(None, "wide", "narrow"),
        P(None, "wide", "narrow"),
        P("wide"),
        P("wide", None),
        P("wide", None, None, "narrow"),
        P("wide", "narrow", None),
        P("wide", None),
        P("wide", None),
        P("wide", None),
    )
    out_specs = (
        P("wide", "narrow"),
        P("wide", "narrow"),
        P("wide"),
        P("wide", None),
        P(None, "wide", "narrow"),
        P(None, "wide", "narrow"),
        P(None, "wide", "narrow"),
        P("wide"),
        P("wide", None),
        P("wide", None, None, "narrow"),
        P("wide", "narrow", None),
    )
    return jax.shard_map(local, mesh=mesh, in_specs=in_specs, out_specs=out_specs, check_vma=False)
```

```python
import jax
import jax.numpy as jnp
from jax import lax
from jax.experimental import pallas as pl
from jax.experimental.pallas import tpu as pltpu
from jax.sharding import PartitionSpec as P

HS = 128
E = 4
TOPK = 2
TOK = 128
SLOTS = 80

EPSILON = 1e-05
NEGATIVE = -1000000000.0
PRECISE = lax.Precision.HIGHEST
F32 = jnp.float32
BF16 = jnp.bfloat16


def dot(left, right, contract, precision=None):
    return lax.dot_general(
        left, right, ((contract[0], contract[1]), ((), ())), precision=precision, preferred_element_type=F32
    )


def xor_shuffle(values, amount):
    count, bit = values.shape[0], 1
    while bit < count:
        split = values.reshape((count // (2 * bit), 2, bit) + values.shape[1:])
        flipped = split[:, ::-1].reshape(values.shape)
        values = jnp.where((amount & bit) != 0, flipped, values)
        bit *= 2
    return values


NN = (((1,), (0,)), ((), ()))
NT = (((1,), (1,)), ((), ()))
TN = (((0,), (0,)), ((), ()))


def mul(left, right, form):
    return lax.dot_general(left, right, form, preferred_element_type=F32)


def shape(dims, dtype):
    return jax.ShapeDtypeStruct(tuple(dims), dtype)


def run(name, body, outs, args, scratch=()):
    vector = pl.BlockSpec(memory_space=pltpu.VMEM)
    return pl.pallas_call(
        body,
        out_shape=tuple(outs),
        in_specs=[pl.BlockSpec(memory_space=pltpu.SMEM)] + [vector] * (len(args) - 1),
        out_specs=tuple(vector for _ in outs),
        scratch_shapes=list(scratch),
        cost_estimate=pl.CostEstimate(flops=1, transcendentals=0, bytes_accessed=1),
        name=name,
    )(*args)


def place(store, parts, sub, first=0):
    for j, part in enumerate(parts):
        rows = part.shape[1]
        start = pl.multiple_of((sub ^ j) * rows, rows)
        for a in range(part.shape[0]):
            store[first + a, pl.ds(start, rows), :] = part[a]


def block(index):
    return pl.ds(pl.multiple_of(index * TOK, TOK), TOK)


def send_blocks(total, outs, order):
    for k in range(E):
        for a in range(total.shape[0]):
            outs[k][a] = total[a, block(order ^ k), :].astype(outs[k].dtype)


def stat_rows(square, logits):
    lane = lax.broadcasted_iota(jnp.int32, (TOK, TOK), 1)
    table = jnp.where(lane == E, square, 0.0)
    for e in range(E):
        table = jnp.where(lane == e, logits[:, e : e + 1], table)
    return jnp.transpose(table)[0:8]


def key_value_body(subs):
    def body(at, *refs):
        rows, gain, router, parts = refs[:E], refs[E], refs[E + 1], refs[E + 2 : E + 2 + subs]
        gained, own_stats, *outs = refs[E + 2 + subs : E + 4 + subs + E]
        weights, total, stats = refs[E + 4 + subs + E :]
        place(weights, parts, at[1])
        for q in range(E):
            wide = rows[q][...].astype(F32)
            scaled = wide * gain[...]
            gained[q * TOK : (q + 1) * TOK, :] = scaled.astype(BF16)
            logits = lax.dot_general(
                scaled, router[...], NT, precision=lax.Precision.HIGHEST, preferred_element_type=F32
            )
            stats[q] = stat_rows(jnp.sum(wide * wide, axis=-1, keepdims=True), logits)
        for a in range(2):
            total[a] = mul(gained[...], weights[a], NN)
        own_stats[...] = stats[at[0]]
        for k in range(E):
            where = block(at[0] ^ k)
            for a in range(2):
                piece = total[a, where, :].astype(outs[k].dtype)
                if k == 0:
                    outs[k][a] = piece
                else:
                    outs[k][a * TOK : (a + 1) * TOK, :] = piece
            if k > 0:
                mine = stats[at[0] ^ k]
                high = mine.astype(BF16).astype(F32)
                pair = jnp.concatenate([high, mine - high], axis=0).astype(BF16)
                outs[k][2 * TOK :, :] = jnp.zeros((16, outs[k].shape[1]), BF16)
                outs[k][2 * TOK :, 0:TOK] = pair

    return body


def routed_body(subs, joined):
    count = 1 if joined else E

    def body(at, *refs):
        rows, hot, parts = refs[:count], refs[count], refs[count + 1 : count + 1 + subs]
        rest = refs[count + 1 + subs :]
        if joined:
            wide = rows[0]
        else:
            wide, rest = rest[0], rest[1:]
            for q in range(E):
                wide[q * TOK : (q + 1) * TOK, :] = rows[q][...]
        outs, weights, total = rest[:E], rest[E], rest[E + 1]
        place(weights, parts, at[1])
        for e in range(E):
            every = mul(wide[...], weights[e], NN)
            for i in range(TOPK):
                mine = every * hot[:, i * E + e : i * E + e + 1]
                total[i] = mine if e == 0 else total[i] + mine
        send_blocks(total, outs, at[0])

    return body


def spread_pairs(at, rows, hot, out, first=0):
    for k in range(E):
        where = block(at[0] ^ k)
        mask = hot[where, :].astype(BF16)
        for e in range(E):
            out[e, where, :] = (
                rows[k][first] * mask[:, e : e + 1]
                + rows[k][first + 1] * mask[:, E + e : E + e + 1]
            )


def fold_out(total, keep_0, keep_2, send):
    keep_0[...] = total[0:TOK]
    keep_2[...] = total[2 * TOK : 3 * TOK]
    send[0] = total[TOK : 2 * TOK].astype(BF16)
    send[1] = total[3 * TOK : 4 * TOK].astype(BF16)


def output_body(subs):
    def body(at, *refs):
        rows, hot, parts = refs[:E], refs[E], refs[E + 1 : E + 1 + subs]
        mixed, keep_0, keep_2, send, weights = refs[E + 1 + subs :]
        place(weights, parts, at[1])
        spread_pairs(at, rows, hot, mixed)
        total = mul(mixed[0], weights[0], NT)
        for e in range(1, E):
            total = total + mul(mixed[e], weights[e], NT)
        fold_out(total, keep_0, keep_2, send)

    return body


def input_body(subs):
    def body(at, *refs):
        rows, dmixed = refs[:E], refs[E]
        kv_parts = refs[E + 1 : E + 1 + subs]
        query_parts = refs[E + 1 + subs : E + 1 + 2 * subs]
        streams = refs[E + 1 + 2 * subs : 2 * E + 1 + 2 * subs]
        dkv_all, gain_row, keep_0, keep_2, send, weights = refs[2 * E + 1 + 2 * subs :]
        place(weights, kv_parts, at[1])
        place(weights, query_parts, at[1], 2)
        for k in range(E):
            for a in range(2):
                dkv_all[a, block(at[0] ^ k), :] = rows[k][a]
        total = mul(dkv_all[0], weights[0], NT) + mul(dkv_all[1], weights[1], NT)
        for e in range(E):
            total = total + mul(dmixed[e], weights[2 + e], NT)
        gain = jnp.zeros((1, total.shape[1]), F32)
        for q in range(E):
            part = total[q * TOK : (q + 1) * TOK] * streams[q][...].astype(F32)
            gain = gain + jnp.sum(part, axis=0, keepdims=True)
        gain_row[...] = gain
        fold_out(total, keep_0, keep_2, send)

    return body


def split_rows(at, rows, other, parts, total):
    for a in range(other.shape[0]):
        total[...] = mul(rows[...], other[a], TN)
        for j, part in enumerate(parts):
            count = part.shape[1]
            start = pl.multiple_of((at[1] ^ j) * count, count)
            part[a] = total[pl.ds(start, count), :].astype(part.dtype)


def weight_grad_body(at, rows, other, *refs):
    split_rows(at, rows, other, refs[:-1], refs[-1])


def query_grad_body(at, rows, hot, *refs):
    dmixed = refs[E]
    spread_pairs(at, refs[:E], hot, dmixed, 2)
    split_rows(at, rows, dmixed, refs[E + 1 : -1], refs[-1])


def attention_mask(at):
    row = lax.broadcasted_iota(jnp.int32, (TOK, TOK), 0)
    col = lax.broadcasted_iota(jnp.int32, (TOK, TOK), 1)
    row_doc, col_doc, end = jnp.zeros_like(row), jnp.zeros_like(row), 0
    for d in range(4):
        end = end + at[d]
        row_doc = row_doc + (row >= end).astype(jnp.int32)
        col_doc = col_doc + (col >= end).astype(jnp.int32)
    return (row_doc == col_doc) & (col <= row)


def attention_body(at, own_kv, *refs):
    got_kv, own_query, got_query = refs[: E - 1], refs[E - 1], refs[E : 2 * E - 1]
    own_stats, hot, rows, low, probs, context, gated = refs[2 * E - 1 :]
    stats = own_stats[...]
    for one in got_kv:
        pair = one[2 * TOK :, 0:TOK].astype(F32)
        stats = stats + pair[0:8] + pair[8:16]
    scale_row = lax.rsqrt(stats[E : E + 1] / (E * own_kv.shape[2]) + EPSILON)
    logits = stats[0:E] * scale_row
    picked = [
        jnp.sum(hot[i * E : (i + 1) * E, :] * logits, axis=0, keepdims=True) for i in range(TOPK)
    ]
    gap = picked[0] - picked[1]
    prob_rows = [1.0 / (1.0 + jnp.exp(-gap)), 1.0 / (1.0 + jnp.exp(gap))]
    rows[0:1, :] = scale_row
    for i in range(TOPK):
        rows[1 + i : 2 + i, :] = prob_rows[i] * hot[8 + i : 9 + i, :]
        rows[3 + i : 4 + i, :] = prob_rows[i]
    rows[5:9, :] = logits
    rows[9:16, :] = jnp.zeros((7, TOK), F32)
    cols = columns(rows[...])
    scale = cols[:, 0:1]
    for a in range(2):
        where = slice(a * TOK, (a + 1) * TOK)
        total, query = own_kv[a], own_query[a]
        for one in got_kv:
            total = total + one[where, :].astype(F32)
        for one in got_query:
            query = query + one[a].astype(F32)
        low[a] = (total * scale).astype(BF16)
        low[2 + a] = (query * scale).astype(BF16)
    allowed = attention_mask(at)
    for h in range(low.shape[2] // HS):
        head = slice(h * HS, (h + 1) * HS)
        for i in range(TOPK):
            scores = mul(low[2 + i, :, head], low[0, :, head], NT) * HS ** (-0.5)
            scores = jnp.where(allowed, scores, NEGATIVE)
            top = jnp.exp(scores - jnp.max(scores, axis=-1, keepdims=True))
            prob = top / jnp.sum(top, axis=-1, keepdims=True)
            probs[h, i * TOK : (i + 1) * TOK, :] = prob
            mixed = mul(prob.astype(BF16), low[1, :, head], NN).astype(BF16)
            context[i, :, head] = mixed
            gated[i, :, head] = (mixed.astype(F32) * cols[:, 1 + i : 2 + i]).astype(BF16)


def attention_back_body(at, own, *refs):
    got = refs[: E - 1]
    rows, low, probs, context, grads, sums = refs[E - 1 :]
    cols = columns(rows[...])
    scale = cols[:, 0:1]
    inner = jnp.zeros((TOK, 1), F32)
    dprob = []
    dcontext = []
    for i in range(TOPK):
        raw = own[i]
        for one in got:
            raw = raw + one[i].astype(F32)
        dprob.append(jnp.sum(context[i].astype(F32) * raw, axis=-1, keepdims=True))
        dcontext.append((raw * cols[:, 1 + i : 2 + i]).astype(BF16))
    for h in range(low.shape[2] // HS):
        head = slice(h * HS, (h + 1) * HS)
        key, value = low[0, :, head], low[1, :, head]
        dkey = jnp.zeros((TOK, HS), F32)
        dvalue = jnp.zeros((TOK, HS), F32)
        for i in range(TOPK):
            query = low[2 + i, :, head]
            grad = dcontext[i][:, head]
            prob = probs[h, i * TOK : (i + 1) * TOK, :]
            dweight = mul(grad, value, NT)
            dscore = prob * (dweight - jnp.sum(prob * dweight, axis=-1, keepdims=True))
            dscore = dscore.astype(BF16)
            done = mul(dscore, key, NN) * HS ** (-0.5)
            dkey = dkey + mul(dscore, query, TN)
            dvalue = dvalue + mul(prob.astype(BF16), grad, TN)
            inner = inner + jnp.sum(done * query.astype(F32), axis=-1, keepdims=True)
            grads[2 + i, :, head] = (done * scale).astype(BF16)
        dkey = dkey * HS ** (-0.5)
        inner = inner + jnp.sum(
            dkey * key.astype(F32) + dvalue * value.astype(F32), axis=-1, keepdims=True
        )
        grads[0, :, head] = (dkey * scale).astype(BF16)
        grads[1, :, head] = (dvalue * scale).astype(BF16)
    lane = lax.broadcasted_iota(jnp.int32, (TOK, TOK), 1)
    table = jnp.where(lane == 0, dprob[0], jnp.where(lane == 1, dprob[1], jnp.where(lane == 2, inner, 0.0)))
    sums[...] = jnp.transpose(table)[0:8]


def columns(rows):
    return jnp.transpose(jnp.concatenate([rows] * (TOK // rows.shape[0]), axis=0))


def pick_row(values, index):
    line = lax.broadcasted_iota(jnp.int32, values.shape, 0)
    return jnp.sum(jnp.where(line == index, values, 0.0), axis=0, keepdims=True)


def route_body(subs, capacity):
    count = E * subs * 8

    def body(at, *refs):
        tables = refs[:E]
        hot_cols, home, turned, mlp_cols, expert_rows, select = refs[E : E + 6]
        both, rank, kept, hot, mlp_hot = refs[E + 6 :]
        expert = lax.broadcasted_iota(jnp.int32, (E, TOK), 0).astype(F32)
        for k in range(E):
            for j in range(subs):
                line = tables[k][j].astype(F32)
                ones = [(line[r : r + 1] == expert).astype(F32) for r in range(4)]
                start = (k * subs + j) * 8
                both[start : start + 4, :] = ones[0] + ones[1]
                both[start + 4 : start + 8, :] = ones[2] + ones[3]
                if j == 0:
                    hot[k, 0:4, :], hot[k, 4:8, :] = ones[0], ones[1]
                    mlp_hot[k, 0:4, :], mlp_hot[k, 4:8, :] = ones[2], ones[3]
        low = both[...].astype(BF16)
        row = lax.broadcasted_iota(jnp.int32, (TOK, TOK), 0)
        col = lax.broadcasted_iota(jnp.int32, (TOK, TOK), 1)
        rank[...] = mul(low, (row < col).astype(F32).astype(BF16), NN)
        row = lax.broadcasted_iota(jnp.int32, (count, count), 0)
        col = lax.broadcasted_iota(jnp.int32, (count, count), 1)
        own = at[2] * subs + at[1]
        ahead = (((col >> 3) ^ own) < ((row >> 3) ^ own)) & ((col & 7) == (row & 7))
        before = mul(ahead.astype(F32).astype(BF16), low, NN)
        place_of = jnp.sum(before, axis=-1, keepdims=True) + rank[...]
        kept[...] = both[...] * (place_of < capacity).astype(F32)

        for k in range(E):
            hot_cols[block(at[0] ^ k), :] = columns(hot[k])[:, 0:8]
        pad = jnp.zeros((6, TOK), F32)
        home[0:8, :] = hot[0]
        for i in range(TOPK):
            home[8 + i : 9 + i, :] = jnp.sum(
                hot[0, i * E : (i + 1) * E, :] * kept[0:E, :], axis=0, keepdims=True
            )
        home[10:16, :] = pad
        mine = mlp_hot[at[0]]
        start = pl.multiple_of(at[0] * (subs * 8), 8)
        kept_mine = kept[pl.ds(start, 8), :][4:8]
        rank_mine = rank[pl.ds(start, 8), :][4:8]
        turned[0:8, :] = mine
        for i in range(TOPK):
            turned[8 + i : 9 + i, :] = jnp.sum(
                mine[i * E : (i + 1) * E] * kept_mine, axis=0, keepdims=True
            )
        turned[10:16, :] = pad
        mlp_cols[...] = columns(mine)[:, 0:8]
        slot = lax.broadcasted_iota(jnp.int32, (SLOTS, TOK), 0).astype(F32)
        for k in range(E):
            e = at[2] ^ k
            for i in range(TOPK):
                expert_rows[2 * k + i : 2 * k + i + 1, :] = pick_row(mine[i * E : (i + 1) * E], e)
            taken = (slot == pick_row(rank_mine, e)) & (pick_row(kept_mine, e) > 0)
            select[k] = taken.astype(F32).astype(BF16)

    return body


def two_halves(values):
    lane = lax.broadcasted_iota(jnp.int32, (values[0].shape[0], 128), 1)
    table = jnp.zeros((values[0].shape[0], 128), F32)
    for i, one in enumerate(values):
        high = one.astype(BF16).astype(F32)
        table = jnp.where(lane == 2 * i, high, table)
        table = jnp.where(lane == 2 * i + 1, one - high, table)
    return table.astype(BF16)


def pick_body(at, stream, keep, got, other, gain, router, mlp_cols, select, *refs):
    hidden, stats, outs = refs[0], refs[1], refs[2:]
    size = hidden.shape[1]
    total = stream[...].astype(F32) + (keep[...] + got[0].astype(F32) + other[...].astype(F32))
    hidden[...] = total
    gained = total * gain[...]
    square = jnp.sum(total * total, axis=-1, keepdims=True)
    logits = lax.dot_general(
        gained, router[...], NT, precision=lax.Precision.HIGHEST, preferred_element_type=F32
    )
    lane = lax.broadcasted_iota(jnp.int32, logits.shape, 1)
    chosen = jnp.zeros_like(square)
    for e in range(E):
        one = mlp_cols[:, e : e + 1] + mlp_cols[:, E + e : E + e + 1]
        chosen = chosen + one * logits[:, e : e + 1]
    low = gained.astype(BF16)
    for k in range(E):
        own = jnp.sum(jnp.where(lane == (at[2] ^ k), logits, 0.0), axis=-1, keepdims=True)
        extra = two_halves([square, 2.0 * own - chosen])
        outs[k][:, :size] = mul(select[k], low, NN).astype(BF16)
        outs[k][:, size:] = mul(select[k], extra, NN).astype(BF16)
    stats[...] = stat_rows(square, logits)


def join_rows_body(at, *refs):
    pieces, out = refs[:E], refs[E]
    size = pieces[0].shape[1] - 128
    join_pieces(at, pieces, out, size)
    total = pieces[0][:, size:].astype(F32)
    for k in range(1, E):
        total = total + pieces[k][:, size:].astype(F32)
    square, gap = total[:, 0:1] + total[:, 1:2], total[:, 2:3] + total[:, 3:4]
    scale = lax.rsqrt(square / (E * size) + EPSILON)
    small = jnp.exp(-jnp.abs(gap * scale))
    gate = jnp.where(gap < 0.0, small, 1.0) / (1.0 + small)
    out[:, E * size :] = two_halves([scale, gate])


def join_pieces(at, pieces, out, size):
    for k in range(E):
        for p in range(E):

            @pl.when((at[2] ^ k) == p)
            def _(k=k, p=p):
                out[:, p * size : (p + 1) * size] = pieces[k][:, :size]


def join_body(at, *refs):
    join_pieces(at, refs[:E], refs[E], refs[0].shape[1])


def split_body(extra):
    def body(at, own, got, *refs):
        outs, store = refs[:E], refs[E]
        store[...] = (own[...] + got[...].astype(F32)).astype(BF16)
        size = outs[0].shape[1] - extra
        for k in range(E):
            for p in range(E):

                @pl.when((at[2] ^ k) == p)
                def _(k=k, p=p):
                    outs[k][:, :size] = store[:, p * size : (p + 1) * size]

            if extra:
                outs[k][:, size:] = store[:, E * size :]

    return body


def local(
    stream,
    out_grad,
    attn_gain,
    attn_router,
    key_value,
    query_proj,
    output_proj,
    mlp_gain,
    mlp_router,
    expert_in,
    expert_down,
    attn_routes,
    mlp_routes,
    doc_lengths,
):
    wide_count = lax.axis_size("wide")
    narrow_count = lax.axis_size("narrow")
    subs = wide_count // E
    wide = lax.axis_index("wide")
    narrow = lax.axis_index("narrow")
    plane, sub = wide // subs, wide % subs
    capacity = 9 * TOK * wide_count * TOPK // (8 * E)
    slice_width = stream.shape[1]
    shard_rows = attn_gain.shape[0]
    width = slice_width * narrow_count
    local_width = key_value.shape[2]
    head_count = local_width // HS
    hidden_units = expert_down.shape[1]
    score_scale = HS ** (-0.5)

    def after(values, *others):
        return lax.optimization_barrier((values, others))[0]

    def by_plane(values, k):
        return lax.ppermute(values, "wide", [(i, i ^ (k * subs)) for i in range(wide_count)])

    def by_sub(values, k):
        return lax.ppermute(values, "wide", [(i, i ^ k) for i in range(wide_count)])

    def by_narrow(values, k):
        return lax.ppermute(values, "narrow", [(i, i ^ k) for i in range(narrow_count)])

    def swap(values):
        pairs = []
        for w in range(wide_count):
            for n in range(narrow_count):
                z, y = w // subs, w % subs
                pairs.append((w * narrow_count + n, (n * subs + y) * narrow_count + z))
        return lax.ppermute(values, ("wide", "narrow"), pairs)

    def by_side(values, side):
        pairs = []
        for w in range(wide_count):
            for n in range(narrow_count):
                other = (w ^ 1, n) if (n & 1) == side else (w, n ^ 2)
                pairs.append((w * narrow_count + n, other[0] * narrow_count + other[1]))
        return lax.ppermute(values, ("wide", "narrow"), pairs)

    def gather_planes(values):
        return [values] + [by_plane(values, k) for k in range(1, E)]

    def exchange_planes(parts):
        return [parts[0]] + [by_plane(parts[k], k) for k in range(1, E)]

    def gather_subs(values, *others):
        parts, bit = [values], 1
        while bit < subs:
            parts = parts + [by_sub(after(one, *others) if others else one, bit) for one in parts]
            bit *= 2
        return parts

    def reduce_subs(parts):
        bit = len(parts) // 2
        while bit >= 1:
            parts = [parts[j] + by_sub(parts[j + bit].astype(BF16), bit).astype(F32) for j in range(bit)]
            bit //= 2
        return parts[0]

    def gather_narrow(values):
        other = by_narrow(values, 2)
        return [values, by_narrow(values, 1), other, by_narrow(other, 1)]

    def reduce_narrow(keep_0, keep_2, send):
        got = by_narrow(send, 1)
        other = by_narrow((keep_2 + got[1].astype(F32)).astype(BF16), 2)
        return keep_0, got, other

    def finish_subs(keep, send):
        bit = len(keep)
        got = [by_sub(send[j], bit) for j in range(bit)]
        return reduce_subs([keep[j] + got[j].astype(F32) for j in range(bit)]), got

    def sum_narrow(values):
        values = values + by_narrow(values, 2)
        return values + by_narrow(values, 1)

    def sum_planes(values):
        values = values + by_plane(values, 1)
        return values + by_plane(values, 2)

    def sum_subs(values):
        bit = 1
        while bit < subs:
            values = values + by_sub(values, bit)
            bit *= 2
        return values

    turned_stream = swap(stream)

    size = max(shard_rows, TOK)

    def pad(rows, count):
        return jnp.pad(rows, ((0, count - rows.shape[0]), (0, size - rows.shape[1])))

    own_routes = jnp.concatenate([attn_routes.T, mlp_routes.T], axis=0).astype(BF16)
    own_rows = jnp.concatenate(
        [attn_gain[None, :], attn_router.T, mlp_gain[None, :], mlp_router.T], axis=0
    )
    parts = gather_subs(jnp.concatenate([pad(own_routes, 8), pad(own_rows, 16)], axis=0))
    parts = jnp.stack(parts)
    near = xor_shuffle(parts[:, 8:, :shard_rows], sub).swapaxes(0, 1).reshape(16, slice_width)
    gain_one_plane = near[0].astype(F32)
    router_one_plane = near[1:5].astype(F32)
    gain_two_plane = near[5].astype(F32)
    router_two_plane = near[6:10].astype(F32)

    at = jnp.stack([narrow ^ plane, sub, plane, narrow]).astype(jnp.int32)
    line_count = wide_count * 8
    hot_cols, home_hot, turned_hot, mlp_cols, expert_hot, select = run(
        "route",
        route_body(subs, capacity),
        [
            shape((E * TOK, 8), F32),
            shape((16, TOK), F32),
            shape((16, TOK), F32),
            shape((TOK, 8), F32),
            shape((8, TOK), F32),
            shape((E, SLOTS, TOK), BF16),
        ],
        [at, *gather_planes(parts[:, :8, :TOK])],
        [pltpu.VMEM((line_count, TOK), F32)] * 3 + [pltpu.VMEM((E, 8, TOK), F32)] * 2,
    )
    hot_one, keep_one = home_hot[0:8].reshape(TOPK, E, TOK), home_hot[8:10]
    hot_two, keep_two = turned_hot[0:8].reshape(TOPK, E, TOK), turned_hot[8:10]
    hot_two_k = expert_hot.reshape(E, TOPK, TOK)

    kv_parts = gather_subs(key_value)
    query_parts = gather_subs(query_proj, kv_parts[-1])
    out_parts = gather_subs(output_proj, query_parts[-1])
    home_stream = stream.astype(F32)

    rows_all = E * TOK
    sent = shape((2, TOK, local_width), BF16)
    kept_own = shape((2, TOK, local_width), F32)
    all_streams = gather_narrow(turned_stream)
    gained, own_stats, *kv_blocks = run(
        "key_value",
        key_value_body(subs),
        [shape((rows_all, slice_width), BF16), shape((8, TOK), F32), kept_own]
        + [shape((2 * TOK + 16, local_width), BF16)] * (E - 1),
        [
            at,
            *all_streams,
            gain_one_plane[None],
            jnp.pad(router_one_plane, ((0, 4), (0, 0))),
            *kv_parts,
        ],
        [
            pltpu.VMEM((2, slice_width, local_width), BF16),
            pltpu.VMEM((2, rows_all, local_width), F32),
            pltpu.VMEM((E, 8, TOK), F32),
        ],
    )
    turned_grad = swap(after(out_grad, own_stats))
    kv_blocks = exchange_planes(kv_blocks)
    routed_scratch = [
        pltpu.VMEM((E, slice_width, local_width), BF16),
        pltpu.VMEM((TOPK, rows_all, local_width), F32),
    ]
    query_blocks = run(
        "query",
        routed_body(subs, True),
        [kept_own] + [sent] * (E - 1),
        [at, after(gained, *kv_blocks[1:]), hot_cols, *query_parts],
        routed_scratch,
    )
    query_blocks = exchange_planes(query_blocks)

    def gates(logits, hots):
        picked = jnp.sum(hots * logits[None], axis=1)
        gap = picked[0] - picked[1]
        return jnp.stack([jax.nn.sigmoid(gap), jax.nn.sigmoid(-gap)])

    def share(full):
        size = full.shape[-1]
        full = jnp.concatenate([full, by_side(full, 0)], axis=0)
        got = by_side(full, 1)
        full = jnp.concatenate([full, got], axis=0)
        bit = 2
        while bit < subs:
            full = jnp.concatenate([full, by_sub(full, bit)], axis=0)
            bit *= 2
        return jnp.concatenate([full, by_narrow(full, 1)], axis=0).reshape(-1, size), got

    picked = jnp.einsum("kst,td->ksd", select, turned_grad, preferred_element_type=F32).astype(BF16)
    token_rows, low, probs, context, gated = run(
        "attention",
        attention_body,
        [
            shape((16, TOK), F32),
            shape((4, TOK, local_width), BF16),
            shape((head_count, TOPK * TOK, TOK), F32),
            sent,
            sent,
        ],
        [doc_lengths[0], *kv_blocks, *query_blocks, own_stats, home_hot],
    )
    scale_one, prob_one, logits_one = token_rows[0], token_rows[3:5], token_rows[5:9]

    (full,) = run(
        "join",
        join_body,
        [shape((SLOTS, width), BF16)],
        [at, *after(exchange_planes([picked[k] for k in range(E)]), gated)],
    )
    grad_rows, grad_got = share(full)
    folded = [shape((TOK, slice_width), F32), shape((TOK, slice_width), F32), shape((2, TOK, slice_width), BF16)]
    mixed, *attention = run(
        "output",
        output_body(subs),
        [shape((E, rows_all, local_width), BF16)] + folded,
        [at, *gather_planes(gated), hot_cols, *out_parts],
        [pltpu.VMEM((E, slice_width, local_width), BF16)],
    )
    weight_in = expert_in[0]
    weight_down = expert_down[0]
    dact_raw = dot(grad_rows, weight_down, ((1,), (1,)))

    hidden, stats_two, *picked = run(
        "pick",
        pick_body,
        [shape((TOK, slice_width), F32), shape((8, TOK), F32)]
        + [shape((SLOTS, slice_width + 128), BF16)] * E,
        [
            at,
            turned_stream,
            *after(reduce_narrow(*attention), grad_got),
            gain_two_plane[None],
            jnp.pad(router_two_plane, ((0, 4), (0, 0))),
            mlp_cols,
            select,
        ],
    )
    (full,) = run(
        "join_rows",
        join_rows_body,
        [shape((SLOTS, width + 128), BF16)],
        [at, *exchange_planes(picked)],
    )
    stats_two = sum_planes(stats_two)
    full, _ = share(full)
    full = after(full, stats_two)
    expert_rows = full[:, :width]
    row_pairs = full[:, width : width + 4].astype(F32)
    row_scale = row_pairs[:, 0:1] + row_pairs[:, 1:2]
    row_gate = row_pairs[:, 2:3] + row_pairs[:, 3:4]
    scale_two = lax.rsqrt(stats_two[E] / width + EPSILON)
    logits_two = stats_two[:E] * scale_two
    prob_two = gates(logits_two, hot_two)

    gate_up = jnp.einsum("rd,dkf->krf", expert_rows, weight_in, preferred_element_type=F32)
    gate_pre = gate_up[0] * row_scale
    up_pre = gate_up[1] * row_scale
    gate_sig = jax.nn.sigmoid(gate_pre)
    silu_gate = gate_pre * gate_sig
    activation = (silu_gate * up_pre).astype(BF16)
    dactiv = dact_raw * row_gate
    dgate_pre = (dactiv * up_pre * gate_sig * (1.0 + gate_pre * (1.0 - gate_sig))).astype(BF16)
    dup_pre = (dactiv * silu_gate).astype(BF16)
    dprob_rows = jnp.sum(activation.astype(F32) * dact_raw, axis=-1)
    inner_rows = jnp.sum(dgate_pre.astype(F32) * gate_pre + dup_pre.astype(F32) * up_pre, axis=-1)
    drows = jnp.einsum(
        "krf,dkf->rd", jnp.stack([dgate_pre, dup_pre]), weight_in, preferred_element_type=F32
    )
    lanes = jnp.arange(128)
    row_stats = jnp.where(
        lanes[None, :] == 0, dprob_rows[:, None], jnp.where(lanes[None, :] == 1, inner_rows[:, None], 0.0)
    )

    def give_back(rows):
        half = rows.shape[0] // 2
        rows = rows[:half] + by_narrow(rows[half:].astype(BF16), 1).astype(F32)
        bit = subs // 2
        while bit > 1:
            half = rows.shape[0] // 2
            rows = rows[:half] + by_sub(rows[half:].astype(BF16), bit).astype(F32)
            bit //= 2
        half = rows.shape[0] // 2
        rows = rows[:half] + by_side(rows[half:].astype(BF16), 1).astype(F32)
        return rows[:SLOTS], by_side(rows[SLOTS:].astype(BF16), 0)

    def from_planes(own, got, extra, last=None):
        if last is not None:
            own = after(own, last)
        pieces = run(
            "split",
            split_body(extra),
            [shape((SLOTS, slice_width + extra), BF16)] * E,
            [at, own, got],
            [pltpu.VMEM(own.shape, BF16)],
        )
        return jnp.stack(exchange_planes(pieces))

    returned = give_back(jnp.concatenate([drows, row_stats], axis=1))
    returned = from_planes(*returned, row_stats.shape[1])
    combined = jnp.einsum("kst,ksd->ktd", select, returned, preferred_element_type=F32)
    per_expert = combined[:, :, slice_width : slice_width + 2]
    dprob_two = keep_two * jnp.sum(hot_two_k * per_expert[:, None, :, 0], axis=0)
    inner_two = jnp.sum(per_expert[:, :, 1], axis=0)
    dnormed_two = jnp.sum(combined[:, :, :slice_width], axis=0)

    def gate_back(prob, dprob, hots):
        dselect = prob * (dprob - jnp.sum(prob * dprob, axis=0, keepdims=True))
        return jnp.sum(hots * dselect[:, None, :], axis=0)

    dlogit_two = gate_back(prob_two, dprob_two, hot_two)
    dnormed_two = dnormed_two + dot(dlogit_two, router_two_plane, ((0,), (0,)), PRECISE)
    inner_two = inner_two + jnp.sum(dlogit_two * logits_two, axis=0)
    dhidden = (
        turned_grad.astype(F32)
        + scale_two[:, None] * (dnormed_two * gain_two_plane)
        - hidden * (scale_two * scale_two * inner_two / width)[:, None]
    )
    scaled_hidden = hidden * scale_two[:, None]
    mlp_terms = jnp.concatenate(
        [
            jnp.sum(dnormed_two * scaled_hidden, axis=0)[None],
            dot(dlogit_two, scaled_hidden * gain_two_plane, ((1,), (0,)), PRECISE),
        ],
        axis=0,
    )

    wide_grad, *dcontext_blocks = run(
        "dcontext",
        routed_body(subs, False),
        [shape((rows_all, slice_width), BF16), kept_own] + [sent] * (E - 1),
        [at, *gather_narrow(dhidden.astype(BF16)), hot_cols, *out_parts],
        routed_scratch,
    )
    dcontext_blocks = exchange_planes(dcontext_blocks)

    def weight_parts(count):
        return [
            shape((count, shard_rows, local_width), F32 if j < subs // 2 else BF16)
            for j in range(subs)
        ]

    def weight_sum(parts):
        return finish_subs(parts[: subs // 2], parts[subs // 2 :])

    weight_scratch = [pltpu.VMEM((slice_width, local_width), F32)]
    output_parts = run(
        "output_grad", weight_grad_body, weight_parts(E), [at, wide_grad, mixed], weight_scratch
    )
    expert_out = dot(activation, weight_down, ((1,), (0,))) * row_gate
    mixture = give_back(expert_out)
    output_grad, output_got = weight_sum(output_parts)
    gated_act = (activation.astype(F32) * row_gate).astype(BF16)
    down_grad = dot(after(gated_act, dcontext_blocks[0]), grad_rows, ((0,), (0,)))
    grads_low, home_sums = run(
        "attention_back",
        attention_back_body,
        [shape((4, TOK, local_width), BF16), shape((8, TOK), F32)],
        [
            at,
            *after(dcontext_blocks, output_parts[-1], down_grad),
            token_rows,
            low,
            probs,
            context,
        ],
    )
    grad_planes = gather_planes(grads_low)
    dboth = jnp.stack(
        [
            (dgate_pre.astype(F32) * row_scale).astype(BF16),
            (dup_pre.astype(F32) * row_scale).astype(BF16),
        ],
        axis=1,
    )
    up_grad = jnp.einsum(
        "rd,rkf->dkf", expert_rows, after(dboth, grad_planes[E - 1]), preferred_element_type=F32
    )
    dmixed, *query_grad_parts = run(
        "query_grad",
        query_grad_body,
        [shape((E, rows_all, local_width), BF16)] + weight_parts(E),
        [at, gained, hot_cols, *after(grad_planes, output_got, up_grad)],
        weight_scratch,
    )
    query_grad, query_got = weight_sum(query_grad_parts)
    dkv_all, gain_row, *dnormed_one = run(
        "input",
        input_body(subs),
        [shape((2, rows_all, local_width), BF16), shape((1, slice_width), F32)] + folded,
        [
            at,
            *after(grad_planes, query_grad_parts[-1]),
            dmixed,
            *kv_parts,
            *query_parts,
            *all_streams,
        ],
        [pltpu.VMEM((2 + E, slice_width, local_width), BF16)],
    )
    home_rows = swap(after(near, own_stats))
    gain_one_home = home_rows[0].astype(F32)
    router_one_home = home_rows[1:5].astype(F32)
    gained_home = home_stream * gain_one_home
    home_sums = sum_narrow(after(home_sums, gain_row))
    dprob_one = keep_one * home_sums[:2]
    dlogit_one = gate_back(prob_one, dprob_one, hot_one)
    inner_one = home_sums[2] + jnp.sum(dlogit_one * logits_one, axis=0)
    dlogit_scaled = dlogit_one * scale_one
    router_term = swap(dot(dlogit_scaled, gained_home, ((1,), (0,)), PRECISE))
    kv_grad_parts = run(
        "key_value_grad", weight_grad_body, weight_parts(2), [at, gained, dkv_all], weight_scratch
    )
    kv_grad, _ = weight_sum(after(kv_grad_parts, query_got))
    keep, got, other = after(reduce_narrow(*dnormed_one), kv_grad_parts[-1], query_got)
    dnormed_one = keep + got[0].astype(F32) + other.astype(F32)
    turned_out = dhidden + dnormed_one * gain_one_plane
    home_out = swap(turned_out.astype(BF16)).astype(F32)
    stream_grad = (
        home_out
        + gain_one_home * dot(dlogit_scaled, router_one_home, ((0,), (0,)), PRECISE)
        - home_stream * (scale_one * scale_one * inner_one / width)[:, None]
    )

    small = jnp.concatenate([mlp_terms, gain_row, router_term], axis=0)
    small = sum_subs(sum_narrow(after(small, query_got)))
    mine = lax.dynamic_slice_in_dim(small, sub * shard_rows, shard_rows, 1)
    router_one_grad = mine[6:10]
    gain_one_grad = mine[5] + jnp.sum(
        router_one_grad * attn_router.T.astype(F32), axis=0
    ) / attn_gain.astype(F32)

    mixture = from_planes(*mixture, 0, gain_row)
    mixture = jnp.einsum("kst,ksd->td", select, after(mixture, turned_out), preferred_element_type=F32)
    layer_out = swap((hidden + mixture).astype(BF16)).astype(F32)
    return (
        layer_out,
        stream_grad,
        gain_one_grad,
        router_one_grad.T,
        kv_grad,
        query_grad,
        output_grad,
        mine[0],
        mine[1:5].T,
        up_grad[None],
        down_grad[None],
    )


def solution(mesh):
    in_specs = (
        P("wide", "narrow"),
        P("wide", "narrow"),
        P("wide"),
        P("wide", None),
        P(None, "wide", "narrow"),
        P(None, "wide", "narrow"),
        P(None, "wide", "narrow"),
        P("wide"),
        P("wide", None),
        P("wide", None, None, "narrow"),
        P("wide", "narrow", None),
        P("wide", None),
        P("wide", None),
        P("wide", None),
    )
    out_specs = (
        P("wide", "narrow"),
        P("wide", "narrow"),
        P("wide"),
        P("wide", None),
        P(None, "wide", "narrow"),
        P(None, "wide", "narrow"),
        P(None, "wide", "narrow"),
        P("wide"),
        P("wide", None),
        P("wide", None, None, "narrow"),
        P("wide", "narrow", None),
    )
    return jax.shard_map(local, mesh=mesh, in_specs=in_specs, out_specs=out_specs, check_vma=False)
```

```python
import jax
import jax.numpy as jnp
from jax import lax
from jax.experimental import pallas as pl
from jax.experimental.pallas import tpu as pltpu
from jax.sharding import PartitionSpec as P

HS = 128
E = 4
TOPK = 2
TOK = 128
SLOTS = 80

EPSILON = 1e-05
NEGATIVE = -1000000000.0
PRECISE = lax.Precision.HIGHEST
F32 = jnp.float32
BF16 = jnp.bfloat16


def dot(left, right, contract, precision=None):
    return lax.dot_general(
        left, right, ((contract[0], contract[1]), ((), ())), precision=precision, preferred_element_type=F32
    )


def xor_shuffle(values, amount):
    count, bit = values.shape[0], 1
    while bit < count:
        split = values.reshape((count // (2 * bit), 2, bit) + values.shape[1:])
        flipped = split[:, ::-1].reshape(values.shape)
        values = jnp.where((amount & bit) != 0, flipped, values)
        bit *= 2
    return values


NN = (((1,), (0,)), ((), ()))
NT = (((1,), (1,)), ((), ()))
TN = (((0,), (0,)), ((), ()))


def mul(left, right, form):
    return lax.dot_general(left, right, form, preferred_element_type=F32)


def shape(dims, dtype):
    return jax.ShapeDtypeStruct(tuple(dims), dtype)


def run(name, body, outs, args, scratch=()):
    vector = pl.BlockSpec(memory_space=pltpu.VMEM)
    return pl.pallas_call(
        body,
        out_shape=tuple(outs),
        in_specs=[pl.BlockSpec(memory_space=pltpu.SMEM)] + [vector] * (len(args) - 1),
        out_specs=tuple(vector for _ in outs),
        scratch_shapes=list(scratch),
        cost_estimate=pl.CostEstimate(flops=1, transcendentals=0, bytes_accessed=1),
        name=name,
    )(*args)


def place(store, parts, sub, first=0):
    for j, part in enumerate(parts):
        rows = part.shape[1]
        start = pl.multiple_of((sub ^ j) * rows, rows)
        for a in range(part.shape[0]):
            store[first + a, pl.ds(start, rows), :] = part[a]


def block(index):
    return pl.ds(pl.multiple_of(index * TOK, TOK), TOK)


def send_blocks(total, outs, order):
    for k in range(E):
        for a in range(total.shape[0]):
            outs[k][a] = total[a, block(order ^ k), :].astype(outs[k].dtype)


def stat_rows(square, logits):
    lane = lax.broadcasted_iota(jnp.int32, (TOK, TOK), 1)
    table = jnp.where(lane == E, square, 0.0)
    for e in range(E):
        table = jnp.where(lane == e, logits[:, e : e + 1], table)
    return jnp.transpose(table)[0:8]


def key_value_body(subs):
    def body(at, *refs):
        rows, gain, router, routes = refs[:E], refs[E], refs[E + 1], refs[E + 2]
        parts = refs[E + 3 : E + 3 + subs]
        gained, own_stats, *outs = refs[E + 3 + subs : E + 5 + subs + E]
        weights, total, stats = refs[E + 5 + subs + E :]
        place(weights, parts, at[1])
        for q in range(E):
            wide = rows[q][...].astype(F32)
            scaled = wide * gain[...]
            gained[q * TOK : (q + 1) * TOK, :] = scaled.astype(BF16)
            logits = lax.dot_general(
                scaled, router[...], NT, precision=lax.Precision.HIGHEST, preferred_element_type=F32
            )
            stats[q] = stat_rows(jnp.sum(wide * wide, axis=-1, keepdims=True), logits)
        for a in range(2):
            total[a] = mul(gained[...], weights[a], NN)
        own_stats[...] = stats[at[0]]
        for k in range(E):
            where = block(at[0] ^ k)
            for a in range(2):
                piece = total[a, where, :].astype(outs[k].dtype)
                if k == 0:
                    outs[k][a] = piece
                else:
                    outs[k][a * TOK : (a + 1) * TOK, :] = piece
            if k > 0:
                mine = stats[at[0] ^ k]
                high = mine.astype(BF16).astype(F32)
                pair = jnp.concatenate([high, mine - high], axis=0).astype(BF16)
                outs[k][2 * TOK :, :] = jnp.zeros((16, outs[k].shape[1]), BF16)
                outs[k][2 * TOK :, 0:TOK] = pair
                for first in range(0, subs, 4):
                    lines = [
                        routes[j][0:4].astype(F32) if j < subs else jnp.zeros((4, TOK), F32)
                        for j in range(first, first + 4)
                    ]
                    start = (1 + first // 4) * TOK
                    outs[k][2 * TOK :, start : start + TOK] = jnp.concatenate(lines, axis=0).astype(BF16)

    return body


def routed_body(subs, joined):
    count = 1 if joined else E

    def body(at, *refs):
        rows, hot, parts = refs[:count], refs[count], refs[count + 1 : count + 1 + subs]
        rest = refs[count + 1 + subs :]
        if joined:
            wide = rows[0]
        else:
            wide, rest = rest[0], rest[1:]
            for q in range(E):
                wide[q * TOK : (q + 1) * TOK, :] = rows[q][...]
        outs, weights, total = rest[:E], rest[E], rest[E + 1]
        place(weights, parts, at[1])
        for e in range(E):
            every = mul(wide[...], weights[e], NN)
            for i in range(TOPK):
                mine = every * hot[:, i * E + e : i * E + e + 1]
                total[i] = mine if e == 0 else total[i] + mine
        send_blocks(total, outs, at[0])

    return body


def spread_pairs(at, rows, hot, out, first=0):
    for k in range(E):
        where = block(at[0] ^ k)
        mask = hot[where, :].astype(BF16)
        for e in range(E):
            out[e, where, :] = (
                rows[k][first] * mask[:, e : e + 1]
                + rows[k][first + 1] * mask[:, E + e : E + e + 1]
            )


def fold_out(total, keep_0, keep_2, send):
    keep_0[...] = total[0:TOK]
    keep_2[...] = total[2 * TOK : 3 * TOK]
    send[0] = total[TOK : 2 * TOK].astype(BF16)
    send[1] = total[3 * TOK : 4 * TOK].astype(BF16)


def output_body(subs):
    def body(at, *refs):
        rows, hot, parts = refs[:E], refs[E], refs[E + 1 : E + 1 + subs]
        mixed, keep_0, keep_2, send, weights = refs[E + 1 + subs :]
        place(weights, parts, at[1])
        spread_pairs(at, rows, hot, mixed)
        total = mul(mixed[0], weights[0], NT)
        for e in range(1, E):
            total = total + mul(mixed[e], weights[e], NT)
        fold_out(total, keep_0, keep_2, send)

    return body


def input_body(subs):
    def body(at, *refs):
        rows, dmixed = refs[:E], refs[E]
        kv_parts = refs[E + 1 : E + 1 + subs]
        query_parts = refs[E + 1 + subs : E + 1 + 2 * subs]
        streams = refs[E + 1 + 2 * subs : 2 * E + 1 + 2 * subs]
        dkv_all, gain_row, keep_0, keep_2, send, weights = refs[2 * E + 1 + 2 * subs :]
        place(weights, kv_parts, at[1])
        place(weights, query_parts, at[1], 2)
        for k in range(E):
            for a in range(2):
                dkv_all[a, block(at[0] ^ k), :] = rows[k][a]
        total = mul(dkv_all[0], weights[0], NT) + mul(dkv_all[1], weights[1], NT)
        for e in range(E):
            total = total + mul(dmixed[e], weights[2 + e], NT)
        gain = jnp.zeros((1, total.shape[1]), F32)
        for q in range(E):
            part = total[q * TOK : (q + 1) * TOK] * streams[q][...].astype(F32)
            gain = gain + jnp.sum(part, axis=0, keepdims=True)
        gain_row[...] = gain
        fold_out(total, keep_0, keep_2, send)

    return body


def split_rows(at, rows, other, parts, total):
    for a in range(other.shape[0]):
        total[...] = mul(rows[...], other[a], TN)
        for j, part in enumerate(parts):
            count = part.shape[1]
            start = pl.multiple_of((at[1] ^ j) * count, count)
            part[a] = total[pl.ds(start, count), :].astype(part.dtype)


def weight_grad_body(at, rows, other, *refs):
    split_rows(at, rows, other, refs[:-1], refs[-1])


def query_grad_body(at, rows, hot, *refs):
    dmixed = refs[E]
    spread_pairs(at, refs[:E], hot, dmixed, 2)
    split_rows(at, rows, dmixed, refs[E + 1 : -1], refs[-1])


def attention_mask(at):
    row = lax.broadcasted_iota(jnp.int32, (TOK, TOK), 0)
    col = lax.broadcasted_iota(jnp.int32, (TOK, TOK), 1)
    row_doc, col_doc, end = jnp.zeros_like(row), jnp.zeros_like(row), 0
    for d in range(4):
        end = end + at[d]
        row_doc = row_doc + (row >= end).astype(jnp.int32)
        col_doc = col_doc + (col >= end).astype(jnp.int32)
    return (row_doc == col_doc) & (col <= row)


def attention_body(at, own_kv, *refs):
    got_kv, own_query, got_query = refs[: E - 1], refs[E - 1], refs[E : 2 * E - 1]
    own_stats, hot, rows, low, probs, context, gated = refs[2 * E - 1 :]
    stats = own_stats[...]
    for one in got_kv:
        pair = one[2 * TOK :, 0:TOK].astype(F32)
        stats = stats + pair[0:8] + pair[8:16]
    scale_row = lax.rsqrt(stats[E : E + 1] / (E * own_kv.shape[2]) + EPSILON)
    logits = stats[0:E] * scale_row
    picked = [
        jnp.sum(hot[i * E : (i + 1) * E, :] * logits, axis=0, keepdims=True) for i in range(TOPK)
    ]
    gap = picked[0] - picked[1]
    prob_rows = [1.0 / (1.0 + jnp.exp(-gap)), 1.0 / (1.0 + jnp.exp(gap))]
    rows[0:1, :] = scale_row
    for i in range(TOPK):
        rows[1 + i : 2 + i, :] = prob_rows[i] * hot[8 + i : 9 + i, :]
        rows[3 + i : 4 + i, :] = prob_rows[i]
    rows[5:9, :] = logits
    rows[9:16, :] = jnp.zeros((7, TOK), F32)
    cols = columns(rows[...])
    scale = cols[:, 0:1]
    for a in range(2):
        where = slice(a * TOK, (a + 1) * TOK)
        total, query = own_kv[a], own_query[a]
        for one in got_kv:
            total = total + one[where, :].astype(F32)
        for one in got_query:
            query = query + one[a].astype(F32)
        low[a] = (total * scale).astype(BF16)
        low[2 + a] = (query * scale).astype(BF16)
    allowed = attention_mask(at)
    for h in range(low.shape[2] // HS):
        head = slice(h * HS, (h + 1) * HS)
        for i in range(TOPK):
            scores = mul(low[2 + i, :, head], low[0, :, head], NT) * HS ** (-0.5)
            scores = jnp.where(allowed, scores, NEGATIVE)
            top = jnp.exp(scores - jnp.max(scores, axis=-1, keepdims=True))
            prob = top / jnp.sum(top, axis=-1, keepdims=True)
            probs[h, i * TOK : (i + 1) * TOK, :] = prob
            mixed = mul(prob.astype(BF16), low[1, :, head], NN).astype(BF16)
            context[i, :, head] = mixed
            gated[i, :, head] = (mixed.astype(F32) * cols[:, 1 + i : 2 + i]).astype(BF16)


def attention_back_body(at, own, *refs):
    got = refs[: E - 1]
    rows, low, probs, context, grads, sums = refs[E - 1 :]
    cols = columns(rows[...])
    scale = cols[:, 0:1]
    inner = jnp.zeros((TOK, 1), F32)
    dprob = []
    dcontext = []
    for i in range(TOPK):
        raw = own[i]
        for one in got:
            raw = raw + one[i].astype(F32)
        dprob.append(jnp.sum(context[i].astype(F32) * raw, axis=-1, keepdims=True))
        dcontext.append((raw * cols[:, 1 + i : 2 + i]).astype(BF16))
    for h in range(low.shape[2] // HS):
        head = slice(h * HS, (h + 1) * HS)
        key, value = low[0, :, head], low[1, :, head]
        dkey = jnp.zeros((TOK, HS), F32)
        dvalue = jnp.zeros((TOK, HS), F32)
        for i in range(TOPK):
            query = low[2 + i, :, head]
            grad = dcontext[i][:, head]
            prob = probs[h, i * TOK : (i + 1) * TOK, :]
            dweight = mul(grad, value, NT)
            dscore = prob * (dweight - jnp.sum(prob * dweight, axis=-1, keepdims=True))
            dscore = dscore.astype(BF16)
            done = mul(dscore, key, NN) * HS ** (-0.5)
            dkey = dkey + mul(dscore, query, TN)
            dvalue = dvalue + mul(prob.astype(BF16), grad, TN)
            inner = inner + jnp.sum(done * query.astype(F32), axis=-1, keepdims=True)
            grads[2 + i, :, head] = (done * scale).astype(BF16)
        dkey = dkey * HS ** (-0.5)
        inner = inner + jnp.sum(
            dkey * key.astype(F32) + dvalue * value.astype(F32), axis=-1, keepdims=True
        )
        grads[0, :, head] = (dkey * scale).astype(BF16)
        grads[1, :, head] = (dvalue * scale).astype(BF16)
    lane = lax.broadcasted_iota(jnp.int32, (TOK, TOK), 1)
    table = jnp.where(lane == 0, dprob[0], jnp.where(lane == 1, dprob[1], jnp.where(lane == 2, inner, 0.0)))
    sums[...] = jnp.transpose(table)[0:8]


def columns(rows):
    return jnp.transpose(jnp.concatenate([rows] * (TOK // rows.shape[0]), axis=0))


def pick_row(values, index):
    line = lax.broadcasted_iota(jnp.int32, values.shape, 0)
    return jnp.sum(jnp.where(line == index, values, 0.0), axis=0, keepdims=True)


def route_body(subs, capacity):
    count = E * subs * 8

    def body(at, *refs):
        tables = refs[:E]
        hot_cols, home, turned, mlp_cols, expert_rows, select = refs[E : E + 6]
        both, rank, kept, hot, mlp_hot = refs[E + 6 :]
        expert = lax.broadcasted_iota(jnp.int32, (E, TOK), 0).astype(F32)
        for k in range(E):
            for j in range(subs):
                if k == 0:
                    line = tables[0][j].astype(F32)
                else:
                    first = (1 + j // 4) * TOK
                    lines = tables[k][2 * TOK :, first : first + TOK].astype(F32)
                    line = lines[(j % 4) * 4 : (j % 4) * 4 + 4]
                ones = [(line[r : r + 1] == expert).astype(F32) for r in range(4)]
                start = (k * subs + j) * 8
                both[start : start + 4, :] = ones[0] + ones[1]
                both[start + 4 : start + 8, :] = ones[2] + ones[3]
                if j == 0:
                    hot[k, 0:4, :], hot[k, 4:8, :] = ones[0], ones[1]
                    mlp_hot[k, 0:4, :], mlp_hot[k, 4:8, :] = ones[2], ones[3]
        low = both[...].astype(BF16)
        row = lax.broadcasted_iota(jnp.int32, (TOK, TOK), 0)
        col = lax.broadcasted_iota(jnp.int32, (TOK, TOK), 1)
        rank[...] = mul(low, (row < col).astype(F32).astype(BF16), NN)
        row = lax.broadcasted_iota(jnp.int32, (count, count), 0)
        col = lax.broadcasted_iota(jnp.int32, (count, count), 1)
        own = at[2] * subs + at[1]
        ahead = (((col >> 3) ^ own) < ((row >> 3) ^ own)) & ((col & 7) == (row & 7))
        before = mul(ahead.astype(F32).astype(BF16), low, NN)
        place_of = jnp.sum(before, axis=-1, keepdims=True) + rank[...]
        kept[...] = both[...] * (place_of < capacity).astype(F32)

        for k in range(E):
            hot_cols[block(at[0] ^ k), :] = columns(hot[k])[:, 0:8]
        pad = jnp.zeros((6, TOK), F32)
        home[0:8, :] = hot[0]
        for i in range(TOPK):
            home[8 + i : 9 + i, :] = jnp.sum(
                hot[0, i * E : (i + 1) * E, :] * kept[0:E, :], axis=0, keepdims=True
            )
        home[10:16, :] = pad
        mine = mlp_hot[at[0]]
        start = pl.multiple_of(at[0] * (subs * 8), 8)
        kept_mine = kept[pl.ds(start, 8), :][4:8]
        rank_mine = rank[pl.ds(start, 8), :][4:8]
        turned[0:8, :] = mine
        for i in range(TOPK):
            turned[8 + i : 9 + i, :] = jnp.sum(
                mine[i * E : (i + 1) * E] * kept_mine, axis=0, keepdims=True
            )
        turned[10:16, :] = pad
        mlp_cols[...] = columns(mine)[:, 0:8]
        slot = lax.broadcasted_iota(jnp.int32, (SLOTS, TOK), 0).astype(F32)
        for k in range(E):
            e = at[2] ^ k
            for i in range(TOPK):
                expert_rows[2 * k + i : 2 * k + i + 1, :] = pick_row(mine[i * E : (i + 1) * E], e)
            taken = (slot == pick_row(rank_mine, e)) & (pick_row(kept_mine, e) > 0)
            select[k] = taken.astype(F32).astype(BF16)

    return body


def two_halves(values):
    lane = lax.broadcasted_iota(jnp.int32, (values[0].shape[0], 128), 1)
    table = jnp.zeros((values[0].shape[0], 128), F32)
    for i, one in enumerate(values):
        high = one.astype(BF16).astype(F32)
        table = jnp.where(lane == 2 * i, high, table)
        table = jnp.where(lane == 2 * i + 1, one - high, table)
    return table.astype(BF16)


def pick_body(at, stream, keep, got, other, gain, router, mlp_cols, select, *refs):
    hidden, stats, outs = refs[0], refs[1], refs[2:]
    size = hidden.shape[1]
    total = stream[...].astype(F32) + (keep[...] + got[0].astype(F32) + other[...].astype(F32))
    hidden[...] = total
    gained = total * gain[...]
    square = jnp.sum(total * total, axis=-1, keepdims=True)
    logits = lax.dot_general(
        gained, router[...], NT, precision=lax.Precision.HIGHEST, preferred_element_type=F32
    )
    lane = lax.broadcasted_iota(jnp.int32, logits.shape, 1)
    chosen = jnp.zeros_like(square)
    for e in range(E):
        one = mlp_cols[:, e : e + 1] + mlp_cols[:, E + e : E + e + 1]
        chosen = chosen + one * logits[:, e : e + 1]
    low = gained.astype(BF16)
    for k in range(E):
        own = jnp.sum(jnp.where(lane == (at[2] ^ k), logits, 0.0), axis=-1, keepdims=True)
        extra = two_halves([square, 2.0 * own - chosen])
        outs[k][:, :size] = mul(select[k], low, NN).astype(BF16)
        outs[k][:, size:] = mul(select[k], extra, NN).astype(BF16)
    stats[...] = stat_rows(square, logits)


def join_rows_body(at, *refs):
    pieces, out = refs[:E], refs[E]
    size = pieces[0].shape[1] - 128
    join_pieces(at, pieces, out, size)
    total = pieces[0][:, size:].astype(F32)
    for k in range(1, E):
        total = total + pieces[k][:, size:].astype(F32)
    square, gap = total[:, 0:1] + total[:, 1:2], total[:, 2:3] + total[:, 3:4]
    scale = lax.rsqrt(square / (E * size) + EPSILON)
    small = jnp.exp(-jnp.abs(gap * scale))
    gate = jnp.where(gap < 0.0, small, 1.0) / (1.0 + small)
    out[:, E * size :] = two_halves([scale, gate])


def join_pieces(at, pieces, out, size):
    for k in range(E):
        for p in range(E):

            @pl.when((at[2] ^ k) == p)
            def _(k=k, p=p):
                out[:, p * size : (p + 1) * size] = pieces[k][:, :size]


def join_body(at, *refs):
    join_pieces(at, refs[:E], refs[E], refs[0].shape[1])


def split_body(extra):
    def body(at, own, got, *refs):
        outs, store = refs[:E], refs[E]
        store[...] = (own[...] + got[...].astype(F32)).astype(BF16)
        size = outs[0].shape[1] - extra
        for k in range(E):
            for p in range(E):

                @pl.when((at[2] ^ k) == p)
                def _(k=k, p=p):
                    outs[k][:, :size] = store[:, p * size : (p + 1) * size]

            if extra:
                outs[k][:, size:] = store[:, E * size :]

    return body


def local(
    stream,
    out_grad,
    attn_gain,
    attn_router,
    key_value,
    query_proj,
    output_proj,
    mlp_gain,
    mlp_router,
    expert_in,
    expert_down,
    attn_routes,
    mlp_routes,
    doc_lengths,
):
    wide_count = lax.axis_size("wide")
    narrow_count = lax.axis_size("narrow")
    subs = wide_count // E
    wide = lax.axis_index("wide")
    narrow = lax.axis_index("narrow")
    plane, sub = wide // subs, wide % subs
    capacity = 9 * TOK * wide_count * TOPK // (8 * E)
    slice_width = stream.shape[1]
    shard_rows = attn_gain.shape[0]
    width = slice_width * narrow_count
    local_width = key_value.shape[2]
    head_count = local_width // HS
    hidden_units = expert_down.shape[1]
    score_scale = HS ** (-0.5)

    def after(values, *others):
        return lax.optimization_barrier((values, others))[0]

    def by_plane(values, k):
        return lax.ppermute(values, "wide", [(i, i ^ (k * subs)) for i in range(wide_count)])

    def by_sub(values, k):
        return lax.ppermute(values, "wide", [(i, i ^ k) for i in range(wide_count)])

    def by_narrow(values, k):
        return lax.ppermute(values, "narrow", [(i, i ^ k) for i in range(narrow_count)])

    def swap(values):
        pairs = []
        for w in range(wide_count):
            for n in range(narrow_count):
                z, y = w // subs, w % subs
                pairs.append((w * narrow_count + n, (n * subs + y) * narrow_count + z))
        return lax.ppermute(values, ("wide", "narrow"), pairs)

    def by_side(values, side):
        pairs = []
        for w in range(wide_count):
            for n in range(narrow_count):
                other = (w ^ 1, n) if (n & 1) == side else (w, n ^ 2)
                pairs.append((w * narrow_count + n, other[0] * narrow_count + other[1]))
        return lax.ppermute(values, ("wide", "narrow"), pairs)

    def gather_planes(values):
        return [values] + [by_plane(values, k) for k in range(1, E)]

    def exchange_planes(parts):
        return [parts[0]] + [by_plane(parts[k], k) for k in range(1, E)]

    def gather_subs(values, *others):
        parts, bit = [values], 1
        while bit < subs:
            parts = parts + [by_sub(after(one, *others) if others else one, bit) for one in parts]
            bit *= 2
        return parts

    def reduce_subs(parts):
        bit = len(parts) // 2
        while bit >= 1:
            parts = [parts[j] + by_sub(parts[j + bit].astype(BF16), bit).astype(F32) for j in range(bit)]
            bit //= 2
        return parts[0]

    def gather_narrow(values):
        other = by_narrow(values, 2)
        return [values, by_narrow(values, 1), other, by_narrow(other, 1)]

    def reduce_narrow(keep_0, keep_2, send):
        got = by_narrow(send, 1)
        other = by_narrow((keep_2 + got[1].astype(F32)).astype(BF16), 2)
        return keep_0, got, other

    def finish_subs(keep, send):
        bit = len(keep)
        got = [by_sub(send[j], bit) for j in range(bit)]
        return reduce_subs([keep[j] + got[j].astype(F32) for j in range(bit)]), got

    def sum_narrow(values):
        values = values + by_narrow(values, 2)
        return values + by_narrow(values, 1)

    def sum_planes(values):
        values = values + by_plane(values, 1)
        return values + by_plane(values, 2)

    def sum_subs(values):
        bit = 1
        while bit < subs:
            values = values + by_sub(values, bit)
            bit *= 2
        return values

    turned_stream = swap(stream)

    size = max(shard_rows, TOK)

    def pad(rows, count):
        return jnp.pad(rows, ((0, count - rows.shape[0]), (0, size - rows.shape[1])))

    own_routes = jnp.concatenate([attn_routes.T, mlp_routes.T], axis=0).astype(BF16)
    own_rows = jnp.concatenate(
        [attn_gain[None, :], attn_router.T, mlp_gain[None, :], mlp_router.T], axis=0
    )
    parts = gather_subs(jnp.concatenate([pad(own_routes, 8), pad(own_rows, 16)], axis=0))
    parts = jnp.stack(parts)
    near = xor_shuffle(parts[:, 8:, :shard_rows], sub).swapaxes(0, 1).reshape(16, slice_width)
    gain_one_plane = near[0].astype(F32)
    router_one_plane = near[1:5].astype(F32)
    gain_two_plane = near[5].astype(F32)
    router_two_plane = near[6:10].astype(F32)

    route_parts = parts[:, :8, :TOK]
    at = jnp.stack([narrow ^ plane, sub, plane, narrow]).astype(jnp.int32)
    kv_parts = gather_subs(key_value)
    query_parts = gather_subs(query_proj, kv_parts[-1])
    out_parts = gather_subs(output_proj, query_parts[-1])
    home_stream = stream.astype(F32)

    rows_all = E * TOK
    sent = shape((2, TOK, local_width), BF16)
    kept_own = shape((2, TOK, local_width), F32)
    all_streams = gather_narrow(turned_stream)
    gained, own_stats, *kv_blocks = run(
        "key_value",
        key_value_body(subs),
        [shape((rows_all, slice_width), BF16), shape((8, TOK), F32), kept_own]
        + [shape((2 * TOK + 16, local_width), BF16)] * (E - 1),
        [
            at,
            *all_streams,
            gain_one_plane[None],
            jnp.pad(router_one_plane, ((0, 4), (0, 0))),
            route_parts,
            *kv_parts,
        ],
        [
            pltpu.VMEM((2, slice_width, local_width), BF16),
            pltpu.VMEM((2, rows_all, local_width), F32),
            pltpu.VMEM((E, 8, TOK), F32),
        ],
    )
    turned_grad = swap(after(out_grad, own_stats))
    kv_blocks = exchange_planes(kv_blocks)
    line_count = wide_count * 8
    hot_cols, home_hot, turned_hot, mlp_cols, expert_hot, select = run(
        "route",
        route_body(subs, capacity),
        [
            shape((E * TOK, 8), F32),
            shape((16, TOK), F32),
            shape((16, TOK), F32),
            shape((TOK, 8), F32),
            shape((8, TOK), F32),
            shape((E, SLOTS, TOK), BF16),
        ],
        [at, route_parts, *kv_blocks[1:]],
        [pltpu.VMEM((line_count, TOK), F32)] * 3 + [pltpu.VMEM((E, 8, TOK), F32)] * 2,
    )
    hot_one, keep_one = home_hot[0:8].reshape(TOPK, E, TOK), home_hot[8:10]
    hot_two, keep_two = turned_hot[0:8].reshape(TOPK, E, TOK), turned_hot[8:10]
    hot_two_k = expert_hot.reshape(E, TOPK, TOK)

    routed_scratch = [
        pltpu.VMEM((E, slice_width, local_width), BF16),
        pltpu.VMEM((TOPK, rows_all, local_width), F32),
    ]
    query_blocks = run(
        "query",
        routed_body(subs, True),
        [kept_own] + [sent] * (E - 1),
        [at, gained, hot_cols, *query_parts],
        routed_scratch,
    )
    query_blocks = exchange_planes(query_blocks)

    def gates(logits, hots):
        picked = jnp.sum(hots * logits[None], axis=1)
        gap = picked[0] - picked[1]
        return jnp.stack([jax.nn.sigmoid(gap), jax.nn.sigmoid(-gap)])

    def share(full):
        size = full.shape[-1]
        full = jnp.concatenate([full, by_side(full, 0)], axis=0)
        got = by_side(full, 1)
        full = jnp.concatenate([full, got], axis=0)
        bit = 2
        while bit < subs:
            full = jnp.concatenate([full, by_sub(full, bit)], axis=0)
            bit *= 2
        return jnp.concatenate([full, by_narrow(full, 1)], axis=0).reshape(-1, size), got

    picked = jnp.einsum("kst,td->ksd", select, turned_grad, preferred_element_type=F32).astype(BF16)
    token_rows, low, probs, context, gated = run(
        "attention",
        attention_body,
        [
            shape((16, TOK), F32),
            shape((4, TOK, local_width), BF16),
            shape((head_count, TOPK * TOK, TOK), F32),
            sent,
            sent,
        ],
        [doc_lengths[0], *kv_blocks, *query_blocks, own_stats, home_hot],
    )
    scale_one, prob_one, logits_one = token_rows[0], token_rows[3:5], token_rows[5:9]

    (full,) = run(
        "join",
        join_body,
        [shape((SLOTS, width), BF16)],
        [at, *after(exchange_planes([picked[k] for k in range(E)]), gated)],
    )
    grad_rows, grad_got = share(full)
    folded = [shape((TOK, slice_width), F32), shape((TOK, slice_width), F32), shape((2, TOK, slice_width), BF16)]
    mixed, *attention = run(
        "output",
        output_body(subs),
        [shape((E, rows_all, local_width), BF16)] + folded,
        [at, *gather_planes(gated), hot_cols, *out_parts],
        [pltpu.VMEM((E, slice_width, local_width), BF16)],
    )
    weight_in = expert_in[0]
    weight_down = expert_down[0]
    dact_raw = dot(grad_rows, weight_down, ((1,), (1,)))

    hidden, stats_two, *picked = run(
        "pick",
        pick_body,
        [shape((TOK, slice_width), F32), shape((8, TOK), F32)]
        + [shape((SLOTS, slice_width + 128), BF16)] * E,
        [
            at,
            turned_stream,
            *after(reduce_narrow(*attention), grad_got),
            gain_two_plane[None],
            jnp.pad(router_two_plane, ((0, 4), (0, 0))),
            mlp_cols,
            select,
        ],
    )
    (full,) = run(
        "join_rows",
        join_rows_body,
        [shape((SLOTS, width + 128), BF16)],
        [at, *exchange_planes(picked)],
    )
    stats_two = sum_planes(stats_two)
    full, _ = share(full)
    full = after(full, stats_two)
    expert_rows = full[:, :width]
    row_pairs = full[:, width : width + 4].astype(F32)
    row_scale = row_pairs[:, 0:1] + row_pairs[:, 1:2]
    row_gate = row_pairs[:, 2:3] + row_pairs[:, 3:4]
    scale_two = lax.rsqrt(stats_two[E] / width + EPSILON)
    logits_two = stats_two[:E] * scale_two
    prob_two = gates(logits_two, hot_two)

    gate_up = jnp.einsum("rd,dkf->krf", expert_rows, weight_in, preferred_element_type=F32)
    gate_pre = gate_up[0] * row_scale
    up_pre = gate_up[1] * row_scale
    gate_sig = jax.nn.sigmoid(gate_pre)
    silu_gate = gate_pre * gate_sig
    activation = (silu_gate * up_pre).astype(BF16)
    dactiv = dact_raw * row_gate
    dgate_pre = (dactiv * up_pre * gate_sig * (1.0 + gate_pre * (1.0 - gate_sig))).astype(BF16)
    dup_pre = (dactiv * silu_gate).astype(BF16)
    dprob_rows = jnp.sum(activation.astype(F32) * dact_raw, axis=-1)
    inner_rows = jnp.sum(dgate_pre.astype(F32) * gate_pre + dup_pre.astype(F32) * up_pre, axis=-1)
    drows = jnp.einsum(
        "krf,dkf->rd", jnp.stack([dgate_pre, dup_pre]), weight_in, preferred_element_type=F32
    )
    lanes = jnp.arange(128)
    row_stats = jnp.where(
        lanes[None, :] == 0, dprob_rows[:, None], jnp.where(lanes[None, :] == 1, inner_rows[:, None], 0.0)
    )

    def give_back(rows):
        half = rows.shape[0] // 2
        rows = rows[:half] + by_narrow(rows[half:].astype(BF16), 1).astype(F32)
        bit = subs // 2
        while bit > 1:
            half = rows.shape[0] // 2
            rows = rows[:half] + by_sub(rows[half:].astype(BF16), bit).astype(F32)
            bit //= 2
        half = rows.shape[0] // 2
        rows = rows[:half] + by_side(rows[half:].astype(BF16), 1).astype(F32)
        return rows[:SLOTS], by_side(rows[SLOTS:].astype(BF16), 0)

    def from_planes(own, got, extra, last=None):
        if last is not None:
            own = after(own, last)
        pieces = run(
            "split",
            split_body(extra),
            [shape((SLOTS, slice_width + extra), BF16)] * E,
            [at, own, got],
            [pltpu.VMEM(own.shape, BF16)],
        )
        return jnp.stack(exchange_planes(pieces))

    returned = give_back(jnp.concatenate([drows, row_stats], axis=1))
    returned = from_planes(*returned, row_stats.shape[1])
    combined = jnp.einsum("kst,ksd->ktd", select, returned, preferred_element_type=F32)
    per_expert = combined[:, :, slice_width : slice_width + 2]
    dprob_two = keep_two * jnp.sum(hot_two_k * per_expert[:, None, :, 0], axis=0)
    inner_two = jnp.sum(per_expert[:, :, 1], axis=0)
    dnormed_two = jnp.sum(combined[:, :, :slice_width], axis=0)

    def gate_back(prob, dprob, hots):
        dselect = prob * (dprob - jnp.sum(prob * dprob, axis=0, keepdims=True))
        return jnp.sum(hots * dselect[:, None, :], axis=0)

    dlogit_two = gate_back(prob_two, dprob_two, hot_two)
    dnormed_two = dnormed_two + dot(dlogit_two, router_two_plane, ((0,), (0,)), PRECISE)
    inner_two = inner_two + jnp.sum(dlogit_two * logits_two, axis=0)
    dhidden = (
        turned_grad.astype(F32)
        + scale_two[:, None] * (dnormed_two * gain_two_plane)
        - hidden * (scale_two * scale_two * inner_two / width)[:, None]
    )
    scaled_hidden = hidden * scale_two[:, None]
    mlp_terms = jnp.concatenate(
        [
            jnp.sum(dnormed_two * scaled_hidden, axis=0)[None],
            dot(dlogit_two, scaled_hidden * gain_two_plane, ((1,), (0,)), PRECISE),
        ],
        axis=0,
    )

    wide_grad, *dcontext_blocks = run(
        "dcontext",
        routed_body(subs, False),
        [shape((rows_all, slice_width), BF16), kept_own] + [sent] * (E - 1),
        [at, *gather_narrow(dhidden.astype(BF16)), hot_cols, *out_parts],
        routed_scratch,
    )
    dcontext_blocks = exchange_planes(dcontext_blocks)

    def weight_parts(count):
        return [
            shape((count, shard_rows, local_width), F32 if j < subs // 2 else BF16)
            for j in range(subs)
        ]

    def weight_sum(parts):
        return finish_subs(parts[: subs // 2], parts[subs // 2 :])

    weight_scratch = [pltpu.VMEM((slice_width, local_width), F32)]
    output_parts = run(
        "output_grad", weight_grad_body, weight_parts(E), [at, wide_grad, mixed], weight_scratch
    )
    expert_out = dot(activation, weight_down, ((1,), (0,))) * row_gate
    mixture = give_back(expert_out)
    output_grad, output_got = weight_sum(output_parts)
    gated_act = (activation.astype(F32) * row_gate).astype(BF16)
    down_grad = dot(after(gated_act, dcontext_blocks[0]), grad_rows, ((0,), (0,)))
    grads_low, home_sums = run(
        "attention_back",
        attention_back_body,
        [shape((4, TOK, local_width), BF16), shape((8, TOK), F32)],
        [
            at,
            *after(dcontext_blocks, output_parts[-1], down_grad),
            token_rows,
            low,
            probs,
            context,
        ],
    )
    grad_planes = gather_planes(grads_low)
    dboth = jnp.stack(
        [
            (dgate_pre.astype(F32) * row_scale).astype(BF16),
            (dup_pre.astype(F32) * row_scale).astype(BF16),
        ],
        axis=1,
    )
    up_grad = jnp.einsum(
        "rd,rkf->dkf", expert_rows, after(dboth, grad_planes[E - 1]), preferred_element_type=F32
    )
    dmixed, *query_grad_parts = run(
        "query_grad",
        query_grad_body,
        [shape((E, rows_all, local_width), BF16)] + weight_parts(E),
        [at, gained, hot_cols, *after(grad_planes, output_got, up_grad)],
        weight_scratch,
    )
    query_grad, query_got = weight_sum(query_grad_parts)
    dkv_all, gain_row, *dnormed_one = run(
        "input",
        input_body(subs),
        [shape((2, rows_all, local_width), BF16), shape((1, slice_width), F32)] + folded,
        [
            at,
            *after(grad_planes, query_grad_parts[-1]),
            dmixed,
            *kv_parts,
            *query_parts,
            *all_streams,
        ],
        [pltpu.VMEM((2 + E, slice_width, local_width), BF16)],
    )
    home_rows = swap(after(near, own_stats))
    gain_one_home = home_rows[0].astype(F32)
    router_one_home = home_rows[1:5].astype(F32)
    gained_home = home_stream * gain_one_home
    home_sums = sum_narrow(after(home_sums, gain_row))
    dprob_one = keep_one * home_sums[:2]
    dlogit_one = gate_back(prob_one, dprob_one, hot_one)
    inner_one = home_sums[2] + jnp.sum(dlogit_one * logits_one, axis=0)
    dlogit_scaled = dlogit_one * scale_one
    router_term = swap(dot(dlogit_scaled, gained_home, ((1,), (0,)), PRECISE))
    kv_grad_parts = run(
        "key_value_grad", weight_grad_body, weight_parts(2), [at, gained, dkv_all], weight_scratch
    )
    kv_grad, kv_got = weight_sum(after(kv_grad_parts, query_got))
    keep, got, other = after(reduce_narrow(*dnormed_one), kv_grad_parts[-1], query_got)
    dnormed_one = keep + got[0].astype(F32) + other.astype(F32)
    turned_out = dhidden + dnormed_one * gain_one_plane
    home_out = swap(turned_out.astype(BF16)).astype(F32)
    stream_grad = (
        home_out
        + gain_one_home * dot(dlogit_scaled, router_one_home, ((0,), (0,)), PRECISE)
        - home_stream * (scale_one * scale_one * inner_one / width)[:, None]
    )

    small = jnp.concatenate([mlp_terms, gain_row, router_term], axis=0)
    small = sum_subs(after(sum_narrow(small), kv_got))
    mine = lax.dynamic_slice_in_dim(small, sub * shard_rows, shard_rows, 1)
    router_one_grad = mine[6:10]
    gain_one_grad = mine[5] + jnp.sum(
        router_one_grad * attn_router.T.astype(F32), axis=0
    ) / attn_gain.astype(F32)

    mixture = from_planes(*mixture, 0, gain_row)
    mixture = jnp.einsum("kst,ksd->td", select, after(mixture, turned_out), preferred_element_type=F32)
    layer_out = swap((hidden + mixture).astype(BF16)).astype(F32)
    return (
        layer_out,
        stream_grad,
        gain_one_grad,
        router_one_grad.T,
        kv_grad,
        query_grad,
        output_grad,
        mine[0],
        mine[1:5].T,
        up_grad[None],
        down_grad[None],
    )


def solution(mesh):
    in_specs = (
        P("wide", "narrow"),
        P("wide", "narrow"),
        P("wide"),
        P("wide", None),
        P(None, "wide", "narrow"),
        P(None, "wide", "narrow"),
        P(None, "wide", "narrow"),
        P("wide"),
        P("wide", None),
        P("wide", None, None, "narrow"),
        P("wide", "narrow", None),
        P("wide", None),
        P("wide", None),
        P("wide", None),
    )
    out_specs = (
        P("wide", "narrow"),
        P("wide", "narrow"),
        P("wide"),
        P("wide", None),
        P(None, "wide", "narrow"),
        P(None, "wide", "narrow"),
        P(None, "wide", "narrow"),
        P("wide"),
        P("wide", None),
        P("wide", None, None, "narrow"),
        P("wide", "narrow", None),
    )
    return jax.shard_map(local, mesh=mesh, in_specs=in_specs, out_specs=out_specs, check_vma=False)
```

```python
import jax
import jax.numpy as jnp
from jax import lax
from jax.experimental import pallas as pl
from jax.experimental.pallas import tpu as pltpu
from jax.sharding import PartitionSpec as P

HS = 128
E = 4
TOPK = 2
TOK = 128
SLOTS = 80

EPSILON = 1e-05
NEGATIVE = -1000000000.0
PRECISE = lax.Precision.HIGHEST
F32 = jnp.float32
BF16 = jnp.bfloat16


def dot(left, right, contract, precision=None):
    return lax.dot_general(
        left, right, ((contract[0], contract[1]), ((), ())), precision=precision, preferred_element_type=F32
    )


def xor_shuffle(values, amount):
    count, bit = values.shape[0], 1
    while bit < count:
        split = values.reshape((count // (2 * bit), 2, bit) + values.shape[1:])
        flipped = split[:, ::-1].reshape(values.shape)
        values = jnp.where((amount & bit) != 0, flipped, values)
        bit *= 2
    return values


NN = (((1,), (0,)), ((), ()))
NT = (((1,), (1,)), ((), ()))
TN = (((0,), (0,)), ((), ()))


def mul(left, right, form):
    return lax.dot_general(left, right, form, preferred_element_type=F32)


def shape(dims, dtype):
    return jax.ShapeDtypeStruct(tuple(dims), dtype)


def run(name, body, outs, args, scratch=()):
    vector = pl.BlockSpec(memory_space=pltpu.VMEM)
    return pl.pallas_call(
        body,
        out_shape=tuple(outs),
        in_specs=[pl.BlockSpec(memory_space=pltpu.SMEM)] + [vector] * (len(args) - 1),
        out_specs=tuple(vector for _ in outs),
        scratch_shapes=list(scratch),
        cost_estimate=pl.CostEstimate(flops=1, transcendentals=0, bytes_accessed=1),
        name=name,
    )(*args)


def loop(count, step):
    def one(i, carry):
        step(i)
        return carry

    lax.fori_loop(0, count, one, 0)


def clear(total):
    def one(i):
        total[i // E, block(i % E), :] = jnp.zeros((TOK, total.shape[2]), F32)

    loop(total.shape[0] * E, one)


def column(values, index):
    lane = lax.broadcasted_iota(jnp.int32, values.shape, 1)
    return jnp.sum(jnp.where(lane == index, values, 0.0), axis=-1, keepdims=True)


def place(store, parts, sub, first=0):
    for j, part in enumerate(parts):
        rows = part.shape[1]
        start = pl.multiple_of((sub ^ j) * rows, rows)

        def one(a, part=part, start=start, rows=rows):
            store[first + a, pl.ds(start, rows), :] = part[a]

        loop(part.shape[0], one)


def block(index):
    return pl.ds(pl.multiple_of(index * TOK, TOK), TOK)


def send_blocks(total, outs, order):
    for k in range(E):

        def one(a, k=k):
            outs[k][a] = total[a, block(order ^ k), :].astype(outs[k].dtype)

        loop(total.shape[0], one)


def stat_rows(square, logits):
    lane = lax.broadcasted_iota(jnp.int32, (TOK, TOK), 1)
    table = jnp.where(lane == E, square, 0.0)
    for e in range(E):
        table = jnp.where(lane == e, logits[:, e : e + 1], table)
    return jnp.transpose(table)[0:8]


def key_value_body(subs):
    def body(at, *refs):
        rows, gain, router, routes = refs[:E], refs[E], refs[E + 1], refs[E + 2]
        parts = refs[E + 3 : E + 3 + subs]
        gained, own_stats, *outs = refs[E + 3 + subs : E + 5 + subs + E]
        weights, total, stats = refs[E + 5 + subs + E :]
        place(weights, parts, at[1])
        for q in range(E):
            wide = rows[q][...].astype(F32)
            scaled = wide * gain[...]
            gained[q * TOK : (q + 1) * TOK, :] = scaled.astype(BF16)
            logits = lax.dot_general(
                scaled, router[...], NT, precision=lax.Precision.HIGHEST, preferred_element_type=F32
            )
            stats[q] = stat_rows(jnp.sum(wide * wide, axis=-1, keepdims=True), logits)

        def project(a):
            total[a] = mul(gained[...], weights[a], NN)

        loop(2, project)
        own_stats[...] = stats[at[0]]
        for k in range(E):
            where = block(at[0] ^ k)
            for a in range(2):
                piece = total[a, where, :].astype(outs[k].dtype)
                if k == 0:
                    outs[k][a] = piece
                else:
                    outs[k][a * TOK : (a + 1) * TOK, :] = piece
            if k > 0:
                mine = stats[at[0] ^ k]
                high = mine.astype(BF16).astype(F32)
                pair = jnp.concatenate([high, mine - high], axis=0).astype(BF16)
                outs[k][2 * TOK :, :] = jnp.zeros((16, outs[k].shape[1]), BF16)
                outs[k][2 * TOK :, 0:TOK] = pair
                for first in range(0, subs, 4):
                    lines = [
                        routes[j][0:4].astype(F32) if j < subs else jnp.zeros((4, TOK), F32)
                        for j in range(first, first + 4)
                    ]
                    start = (1 + first // 4) * TOK
                    outs[k][2 * TOK :, start : start + TOK] = jnp.concatenate(lines, axis=0).astype(BF16)

    return body


def routed_body(subs, joined):
    count = 1 if joined else E

    def body(at, *refs):
        rows, hot, parts = refs[:count], refs[count], refs[count + 1 : count + 1 + subs]
        rest = refs[count + 1 + subs :]
        if joined:
            wide = rows[0]
        else:
            wide, rest = rest[0], rest[1:]
            for q in range(E):
                wide[q * TOK : (q + 1) * TOK, :] = rows[q][...]
        outs, weights, total = rest[:E], rest[E], rest[E + 1]
        place(weights, parts, at[1])
        clear(total)

        def project(e):
            every = mul(wide[...], weights[e], NN)
            for i in range(TOPK):
                total[i] = total[i] + every * column(hot[...], i * E + e)

        loop(E, project)
        send_blocks(total, outs, at[0])

    return body


def spread_pairs(at, rows, hot, out, first=0):
    for k in range(E):
        where = block(at[0] ^ k)
        mask = hot[where, :]

        def one(e, k=k, where=where, mask=mask):
            out[e, where, :] = rows[k][first] * column(mask, e).astype(BF16) + rows[k][
                first + 1
            ] * column(mask, E + e).astype(BF16)

        loop(E, one)


def fold_out(total, keep_0, keep_2, send):
    keep_0[...] = total[0:TOK]
    keep_2[...] = total[2 * TOK : 3 * TOK]
    send[0] = total[TOK : 2 * TOK].astype(BF16)
    send[1] = total[3 * TOK : 4 * TOK].astype(BF16)


def output_body(subs):
    def body(at, *refs):
        rows, hot, parts = refs[:E], refs[E], refs[E + 1 : E + 1 + subs]
        mixed, keep_0, keep_2, send, weights, total = refs[E + 1 + subs :]
        place(weights, parts, at[1])
        spread_pairs(at, rows, hot, mixed)
        clear(total)

        def project(e):
            total[0] = total[0] + mul(mixed[e], weights[e], NT)

        loop(E, project)
        fold_out(total[0], keep_0, keep_2, send)

    return body


def input_body(subs):
    def body(at, *refs):
        rows, dmixed = refs[:E], refs[E]
        kv_parts = refs[E + 1 : E + 1 + subs]
        query_parts = refs[E + 1 + subs : E + 1 + 2 * subs]
        streams = refs[E + 1 + 2 * subs : 2 * E + 1 + 2 * subs]
        dkv_all, gain_row, keep_0, keep_2, send, weights, store = refs[2 * E + 1 + 2 * subs :]
        place(weights, kv_parts, at[1])
        place(weights, query_parts, at[1], 2)
        for k in range(E):
            for a in range(2):
                dkv_all[a, block(at[0] ^ k), :] = rows[k][a]
        clear(store)

        def project_kv(a):
            store[0] = store[0] + mul(dkv_all[a], weights[a], NT)

        def project(e):
            store[0] = store[0] + mul(dmixed[e], weights[2 + e], NT)

        loop(2, project_kv)
        loop(E, project)
        total = store[0]
        gain = jnp.zeros((1, total.shape[1]), F32)
        for q in range(E):
            part = total[q * TOK : (q + 1) * TOK] * streams[q][...].astype(F32)
            gain = gain + jnp.sum(part, axis=0, keepdims=True)
        gain_row[...] = gain
        fold_out(total, keep_0, keep_2, send)

    return body


def split_rows(at, rows, other, parts, total):
    def one(a):
        total[...] = mul(rows[...], other[a], TN)
        for j, part in enumerate(parts):
            count = part.shape[1]
            start = pl.multiple_of((at[1] ^ j) * count, count)
            part[a] = total[pl.ds(start, count), :].astype(part.dtype)

    loop(other.shape[0], one)


def weight_grad_body(at, rows, other, *refs):
    split_rows(at, rows, other, refs[:-1], refs[-1])


def query_grad_body(at, rows, hot, *refs):
    dmixed = refs[E]
    spread_pairs(at, refs[:E], hot, dmixed, 2)
    split_rows(at, rows, dmixed, refs[E + 1 : -1], refs[-1])


def attention_mask(at):
    row = lax.broadcasted_iota(jnp.int32, (TOK, TOK), 0)
    col = lax.broadcasted_iota(jnp.int32, (TOK, TOK), 1)
    row_doc, col_doc, end = jnp.zeros_like(row), jnp.zeros_like(row), 0
    for d in range(4):
        end = end + at[d]
        row_doc = row_doc + (row >= end).astype(jnp.int32)
        col_doc = col_doc + (col >= end).astype(jnp.int32)
    return (row_doc == col_doc) & (col <= row)


def attention_body(at, own_kv, *refs):
    got_kv, own_query, got_query = refs[: E - 1], refs[E - 1], refs[E : 2 * E - 1]
    own_stats, hot, rows, low, probs, context, gated = refs[2 * E - 1 :]
    stats = own_stats[...]
    for one in got_kv:
        pair = one[2 * TOK :, 0:TOK].astype(F32)
        stats = stats + pair[0:8] + pair[8:16]
    scale_row = lax.rsqrt(stats[E : E + 1] / (E * own_kv.shape[2]) + EPSILON)
    logits = stats[0:E] * scale_row
    picked = [
        jnp.sum(hot[i * E : (i + 1) * E, :] * logits, axis=0, keepdims=True) for i in range(TOPK)
    ]
    gap = picked[0] - picked[1]
    prob_rows = [1.0 / (1.0 + jnp.exp(-gap)), 1.0 / (1.0 + jnp.exp(gap))]
    rows[0:1, :] = scale_row
    for i in range(TOPK):
        rows[1 + i : 2 + i, :] = prob_rows[i] * hot[8 + i : 9 + i, :]
        rows[3 + i : 4 + i, :] = prob_rows[i]
    rows[5:9, :] = logits
    rows[9:16, :] = jnp.zeros((7, TOK), F32)
    cols = columns(rows[...])
    scale = cols[:, 0:1]
    for a in range(2):
        where = slice(a * TOK, (a + 1) * TOK)
        total, query = own_kv[a], own_query[a]
        for one in got_kv:
            total = total + one[where, :].astype(F32)
        for one in got_query:
            query = query + one[a].astype(F32)
        low[a] = (total * scale).astype(BF16)
        low[2 + a] = (query * scale).astype(BF16)
    allowed = attention_mask(at)

    def attend(h):
        head = pl.ds(pl.multiple_of(h * HS, HS), HS)
        for i in range(TOPK):
            scores = mul(low[2 + i, :, head], low[0, :, head], NT) * HS ** (-0.5)
            scores = jnp.where(allowed, scores, NEGATIVE)
            top = jnp.exp(scores - jnp.max(scores, axis=-1, keepdims=True))
            prob = top / jnp.sum(top, axis=-1, keepdims=True)
            probs[h, i * TOK : (i + 1) * TOK, :] = prob
            mixed = mul(prob.astype(BF16), low[1, :, head], NN).astype(BF16)
            context[i, :, head] = mixed
            gated[i, :, head] = (mixed.astype(F32) * cols[:, 1 + i : 2 + i]).astype(BF16)

    loop(low.shape[2] // HS, attend)


def attention_back_body(at, own, *refs):
    got = refs[: E - 1]
    rows, low, probs, context, grads, sums, dcontext, inner = refs[E - 1 :]
    cols = columns(rows[...])
    scale = cols[:, 0:1]
    inner[...] = jnp.zeros((TOK, HS), F32)
    dprob = []
    for i in range(TOPK):
        raw = own[i]
        for one in got:
            raw = raw + one[i].astype(F32)
        dprob.append(jnp.sum(context[i].astype(F32) * raw, axis=-1, keepdims=True))
        dcontext[i] = (raw * cols[:, 1 + i : 2 + i]).astype(BF16)

    def attend(h):
        head = pl.ds(pl.multiple_of(h * HS, HS), HS)
        key, value = low[0, :, head], low[1, :, head]
        dkey = jnp.zeros((TOK, HS), F32)
        dvalue = jnp.zeros((TOK, HS), F32)
        for i in range(TOPK):
            query = low[2 + i, :, head]
            grad = dcontext[i, :, head]
            prob = probs[h, i * TOK : (i + 1) * TOK, :]
            dweight = mul(grad, value, NT)
            dscore = prob * (dweight - jnp.sum(prob * dweight, axis=-1, keepdims=True))
            dscore = dscore.astype(BF16)
            done = mul(dscore, key, NN) * HS ** (-0.5)
            dkey = dkey + mul(dscore, query, TN)
            dvalue = dvalue + mul(prob.astype(BF16), grad, TN)
            inner[...] = inner[...] + done * query.astype(F32)
            grads[2 + i, :, head] = (done * scale).astype(BF16)
        dkey = dkey * HS ** (-0.5)
        inner[...] = inner[...] + dkey * key.astype(F32) + dvalue * value.astype(F32)
        grads[0, :, head] = (dkey * scale).astype(BF16)
        grads[1, :, head] = (dvalue * scale).astype(BF16)

    loop(low.shape[2] // HS, attend)
    total = jnp.sum(inner[...], axis=-1, keepdims=True)
    lane = lax.broadcasted_iota(jnp.int32, (TOK, TOK), 1)
    table = jnp.where(lane == 0, dprob[0], jnp.where(lane == 1, dprob[1], jnp.where(lane == 2, total, 0.0)))
    sums[...] = jnp.transpose(table)[0:8]


def expert_grad_body(at, dgate, dup, weights, stats, own, send):
    half, size = own.shape[0], weights.shape[2]

    def one(n):
        where = pl.ds(pl.multiple_of(n * 256, 256), 256)
        total = mul(dgate[...], weights[0, :, where], NN) + mul(dup[...], weights[1, :, where], NN)
        own[:, where] = total[:half]
        send[:, where] = total[half:].astype(BF16)

    loop(size // 256, one)
    own[:, size:] = stats[:half, :]
    send[:, size:] = stats[half:, :].astype(BF16)


def expert_out_body(at, rows, weights, pairs, own, send):
    half, size = own.shape[0], weights.shape[1]
    gate = pairs[:, 2:3].astype(F32) + pairs[:, 3:4].astype(F32)

    def one(n):
        where = pl.ds(pl.multiple_of(n * 256, 256), 256)
        total = mul(rows[...], weights[:, where], NN) * gate
        own[:, where] = total[:half]
        send[:, where] = total[half:].astype(BF16)

    loop(size // 256, one)


def columns(rows):
    return jnp.transpose(jnp.concatenate([rows] * (TOK // rows.shape[0]), axis=0))


def pick_row(values, index):
    line = lax.broadcasted_iota(jnp.int32, values.shape, 0)
    return jnp.sum(jnp.where(line == index, values, 0.0), axis=0, keepdims=True)


def route_body(subs, capacity):
    count = E * subs * 8

    def body(at, *refs):
        tables = refs[:E]
        hot_cols, home, turned, mlp_cols, expert_rows, select = refs[E : E + 6]
        both, rank, kept, hot, mlp_hot = refs[E + 6 :]
        expert = lax.broadcasted_iota(jnp.int32, (E, TOK), 0).astype(F32)
        for k in range(E):
            for j in range(subs):
                if k == 0:
                    line = tables[0][j].astype(F32)
                else:
                    first = (1 + j // 4) * TOK
                    lines = tables[k][2 * TOK :, first : first + TOK].astype(F32)
                    line = lines[(j % 4) * 4 : (j % 4) * 4 + 4]
                ones = [(line[r : r + 1] == expert).astype(F32) for r in range(4)]
                start = (k * subs + j) * 8
                both[start : start + 4, :] = ones[0] + ones[1]
                both[start + 4 : start + 8, :] = ones[2] + ones[3]
                if j == 0:
                    hot[k, 0:4, :], hot[k, 4:8, :] = ones[0], ones[1]
                    mlp_hot[k, 0:4, :], mlp_hot[k, 4:8, :] = ones[2], ones[3]
        low = both[...].astype(BF16)
        row = lax.broadcasted_iota(jnp.int32, (TOK, TOK), 0)
        col = lax.broadcasted_iota(jnp.int32, (TOK, TOK), 1)
        rank[...] = mul(low, (row < col).astype(F32).astype(BF16), NN)
        row = lax.broadcasted_iota(jnp.int32, (count, count), 0)
        col = lax.broadcasted_iota(jnp.int32, (count, count), 1)
        own = at[2] * subs + at[1]
        ahead = (((col >> 3) ^ own) < ((row >> 3) ^ own)) & ((col & 7) == (row & 7))
        before = mul(ahead.astype(F32).astype(BF16), low, NN)
        place_of = jnp.sum(before, axis=-1, keepdims=True) + rank[...]
        kept[...] = both[...] * (place_of < capacity).astype(F32)

        for k in range(E):
            hot_cols[block(at[0] ^ k), :] = columns(hot[k])[:, 0:8]
        pad = jnp.zeros((6, TOK), F32)
        home[0:8, :] = hot[0]
        for i in range(TOPK):
            home[8 + i : 9 + i, :] = jnp.sum(
                hot[0, i * E : (i + 1) * E, :] * kept[0:E, :], axis=0, keepdims=True
            )
        home[10:16, :] = pad
        mine = mlp_hot[at[0]]
        start = pl.multiple_of(at[0] * (subs * 8), 8)
        kept_mine = kept[pl.ds(start, 8), :][4:8]
        rank_mine = rank[pl.ds(start, 8), :][4:8]
        turned[0:8, :] = mine
        for i in range(TOPK):
            turned[8 + i : 9 + i, :] = jnp.sum(
                mine[i * E : (i + 1) * E] * kept_mine, axis=0, keepdims=True
            )
        turned[10:16, :] = pad
        mlp_cols[...] = columns(mine)[:, 0:8]
        slot = lax.broadcasted_iota(jnp.int32, (SLOTS, TOK), 0).astype(F32)
        for k in range(E):
            e = at[2] ^ k
            for i in range(TOPK):
                expert_rows[2 * k + i : 2 * k + i + 1, :] = pick_row(mine[i * E : (i + 1) * E], e)
            taken = (slot == pick_row(rank_mine, e)) & (pick_row(kept_mine, e) > 0)
            select[k] = taken.astype(F32).astype(BF16)

    return body


def two_halves(values):
    lane = lax.broadcasted_iota(jnp.int32, (values[0].shape[0], 128), 1)
    table = jnp.zeros((values[0].shape[0], 128), F32)
    for i, one in enumerate(values):
        high = one.astype(BF16).astype(F32)
        table = jnp.where(lane == 2 * i, high, table)
        table = jnp.where(lane == 2 * i + 1, one - high, table)
    return table.astype(BF16)


def pick_body(at, stream, keep, got, other, gain, router, mlp_cols, select, *refs):
    hidden, stats, outs = refs[0], refs[1], refs[2:]
    size = hidden.shape[1]
    total = stream[...].astype(F32) + (keep[...] + got[0].astype(F32) + other[...].astype(F32))
    hidden[...] = total
    gained = total * gain[...]
    square = jnp.sum(total * total, axis=-1, keepdims=True)
    logits = lax.dot_general(
        gained, router[...], NT, precision=lax.Precision.HIGHEST, preferred_element_type=F32
    )
    lane = lax.broadcasted_iota(jnp.int32, logits.shape, 1)
    chosen = jnp.zeros_like(square)
    for e in range(E):
        one = mlp_cols[:, e : e + 1] + mlp_cols[:, E + e : E + e + 1]
        chosen = chosen + one * logits[:, e : e + 1]
    low = gained.astype(BF16)
    for k in range(E):
        own = jnp.sum(jnp.where(lane == (at[2] ^ k), logits, 0.0), axis=-1, keepdims=True)
        extra = two_halves([square, 2.0 * own - chosen])
        outs[k][:, :size] = mul(select[k], low, NN).astype(BF16)
        outs[k][:, size:] = mul(select[k], extra, NN).astype(BF16)
    stats[...] = stat_rows(square, logits)


def join_rows_body(at, *refs):
    pieces, out = refs[:E], refs[E]
    size = pieces[0].shape[1] - 128
    join_pieces(at, pieces, out, size)
    total = pieces[0][:, size:].astype(F32)
    for k in range(1, E):
        total = total + pieces[k][:, size:].astype(F32)
    square, gap = total[:, 0:1] + total[:, 1:2], total[:, 2:3] + total[:, 3:4]
    scale = lax.rsqrt(square / (E * size) + EPSILON)
    small = jnp.exp(-jnp.abs(gap * scale))
    gate = jnp.where(gap < 0.0, small, 1.0) / (1.0 + small)
    out[:, E * size :] = two_halves([scale, gate])


def join_pieces(at, pieces, out, size):
    for k in range(E):
        for p in range(E):

            @pl.when((at[2] ^ k) == p)
            def _(k=k, p=p):
                out[:, p * size : (p + 1) * size] = pieces[k][:, :size]


def join_body(at, *refs):
    join_pieces(at, refs[:E], refs[E], refs[0].shape[1])


def split_body(extra):
    def body(at, own, got, *refs):
        outs, store = refs[:E], refs[E]
        store[...] = (own[...] + got[...].astype(F32)).astype(BF16)
        size = outs[0].shape[1] - extra
        for k in range(E):
            for p in range(E):

                @pl.when((at[2] ^ k) == p)
                def _(k=k, p=p):
                    outs[k][:, :size] = store[:, p * size : (p + 1) * size]

            if extra:
                outs[k][:, size:] = store[:, E * size :]

    return body


def local(
    stream,
    out_grad,
    attn_gain,
    attn_router,
    key_value,
    query_proj,
    output_proj,
    mlp_gain,
    mlp_router,
    expert_in,
    expert_down,
    attn_routes,
    mlp_routes,
    doc_lengths,
):
    wide_count = lax.axis_size("wide")
    narrow_count = lax.axis_size("narrow")
    subs = wide_count // E
    wide = lax.axis_index("wide")
    narrow = lax.axis_index("narrow")
    plane, sub = wide // subs, wide % subs
    capacity = 9 * TOK * wide_count * TOPK // (8 * E)
    slice_width = stream.shape[1]
    shard_rows = attn_gain.shape[0]
    width = slice_width * narrow_count
    local_width = key_value.shape[2]
    head_count = local_width // HS
    hidden_units = expert_down.shape[1]
    score_scale = HS ** (-0.5)

    def after(values, *others):
        return lax.optimization_barrier((values, others))[0]

    def by_plane(values, k):
        return lax.ppermute(values, "wide", [(i, i ^ (k * subs)) for i in range(wide_count)])

    def by_sub(values, k):
        return lax.ppermute(values, "wide", [(i, i ^ k) for i in range(wide_count)])

    def by_narrow(values, k):
        return lax.ppermute(values, "narrow", [(i, i ^ k) for i in range(narrow_count)])

    def swap(values):
        pairs = []
        for w in range(wide_count):
            for n in range(narrow_count):
                z, y = w // subs, w % subs
                pairs.append((w * narrow_count + n, (n * subs + y) * narrow_count + z))
        return lax.ppermute(values, ("wide", "narrow"), pairs)

    def by_side(values, side):
        pairs = []
        for w in range(wide_count):
            for n in range(narrow_count):
                other = (w ^ 1, n) if (n & 1) == side else (w, n ^ 2)
                pairs.append((w * narrow_count + n, other[0] * narrow_count + other[1]))
        return lax.ppermute(values, ("wide", "narrow"), pairs)

    def gather_planes(values):
        return [values] + [by_plane(values, k) for k in range(1, E)]

    def exchange_planes(parts):
        return [parts[0]] + [by_plane(parts[k], k) for k in range(1, E)]

    def gather_subs(values, *others):
        parts, bit = [values], 1
        while bit < subs:
            parts = parts + [by_sub(after(one, *others) if others else one, bit) for one in parts]
            bit *= 2
        return parts

    def reduce_subs(parts):
        bit = len(parts) // 2
        while bit >= 1:
            parts = [parts[j] + by_sub(parts[j + bit].astype(BF16), bit).astype(F32) for j in range(bit)]
            bit //= 2
        return parts[0]

    def gather_narrow(values):
        other = by_narrow(values, 2)
        return [values, by_narrow(values, 1), other, by_narrow(other, 1)]

    def reduce_narrow(keep_0, keep_2, send):
        got = by_narrow(send, 1)
        other = by_narrow((keep_2 + got[1].astype(F32)).astype(BF16), 2)
        return keep_0, got, other

    def finish_subs(keep, send):
        bit = len(keep)
        got = [by_sub(send[j], bit) for j in range(bit)]
        return reduce_subs([keep[j] + got[j].astype(F32) for j in range(bit)]), got

    def sum_narrow(values):
        values = values + by_narrow(values, 2)
        return values + by_narrow(values, 1)

    def sum_planes(values):
        values = values + by_plane(values, 1)
        return values + by_plane(values, 2)

    def sum_subs(values):
        bit = 1
        while bit < subs:
            values = values + by_sub(values, bit)
            bit *= 2
        return values

    turned_stream = swap(stream)

    size = max(shard_rows, TOK)

    def pad(rows, count):
        return jnp.pad(rows, ((0, count - rows.shape[0]), (0, size - rows.shape[1])))

    own_routes = jnp.concatenate([attn_routes.T, mlp_routes.T], axis=0).astype(BF16)
    own_rows = jnp.concatenate(
        [attn_gain[None, :], attn_router.T, mlp_gain[None, :], mlp_router.T], axis=0
    )
    parts = gather_subs(jnp.concatenate([pad(own_routes, 8), pad(own_rows, 16)], axis=0))
    parts = jnp.stack(parts)
    near = xor_shuffle(parts[:, 8:, :shard_rows], sub).swapaxes(0, 1).reshape(16, slice_width)
    gain_one_plane = near[0].astype(F32)
    router_one_plane = near[1:5].astype(F32)
    gain_two_plane = near[5].astype(F32)
    router_two_plane = near[6:10].astype(F32)

    route_parts = parts[:, :8, :TOK]
    at = jnp.stack([narrow ^ plane, sub, plane, narrow]).astype(jnp.int32)
    kv_parts = gather_subs(key_value)
    query_parts = gather_subs(query_proj, kv_parts[-1])
    out_parts = gather_subs(output_proj, query_parts[-1])
    home_stream = stream.astype(F32)

    rows_all = E * TOK
    sent = shape((2, TOK, local_width), BF16)
    kept_own = shape((2, TOK, local_width), F32)
    all_streams = gather_narrow(turned_stream)
    gained, own_stats, *kv_blocks = run(
        "key_value",
        key_value_body(subs),
        [shape((rows_all, slice_width), BF16), shape((8, TOK), F32), kept_own]
        + [shape((2 * TOK + 16, local_width), BF16)] * (E - 1),
        [
            at,
            *all_streams,
            gain_one_plane[None],
            jnp.pad(router_one_plane, ((0, 4), (0, 0))),
            route_parts,
            *kv_parts,
        ],
        [
            pltpu.VMEM((2, slice_width, local_width), BF16),
            pltpu.VMEM((2, rows_all, local_width), F32),
            pltpu.VMEM((E, 8, TOK), F32),
        ],
    )
    turned_grad = swap(after(out_grad, own_stats))
    kv_blocks = exchange_planes(kv_blocks)
    line_count = wide_count * 8
    hot_cols, home_hot, turned_hot, mlp_cols, expert_hot, select = run(
        "route",
        route_body(subs, capacity),
        [
            shape((E * TOK, 8), F32),
            shape((16, TOK), F32),
            shape((16, TOK), F32),
            shape((TOK, 8), F32),
            shape((8, TOK), F32),
            shape((E, SLOTS, TOK), BF16),
        ],
        [at, route_parts, *kv_blocks[1:]],
        [pltpu.VMEM((line_count, TOK), F32)] * 3 + [pltpu.VMEM((E, 8, TOK), F32)] * 2,
    )
    hot_one, keep_one = home_hot[0:8].reshape(TOPK, E, TOK), home_hot[8:10]
    hot_two, keep_two = turned_hot[0:8].reshape(TOPK, E, TOK), turned_hot[8:10]
    hot_two_k = expert_hot.reshape(E, TOPK, TOK)

    routed_scratch = [
        pltpu.VMEM((E, slice_width, local_width), BF16),
        pltpu.VMEM((TOPK, rows_all, local_width), F32),
    ]
    query_blocks = run(
        "query",
        routed_body(subs, True),
        [kept_own] + [sent] * (E - 1),
        [at, gained, hot_cols, *query_parts],
        routed_scratch,
    )
    query_blocks = exchange_planes(query_blocks)

    def gates(logits, hots):
        picked = jnp.sum(hots * logits[None], axis=1)
        gap = picked[0] - picked[1]
        return jnp.stack([jax.nn.sigmoid(gap), jax.nn.sigmoid(-gap)])

    def share(full):
        size = full.shape[-1]
        full = jnp.concatenate([full, by_side(full, 0)], axis=0)
        got = by_side(full, 1)
        full = jnp.concatenate([full, got], axis=0)
        bit = 2
        while bit < subs:
            full = jnp.concatenate([full, by_sub(full, bit)], axis=0)
            bit *= 2
        return jnp.concatenate([full, by_narrow(full, 1)], axis=0).reshape(-1, size), got

    picked = jnp.einsum("kst,td->ksd", select, turned_grad, preferred_element_type=F32).astype(BF16)
    token_rows, low, probs, context, gated = run(
        "attention",
        attention_body,
        [
            shape((16, TOK), F32),
            shape((4, TOK, local_width), BF16),
            shape((head_count, TOPK * TOK, TOK), F32),
            sent,
            sent,
        ],
        [doc_lengths[0], *kv_blocks, *query_blocks, own_stats, home_hot],
    )
    scale_one, prob_one, logits_one = token_rows[0], token_rows[3:5], token_rows[5:9]

    (full,) = run(
        "join",
        join_body,
        [shape((SLOTS, width), BF16)],
        [at, *after(exchange_planes([picked[k] for k in range(E)]), gated)],
    )
    grad_rows, grad_got = share(full)
    folded = [shape((TOK, slice_width), F32), shape((TOK, slice_width), F32), shape((2, TOK, slice_width), BF16)]
    mixed, *attention = run(
        "output",
        output_body(subs),
        [shape((E, rows_all, local_width), BF16)] + folded,
        [at, *gather_planes(gated), hot_cols, *out_parts],
        [
            pltpu.VMEM((E, slice_width, local_width), BF16),
            pltpu.VMEM((1, rows_all, slice_width), F32),
        ],
    )
    weight_in = expert_in[0]
    weight_down = expert_down[0]
    dact_raw = dot(grad_rows, weight_down, ((1,), (1,)))

    hidden, stats_two, *picked = run(
        "pick",
        pick_body,
        [shape((TOK, slice_width), F32), shape((8, TOK), F32)]
        + [shape((SLOTS, slice_width + 128), BF16)] * E,
        [
            at,
            turned_stream,
            *after(reduce_narrow(*attention), grad_got),
            gain_two_plane[None],
            jnp.pad(router_two_plane, ((0, 4), (0, 0))),
            mlp_cols,
            select,
        ],
    )
    (full,) = run(
        "join_rows",
        join_rows_body,
        [shape((SLOTS, width + 128), BF16)],
        [at, *exchange_planes(picked)],
    )
    stats_two = sum_planes(stats_two)
    full, _ = share(full)
    full = after(full, stats_two)
    expert_rows = full[:, :width]
    row_pairs = full[:, width : width + 4].astype(F32)
    row_scale = row_pairs[:, 0:1] + row_pairs[:, 1:2]
    row_gate = row_pairs[:, 2:3] + row_pairs[:, 3:4]
    scale_two = lax.rsqrt(stats_two[E] / width + EPSILON)
    logits_two = stats_two[:E] * scale_two
    prob_two = gates(logits_two, hot_two)

    gate_up = jnp.einsum("rd,dkf->krf", expert_rows, weight_in, preferred_element_type=F32)
    gate_pre = gate_up[0] * row_scale
    up_pre = gate_up[1] * row_scale
    gate_sig = jax.nn.sigmoid(gate_pre)
    silu_gate = gate_pre * gate_sig
    activation = (silu_gate * up_pre).astype(BF16)
    dactiv = dact_raw * row_gate
    dgate_pre = (dactiv * up_pre * gate_sig * (1.0 + gate_pre * (1.0 - gate_sig))).astype(BF16)
    dup_pre = (dactiv * silu_gate).astype(BF16)
    dprob_rows = jnp.sum(activation.astype(F32) * dact_raw, axis=-1)
    inner_rows = jnp.sum(dgate_pre.astype(F32) * gate_pre + dup_pre.astype(F32) * up_pre, axis=-1)
    lanes = jnp.arange(128)
    row_stats = jnp.where(
        lanes[None, :] == 0, dprob_rows[:, None], jnp.where(lanes[None, :] == 1, inner_rows[:, None], 0.0)
    )

    def give_back(own, send):
        rows = own + by_narrow(send, 1).astype(F32)
        bit = subs // 2
        while bit > 1:
            half = rows.shape[0] // 2
            rows = rows[:half] + by_sub(rows[half:].astype(BF16), bit).astype(F32)
            bit //= 2
        half = rows.shape[0] // 2
        rows = rows[:half] + by_side(rows[half:].astype(BF16), 1).astype(F32)
        return rows[:SLOTS], by_side(rows[SLOTS:].astype(BF16), 0)

    def from_planes(own, got, extra, last=None):
        if last is not None:
            own = after(own, last)
        pieces = run(
            "split",
            split_body(extra),
            [shape((SLOTS, slice_width + extra), BF16)] * E,
            [at, own, got],
            [pltpu.VMEM(own.shape, BF16)],
        )
        return jnp.stack(exchange_planes(pieces))

    half = expert_rows.shape[0] // 2
    returned = run(
        "expert_grad",
        expert_grad_body,
        [shape((half, width + 128), F32), shape((half, width + 128), BF16)],
        [at, dgate_pre, dup_pre, jnp.transpose(weight_in, (1, 2, 0)), row_stats],
    )
    returned = give_back(*returned)
    returned = from_planes(*returned, row_stats.shape[1])
    combined = jnp.einsum("kst,ksd->ktd", select, returned, preferred_element_type=F32)
    per_expert = combined[:, :, slice_width : slice_width + 2]
    dprob_two = keep_two * jnp.sum(hot_two_k * per_expert[:, None, :, 0], axis=0)
    inner_two = jnp.sum(per_expert[:, :, 1], axis=0)
    dnormed_two = jnp.sum(combined[:, :, :slice_width], axis=0)

    def gate_back(prob, dprob, hots):
        dselect = prob * (dprob - jnp.sum(prob * dprob, axis=0, keepdims=True))
        return jnp.sum(hots * dselect[:, None, :], axis=0)

    dlogit_two = gate_back(prob_two, dprob_two, hot_two)
    dnormed_two = dnormed_two + dot(dlogit_two, router_two_plane, ((0,), (0,)), PRECISE)
    inner_two = inner_two + jnp.sum(dlogit_two * logits_two, axis=0)
    dhidden = (
        turned_grad.astype(F32)
        + scale_two[:, None] * (dnormed_two * gain_two_plane)
        - hidden * (scale_two * scale_two * inner_two / width)[:, None]
    )
    scaled_hidden = hidden * scale_two[:, None]
    mlp_terms = jnp.concatenate(
        [
            jnp.sum(dnormed_two * scaled_hidden, axis=0)[None],
            dot(dlogit_two, scaled_hidden * gain_two_plane, ((1,), (0,)), PRECISE),
        ],
        axis=0,
    )

    wide_grad, *dcontext_blocks = run(
        "dcontext",
        routed_body(subs, False),
        [shape((rows_all, slice_width), BF16), kept_own] + [sent] * (E - 1),
        [at, *gather_narrow(dhidden.astype(BF16)), hot_cols, *out_parts],
        routed_scratch,
    )
    dcontext_blocks = exchange_planes(dcontext_blocks)

    def weight_parts(count):
        return [
            shape((count, shard_rows, local_width), F32 if j < subs // 2 else BF16)
            for j in range(subs)
        ]

    def weight_sum(parts):
        return finish_subs(parts[: subs // 2], parts[subs // 2 :])

    weight_scratch = [pltpu.VMEM((slice_width, local_width), F32)]
    output_parts = run(
        "output_grad", weight_grad_body, weight_parts(E), [at, wide_grad, mixed], weight_scratch
    )
    expert_out = run(
        "expert_out",
        expert_out_body,
        [shape((half, width), F32), shape((half, width), BF16)],
        [at, activation, weight_down, full[:, width:]],
    )
    mixture = give_back(*expert_out)
    output_grad, output_got = weight_sum(output_parts)
    gated_act = (activation.astype(F32) * row_gate).astype(BF16)
    down_grad = dot(after(gated_act, dcontext_blocks[0]), grad_rows, ((0,), (0,)))
    grads_low, home_sums = run(
        "attention_back",
        attention_back_body,
        [shape((4, TOK, local_width), BF16), shape((8, TOK), F32)],
        [
            at,
            *after(dcontext_blocks, output_parts[-1], down_grad),
            token_rows,
            low,
            probs,
            context,
        ],
        [pltpu.VMEM((TOPK, TOK, local_width), BF16), pltpu.VMEM((TOK, HS), F32)],
    )
    grad_planes = gather_planes(grads_low)
    dboth = jnp.stack(
        [
            (dgate_pre.astype(F32) * row_scale).astype(BF16),
            (dup_pre.astype(F32) * row_scale).astype(BF16),
        ],
        axis=1,
    )
    up_grad = jnp.einsum(
        "rd,rkf->dkf", expert_rows, after(dboth, grad_planes[E - 1]), preferred_element_type=F32
    )
    dmixed, *query_grad_parts = run(
        "query_grad",
        query_grad_body,
        [shape((E, rows_all, local_width), BF16)] + weight_parts(E),
        [at, gained, hot_cols, *after(grad_planes, output_got, up_grad)],
        weight_scratch,
    )
    query_grad, query_got = weight_sum(query_grad_parts)
    dkv_all, gain_row, *dnormed_one = run(
        "input",
        input_body(subs),
        [shape((2, rows_all, local_width), BF16), shape((1, slice_width), F32)] + folded,
        [
            at,
            *after(grad_planes, query_grad_parts[-1]),
            dmixed,
            *kv_parts,
            *query_parts,
            *all_streams,
        ],
        [
            pltpu.VMEM((2 + E, slice_width, local_width), BF16),
            pltpu.VMEM((1, rows_all, slice_width), F32),
        ],
    )
    home_rows = swap(after(near, own_stats))
    gain_one_home = home_rows[0].astype(F32)
    router_one_home = home_rows[1:5].astype(F32)
    gained_home = home_stream * gain_one_home
    home_sums = sum_narrow(after(home_sums, gain_row))
    dprob_one = keep_one * home_sums[:2]
    dlogit_one = gate_back(prob_one, dprob_one, hot_one)
    inner_one = home_sums[2] + jnp.sum(dlogit_one * logits_one, axis=0)
    dlogit_scaled = dlogit_one * scale_one
    router_term = swap(dot(dlogit_scaled, gained_home, ((1,), (0,)), PRECISE))
    kv_grad_parts = run(
        "key_value_grad", weight_grad_body, weight_parts(2), [at, gained, dkv_all], weight_scratch
    )
    kv_grad, kv_got = weight_sum(after(kv_grad_parts, query_got))
    keep, got, other = after(reduce_narrow(*dnormed_one), kv_grad_parts[-1], query_got)
    dnormed_one = keep + got[0].astype(F32) + other.astype(F32)
    turned_out = dhidden + dnormed_one * gain_one_plane
    home_out = swap(turned_out.astype(BF16)).astype(F32)
    stream_grad = (
        home_out
        + gain_one_home * dot(dlogit_scaled, router_one_home, ((0,), (0,)), PRECISE)
        - home_stream * (scale_one * scale_one * inner_one / width)[:, None]
    )

    small = jnp.concatenate([mlp_terms, gain_row, router_term], axis=0)
    small = sum_subs(after(sum_narrow(small), kv_got))
    mine = lax.dynamic_slice_in_dim(small, sub * shard_rows, shard_rows, 1)
    router_one_grad = mine[6:10]
    gain_one_grad = mine[5] + jnp.sum(
        router_one_grad * attn_router.T.astype(F32), axis=0
    ) / attn_gain.astype(F32)

    mixture = from_planes(*mixture, 0, gain_row)
    mixture = jnp.einsum("kst,ksd->td", select, after(mixture, turned_out), preferred_element_type=F32)
    layer_out = swap((hidden + mixture).astype(BF16)).astype(F32)
    return (
        layer_out,
        stream_grad,
        gain_one_grad,
        router_one_grad.T,
        kv_grad,
        query_grad,
        output_grad,
        mine[0],
        mine[1:5].T,
        up_grad[None],
        down_grad[None],
    )


def solution(mesh):
    in_specs = (
        P("wide", "narrow"),
        P("wide", "narrow"),
        P("wide"),
        P("wide", None),
        P(None, "wide", "narrow"),
        P(None, "wide", "narrow"),
        P(None, "wide", "narrow"),
        P("wide"),
        P("wide", None),
        P("wide", None, None, "narrow"),
        P("wide", "narrow", None),
        P("wide", None),
        P("wide", None),
        P("wide", None),
    )
    out_specs = (
        P("wide", "narrow"),
        P("wide", "narrow"),
        P("wide"),
        P("wide", None),
        P(None, "wide", "narrow"),
        P(None, "wide", "narrow"),
        P(None, "wide", "narrow"),
        P("wide"),
        P("wide", None),
        P("wide", None, None, "narrow"),
        P("wide", "narrow", None),
    )
    return jax.shard_map(local, mesh=mesh, in_specs=in_specs, out_specs=out_specs, check_vma=False)
```

```python
import jax
import jax.numpy as jnp
from jax import lax
from jax.experimental import pallas as pl
from jax.experimental.pallas import tpu as pltpu
from jax.sharding import PartitionSpec as P

HS = 128
E = 4
TOPK = 2
TOK = 128
SLOTS = 80

EPSILON = 1e-05
NEGATIVE = -1000000000.0
PRECISE = lax.Precision.HIGHEST
F32 = jnp.float32
BF16 = jnp.bfloat16


def dot(left, right, contract, precision=None):
    return lax.dot_general(
        left, right, ((contract[0], contract[1]), ((), ())), precision=precision, preferred_element_type=F32
    )


def xor_shuffle(values, amount):
    count, bit = values.shape[0], 1
    while bit < count:
        split = values.reshape((count // (2 * bit), 2, bit) + values.shape[1:])
        flipped = split[:, ::-1].reshape(values.shape)
        values = jnp.where((amount & bit) != 0, flipped, values)
        bit *= 2
    return values


NN = (((1,), (0,)), ((), ()))
NT = (((1,), (1,)), ((), ()))
TN = (((0,), (0,)), ((), ()))


def mul(left, right, form):
    return lax.dot_general(left, right, form, preferred_element_type=F32)


def shape(dims, dtype):
    return jax.ShapeDtypeStruct(tuple(dims), dtype)


def run(name, body, outs, args, scratch=(), flops=1):
    vector = pl.BlockSpec(memory_space=pltpu.VMEM)
    return pl.pallas_call(
        body,
        out_shape=tuple(outs),
        in_specs=[pl.BlockSpec(memory_space=pltpu.SMEM)] + [vector] * (len(args) - 1),
        out_specs=tuple(vector for _ in outs),
        scratch_shapes=list(scratch),
        cost_estimate=pl.CostEstimate(flops=flops, transcendentals=0, bytes_accessed=1),
        name=name,
    )(*args)


def loop(count, step):
    def one(i, carry):
        step(i)
        return carry

    lax.fori_loop(0, count, one, 0)


def column(values, index):
    lane = lax.broadcasted_iota(jnp.int32, values.shape, 1)
    return jnp.sum(jnp.where(lane == index, values, 0.0), axis=-1, keepdims=True)


def place(store, parts, sub, first=0):
    for j, part in enumerate(parts):
        rows = part.shape[1]
        start = pl.multiple_of((sub ^ j) * rows, rows)
        for a in range(part.shape[0]):
            store[first + a, pl.ds(start, rows), :] = part[a]


def block(index):
    return pl.ds(pl.multiple_of(index * TOK, TOK), TOK)


def send_blocks(total, outs, order):
    for k in range(E):

        def one(a, k=k):
            outs[k][a] = total[a, block(order ^ k), :].astype(outs[k].dtype)

        loop(total.shape[0], one)


def stat_rows(square, logits):
    lane = lax.broadcasted_iota(jnp.int32, (TOK, TOK), 1)
    table = jnp.where(lane == E, square, 0.0)
    for e in range(E):
        table = jnp.where(lane == e, logits[:, e : e + 1], table)
    return jnp.transpose(table)[0:8]


def key_value_body(subs):
    def body(at, *refs):
        rows, gain, router, routes = refs[:E], refs[E], refs[E + 1], refs[E + 2]
        parts = refs[E + 3 : E + 3 + subs]
        gained, own_stats, *outs = refs[E + 3 + subs : E + 5 + subs + E]
        weights, total, stats = refs[E + 5 + subs + E :]
        place(weights, parts, at[1])
        for q in range(E):
            wide = rows[q][...].astype(F32)
            scaled = wide * gain[...]
            gained[q * TOK : (q + 1) * TOK, :] = scaled.astype(BF16)
            logits = lax.dot_general(
                scaled, router[...], NT, precision=lax.Precision.HIGHEST, preferred_element_type=F32
            )
            stats[q] = stat_rows(jnp.sum(wide * wide, axis=-1, keepdims=True), logits)
        for a in range(2):
            total[a] = mul(gained[...], weights[a], NN)
        own_stats[...] = stats[at[0]]
        for k in range(E):
            where = block(at[0] ^ k)
            for a in range(2):
                piece = total[a, where, :].astype(outs[k].dtype)
                if k == 0:
                    outs[k][a] = piece
                else:
                    outs[k][a * TOK : (a + 1) * TOK, :] = piece
            if k > 0:
                mine = stats[at[0] ^ k]
                high = mine.astype(BF16).astype(F32)
                pair = jnp.concatenate([high, mine - high], axis=0).astype(BF16)
                outs[k][2 * TOK :, :] = jnp.zeros((16, outs[k].shape[1]), BF16)
                outs[k][2 * TOK :, 0:TOK] = pair
                for first in range(0, subs, 4):
                    lines = [
                        routes[j][0:4].astype(F32) if j < subs else jnp.zeros((4, TOK), F32)
                        for j in range(first, first + 4)
                    ]
                    start = (1 + first // 4) * TOK
                    outs[k][2 * TOK :, start : start + TOK] = jnp.concatenate(lines, axis=0).astype(BF16)

    return body


def routed_body(subs, joined):
    count = 1 if joined else E

    def body(at, *refs):
        rows, hot, parts = refs[:count], refs[count], refs[count + 1 : count + 1 + subs]
        rest = refs[count + 1 + subs :]
        if joined:
            wide = rows[0]
        else:
            wide, rest = rest[0], rest[1:]
            for q in range(E):
                wide[q * TOK : (q + 1) * TOK, :] = rows[q][...]
        outs, weights, total = rest[:E], rest[E], rest[E + 1]
        if joined:
            place(weights, parts, at[1])
            for e in range(E):
                every = mul(wide[...], weights[e], NN)
                for i in range(TOPK):
                    mine = every * hot[:, i * E + e : i * E + e + 1]
                    total[i] = mine if e == 0 else total[i] + mine
            send_blocks(total, outs, at[0])
            return

        for j, part in enumerate(parts):
            size = part.shape[1]
            start = pl.multiple_of((at[1] ^ j) * size, size)

            def move(e, part=part, start=start, size=size):
                weights[e, pl.ds(start, size), :] = part[e]

            loop(E, move)

        def empty(n):
            total[n // E, block(n % E), :] = jnp.zeros((TOK, total.shape[2]), F32)

        loop(TOPK * E, empty)

        def project(e):
            every = mul(wide[...], weights[e], NN)
            for i in range(TOPK):
                total[i] = total[i] + every * column(hot[...], i * E + e)

        loop(E, project)
        send_blocks(total, outs, at[0])

    return body


def spread_pairs(at, rows, hot, out, first=0):
    for k in range(E):
        where = block(at[0] ^ k)
        mask = hot[where, :].astype(BF16)
        for e in range(E):
            out[e, where, :] = (
                rows[k][first] * mask[:, e : e + 1]
                + rows[k][first + 1] * mask[:, E + e : E + e + 1]
            )


def fold_out(total, keep_0, keep_2, send):
    keep_0[...] = total[0:TOK]
    keep_2[...] = total[2 * TOK : 3 * TOK]
    send[0] = total[TOK : 2 * TOK].astype(BF16)
    send[1] = total[3 * TOK : 4 * TOK].astype(BF16)


def output_body(subs):
    def body(at, *refs):
        rows, hot, parts = refs[:E], refs[E], refs[E + 1 : E + 1 + subs]
        mixed, keep_0, keep_2, send, weights = refs[E + 1 + subs :]
        place(weights, parts, at[1])
        spread_pairs(at, rows, hot, mixed)
        total = mul(mixed[0], weights[0], NT)
        for e in range(1, E):
            total = total + mul(mixed[e], weights[e], NT)
        fold_out(total, keep_0, keep_2, send)

    return body


def input_body(subs):
    def body(at, *refs):
        rows, dmixed = refs[:E], refs[E]
        kv_parts = refs[E + 1 : E + 1 + subs]
        query_parts = refs[E + 1 + subs : E + 1 + 2 * subs]
        streams = refs[E + 1 + 2 * subs : 2 * E + 1 + 2 * subs]
        dkv_all, gain_row, keep_0, keep_2, send, weights = refs[2 * E + 1 + 2 * subs :]
        place(weights, kv_parts, at[1])
        place(weights, query_parts, at[1], 2)
        for k in range(E):
            for a in range(2):
                dkv_all[a, block(at[0] ^ k), :] = rows[k][a]
        total = mul(dkv_all[0], weights[0], NT) + mul(dkv_all[1], weights[1], NT)
        for e in range(E):
            total = total + mul(dmixed[e], weights[2 + e], NT)
        gain = jnp.zeros((1, total.shape[1]), F32)
        for q in range(E):
            part = total[q * TOK : (q + 1) * TOK] * streams[q][...].astype(F32)
            gain = gain + jnp.sum(part, axis=0, keepdims=True)
        gain_row[...] = gain
        fold_out(total, keep_0, keep_2, send)

    return body


def split_rows(at, rows, other, parts, total, a):
    total[...] = mul(rows[...], other[a], TN)
    for j, part in enumerate(parts):
        count = part.shape[1]
        start = pl.multiple_of((at[1] ^ j) * count, count)
        part[a] = total[pl.ds(start, count), :].astype(part.dtype)


def weight_grad_body(at, rows, other, *refs):
    loop(other.shape[0], lambda a: split_rows(at, rows, other, refs[:-1], refs[-1], a))


def query_grad_body(at, rows, hot, *refs):
    dmixed = refs[E]
    spread_pairs(at, refs[:E], hot, dmixed, 2)
    for e in range(E):
        split_rows(at, rows, dmixed, refs[E + 1 : -1], refs[-1], e)


def attention_mask(at):
    row = lax.broadcasted_iota(jnp.int32, (TOK, TOK), 0)
    col = lax.broadcasted_iota(jnp.int32, (TOK, TOK), 1)
    row_doc, col_doc, end = jnp.zeros_like(row), jnp.zeros_like(row), 0
    for d in range(4):
        end = end + at[d]
        row_doc = row_doc + (row >= end).astype(jnp.int32)
        col_doc = col_doc + (col >= end).astype(jnp.int32)
    return (row_doc == col_doc) & (col <= row)


def attention_body(at, own_kv, *refs):
    got_kv, own_query, got_query = refs[: E - 1], refs[E - 1], refs[E : 2 * E - 1]
    own_stats, hot, rows, low, probs, context, gated = refs[2 * E - 1 :]
    stats = own_stats[...]
    for one in got_kv:
        pair = one[2 * TOK :, 0:TOK].astype(F32)
        stats = stats + pair[0:8] + pair[8:16]
    scale_row = lax.rsqrt(stats[E : E + 1] / (E * own_kv.shape[2]) + EPSILON)
    logits = stats[0:E] * scale_row
    picked = [
        jnp.sum(hot[i * E : (i + 1) * E, :] * logits, axis=0, keepdims=True) for i in range(TOPK)
    ]
    gap = picked[0] - picked[1]
    prob_rows = [1.0 / (1.0 + jnp.exp(-gap)), 1.0 / (1.0 + jnp.exp(gap))]
    rows[0:1, :] = scale_row
    for i in range(TOPK):
        rows[1 + i : 2 + i, :] = prob_rows[i] * hot[8 + i : 9 + i, :]
        rows[3 + i : 4 + i, :] = prob_rows[i]
    rows[5:9, :] = logits
    rows[9:16, :] = jnp.zeros((7, TOK), F32)
    cols = columns(rows[...])
    scale = cols[:, 0:1]
    for a in range(2):
        where = slice(a * TOK, (a + 1) * TOK)
        total, query = own_kv[a], own_query[a]
        for one in got_kv:
            total = total + one[where, :].astype(F32)
        for one in got_query:
            query = query + one[a].astype(F32)
        low[a] = (total * scale).astype(BF16)
        low[2 + a] = (query * scale).astype(BF16)
    allowed = attention_mask(at)
    for h in range(low.shape[2] // HS):
        head = slice(h * HS, (h + 1) * HS)
        for i in range(TOPK):
            scores = mul(low[2 + i, :, head], low[0, :, head], NT) * HS ** (-0.5)
            scores = jnp.where(allowed, scores, NEGATIVE)
            top = jnp.exp(scores - jnp.max(scores, axis=-1, keepdims=True))
            prob = top / jnp.sum(top, axis=-1, keepdims=True)
            probs[h, i * TOK : (i + 1) * TOK, :] = prob
            mixed = mul(prob.astype(BF16), low[1, :, head], NN).astype(BF16)
            context[i, :, head] = mixed
            gated[i, :, head] = (mixed.astype(F32) * cols[:, 1 + i : 2 + i]).astype(BF16)


def attention_back_body(at, own, *refs):
    got = refs[: E - 1]
    rows, low, probs, context, grads, sums, dcontext, inner = refs[E - 1 :]
    cols = columns(rows[...])
    scale = cols[:, 0:1]
    inner[...] = jnp.zeros((TOK, HS), F32)
    dprob = []
    for i in range(TOPK):
        raw = own[i]
        for one in got:
            raw = raw + one[i].astype(F32)
        dprob.append(jnp.sum(context[i].astype(F32) * raw, axis=-1, keepdims=True))
        dcontext[i] = (raw * cols[:, 1 + i : 2 + i]).astype(BF16)

    def attend(h):
        head = pl.ds(pl.multiple_of(h * HS, HS), HS)
        key, value = low[0, :, head], low[1, :, head]
        dkey = jnp.zeros((TOK, HS), F32)
        dvalue = jnp.zeros((TOK, HS), F32)
        for i in range(TOPK):
            query = low[2 + i, :, head]
            grad = dcontext[i, :, head]
            prob = probs[h, i * TOK : (i + 1) * TOK, :]
            dweight = mul(grad, value, NT)
            dscore = prob * (dweight - jnp.sum(prob * dweight, axis=-1, keepdims=True))
            dscore = dscore.astype(BF16)
            done = mul(dscore, key, NN) * HS ** (-0.5)
            dkey = dkey + mul(dscore, query, TN)
            dvalue = dvalue + mul(prob.astype(BF16), grad, TN)
            inner[...] = inner[...] + done * query.astype(F32)
            grads[2 + i, :, head] = (done * scale).astype(BF16)
        dkey = dkey * HS ** (-0.5)
        inner[...] = inner[...] + dkey * key.astype(F32) + dvalue * value.astype(F32)
        grads[0, :, head] = (dkey * scale).astype(BF16)
        grads[1, :, head] = (dvalue * scale).astype(BF16)

    loop(low.shape[2] // HS, attend)
    total = jnp.sum(inner[...], axis=-1, keepdims=True)
    lane = lax.broadcasted_iota(jnp.int32, (TOK, TOK), 1)
    table = jnp.where(lane == 0, dprob[0], jnp.where(lane == 1, dprob[1], jnp.where(lane == 2, total, 0.0)))
    sums[...] = jnp.transpose(table)[0:8]


def expert_body(at, gate_up, dact, full, act, gated, dpair, scaled, stats):
    def one(n):
        where = pl.ds(pl.multiple_of(n * SLOTS, SLOTS), SLOTS)
        pairs = full[where, full.shape[1] - 128 :].astype(F32)
        scale, gate = pairs[:, 0:1] + pairs[:, 1:2], pairs[:, 2:3] + pairs[:, 3:4]
        gate_pre, up_pre = gate_up[0, where, :] * scale, gate_up[1, where, :] * scale
        sig = 1.0 / (1.0 + jnp.exp(-gate_pre))
        silu = gate_pre * sig
        low = (silu * up_pre).astype(BF16)
        raw = dact[where, :]
        grad = raw * gate
        dgate = (grad * up_pre * sig * (1.0 + gate_pre * (1.0 - sig))).astype(BF16)
        dup = (grad * silu).astype(BF16)
        wide, dgate_wide, dup_wide = low.astype(F32), dgate.astype(F32), dup.astype(F32)
        act[where, :] = low
        gated[where, :] = (wide * gate).astype(BF16)
        dpair[0, where, :], dpair[1, where, :] = dgate, dup
        scaled[0, where, :] = (dgate_wide * scale).astype(BF16)
        scaled[1, where, :] = (dup_wide * scale).astype(BF16)
        dprob = jnp.sum(wide * raw, axis=-1, keepdims=True)
        inner = jnp.sum(dgate_wide * gate_pre + dup_wide * up_pre, axis=-1, keepdims=True)
        lane = lax.broadcasted_iota(jnp.int32, (SLOTS, 128), 1)
        stats[where, :] = jnp.where(lane == 0, dprob, jnp.where(lane == 1, inner, 0.0))

    loop(dact.shape[0] // SLOTS, one)


def rows_grad_body(at, left, right, out):
    part = 512

    def one(n):
        a, where = n % left.shape[0], pl.ds(pl.multiple_of((n // left.shape[0]) * part, part), part)
        out[a, :, where] = mul(left[a], right[:, where], TN)

    loop(left.shape[0] * (out.shape[2] // part), one)


def columns(rows):
    return jnp.transpose(jnp.concatenate([rows] * (TOK // rows.shape[0]), axis=0))


def pick_row(values, index):
    line = lax.broadcasted_iota(jnp.int32, values.shape, 0)
    return jnp.sum(jnp.where(line == index, values, 0.0), axis=0, keepdims=True)


def route_body(subs, capacity):
    count = E * subs * 8

    def body(at, *refs):
        tables = refs[:E]
        hot_cols, home, turned, mlp_cols, expert_rows, select = refs[E : E + 6]
        both, rank, kept, hot, mlp_hot = refs[E + 6 :]
        expert = lax.broadcasted_iota(jnp.int32, (E, TOK), 0).astype(F32)
        for k in range(E):
            for j in range(subs):
                if k == 0:
                    line = tables[0][j].astype(F32)
                else:
                    first = (1 + j // 4) * TOK
                    lines = tables[k][2 * TOK :, first : first + TOK].astype(F32)
                    line = lines[(j % 4) * 4 : (j % 4) * 4 + 4]
                ones = [(line[r : r + 1] == expert).astype(F32) for r in range(4)]
                start = (k * subs + j) * 8
                both[start : start + 4, :] = ones[0] + ones[1]
                both[start + 4 : start + 8, :] = ones[2] + ones[3]
                if j == 0:
                    hot[k, 0:4, :], hot[k, 4:8, :] = ones[0], ones[1]
                    mlp_hot[k, 0:4, :], mlp_hot[k, 4:8, :] = ones[2], ones[3]
        low = both[...].astype(BF16)
        row = lax.broadcasted_iota(jnp.int32, (TOK, TOK), 0)
        col = lax.broadcasted_iota(jnp.int32, (TOK, TOK), 1)
        rank[...] = mul(low, (row < col).astype(F32).astype(BF16), NN)
        row = lax.broadcasted_iota(jnp.int32, (count, count), 0)
        col = lax.broadcasted_iota(jnp.int32, (count, count), 1)
        own = at[2] * subs + at[1]
        ahead = (((col >> 3) ^ own) < ((row >> 3) ^ own)) & ((col & 7) == (row & 7))
        before = mul(ahead.astype(F32).astype(BF16), low, NN)
        place_of = jnp.sum(before, axis=-1, keepdims=True) + rank[...]
        kept[...] = both[...] * (place_of < capacity).astype(F32)

        for k in range(E):
            hot_cols[block(at[0] ^ k), :] = columns(hot[k])[:, 0:8]
        pad = jnp.zeros((6, TOK), F32)
        home[0:8, :] = hot[0]
        for i in range(TOPK):
            home[8 + i : 9 + i, :] = jnp.sum(
                hot[0, i * E : (i + 1) * E, :] * kept[0:E, :], axis=0, keepdims=True
            )
        home[10:16, :] = pad
        mine = mlp_hot[at[0]]
        start = pl.multiple_of(at[0] * (subs * 8), 8)
        kept_mine = kept[pl.ds(start, 8), :][4:8]
        rank_mine = rank[pl.ds(start, 8), :][4:8]
        turned[0:8, :] = mine
        for i in range(TOPK):
            turned[8 + i : 9 + i, :] = jnp.sum(
                mine[i * E : (i + 1) * E] * kept_mine, axis=0, keepdims=True
            )
        turned[10:16, :] = pad
        mlp_cols[...] = columns(mine)[:, 0:8]
        slot = lax.broadcasted_iota(jnp.int32, (SLOTS, TOK), 0).astype(F32)
        for k in range(E):
            e = at[2] ^ k
            for i in range(TOPK):
                expert_rows[2 * k + i : 2 * k + i + 1, :] = pick_row(mine[i * E : (i + 1) * E], e)
            taken = (slot == pick_row(rank_mine, e)) & (pick_row(kept_mine, e) > 0)
            select[k] = taken.astype(F32).astype(BF16)

    return body


def two_halves(values):
    lane = lax.broadcasted_iota(jnp.int32, (values[0].shape[0], 128), 1)
    table = jnp.zeros((values[0].shape[0], 128), F32)
    for i, one in enumerate(values):
        high = one.astype(BF16).astype(F32)
        table = jnp.where(lane == 2 * i, high, table)
        table = jnp.where(lane == 2 * i + 1, one - high, table)
    return table.astype(BF16)


def pick_body(at, stream, keep, got, other, gain, router, mlp_cols, select, *refs):
    hidden, stats, outs = refs[0], refs[1], refs[2:]
    size = hidden.shape[1]
    total = stream[...].astype(F32) + (keep[...] + got[0].astype(F32) + other[...].astype(F32))
    hidden[...] = total
    gained = total * gain[...]
    square = jnp.sum(total * total, axis=-1, keepdims=True)
    logits = lax.dot_general(
        gained, router[...], NT, precision=lax.Precision.HIGHEST, preferred_element_type=F32
    )
    lane = lax.broadcasted_iota(jnp.int32, logits.shape, 1)
    chosen = jnp.zeros_like(square)
    for e in range(E):
        one = mlp_cols[:, e : e + 1] + mlp_cols[:, E + e : E + e + 1]
        chosen = chosen + one * logits[:, e : e + 1]
    low = gained.astype(BF16)
    for k in range(E):
        own = jnp.sum(jnp.where(lane == (at[2] ^ k), logits, 0.0), axis=-1, keepdims=True)
        extra = two_halves([square, 2.0 * own - chosen])
        outs[k][:, :size] = mul(select[k], low, NN).astype(BF16)
        outs[k][:, size:] = mul(select[k], extra, NN).astype(BF16)
    stats[...] = stat_rows(square, logits)


def join_rows_body(at, *refs):
    pieces, out = refs[:E], refs[E]
    size = pieces[0].shape[1] - 128
    join_pieces(at, pieces, out, size)
    total = pieces[0][:, size:].astype(F32)
    for k in range(1, E):
        total = total + pieces[k][:, size:].astype(F32)
    square, gap = total[:, 0:1] + total[:, 1:2], total[:, 2:3] + total[:, 3:4]
    scale = lax.rsqrt(square / (E * size) + EPSILON)
    small = jnp.exp(-jnp.abs(gap * scale))
    gate = jnp.where(gap < 0.0, small, 1.0) / (1.0 + small)
    out[:, E * size :] = two_halves([scale, gate])


def piece_of(plane, k, size):
    return pl.ds(pl.multiple_of((plane ^ k) * size, size), size)


def join_pieces(at, pieces, out, size):
    for k in range(E):
        out[:, piece_of(at[2], k, size)] = pieces[k][:, :size]


def join_body(at, *refs):
    join_pieces(at, refs[:E], refs[E], refs[0].shape[1])


def split_body(extra):
    def body(at, own, got, *refs):
        outs, store = refs[:E], refs[E]
        store[...] = (own[...] + got[...].astype(F32)).astype(BF16)
        size = outs[0].shape[1] - extra
        for k in range(E):
            outs[k][:, :size] = store[:, piece_of(at[2], k, size)]
            if extra:
                outs[k][:, size:] = store[:, E * size :]

    return body


def local(
    stream,
    out_grad,
    attn_gain,
    attn_router,
    key_value,
    query_proj,
    output_proj,
    mlp_gain,
    mlp_router,
    expert_in,
    expert_down,
    attn_routes,
    mlp_routes,
    doc_lengths,
):
    wide_count = lax.axis_size("wide")
    narrow_count = lax.axis_size("narrow")
    subs = wide_count // E
    wide = lax.axis_index("wide")
    narrow = lax.axis_index("narrow")
    plane, sub = wide // subs, wide % subs
    capacity = 9 * TOK * wide_count * TOPK // (8 * E)
    slice_width = stream.shape[1]
    shard_rows = attn_gain.shape[0]
    width = slice_width * narrow_count
    local_width = key_value.shape[2]
    head_count = local_width // HS
    hidden_units = expert_down.shape[1]
    score_scale = HS ** (-0.5)

    def after(values, *others):
        return lax.optimization_barrier((values, others))[0]

    def by_plane(values, k):
        return lax.ppermute(values, "wide", [(i, i ^ (k * subs)) for i in range(wide_count)])

    def by_sub(values, k):
        return lax.ppermute(values, "wide", [(i, i ^ k) for i in range(wide_count)])

    def by_narrow(values, k):
        return lax.ppermute(values, "narrow", [(i, i ^ k) for i in range(narrow_count)])

    def swap(values):
        pairs = []
        for w in range(wide_count):
            for n in range(narrow_count):
                z, y = w // subs, w % subs
                pairs.append((w * narrow_count + n, (n * subs + y) * narrow_count + z))
        return lax.ppermute(values, ("wide", "narrow"), pairs)

    def by_side(values, side):
        pairs = []
        for w in range(wide_count):
            for n in range(narrow_count):
                other = (w ^ 1, n) if (n & 1) == side else (w, n ^ 2)
                pairs.append((w * narrow_count + n, other[0] * narrow_count + other[1]))
        return lax.ppermute(values, ("wide", "narrow"), pairs)

    def gather_planes(values):
        return [values] + [by_plane(values, k) for k in range(1, E)]

    def exchange_planes(parts):
        return [parts[0]] + [by_plane(parts[k], k) for k in range(1, E)]

    def gather_subs(values, *others):
        parts, bit = [values], 1
        while bit < subs:
            parts = parts + [by_sub(after(one, *others) if others else one, bit) for one in parts]
            bit *= 2
        return parts

    def reduce_subs(parts):
        bit = len(parts) // 2
        while bit >= 1:
            parts = [parts[j] + by_sub(parts[j + bit].astype(BF16), bit).astype(F32) for j in range(bit)]
            bit //= 2
        return parts[0]

    def gather_narrow(values):
        other = by_narrow(values, 2)
        return [values, by_narrow(values, 1), other, by_narrow(other, 1)]

    def reduce_narrow(keep_0, keep_2, send):
        got = by_narrow(send, 1)
        other = by_narrow((keep_2 + got[1].astype(F32)).astype(BF16), 2)
        return keep_0, got, other

    def finish_subs(keep, send):
        bit = len(keep)
        got = [by_sub(send[j], bit) for j in range(bit)]
        return reduce_subs([keep[j] + got[j].astype(F32) for j in range(bit)]), got

    def sum_narrow(values):
        values = values + by_narrow(values, 2)
        return values + by_narrow(values, 1)

    def sum_planes(values):
        values = values + by_plane(values, 1)
        return values + by_plane(values, 2)

    def sum_subs(values):
        bit = 1
        while bit < subs:
            values = values + by_sub(values, bit)
            bit *= 2
        return values

    turned_stream = swap(stream)

    size = max(shard_rows, TOK)

    def pad(rows, count):
        return jnp.pad(rows, ((0, count - rows.shape[0]), (0, size - rows.shape[1])))

    own_routes = jnp.concatenate([attn_routes.T, mlp_routes.T], axis=0).astype(BF16)
    own_rows = jnp.concatenate(
        [attn_gain[None, :], attn_router.T, mlp_gain[None, :], mlp_router.T], axis=0
    )
    parts = gather_subs(jnp.concatenate([pad(own_routes, 8), pad(own_rows, 16)], axis=0))
    parts = jnp.stack(parts)
    near = xor_shuffle(parts[:, 8:, :shard_rows], sub).swapaxes(0, 1).reshape(16, slice_width)
    gain_one_plane = near[0].astype(F32)
    router_one_plane = near[1:5].astype(F32)
    gain_two_plane = near[5].astype(F32)
    router_two_plane = near[6:10].astype(F32)

    route_parts = parts[:, :8, :TOK]
    at = jnp.stack([narrow ^ plane, sub, plane, narrow]).astype(jnp.int32)
    kv_parts = gather_subs(key_value)
    query_parts = gather_subs(query_proj, kv_parts[-1])
    out_parts = gather_subs(output_proj, query_parts[-1])
    home_stream = stream.astype(F32)

    rows_all = E * TOK
    sent = shape((2, TOK, local_width), BF16)
    kept_own = shape((2, TOK, local_width), F32)
    all_streams = gather_narrow(turned_stream)
    gained, own_stats, *kv_blocks = run(
        "key_value",
        key_value_body(subs),
        [shape((rows_all, slice_width), BF16), shape((8, TOK), F32), kept_own]
        + [shape((2 * TOK + 16, local_width), BF16)] * (E - 1),
        [
            at,
            *all_streams,
            gain_one_plane[None],
            jnp.pad(router_one_plane, ((0, 4), (0, 0))),
            route_parts,
            *kv_parts,
        ],
        [
            pltpu.VMEM((2, slice_width, local_width), BF16),
            pltpu.VMEM((2, rows_all, local_width), F32),
            pltpu.VMEM((E, 8, TOK), F32),
        ],
    )
    turned_grad = swap(after(out_grad, own_stats))
    kv_blocks = exchange_planes(kv_blocks)
    line_count = wide_count * 8
    hot_cols, home_hot, turned_hot, mlp_cols, expert_hot, select = run(
        "route",
        route_body(subs, capacity),
        [
            shape((E * TOK, 8), F32),
            shape((16, TOK), F32),
            shape((16, TOK), F32),
            shape((TOK, 8), F32),
            shape((8, TOK), F32),
            shape((E, SLOTS, TOK), BF16),
        ],
        [at, route_parts, *kv_blocks[1:]],
        [pltpu.VMEM((line_count, TOK), F32)] * 3 + [pltpu.VMEM((E, 8, TOK), F32)] * 2,
    )
    hot_one, keep_one = home_hot[0:8].reshape(TOPK, E, TOK), home_hot[8:10]
    hot_two, keep_two = turned_hot[0:8].reshape(TOPK, E, TOK), turned_hot[8:10]
    hot_two_k = expert_hot.reshape(E, TOPK, TOK)

    routed_scratch = [
        pltpu.VMEM((E, slice_width, local_width), BF16),
        pltpu.VMEM((TOPK, rows_all, local_width), F32),
    ]
    query_blocks = run(
        "query",
        routed_body(subs, True),
        [kept_own] + [sent] * (E - 1),
        [at, gained, hot_cols, *query_parts],
        routed_scratch,
    )
    query_blocks = exchange_planes(query_blocks)

    def gates(logits, hots):
        picked = jnp.sum(hots * logits[None], axis=1)
        gap = picked[0] - picked[1]
        return jnp.stack([jax.nn.sigmoid(gap), jax.nn.sigmoid(-gap)])

    def share(full):
        size = full.shape[-1]
        full = jnp.concatenate([full, by_side(full, 0)], axis=0)
        got = by_side(full, 1)
        full = jnp.concatenate([full, got], axis=0)
        bit = 2
        while bit < subs:
            full = jnp.concatenate([full, by_sub(full, bit)], axis=0)
            bit *= 2
        return jnp.concatenate([full, by_narrow(full, 1)], axis=0).reshape(-1, size), got

    picked = jnp.einsum("kst,td->ksd", select, turned_grad, preferred_element_type=F32).astype(BF16)
    token_rows, low, probs, context, gated = run(
        "attention",
        attention_body,
        [
            shape((16, TOK), F32),
            shape((4, TOK, local_width), BF16),
            shape((head_count, TOPK * TOK, TOK), F32),
            sent,
            sent,
        ],
        [doc_lengths[0], *kv_blocks, *query_blocks, own_stats, home_hot],
    )
    scale_one, prob_one, logits_one = token_rows[0], token_rows[3:5], token_rows[5:9]

    (full,) = run(
        "join",
        join_body,
        [shape((SLOTS, width), BF16)],
        [at, *after(exchange_planes([picked[k] for k in range(E)]), gated)],
    )
    grad_rows, grad_got = share(full)
    folded = [shape((TOK, slice_width), F32), shape((TOK, slice_width), F32), shape((2, TOK, slice_width), BF16)]
    mixed, *attention = run(
        "output",
        output_body(subs),
        [shape((E, rows_all, local_width), BF16)] + folded,
        [at, *gather_planes(gated), hot_cols, *out_parts],
        [pltpu.VMEM((E, slice_width, local_width), BF16)],
    )
    weight_in = expert_in[0]
    weight_down = expert_down[0]
    dact_raw = dot(grad_rows, weight_down, ((1,), (1,)))

    hidden, stats_two, *picked = run(
        "pick",
        pick_body,
        [shape((TOK, slice_width), F32), shape((8, TOK), F32)]
        + [shape((SLOTS, slice_width + 128), BF16)] * E,
        [
            at,
            turned_stream,
            *after(reduce_narrow(*attention), grad_got),
            gain_two_plane[None],
            jnp.pad(router_two_plane, ((0, 4), (0, 0))),
            mlp_cols,
            select,
        ],
    )
    (full,) = run(
        "join_rows",
        join_rows_body,
        [shape((SLOTS, width + 128), BF16)],
        [at, *exchange_planes(picked)],
    )
    stats_two = sum_planes(stats_two)
    full, _ = share(full)
    full = after(full, stats_two)
    expert_rows = full[:, :width]
    row_gate = jnp.sum(full[:, width + 2 : width + 4].astype(F32), axis=-1, keepdims=True)
    scale_two = lax.rsqrt(stats_two[E] / width + EPSILON)
    logits_two = stats_two[:E] * scale_two
    prob_two = gates(logits_two, hot_two)

    gate_up = jnp.einsum("rd,dkf->krf", expert_rows, weight_in, preferred_element_type=F32)
    row_count = expert_rows.shape[0]
    activation, gated_act, dpair, dboth, row_stats = run(
        "expert",
        expert_body,
        [shape((row_count, hidden_units), BF16)] * 2
        + [shape((2, row_count, hidden_units), BF16)] * 2
        + [shape((row_count, 128), F32)],
        [at, gate_up, dact_raw, full],
    )
    drows = jnp.einsum("krf,dkf->rd", dpair, weight_in, preferred_element_type=F32)

    def give_back(rows):
        half = rows.shape[0] // 2
        rows = rows[:half] + by_narrow(rows[half:].astype(BF16), 1).astype(F32)
        bit = subs // 2
        while bit > 1:
            half = rows.shape[0] // 2
            rows = rows[:half] + by_sub(rows[half:].astype(BF16), bit).astype(F32)
            bit //= 2
        half = rows.shape[0] // 2
        rows = rows[:half] + by_side(rows[half:].astype(BF16), 1).astype(F32)
        return rows[:SLOTS], by_side(rows[SLOTS:].astype(BF16), 0)

    def from_planes(own, got, extra, last=None):
        if last is not None:
            own = after(own, last)
        pieces = run(
            "split",
            split_body(extra),
            [shape((SLOTS, slice_width + extra), BF16)] * E,
            [at, own, got],
            [pltpu.VMEM(own.shape, BF16)],
        )
        return jnp.stack(exchange_planes(pieces))

    returned = give_back(jnp.concatenate([drows, row_stats], axis=1))
    returned = from_planes(*returned, row_stats.shape[1])
    combined = jnp.einsum("kst,ksd->ktd", select, returned, preferred_element_type=F32)
    per_expert = combined[:, :, slice_width : slice_width + 2]
    dprob_two = keep_two * jnp.sum(hot_two_k * per_expert[:, None, :, 0], axis=0)
    inner_two = jnp.sum(per_expert[:, :, 1], axis=0)
    dnormed_two = jnp.sum(combined[:, :, :slice_width], axis=0)

    def gate_back(prob, dprob, hots):
        dselect = prob * (dprob - jnp.sum(prob * dprob, axis=0, keepdims=True))
        return jnp.sum(hots * dselect[:, None, :], axis=0)

    dlogit_two = gate_back(prob_two, dprob_two, hot_two)
    dnormed_two = dnormed_two + dot(dlogit_two, router_two_plane, ((0,), (0,)), PRECISE)
    inner_two = inner_two + jnp.sum(dlogit_two * logits_two, axis=0)
    dhidden = (
        turned_grad.astype(F32)
        + scale_two[:, None] * (dnormed_two * gain_two_plane)
        - hidden * (scale_two * scale_two * inner_two / width)[:, None]
    )
    scaled_hidden = hidden * scale_two[:, None]
    mlp_terms = jnp.concatenate(
        [
            jnp.sum(dnormed_two * scaled_hidden, axis=0)[None],
            dot(dlogit_two, scaled_hidden * gain_two_plane, ((1,), (0,)), PRECISE),
        ],
        axis=0,
    )

    wide_grad, *dcontext_blocks = run(
        "dcontext",
        routed_body(subs, False),
        [shape((rows_all, slice_width), BF16), kept_own] + [sent] * (E - 1),
        [at, *gather_narrow(dhidden.astype(BF16)), hot_cols, *out_parts],
        routed_scratch,
    )
    dcontext_blocks = exchange_planes(dcontext_blocks)

    def weight_parts(count):
        return [
            shape((count, shard_rows, local_width), F32 if j < subs // 2 else BF16)
            for j in range(subs)
        ]

    def weight_sum(parts):
        return finish_subs(parts[: subs // 2], parts[subs // 2 :])

    weight_scratch = [pltpu.VMEM((slice_width, local_width), F32)]
    output_parts = run(
        "output_grad", weight_grad_body, weight_parts(E), [at, wide_grad, mixed], weight_scratch
    )
    expert_out = dot(activation, weight_down, ((1,), (0,))) * row_gate
    mixture = give_back(expert_out)
    output_grad, output_got = weight_sum(output_parts)
    (down_grad,) = run(
        "down_grad",
        rows_grad_body,
        [shape((1, hidden_units, width), F32)],
        [at, after(gated_act, dcontext_blocks[0])[None], grad_rows],
        flops=4 * row_count * hidden_units * width,
    )
    grads_low, home_sums = run(
        "attention_back",
        attention_back_body,
        [shape((4, TOK, local_width), BF16), shape((8, TOK), F32)],
        [
            at,
            *after(dcontext_blocks, output_parts[-1], down_grad),
            token_rows,
            low,
            probs,
            context,
        ],
        [pltpu.VMEM((TOPK, TOK, local_width), BF16), pltpu.VMEM((TOK, HS), F32)],
    )
    grad_planes = gather_planes(grads_low)
    (up_grad,) = run(
        "up_grad",
        rows_grad_body,
        [shape((2, hidden_units, width), F32)],
        [at, after(dboth, grad_planes[E - 1]), expert_rows],
        flops=4 * row_count * hidden_units * width,
    )
    dmixed, *query_grad_parts = run(
        "query_grad",
        query_grad_body,
        [shape((E, rows_all, local_width), BF16)] + weight_parts(E),
        [at, gained, hot_cols, *after(grad_planes, output_got, up_grad)],
        weight_scratch,
    )
    query_grad, query_got = weight_sum(query_grad_parts)
    dkv_all, gain_row, *dnormed_one = run(
        "input",
        input_body(subs),
        [shape((2, rows_all, local_width), BF16), shape((1, slice_width), F32)] + folded,
        [
            at,
            *after(grad_planes, query_grad_parts[-1]),
            dmixed,
            *kv_parts,
            *query_parts,
            *all_streams,
        ],
        [pltpu.VMEM((2 + E, slice_width, local_width), BF16)],
    )
    home_rows = swap(after(near, own_stats))
    gain_one_home = home_rows[0].astype(F32)
    router_one_home = home_rows[1:5].astype(F32)
    gained_home = home_stream * gain_one_home
    home_sums = sum_narrow(after(home_sums, gain_row))
    dprob_one = keep_one * home_sums[:2]
    dlogit_one = gate_back(prob_one, dprob_one, hot_one)
    inner_one = home_sums[2] + jnp.sum(dlogit_one * logits_one, axis=0)
    dlogit_scaled = dlogit_one * scale_one
    router_term = swap(dot(dlogit_scaled, gained_home, ((1,), (0,)), PRECISE))
    kv_grad_parts = run(
        "key_value_grad", weight_grad_body, weight_parts(2), [at, gained, dkv_all], weight_scratch
    )
    kv_grad, kv_got = weight_sum(after(kv_grad_parts, query_got))
    keep, got, other = after(reduce_narrow(*dnormed_one), kv_grad_parts[-1], query_got)
    dnormed_one = keep + got[0].astype(F32) + other.astype(F32)
    turned_out = dhidden + dnormed_one * gain_one_plane
    home_out = swap(turned_out.astype(BF16)).astype(F32)
    stream_grad = (
        home_out
        + gain_one_home * dot(dlogit_scaled, router_one_home, ((0,), (0,)), PRECISE)
        - home_stream * (scale_one * scale_one * inner_one / width)[:, None]
    )

    small = jnp.concatenate([mlp_terms, gain_row, router_term], axis=0)
    small = sum_subs(after(sum_narrow(small), kv_got))
    mine = lax.dynamic_slice_in_dim(small, sub * shard_rows, shard_rows, 1)
    router_one_grad = mine[6:10]
    gain_one_grad = mine[5] + jnp.sum(
        router_one_grad * attn_router.T.astype(F32), axis=0
    ) / attn_gain.astype(F32)

    mixture = from_planes(*mixture, 0, gain_row)
    mixture = jnp.einsum("kst,ksd->td", select, after(mixture, turned_out), preferred_element_type=F32)
    layer_out = swap((hidden + mixture).astype(BF16)).astype(F32)
    return (
        layer_out,
        stream_grad,
        gain_one_grad,
        router_one_grad.T,
        kv_grad,
        query_grad,
        output_grad,
        mine[0],
        mine[1:5].T,
        up_grad.transpose(2, 0, 1)[None],
        down_grad,
    )


def solution(mesh):
    in_specs = (
        P("wide", "narrow"),
        P("wide", "narrow"),
        P("wide"),
        P("wide", None),
        P(None, "wide", "narrow"),
        P(None, "wide", "narrow"),
        P(None, "wide", "narrow"),
        P("wide"),
        P("wide", None),
        P("wide", None, None, "narrow"),
        P("wide", "narrow", None),
        P("wide", None),
        P("wide", None),
        P("wide", None),
    )
    out_specs = (
        P("wide", "narrow"),
        P("wide", "narrow"),
        P("wide"),
        P("wide", None),
        P(None, "wide", "narrow"),
        P(None, "wide", "narrow"),
        P(None, "wide", "narrow"),
        P("wide"),
        P("wide", None),
        P("wide", None, None, "narrow"),
        P("wide", "narrow", None),
    )
    return jax.shard_map(local, mesh=mesh, in_specs=in_specs, out_specs=out_specs, check_vma=False)
```

```python
import jax
import jax.numpy as jnp
from jax import lax
from jax.experimental import pallas as pl
from jax.experimental.pallas import tpu as pltpu
from jax.sharding import PartitionSpec as P

HS = 128
E = 4
TOPK = 2
TOK = 128
SLOTS = 80

EPSILON = 1e-05
NEGATIVE = -1000000000.0
PRECISE = lax.Precision.HIGHEST
F32 = jnp.float32
BF16 = jnp.bfloat16


def dot(left, right, contract, precision=None):
    return lax.dot_general(
        left, right, ((contract[0], contract[1]), ((), ())), precision=precision, preferred_element_type=F32
    )


def xor_shuffle(values, amount):
    count, bit = values.shape[0], 1
    while bit < count:
        split = values.reshape((count // (2 * bit), 2, bit) + values.shape[1:])
        flipped = split[:, ::-1].reshape(values.shape)
        values = jnp.where((amount & bit) != 0, flipped, values)
        bit *= 2
    return values


NN = (((1,), (0,)), ((), ()))
NT = (((1,), (1,)), ((), ()))
TN = (((0,), (0,)), ((), ()))


def mul(left, right, form):
    return lax.dot_general(left, right, form, preferred_element_type=F32)


def shape(dims, dtype):
    return jax.ShapeDtypeStruct(tuple(dims), dtype)


def run(name, body, outs, args, scratch=(), flops=1):
    vector = pl.BlockSpec(memory_space=pltpu.VMEM)
    return pl.pallas_call(
        body,
        out_shape=tuple(outs),
        in_specs=[pl.BlockSpec(memory_space=pltpu.SMEM)] + [vector] * (len(args) - 1),
        out_specs=tuple(vector for _ in outs),
        scratch_shapes=list(scratch),
        cost_estimate=pl.CostEstimate(flops=flops, transcendentals=0, bytes_accessed=1),
        name=name,
    )(*args)


def place(store, parts, sub, first=0):
    for j, part in enumerate(parts):
        rows = part.shape[1]
        start = pl.multiple_of((sub ^ j) * rows, rows)
        for a in range(part.shape[0]):
            store[first + a, pl.ds(start, rows), :] = part[a]


def block(index):
    return pl.ds(pl.multiple_of(index * TOK, TOK), TOK)


def send_blocks(total, outs, order):
    for k in range(E):
        for a in range(total.shape[0]):
            outs[k][a] = total[a, block(order ^ k), :].astype(outs[k].dtype)


def stat_rows(square, logits):
    lane = lax.broadcasted_iota(jnp.int32, (TOK, TOK), 1)
    table = jnp.where(lane == E, square, 0.0)
    for e in range(E):
        table = jnp.where(lane == e, logits[:, e : e + 1], table)
    return jnp.transpose(table)[0:8]


def key_value_body(subs):
    def body(at, *refs):
        rows, gain, router, routes = refs[:E], refs[E], refs[E + 1], refs[E + 2]
        parts = refs[E + 3 : E + 3 + subs]
        gained, own_stats, *outs = refs[E + 3 + subs : E + 5 + subs + E]
        weights, total, stats = refs[E + 5 + subs + E :]
        place(weights, parts, at[1])
        for q in range(E):
            wide = rows[q][...].astype(F32)
            scaled = wide * gain[...]
            gained[q * TOK : (q + 1) * TOK, :] = scaled.astype(BF16)
            logits = lax.dot_general(
                scaled, router[...], NT, precision=lax.Precision.HIGHEST, preferred_element_type=F32
            )
            stats[q] = stat_rows(jnp.sum(wide * wide, axis=-1, keepdims=True), logits)
        for a in range(2):
            total[a] = mul(gained[...], weights[a], NN)
        own_stats[...] = stats[at[0]]
        for k in range(E):
            where = block(at[0] ^ k)
            for a in range(2):
                piece = total[a, where, :].astype(outs[k].dtype)
                if k == 0:
                    outs[k][a] = piece
                else:
                    outs[k][a * TOK : (a + 1) * TOK, :] = piece
            if k > 0:
                mine = stats[at[0] ^ k]
                high = mine.astype(BF16).astype(F32)
                pair = jnp.concatenate([high, mine - high], axis=0).astype(BF16)
                outs[k][2 * TOK :, :] = jnp.zeros((16, outs[k].shape[1]), BF16)
                outs[k][2 * TOK :, 0:TOK] = pair
                for first in range(0, subs, 4):
                    lines = [
                        routes[j][0:4].astype(F32) if j < subs else jnp.zeros((4, TOK), F32)
                        for j in range(first, first + 4)
                    ]
                    start = (1 + first // 4) * TOK
                    outs[k][2 * TOK :, start : start + TOK] = jnp.concatenate(lines, axis=0).astype(BF16)

    return body


def routed_body(subs, joined):
    count = 1 if joined else E

    def body(at, *refs):
        rows, hot, parts = refs[:count], refs[count], refs[count + 1 : count + 1 + subs]
        rest = refs[count + 1 + subs :]
        if joined:
            wide = rows[0]
        else:
            wide, rest = rest[0], rest[1:]
            for q in range(E):
                wide[q * TOK : (q + 1) * TOK, :] = rows[q][...]
        outs, weights, total = rest[:E], rest[E], rest[E + 1]
        place(weights, parts, at[1])
        for e in range(E):
            every = mul(wide[...], weights[e], NN)
            for i in range(TOPK):
                mine = every * hot[:, i * E + e : i * E + e + 1]
                total[i] = mine if e == 0 else total[i] + mine
        send_blocks(total, outs, at[0])

    return body


def spread_pairs(at, rows, hot, out, first=0):
    for k in range(E):
        where = block(at[0] ^ k)
        mask = hot[where, :].astype(BF16)
        for e in range(E):
            out[e, where, :] = (
                rows[k][first] * mask[:, e : e + 1]
                + rows[k][first + 1] * mask[:, E + e : E + e + 1]
            )


def fold_out(total, keep_0, keep_2, send):
    keep_0[...] = total[0:TOK]
    keep_2[...] = total[2 * TOK : 3 * TOK]
    send[0] = total[TOK : 2 * TOK].astype(BF16)
    send[1] = total[3 * TOK : 4 * TOK].astype(BF16)


def output_body(subs):
    def body(at, *refs):
        rows, hot, parts = refs[:E], refs[E], refs[E + 1 : E + 1 + subs]
        mixed, keep_0, keep_2, send, weights = refs[E + 1 + subs :]
        place(weights, parts, at[1])
        spread_pairs(at, rows, hot, mixed)
        total = mul(mixed[0], weights[0], NT)
        for e in range(1, E):
            total = total + mul(mixed[e], weights[e], NT)
        fold_out(total, keep_0, keep_2, send)

    return body


def input_body(subs):
    def body(at, *refs):
        rows, dmixed = refs[:E], refs[E]
        kv_parts = refs[E + 1 : E + 1 + subs]
        query_parts = refs[E + 1 + subs : E + 1 + 2 * subs]
        streams = refs[E + 1 + 2 * subs : 2 * E + 1 + 2 * subs]
        dkv_all, gain_row, keep_0, keep_2, send, weights = refs[2 * E + 1 + 2 * subs :]
        place(weights, kv_parts, at[1])
        place(weights, query_parts, at[1], 2)
        for k in range(E):
            for a in range(2):
                dkv_all[a, block(at[0] ^ k), :] = rows[k][a]
        total = mul(dkv_all[0], weights[0], NT) + mul(dkv_all[1], weights[1], NT)
        for e in range(E):
            total = total + mul(dmixed[e], weights[2 + e], NT)
        gain = jnp.zeros((1, total.shape[1]), F32)
        for q in range(E):
            part = total[q * TOK : (q + 1) * TOK] * streams[q][...].astype(F32)
            gain = gain + jnp.sum(part, axis=0, keepdims=True)
        gain_row[...] = gain
        fold_out(total, keep_0, keep_2, send)

    return body


def split_rows(at, rows, other, parts, total):
    for a in range(other.shape[0]):
        total[...] = mul(rows[...], other[a], TN)
        for j, part in enumerate(parts):
            count = part.shape[1]
            start = pl.multiple_of((at[1] ^ j) * count, count)
            part[a] = total[pl.ds(start, count), :].astype(part.dtype)


def weight_grad_body(at, rows, other, *refs):
    split_rows(at, rows, other, refs[:-1], refs[-1])


def query_grad_body(at, rows, hot, *refs):
    dmixed = refs[E]
    spread_pairs(at, refs[:E], hot, dmixed, 2)
    split_rows(at, rows, dmixed, refs[E + 1 : -1], refs[-1])


def attention_mask(at):
    row = lax.broadcasted_iota(jnp.int32, (TOK, TOK), 0)
    col = lax.broadcasted_iota(jnp.int32, (TOK, TOK), 1)
    row_doc, col_doc, end = jnp.zeros_like(row), jnp.zeros_like(row), 0
    for d in range(4):
        end = end + at[d]
        row_doc = row_doc + (row >= end).astype(jnp.int32)
        col_doc = col_doc + (col >= end).astype(jnp.int32)
    return (row_doc == col_doc) & (col <= row)


def attention_body(at, own_kv, *refs):
    got_kv, own_query, got_query = refs[: E - 1], refs[E - 1], refs[E : 2 * E - 1]
    own_stats, hot, rows, low, probs, context, gated = refs[2 * E - 1 :]
    stats = own_stats[...]
    for one in got_kv:
        pair = one[2 * TOK :, 0:TOK].astype(F32)
        stats = stats + pair[0:8] + pair[8:16]
    scale_row = lax.rsqrt(stats[E : E + 1] / (E * own_kv.shape[2]) + EPSILON)
    logits = stats[0:E] * scale_row
    picked = [
        jnp.sum(hot[i * E : (i + 1) * E, :] * logits, axis=0, keepdims=True) for i in range(TOPK)
    ]
    gap = picked[0] - picked[1]
    prob_rows = [1.0 / (1.0 + jnp.exp(-gap)), 1.0 / (1.0 + jnp.exp(gap))]
    rows[0:1, :] = scale_row
    for i in range(TOPK):
        rows[1 + i : 2 + i, :] = prob_rows[i] * hot[8 + i : 9 + i, :]
        rows[3 + i : 4 + i, :] = prob_rows[i]
    rows[5:9, :] = logits
    rows[9:16, :] = jnp.zeros((7, TOK), F32)
    cols = columns(rows[...])
    scale = cols[:, 0:1]
    for a in range(2):
        where = slice(a * TOK, (a + 1) * TOK)
        total, query = own_kv[a], own_query[a]
        for one in got_kv:
            total = total + one[where, :].astype(F32)
        for one in got_query:
            query = query + one[a].astype(F32)
        low[a] = (total * scale).astype(BF16)
        low[2 + a] = (query * scale).astype(BF16)
    allowed = attention_mask(at)
    for h in range(low.shape[2] // HS):
        head = slice(h * HS, (h + 1) * HS)
        for i in range(TOPK):
            scores = mul(low[2 + i, :, head], low[0, :, head], NT) * HS ** (-0.5)
            scores = jnp.where(allowed, scores, NEGATIVE)
            top = jnp.exp(scores - jnp.max(scores, axis=-1, keepdims=True))
            prob = top / jnp.sum(top, axis=-1, keepdims=True)
            probs[h, i * TOK : (i + 1) * TOK, :] = prob
            mixed = mul(prob.astype(BF16), low[1, :, head], NN).astype(BF16)
            context[i, :, head] = mixed
            gated[i, :, head] = (mixed.astype(F32) * cols[:, 1 + i : 2 + i]).astype(BF16)


def attention_back_body(at, own, *refs):
    got = refs[: E - 1]
    rows, low, probs, context, grads, sums = refs[E - 1 :]
    cols = columns(rows[...])
    scale = cols[:, 0:1]
    inner = jnp.zeros((TOK, 1), F32)
    dprob = []
    dcontext = []
    for i in range(TOPK):
        raw = own[i]
        for one in got:
            raw = raw + one[i].astype(F32)
        dprob.append(jnp.sum(context[i].astype(F32) * raw, axis=-1, keepdims=True))
        dcontext.append((raw * cols[:, 1 + i : 2 + i]).astype(BF16))
    for h in range(low.shape[2] // HS):
        head = slice(h * HS, (h + 1) * HS)
        key, value = low[0, :, head], low[1, :, head]
        dkey = jnp.zeros((TOK, HS), F32)
        dvalue = jnp.zeros((TOK, HS), F32)
        for i in range(TOPK):
            query = low[2 + i, :, head]
            grad = dcontext[i][:, head]
            prob = probs[h, i * TOK : (i + 1) * TOK, :]
            dweight = mul(grad, value, NT)
            dscore = prob * (dweight - jnp.sum(prob * dweight, axis=-1, keepdims=True))
            dscore = dscore.astype(BF16)
            done = mul(dscore, key, NN) * HS ** (-0.5)
            dkey = dkey + mul(dscore, query, TN)
            dvalue = dvalue + mul(prob.astype(BF16), grad, TN)
            inner = inner + jnp.sum(done * query.astype(F32), axis=-1, keepdims=True)
            grads[2 + i, :, head] = (done * scale).astype(BF16)
        dkey = dkey * HS ** (-0.5)
        inner = inner + jnp.sum(
            dkey * key.astype(F32) + dvalue * value.astype(F32), axis=-1, keepdims=True
        )
        grads[0, :, head] = (dkey * scale).astype(BF16)
        grads[1, :, head] = (dvalue * scale).astype(BF16)
    lane = lax.broadcasted_iota(jnp.int32, (TOK, TOK), 1)
    table = jnp.where(lane == 0, dprob[0], jnp.where(lane == 1, dprob[1], jnp.where(lane == 2, inner, 0.0)))
    sums[...] = jnp.transpose(table)[0:8]


def columns(rows):
    return jnp.transpose(jnp.concatenate([rows] * (TOK // rows.shape[0]), axis=0))


def pick_row(values, index):
    line = lax.broadcasted_iota(jnp.int32, values.shape, 0)
    return jnp.sum(jnp.where(line == index, values, 0.0), axis=0, keepdims=True)


def route_body(subs, capacity):
    count = E * subs * 8

    def body(at, *refs):
        tables = refs[:E]
        hot_cols, home, turned, mlp_cols, expert_rows, select = refs[E : E + 6]
        both, rank, kept, hot, mlp_hot = refs[E + 6 :]
        expert = lax.broadcasted_iota(jnp.int32, (E, TOK), 0).astype(F32)
        for k in range(E):
            for j in range(subs):
                if k == 0:
                    line = tables[0][j].astype(F32)
                else:
                    first = (1 + j // 4) * TOK
                    lines = tables[k][2 * TOK :, first : first + TOK].astype(F32)
                    line = lines[(j % 4) * 4 : (j % 4) * 4 + 4]
                ones = [(line[r : r + 1] == expert).astype(F32) for r in range(4)]
                start = (k * subs + j) * 8
                both[start : start + 4, :] = ones[0] + ones[1]
                both[start + 4 : start + 8, :] = ones[2] + ones[3]
                if j == 0:
                    hot[k, 0:4, :], hot[k, 4:8, :] = ones[0], ones[1]
                    mlp_hot[k, 0:4, :], mlp_hot[k, 4:8, :] = ones[2], ones[3]
        low = both[...].astype(BF16)
        row = lax.broadcasted_iota(jnp.int32, (TOK, TOK), 0)
        col = lax.broadcasted_iota(jnp.int32, (TOK, TOK), 1)
        rank[...] = mul(low, (row < col).astype(F32).astype(BF16), NN)
        row = lax.broadcasted_iota(jnp.int32, (count, count), 0)
        col = lax.broadcasted_iota(jnp.int32, (count, count), 1)
        own = at[2] * subs + at[1]
        ahead = (((col >> 3) ^ own) < ((row >> 3) ^ own)) & ((col & 7) == (row & 7))
        before = mul(ahead.astype(F32).astype(BF16), low, NN)
        place_of = jnp.sum(before, axis=-1, keepdims=True) + rank[...]
        kept[...] = both[...] * (place_of < capacity).astype(F32)

        for k in range(E):
            hot_cols[block(at[0] ^ k), :] = columns(hot[k])[:, 0:8]
        pad = jnp.zeros((6, TOK), F32)
        home[0:8, :] = hot[0]
        for i in range(TOPK):
            home[8 + i : 9 + i, :] = jnp.sum(
                hot[0, i * E : (i + 1) * E, :] * kept[0:E, :], axis=0, keepdims=True
            )
        home[10:16, :] = pad
        mine = mlp_hot[at[0]]
        start = pl.multiple_of(at[0] * (subs * 8), 8)
        kept_mine = kept[pl.ds(start, 8), :][4:8]
        rank_mine = rank[pl.ds(start, 8), :][4:8]
        turned[0:8, :] = mine
        for i in range(TOPK):
            turned[8 + i : 9 + i, :] = jnp.sum(
                mine[i * E : (i + 1) * E] * kept_mine, axis=0, keepdims=True
            )
        turned[10:16, :] = pad
        mlp_cols[...] = columns(mine)[:, 0:8]
        slot = lax.broadcasted_iota(jnp.int32, (SLOTS, TOK), 0).astype(F32)
        for k in range(E):
            e = at[2] ^ k
            for i in range(TOPK):
                expert_rows[2 * k + i : 2 * k + i + 1, :] = pick_row(mine[i * E : (i + 1) * E], e)
            taken = (slot == pick_row(rank_mine, e)) & (pick_row(kept_mine, e) > 0)
            select[k] = taken.astype(F32).astype(BF16)

    return body


def two_halves(values):
    lane = lax.broadcasted_iota(jnp.int32, (values[0].shape[0], 128), 1)
    table = jnp.zeros((values[0].shape[0], 128), F32)
    for i, one in enumerate(values):
        high = one.astype(BF16).astype(F32)
        table = jnp.where(lane == 2 * i, high, table)
        table = jnp.where(lane == 2 * i + 1, one - high, table)
    return table.astype(BF16)


def pick_body(at, stream, keep, got, other, gain, router, mlp_cols, select, *refs):
    hidden, stats, outs = refs[0], refs[1], refs[2:]
    size = hidden.shape[1]
    total = stream[...].astype(F32) + (keep[...] + got[0].astype(F32) + other[...].astype(F32))
    hidden[...] = total
    gained = total * gain[...]
    square = jnp.sum(total * total, axis=-1, keepdims=True)
    logits = lax.dot_general(
        gained, router[...], NT, precision=lax.Precision.HIGHEST, preferred_element_type=F32
    )
    lane = lax.broadcasted_iota(jnp.int32, logits.shape, 1)
    chosen = jnp.zeros_like(square)
    for e in range(E):
        one = mlp_cols[:, e : e + 1] + mlp_cols[:, E + e : E + e + 1]
        chosen = chosen + one * logits[:, e : e + 1]
    low = gained.astype(BF16)
    for k in range(E):
        own = jnp.sum(jnp.where(lane == (at[2] ^ k), logits, 0.0), axis=-1, keepdims=True)
        extra = two_halves([square, 2.0 * own - chosen])
        outs[k][:, :size] = mul(select[k], low, NN).astype(BF16)
        outs[k][:, size:] = mul(select[k], extra, NN).astype(BF16)
    stats[...] = stat_rows(square, logits)


def join_rows_body(at, *refs):
    pieces, out = refs[:E], refs[E]
    size = pieces[0].shape[1] - 128
    join_pieces(at, pieces, out, size)
    total = pieces[0][:, size:].astype(F32)
    for k in range(1, E):
        total = total + pieces[k][:, size:].astype(F32)
    square, gap = total[:, 0:1] + total[:, 1:2], total[:, 2:3] + total[:, 3:4]
    scale = lax.rsqrt(square / (E * size) + EPSILON)
    small = jnp.exp(-jnp.abs(gap * scale))
    gate = jnp.where(gap < 0.0, small, 1.0) / (1.0 + small)
    out[:, E * size :] = two_halves([scale, gate])


def join_pieces(at, pieces, out, size):
    for k in range(E):
        for p in range(E):

            @pl.when((at[2] ^ k) == p)
            def _(k=k, p=p):
                out[:, p * size : (p + 1) * size] = pieces[k][:, :size]


def join_body(at, *refs):
    join_pieces(at, refs[:E], refs[E], refs[0].shape[1])


def split_body(extra):
    def body(at, own, got, *refs):
        outs, store = refs[:E], refs[E]
        store[...] = (own[...] + got[...].astype(F32)).astype(BF16)
        size = outs[0].shape[1] - extra
        for k in range(E):
            for p in range(E):

                @pl.when((at[2] ^ k) == p)
                def _(k=k, p=p):
                    outs[k][:, :size] = store[:, p * size : (p + 1) * size]

            if extra:
                outs[k][:, size:] = store[:, E * size :]

    return body


def local(
    stream,
    out_grad,
    attn_gain,
    attn_router,
    key_value,
    query_proj,
    output_proj,
    mlp_gain,
    mlp_router,
    expert_in,
    expert_down,
    attn_routes,
    mlp_routes,
    doc_lengths,
):
    wide_count = lax.axis_size("wide")
    narrow_count = lax.axis_size("narrow")
    subs = wide_count // E
    wide = lax.axis_index("wide")
    narrow = lax.axis_index("narrow")
    plane, sub = wide // subs, wide % subs
    capacity = 9 * TOK * wide_count * TOPK // (8 * E)
    slice_width = stream.shape[1]
    shard_rows = attn_gain.shape[0]
    width = slice_width * narrow_count
    local_width = key_value.shape[2]
    head_count = local_width // HS
    hidden_units = expert_down.shape[1]
    score_scale = HS ** (-0.5)

    def after(values, *others):
        return lax.optimization_barrier((values, others))[0]

    def by_plane(values, k):
        return lax.ppermute(values, "wide", [(i, i ^ (k * subs)) for i in range(wide_count)])

    def by_sub(values, k):
        return lax.ppermute(values, "wide", [(i, i ^ k) for i in range(wide_count)])

    def by_narrow(values, k):
        return lax.ppermute(values, "narrow", [(i, i ^ k) for i in range(narrow_count)])

    def swap(values):
        pairs = []
        for w in range(wide_count):
            for n in range(narrow_count):
                z, y = w // subs, w % subs
                pairs.append((w * narrow_count + n, (n * subs + y) * narrow_count + z))
        return lax.ppermute(values, ("wide", "narrow"), pairs)

    def by_side(values, side):
        pairs = []
        for w in range(wide_count):
            for n in range(narrow_count):
                other = (w ^ 1, n) if (n & 1) == side else (w, n ^ 2)
                pairs.append((w * narrow_count + n, other[0] * narrow_count + other[1]))
        return lax.ppermute(values, ("wide", "narrow"), pairs)

    def gather_planes(values):
        return [values] + [by_plane(values, k) for k in range(1, E)]

    def exchange_planes(parts):
        return [parts[0]] + [by_plane(parts[k], k) for k in range(1, E)]

    def gather_subs(values, *others):
        parts, bit = [values], 1
        while bit < subs:
            parts = parts + [by_sub(after(one, *others) if others else one, bit) for one in parts]
            bit *= 2
        return parts

    def reduce_subs(parts):
        bit = len(parts) // 2
        while bit >= 1:
            parts = [parts[j] + by_sub(parts[j + bit].astype(BF16), bit).astype(F32) for j in range(bit)]
            bit //= 2
        return parts[0]

    def gather_narrow(values):
        other = by_narrow(values, 2)
        return [values, by_narrow(values, 1), other, by_narrow(other, 1)]

    def reduce_narrow(keep_0, keep_2, send, *others):
        got = by_narrow(send, 1)
        if others:
            got = after(got, *others)
        other = by_narrow((keep_2 + got[1].astype(F32)).astype(BF16), 2)
        return keep_0, got, other

    def finish_subs(keep, send):
        bit = len(keep)
        got = [by_sub(send[j], bit) for j in range(bit)]
        return reduce_subs([keep[j] + got[j].astype(F32) for j in range(bit)]), got

    def sum_narrow(values):
        values = values + by_narrow(values, 2)
        return values + by_narrow(values, 1)

    def sum_planes(values):
        values = values + by_plane(values, 1)
        return values + by_plane(values, 2)

    def sum_subs(values):
        bit = 1
        while bit < subs:
            values = values + by_sub(values, bit)
            bit *= 2
        return values

    turned_stream = swap(stream)

    size = max(shard_rows, TOK)

    def pad(rows, count):
        return jnp.pad(rows, ((0, count - rows.shape[0]), (0, size - rows.shape[1])))

    own_routes = jnp.concatenate([attn_routes.T, mlp_routes.T], axis=0).astype(BF16)
    own_rows = jnp.concatenate(
        [attn_gain[None, :], attn_router.T, mlp_gain[None, :], mlp_router.T], axis=0
    )
    parts = gather_subs(jnp.concatenate([pad(own_routes, 8), pad(own_rows, 16)], axis=0))
    parts = jnp.stack(parts)
    near = xor_shuffle(parts[:, 8:, :shard_rows], sub).swapaxes(0, 1).reshape(16, slice_width)
    gain_one_plane = near[0].astype(F32)
    router_one_plane = near[1:5].astype(F32)
    gain_two_plane = near[5].astype(F32)
    router_two_plane = near[6:10].astype(F32)

    route_parts = parts[:, :8, :TOK]
    at = jnp.stack([narrow ^ plane, sub, plane, narrow]).astype(jnp.int32)
    kv_parts = gather_subs(key_value)
    query_parts = gather_subs(query_proj, kv_parts[-1])
    out_parts = gather_subs(output_proj, query_parts[-1])
    home_stream = stream.astype(F32)

    rows_all = E * TOK
    sent = shape((2, TOK, local_width), BF16)
    kept_own = shape((2, TOK, local_width), F32)
    all_streams = gather_narrow(turned_stream)
    gained, own_stats, *kv_blocks = run(
        "key_value",
        key_value_body(subs),
        [shape((rows_all, slice_width), BF16), shape((8, TOK), F32), kept_own]
        + [shape((2 * TOK + 16, local_width), BF16)] * (E - 1),
        [
            at,
            *all_streams,
            gain_one_plane[None],
            jnp.pad(router_one_plane, ((0, 4), (0, 0))),
            route_parts,
            *kv_parts,
        ],
        [
            pltpu.VMEM((2, slice_width, local_width), BF16),
            pltpu.VMEM((2, rows_all, local_width), F32),
            pltpu.VMEM((E, 8, TOK), F32),
        ],
    )
    turned_grad = swap(after(out_grad, own_stats))
    kv_blocks = exchange_planes(kv_blocks)
    line_count = wide_count * 8
    hot_cols, home_hot, turned_hot, mlp_cols, expert_hot, select = run(
        "route",
        route_body(subs, capacity),
        [
            shape((E * TOK, 8), F32),
            shape((16, TOK), F32),
            shape((16, TOK), F32),
            shape((TOK, 8), F32),
            shape((8, TOK), F32),
            shape((E, SLOTS, TOK), BF16),
        ],
        [at, route_parts, *kv_blocks[1:]],
        [pltpu.VMEM((line_count, TOK), F32)] * 3 + [pltpu.VMEM((E, 8, TOK), F32)] * 2,
    )
    hot_one, keep_one = home_hot[0:8].reshape(TOPK, E, TOK), home_hot[8:10]
    hot_two, keep_two = turned_hot[0:8].reshape(TOPK, E, TOK), turned_hot[8:10]
    hot_two_k = expert_hot.reshape(E, TOPK, TOK)

    routed_scratch = [
        pltpu.VMEM((E, slice_width, local_width), BF16),
        pltpu.VMEM((TOPK, rows_all, local_width), F32),
    ]
    query_blocks = run(
        "query",
        routed_body(subs, True),
        [kept_own] + [sent] * (E - 1),
        [at, gained, hot_cols, *query_parts],
        routed_scratch,
    )
    query_blocks = exchange_planes(query_blocks)

    def gates(logits, hots):
        picked = jnp.sum(hots * logits[None], axis=1)
        gap = picked[0] - picked[1]
        return jnp.stack([jax.nn.sigmoid(gap), jax.nn.sigmoid(-gap)])

    def share(full):
        size = full.shape[-1]
        full = jnp.concatenate([full, by_side(full, 0)], axis=0)
        got = by_side(full, 1)
        full = jnp.concatenate([full, got], axis=0)
        bit = 2
        while bit < subs:
            full = jnp.concatenate([full, by_sub(full, bit)], axis=0)
            bit *= 2
        return jnp.concatenate([full, by_narrow(full, 1)], axis=0).reshape(-1, size), got

    picked = jnp.einsum("kst,td->ksd", select, turned_grad, preferred_element_type=F32).astype(BF16)
    token_rows, low, probs, context, gated = run(
        "attention",
        attention_body,
        [
            shape((16, TOK), F32),
            shape((4, TOK, local_width), BF16),
            shape((head_count, TOPK * TOK, TOK), F32),
            sent,
            sent,
        ],
        [doc_lengths[0], *kv_blocks, *query_blocks, own_stats, home_hot],
    )
    scale_one, prob_one, logits_one = token_rows[0], token_rows[3:5], token_rows[5:9]

    (full,) = run(
        "join",
        join_body,
        [shape((SLOTS, width), BF16)],
        [at, *after(exchange_planes([picked[k] for k in range(E)]), gated)],
    )
    grad_rows, grad_got = share(full)
    folded = [shape((TOK, slice_width), F32), shape((TOK, slice_width), F32), shape((2, TOK, slice_width), BF16)]
    mixed, *attention = run(
        "output",
        output_body(subs),
        [shape((E, rows_all, local_width), BF16)] + folded,
        [at, *gather_planes(gated), hot_cols, *out_parts],
        [pltpu.VMEM((E, slice_width, local_width), BF16)],
    )
    weight_in = expert_in[0]
    weight_down = expert_down[0]
    dact_raw = dot(grad_rows, weight_down, ((1,), (1,)))

    hidden, stats_two, *picked = run(
        "pick",
        pick_body,
        [shape((TOK, slice_width), F32), shape((8, TOK), F32)]
        + [shape((SLOTS, slice_width + 128), BF16)] * E,
        [
            at,
            turned_stream,
            *after(reduce_narrow(*attention), grad_got),
            gain_two_plane[None],
            jnp.pad(router_two_plane, ((0, 4), (0, 0))),
            mlp_cols,
            select,
        ],
    )
    (full,) = run(
        "join_rows",
        join_rows_body,
        [shape((SLOTS, width + 128), BF16)],
        [at, *exchange_planes(picked)],
    )
    stats_two = sum_planes(stats_two)
    full, _ = share(full)
    full = after(full, stats_two)
    expert_rows = full[:, :width]
    row_pairs = full[:, width : width + 4].astype(F32)
    row_scale = row_pairs[:, 0:1] + row_pairs[:, 1:2]
    row_gate = row_pairs[:, 2:3] + row_pairs[:, 3:4]
    scale_two = lax.rsqrt(stats_two[E] / width + EPSILON)
    logits_two = stats_two[:E] * scale_two
    prob_two = gates(logits_two, hot_two)

    gate_up = jnp.einsum("rd,dkf->krf", expert_rows, weight_in, preferred_element_type=F32)
    gate_pre = gate_up[0] * row_scale
    up_pre = gate_up[1] * row_scale
    gate_sig = jax.nn.sigmoid(gate_pre)
    silu_gate = gate_pre * gate_sig
    activation = (silu_gate * up_pre).astype(BF16)
    dactiv = dact_raw * row_gate
    dgate_pre = (dactiv * up_pre * gate_sig * (1.0 + gate_pre * (1.0 - gate_sig))).astype(BF16)
    dup_pre = (dactiv * silu_gate).astype(BF16)
    dprob_rows = jnp.sum(activation.astype(F32) * dact_raw, axis=-1)
    inner_rows = jnp.sum(dgate_pre.astype(F32) * gate_pre + dup_pre.astype(F32) * up_pre, axis=-1)
    drows = jnp.einsum(
        "krf,dkf->rd", jnp.stack([dgate_pre, dup_pre]), weight_in, preferred_element_type=F32
    )
    lanes = jnp.arange(128)
    row_stats = jnp.where(
        lanes[None, :] == 0, dprob_rows[:, None], jnp.where(lanes[None, :] == 1, inner_rows[:, None], 0.0)
    )

    def give_back(rows):
        half = rows.shape[0] // 2
        rows = rows[:half] + by_narrow(rows[half:].astype(BF16), 1).astype(F32)
        bit = subs // 2
        while bit > 1:
            half = rows.shape[0] // 2
            rows = rows[:half] + by_sub(rows[half:].astype(BF16), bit).astype(F32)
            bit //= 2
        half = rows.shape[0] // 2
        rows = rows[:half] + by_side(rows[half:].astype(BF16), 1).astype(F32)
        return rows[:SLOTS], by_side(rows[SLOTS:].astype(BF16), 0)

    def from_planes(own, got, extra, last=None):
        if last is not None:
            own = after(own, last)
        pieces = run(
            "split",
            split_body(extra),
            [shape((SLOTS, slice_width + extra), BF16)] * E,
            [at, own, got],
            [pltpu.VMEM(own.shape, BF16)],
        )
        return jnp.stack(exchange_planes(pieces))

    returned = give_back(jnp.concatenate([drows, row_stats], axis=1))
    returned = from_planes(*returned, row_stats.shape[1])
    combined = jnp.einsum("kst,ksd->ktd", select, returned, preferred_element_type=F32)
    per_expert = combined[:, :, slice_width : slice_width + 2]
    dprob_two = keep_two * jnp.sum(hot_two_k * per_expert[:, None, :, 0], axis=0)
    inner_two = jnp.sum(per_expert[:, :, 1], axis=0)
    dnormed_two = jnp.sum(combined[:, :, :slice_width], axis=0)

    def gate_back(prob, dprob, hots):
        dselect = prob * (dprob - jnp.sum(prob * dprob, axis=0, keepdims=True))
        return jnp.sum(hots * dselect[:, None, :], axis=0)

    dlogit_two = gate_back(prob_two, dprob_two, hot_two)
    dnormed_two = dnormed_two + dot(dlogit_two, router_two_plane, ((0,), (0,)), PRECISE)
    inner_two = inner_two + jnp.sum(dlogit_two * logits_two, axis=0)
    dhidden = (
        turned_grad.astype(F32)
        + scale_two[:, None] * (dnormed_two * gain_two_plane)
        - hidden * (scale_two * scale_two * inner_two / width)[:, None]
    )
    scaled_hidden = hidden * scale_two[:, None]
    mlp_terms = jnp.concatenate(
        [
            jnp.sum(dnormed_two * scaled_hidden, axis=0)[None],
            dot(dlogit_two, scaled_hidden * gain_two_plane, ((1,), (0,)), PRECISE),
        ],
        axis=0,
    )

    wide_grad, *dcontext_blocks = run(
        "dcontext",
        routed_body(subs, False),
        [shape((rows_all, slice_width), BF16), kept_own] + [sent] * (E - 1),
        [at, *gather_narrow(dhidden.astype(BF16)), hot_cols, *out_parts],
        routed_scratch,
    )
    dcontext_blocks = exchange_planes(dcontext_blocks)

    def weight_parts(count):
        return [
            shape((count, shard_rows, local_width), F32 if j < subs // 2 else BF16)
            for j in range(subs)
        ]

    def weight_sum(parts):
        return finish_subs(parts[: subs // 2], parts[subs // 2 :])

    weight_scratch = [pltpu.VMEM((slice_width, local_width), F32)]
    output_parts = run(
        "output_grad", weight_grad_body, weight_parts(E), [at, wide_grad, mixed], weight_scratch
    )
    expert_out = dot(activation, weight_down, ((1,), (0,))) * row_gate
    mixture = give_back(expert_out)
    output_grad, output_got = weight_sum(output_parts)
    gated_act = (activation.astype(F32) * row_gate).astype(BF16)
    down_grad = dot(after(gated_act, dcontext_blocks[0]), grad_rows, ((0,), (0,)))
    grads_low, home_sums = run(
        "attention_back",
        attention_back_body,
        [shape((4, TOK, local_width), BF16), shape((8, TOK), F32)],
        [
            at,
            *after(dcontext_blocks, output_parts[-1], down_grad),
            token_rows,
            low,
            probs,
            context,
        ],
    )
    grad_planes = gather_planes(grads_low)
    dboth = jnp.stack(
        [
            (dgate_pre.astype(F32) * row_scale).astype(BF16),
            (dup_pre.astype(F32) * row_scale).astype(BF16),
        ],
        axis=1,
    )
    up_grad = jnp.einsum(
        "rd,rkf->dkf", expert_rows, after(dboth, grad_planes[E - 1]), preferred_element_type=F32
    )
    dmixed, *query_grad_parts = run(
        "query_grad",
        query_grad_body,
        [shape((E, rows_all, local_width), BF16)] + weight_parts(E),
        [at, gained, hot_cols, *after(grad_planes, output_got, up_grad)],
        weight_scratch,
    )
    query_grad, query_got = weight_sum(query_grad_parts)
    dkv_all, gain_row, *dnormed_one = run(
        "input",
        input_body(subs),
        [shape((2, rows_all, local_width), BF16), shape((1, slice_width), F32)] + folded,
        [
            at,
            *after(grad_planes, query_grad_parts[-1]),
            dmixed,
            *kv_parts,
            *query_parts,
            *all_streams,
        ],
        [pltpu.VMEM((2 + E, slice_width, local_width), BF16)],
        flops=14 * rows_all * slice_width * local_width,
    )
    home_rows = swap(after(near, own_stats))
    gain_one_home = home_rows[0].astype(F32)
    router_one_home = home_rows[1:5].astype(F32)
    gained_home = home_stream * gain_one_home
    home_sums = sum_narrow(after(home_sums, gain_row))
    dprob_one = keep_one * home_sums[:2]
    dlogit_one = gate_back(prob_one, dprob_one, hot_one)
    inner_one = home_sums[2] + jnp.sum(dlogit_one * logits_one, axis=0)
    dlogit_scaled = dlogit_one * scale_one
    router_term = swap(dot(dlogit_scaled, gained_home, ((1,), (0,)), PRECISE))
    kv_grad_parts = run(
        "key_value_grad", weight_grad_body, weight_parts(2), [at, gained, dkv_all], weight_scratch
    )
    kv_grad, kv_got = weight_sum(after(kv_grad_parts, query_got))
    keep, got, other = after(reduce_narrow(*dnormed_one, query_got), kv_grad_parts[-1])
    dnormed_one = keep + got[0].astype(F32) + other.astype(F32)
    turned_out = dhidden + dnormed_one * gain_one_plane
    home_out = swap(turned_out.astype(BF16)).astype(F32)
    stream_grad = (
        home_out
        + gain_one_home * dot(dlogit_scaled, router_one_home, ((0,), (0,)), PRECISE)
        - home_stream * (scale_one * scale_one * inner_one / width)[:, None]
    )

    small = jnp.concatenate([mlp_terms, gain_row, router_term], axis=0)
    small = sum_subs(sum_narrow(after(small, query_got)))
    mine = lax.dynamic_slice_in_dim(small, sub * shard_rows, shard_rows, 1)
    router_one_grad = mine[6:10]
    gain_one_grad = mine[5] + jnp.sum(
        router_one_grad * attn_router.T.astype(F32), axis=0
    ) / attn_gain.astype(F32)

    mixture = from_planes(*mixture, 0, gain_row)
    mixture = jnp.einsum("kst,ksd->td", select, after(mixture, turned_out), preferred_element_type=F32)
    layer_out = swap((hidden + mixture).astype(BF16)).astype(F32)
    return (
        layer_out,
        stream_grad,
        gain_one_grad,
        router_one_grad.T,
        kv_grad,
        query_grad,
        output_grad,
        mine[0],
        mine[1:5].T,
        up_grad[None],
        down_grad[None],
    )


def solution(mesh):
    in_specs = (
        P("wide", "narrow"),
        P("wide", "narrow"),
        P("wide"),
        P("wide", None),
        P(None, "wide", "narrow"),
        P(None, "wide", "narrow"),
        P(None, "wide", "narrow"),
        P("wide"),
        P("wide", None),
        P("wide", None, None, "narrow"),
        P("wide", "narrow", None),
        P("wide", None),
        P("wide", None),
        P("wide", None),
    )
    out_specs = (
        P("wide", "narrow"),
        P("wide", "narrow"),
        P("wide"),
        P("wide", None),
        P(None, "wide", "narrow"),
        P(None, "wide", "narrow"),
        P(None, "wide", "narrow"),
        P("wide"),
        P("wide", None),
        P("wide", None, None, "narrow"),
        P("wide", "narrow", None),
    )
    return jax.shard_map(local, mesh=mesh, in_specs=in_specs, out_specs=out_specs, check_vma=False)
```

```python
import jax
import jax.numpy as jnp
from jax import lax
from jax.experimental import pallas as pl
from jax.experimental.pallas import tpu as pltpu
from jax.sharding import PartitionSpec as P

HS = 128
E = 4
TOPK = 2
TOK = 128
SLOTS = 80

EPSILON = 1e-05
NEGATIVE = -1000000000.0
PRECISE = lax.Precision.HIGHEST
F32 = jnp.float32
BF16 = jnp.bfloat16


def dot(left, right, contract, precision=None):
    return lax.dot_general(
        left, right, ((contract[0], contract[1]), ((), ())), precision=precision, preferred_element_type=F32
    )


def xor_shuffle(values, amount):
    count, bit = values.shape[0], 1
    while bit < count:
        split = values.reshape((count // (2 * bit), 2, bit) + values.shape[1:])
        flipped = split[:, ::-1].reshape(values.shape)
        values = jnp.where((amount & bit) != 0, flipped, values)
        bit *= 2
    return values


NN = (((1,), (0,)), ((), ()))
NT = (((1,), (1,)), ((), ()))
TN = (((0,), (0,)), ((), ()))


def mul(left, right, form):
    return lax.dot_general(left, right, form, preferred_element_type=F32)


def shape(dims, dtype):
    return jax.ShapeDtypeStruct(tuple(dims), dtype)


def run(name, body, outs, args, scratch=(), flops=1):
    vector = pl.BlockSpec(memory_space=pltpu.VMEM)
    return pl.pallas_call(
        body,
        out_shape=tuple(outs),
        in_specs=[pl.BlockSpec(memory_space=pltpu.SMEM)] + [vector] * (len(args) - 1),
        out_specs=tuple(vector for _ in outs),
        scratch_shapes=list(scratch),
        cost_estimate=pl.CostEstimate(flops=flops, transcendentals=0, bytes_accessed=1),
        name=name,
    )(*args)


def place(store, parts, sub, first=0):
    for j, part in enumerate(parts):
        rows = part.shape[1]
        start = pl.multiple_of((sub ^ j) * rows, rows)
        for a in range(part.shape[0]):
            store[first + a, pl.ds(start, rows), :] = part[a]


def block(index):
    return pl.ds(pl.multiple_of(index * TOK, TOK), TOK)


def send_blocks(total, outs, order):
    for k in range(E):
        for a in range(total.shape[0]):
            outs[k][a] = total[a, block(order ^ k), :].astype(outs[k].dtype)


def stat_rows(square, logits):
    lane = lax.broadcasted_iota(jnp.int32, (TOK, TOK), 1)
    table = jnp.where(lane == E, square, 0.0)
    for e in range(E):
        table = jnp.where(lane == e, logits[:, e : e + 1], table)
    return jnp.transpose(table)[0:8]


def key_value_body(subs):
    def body(at, *refs):
        rows, gain, router, routes = refs[:E], refs[E], refs[E + 1], refs[E + 2]
        parts = refs[E + 3 : E + 3 + subs]
        gained, own_stats, *outs = refs[E + 3 + subs : E + 5 + subs + E]
        weights, total, stats = refs[E + 5 + subs + E :]
        place(weights, parts, at[1])
        for q in range(E):
            wide = rows[q][...].astype(F32)
            scaled = wide * gain[...]
            gained[q * TOK : (q + 1) * TOK, :] = scaled.astype(BF16)
            logits = lax.dot_general(
                scaled, router[...], NT, precision=lax.Precision.HIGHEST, preferred_element_type=F32
            )
            stats[q] = stat_rows(jnp.sum(wide * wide, axis=-1, keepdims=True), logits)
        for a in range(2):
            total[a] = mul(gained[...], weights[a], NN)
        own_stats[...] = stats[at[0]]
        for k in range(E):
            where = block(at[0] ^ k)
            for a in range(2):
                piece = total[a, where, :].astype(outs[k].dtype)
                if k == 0:
                    outs[k][a] = piece
                else:
                    outs[k][a * TOK : (a + 1) * TOK, :] = piece
            if k > 0:
                mine = stats[at[0] ^ k]
                high = mine.astype(BF16).astype(F32)
                pair = jnp.concatenate([high, mine - high], axis=0).astype(BF16)
                outs[k][2 * TOK :, :] = jnp.zeros((16, outs[k].shape[1]), BF16)
                outs[k][2 * TOK :, 0:TOK] = pair
                for first in range(0, subs, 4):
                    lines = [
                        routes[j][0:4].astype(F32) if j < subs else jnp.zeros((4, TOK), F32)
                        for j in range(first, first + 4)
                    ]
                    start = (1 + first // 4) * TOK
                    outs[k][2 * TOK :, start : start + TOK] = jnp.concatenate(lines, axis=0).astype(BF16)

    return body


def routed_body(subs, joined):
    count = 1 if joined else E

    def body(at, *refs):
        rows, hot, parts = refs[:count], refs[count], refs[count + 1 : count + 1 + subs]
        rest = refs[count + 1 + subs :]
        if joined:
            wide = rows[0]
        else:
            wide, rest = rest[0], rest[1:]
            for q in range(E):
                wide[q * TOK : (q + 1) * TOK, :] = rows[q][...]
        outs, weights, total = rest[:E], rest[E], rest[E + 1]
        place(weights, parts, at[1])
        for e in range(E):
            every = mul(wide[...], weights[e], NN)
            for i in range(TOPK):
                mine = every * hot[:, i * E + e : i * E + e + 1]
                total[i] = mine if e == 0 else total[i] + mine
        send_blocks(total, outs, at[0])

    return body


def spread_pairs(at, rows, hot, out, first=0):
    for k in range(E):
        where = block(at[0] ^ k)
        mask = hot[where, :].astype(BF16)
        for e in range(E):
            out[e, where, :] = (
                rows[k][first] * mask[:, e : e + 1]
                + rows[k][first + 1] * mask[:, E + e : E + e + 1]
            )


def fold_out(total, keep_0, keep_2, send):
    keep_0[...] = total[0:TOK]
    keep_2[...] = total[2 * TOK : 3 * TOK]
    send[0] = total[TOK : 2 * TOK].astype(BF16)
    send[1] = total[3 * TOK : 4 * TOK].astype(BF16)


def output_body(subs):
    def body(at, *refs):
        rows, hot, parts = refs[:E], refs[E], refs[E + 1 : E + 1 + subs]
        mixed, keep_0, keep_2, send, weights = refs[E + 1 + subs :]
        place(weights, parts, at[1])
        spread_pairs(at, rows, hot, mixed)
        total = mul(mixed[0], weights[0], NT)
        for e in range(1, E):
            total = total + mul(mixed[e], weights[e], NT)
        fold_out(total, keep_0, keep_2, send)

    return body


def input_body(subs):
    def body(at, *refs):
        rows, dmixed = refs[:E], refs[E]
        kv_parts = refs[E + 1 : E + 1 + subs]
        query_parts = refs[E + 1 + subs : E + 1 + 2 * subs]
        streams = refs[E + 1 + 2 * subs : 2 * E + 1 + 2 * subs]
        dkv_all, gain_row, keep_0, keep_2, send, weights = refs[2 * E + 1 + 2 * subs :]
        place(weights, kv_parts, at[1])
        place(weights, query_parts, at[1], 2)
        for k in range(E):
            for a in range(2):
                dkv_all[a, block(at[0] ^ k), :] = rows[k][a]
        total = mul(dkv_all[0], weights[0], NT) + mul(dkv_all[1], weights[1], NT)
        for e in range(E):
            total = total + mul(dmixed[e], weights[2 + e], NT)
        gain = jnp.zeros((1, total.shape[1]), F32)
        for q in range(E):
            part = total[q * TOK : (q + 1) * TOK] * streams[q][...].astype(F32)
            gain = gain + jnp.sum(part, axis=0, keepdims=True)
        gain_row[...] = gain
        fold_out(total, keep_0, keep_2, send)

    return body


def split_rows(at, rows, other, parts, total):
    for a in range(other.shape[0]):
        total[...] = mul(rows[...], other[a], TN)
        for j, part in enumerate(parts):
            count = part.shape[1]
            start = pl.multiple_of((at[1] ^ j) * count, count)
            part[a] = total[pl.ds(start, count), :].astype(part.dtype)


def weight_grad_body(at, rows, other, *refs):
    split_rows(at, rows, other, refs[:-1], refs[-1])


def query_grad_body(at, rows, hot, *refs):
    dmixed = refs[E]
    spread_pairs(at, refs[:E], hot, dmixed, 2)
    split_rows(at, rows, dmixed, refs[E + 1 : -1], refs[-1])


def attention_mask(at):
    row = lax.broadcasted_iota(jnp.int32, (TOK, TOK), 0)
    col = lax.broadcasted_iota(jnp.int32, (TOK, TOK), 1)
    row_doc, col_doc, end = jnp.zeros_like(row), jnp.zeros_like(row), 0
    for d in range(4):
        end = end + at[d]
        row_doc = row_doc + (row >= end).astype(jnp.int32)
        col_doc = col_doc + (col >= end).astype(jnp.int32)
    return (row_doc == col_doc) & (col <= row)


def attention_body(at, own_kv, *refs):
    got_kv, own_query, got_query = refs[: E - 1], refs[E - 1], refs[E : 2 * E - 1]
    own_stats, hot, rows, low, probs, context, gated = refs[2 * E - 1 :]
    stats = own_stats[...]
    for one in got_kv:
        pair = one[2 * TOK :, 0:TOK].astype(F32)
        stats = stats + pair[0:8] + pair[8:16]
    scale_row = lax.rsqrt(stats[E : E + 1] / (E * own_kv.shape[2]) + EPSILON)
    logits = stats[0:E] * scale_row
    picked = [
        jnp.sum(hot[i * E : (i + 1) * E, :] * logits, axis=0, keepdims=True) for i in range(TOPK)
    ]
    gap = picked[0] - picked[1]
    prob_rows = [1.0 / (1.0 + jnp.exp(-gap)), 1.0 / (1.0 + jnp.exp(gap))]
    rows[0:1, :] = scale_row
    for i in range(TOPK):
        rows[1 + i : 2 + i, :] = prob_rows[i] * hot[8 + i : 9 + i, :]
        rows[3 + i : 4 + i, :] = prob_rows[i]
    rows[5:9, :] = logits
    rows[9:16, :] = jnp.zeros((7, TOK), F32)
    cols = columns(rows[...])
    scale = cols[:, 0:1]
    for a in range(2):
        where = slice(a * TOK, (a + 1) * TOK)
        total, query = own_kv[a], own_query[a]
        for one in got_kv:
            total = total + one[where, :].astype(F32)
        for one in got_query:
            query = query + one[a].astype(F32)
        low[a] = (total * scale).astype(BF16)
        low[2 + a] = (query * scale).astype(BF16)
    allowed = attention_mask(at)
    for h in range(low.shape[2] // HS):
        head = slice(h * HS, (h + 1) * HS)
        for i in range(TOPK):
            scores = mul(low[2 + i, :, head], low[0, :, head], NT) * HS ** (-0.5)
            scores = jnp.where(allowed, scores, NEGATIVE)
            top = jnp.exp(scores - jnp.max(scores, axis=-1, keepdims=True))
            prob = top / jnp.sum(top, axis=-1, keepdims=True)
            probs[h, i * TOK : (i + 1) * TOK, :] = prob
            mixed = mul(prob.astype(BF16), low[1, :, head], NN).astype(BF16)
            context[i, :, head] = mixed
            gated[i, :, head] = (mixed.astype(F32) * cols[:, 1 + i : 2 + i]).astype(BF16)


def attention_back_body(at, own, *refs):
    got = refs[: E - 1]
    rows, low, probs, context, grads, sums = refs[E - 1 :]
    cols = columns(rows[...])
    scale = cols[:, 0:1]
    inner = jnp.zeros((TOK, 1), F32)
    dprob = []
    dcontext = []
    for i in range(TOPK):
        raw = own[i]
        for one in got:
            raw = raw + one[i].astype(F32)
        dprob.append(jnp.sum(context[i].astype(F32) * raw, axis=-1, keepdims=True))
        dcontext.append((raw * cols[:, 1 + i : 2 + i]).astype(BF16))
    for h in range(low.shape[2] // HS):
        head = slice(h * HS, (h + 1) * HS)
        key, value = low[0, :, head], low[1, :, head]
        dkey = jnp.zeros((TOK, HS), F32)
        dvalue = jnp.zeros((TOK, HS), F32)
        for i in range(TOPK):
            query = low[2 + i, :, head]
            grad = dcontext[i][:, head]
            prob = probs[h, i * TOK : (i + 1) * TOK, :]
            dweight = mul(grad, value, NT)
            dscore = prob * (dweight - jnp.sum(prob * dweight, axis=-1, keepdims=True))
            dscore = dscore.astype(BF16)
            done = mul(dscore, key, NN) * HS ** (-0.5)
            dkey = dkey + mul(dscore, query, TN)
            dvalue = dvalue + mul(prob.astype(BF16), grad, TN)
            inner = inner + jnp.sum(done * query.astype(F32), axis=-1, keepdims=True)
            grads[2 + i, :, head] = (done * scale).astype(BF16)
        dkey = dkey * HS ** (-0.5)
        inner = inner + jnp.sum(
            dkey * key.astype(F32) + dvalue * value.astype(F32), axis=-1, keepdims=True
        )
        grads[0, :, head] = (dkey * scale).astype(BF16)
        grads[1, :, head] = (dvalue * scale).astype(BF16)
    lane = lax.broadcasted_iota(jnp.int32, (TOK, TOK), 1)
    table = jnp.where(lane == 0, dprob[0], jnp.where(lane == 1, dprob[1], jnp.where(lane == 2, inner, 0.0)))
    sums[...] = jnp.transpose(table)[0:8]


def columns(rows):
    return jnp.transpose(jnp.concatenate([rows] * (TOK // rows.shape[0]), axis=0))


def pick_row(values, index):
    line = lax.broadcasted_iota(jnp.int32, values.shape, 0)
    return jnp.sum(jnp.where(line == index, values, 0.0), axis=0, keepdims=True)


def route_body(subs, capacity):
    count = E * subs * 8

    def body(at, *refs):
        tables = refs[:E]
        hot_cols, home, turned, mlp_cols, expert_rows, select = refs[E : E + 6]
        both, rank, kept, hot, mlp_hot = refs[E + 6 :]
        expert = lax.broadcasted_iota(jnp.int32, (E, TOK), 0).astype(F32)
        for k in range(E):
            for j in range(subs):
                if k == 0:
                    line = tables[0][j].astype(F32)
                else:
                    first = (1 + j // 4) * TOK
                    lines = tables[k][2 * TOK :, first : first + TOK].astype(F32)
                    line = lines[(j % 4) * 4 : (j % 4) * 4 + 4]
                ones = [(line[r : r + 1] == expert).astype(F32) for r in range(4)]
                start = (k * subs + j) * 8
                both[start : start + 4, :] = ones[0] + ones[1]
                both[start + 4 : start + 8, :] = ones[2] + ones[3]
                if j == 0:
                    hot[k, 0:4, :], hot[k, 4:8, :] = ones[0], ones[1]
                    mlp_hot[k, 0:4, :], mlp_hot[k, 4:8, :] = ones[2], ones[3]
        low = both[...].astype(BF16)
        row = lax.broadcasted_iota(jnp.int32, (TOK, TOK), 0)
        col = lax.broadcasted_iota(jnp.int32, (TOK, TOK), 1)
        rank[...] = mul(low, (row < col).astype(F32).astype(BF16), NN)
        row = lax.broadcasted_iota(jnp.int32, (count, count), 0)
        col = lax.broadcasted_iota(jnp.int32, (count, count), 1)
        own = at[2] * subs + at[1]
        ahead = (((col >> 3) ^ own) < ((row >> 3) ^ own)) & ((col & 7) == (row & 7))
        before = mul(ahead.astype(F32).astype(BF16), low, NN)
        place_of = jnp.sum(before, axis=-1, keepdims=True) + rank[...]
        kept[...] = both[...] * (place_of < capacity).astype(F32)

        for k in range(E):
            hot_cols[block(at[0] ^ k), :] = columns(hot[k])[:, 0:8]
        pad = jnp.zeros((6, TOK), F32)
        home[0:8, :] = hot[0]
        for i in range(TOPK):
            home[8 + i : 9 + i, :] = jnp.sum(
                hot[0, i * E : (i + 1) * E, :] * kept[0:E, :], axis=0, keepdims=True
            )
        home[10:16, :] = pad
        mine = mlp_hot[at[0]]
        start = pl.multiple_of(at[0] * (subs * 8), 8)
        kept_mine = kept[pl.ds(start, 8), :][4:8]
        rank_mine = rank[pl.ds(start, 8), :][4:8]
        turned[0:8, :] = mine
        for i in range(TOPK):
            turned[8 + i : 9 + i, :] = jnp.sum(
                mine[i * E : (i + 1) * E] * kept_mine, axis=0, keepdims=True
            )
        turned[10:16, :] = pad
        mlp_cols[...] = columns(mine)[:, 0:8]
        slot = lax.broadcasted_iota(jnp.int32, (SLOTS, TOK), 0).astype(F32)
        for k in range(E):
            e = at[2] ^ k
            for i in range(TOPK):
                expert_rows[2 * k + i : 2 * k + i + 1, :] = pick_row(mine[i * E : (i + 1) * E], e)
            taken = (slot == pick_row(rank_mine, e)) & (pick_row(kept_mine, e) > 0)
            select[k] = taken.astype(F32).astype(BF16)

    return body


def two_halves(values):
    lane = lax.broadcasted_iota(jnp.int32, (values[0].shape[0], 128), 1)
    table = jnp.zeros((values[0].shape[0], 128), F32)
    for i, one in enumerate(values):
        high = one.astype(BF16).astype(F32)
        table = jnp.where(lane == 2 * i, high, table)
        table = jnp.where(lane == 2 * i + 1, one - high, table)
    return table.astype(BF16)


def pick_body(at, stream, keep, got, other, gain, router, mlp_cols, select, *refs):
    hidden, stats, outs = refs[0], refs[1], refs[2:]
    size = hidden.shape[1]
    total = stream[...].astype(F32) + (keep[...] + got[0].astype(F32) + other[...].astype(F32))
    hidden[...] = total
    gained = total * gain[...]
    square = jnp.sum(total * total, axis=-1, keepdims=True)
    logits = lax.dot_general(
        gained, router[...], NT, precision=lax.Precision.HIGHEST, preferred_element_type=F32
    )
    lane = lax.broadcasted_iota(jnp.int32, logits.shape, 1)
    chosen = jnp.zeros_like(square)
    for e in range(E):
        one = mlp_cols[:, e : e + 1] + mlp_cols[:, E + e : E + e + 1]
        chosen = chosen + one * logits[:, e : e + 1]
    low = gained.astype(BF16)
    for k in range(E):
        own = jnp.sum(jnp.where(lane == (at[2] ^ k), logits, 0.0), axis=-1, keepdims=True)
        extra = two_halves([square, 2.0 * own - chosen])
        outs[k][:, :size] = mul(select[k], low, NN).astype(BF16)
        outs[k][:, size:] = mul(select[k], extra, NN).astype(BF16)
    stats[...] = stat_rows(square, logits)


def join_rows_body(at, *refs):
    pieces, out = refs[:E], refs[E]
    size = pieces[0].shape[1] - 128
    join_pieces(at, pieces, out, size)
    total = pieces[0][:, size:].astype(F32)
    for k in range(1, E):
        total = total + pieces[k][:, size:].astype(F32)
    square, gap = total[:, 0:1] + total[:, 1:2], total[:, 2:3] + total[:, 3:4]
    scale = lax.rsqrt(square / (E * size) + EPSILON)
    small = jnp.exp(-jnp.abs(gap * scale))
    gate = jnp.where(gap < 0.0, small, 1.0) / (1.0 + small)
    out[:, E * size :] = two_halves([scale, gate])


def join_pieces(at, pieces, out, size):
    for k in range(E):
        for p in range(E):

            @pl.when((at[2] ^ k) == p)
            def _(k=k, p=p):
                out[:, p * size : (p + 1) * size] = pieces[k][:, :size]


def join_body(at, *refs):
    join_pieces(at, refs[:E], refs[E], refs[0].shape[1])


def split_body(extra):
    def body(at, own, got, *refs):
        outs, store = refs[:E], refs[E]
        store[...] = (own[...] + got[...].astype(F32)).astype(BF16)
        size = outs[0].shape[1] - extra
        for k in range(E):
            for p in range(E):

                @pl.when((at[2] ^ k) == p)
                def _(k=k, p=p):
                    outs[k][:, :size] = store[:, p * size : (p + 1) * size]

            if extra:
                outs[k][:, size:] = store[:, E * size :]

    return body


def local(
    stream,
    out_grad,
    attn_gain,
    attn_router,
    key_value,
    query_proj,
    output_proj,
    mlp_gain,
    mlp_router,
    expert_in,
    expert_down,
    attn_routes,
    mlp_routes,
    doc_lengths,
):
    wide_count = lax.axis_size("wide")
    narrow_count = lax.axis_size("narrow")
    subs = wide_count // E
    wide = lax.axis_index("wide")
    narrow = lax.axis_index("narrow")
    plane, sub = wide // subs, wide % subs
    capacity = 9 * TOK * wide_count * TOPK // (8 * E)
    slice_width = stream.shape[1]
    shard_rows = attn_gain.shape[0]
    width = slice_width * narrow_count
    local_width = key_value.shape[2]
    head_count = local_width // HS
    hidden_units = expert_down.shape[1]
    score_scale = HS ** (-0.5)

    def after(values, *others):
        return lax.optimization_barrier((values, others))[0]

    def by_plane(values, k):
        return lax.ppermute(values, "wide", [(i, i ^ (k * subs)) for i in range(wide_count)])

    def by_sub(values, k):
        return lax.ppermute(values, "wide", [(i, i ^ k) for i in range(wide_count)])

    def by_narrow(values, k):
        return lax.ppermute(values, "narrow", [(i, i ^ k) for i in range(narrow_count)])

    def swap(values):
        pairs = []
        for w in range(wide_count):
            for n in range(narrow_count):
                z, y = w // subs, w % subs
                pairs.append((w * narrow_count + n, (n * subs + y) * narrow_count + z))
        return lax.ppermute(values, ("wide", "narrow"), pairs)

    def by_side(values, side):
        pairs = []
        for w in range(wide_count):
            for n in range(narrow_count):
                other = (w ^ 1, n) if (n & 1) == side else (w, n ^ 2)
                pairs.append((w * narrow_count + n, other[0] * narrow_count + other[1]))
        return lax.ppermute(values, ("wide", "narrow"), pairs)

    def gather_planes(values):
        return [values] + [by_plane(values, k) for k in range(1, E)]

    def exchange_planes(parts):
        return [parts[0]] + [by_plane(parts[k], k) for k in range(1, E)]

    def gather_subs(values, *others):
        parts, bit = [values], 1
        while bit < subs:
            parts = parts + [by_sub(after(one, *others) if others else one, bit) for one in parts]
            bit *= 2
        return parts

    def reduce_subs(parts):
        bit = len(parts) // 2
        while bit >= 1:
            parts = [parts[j] + by_sub(parts[j + bit].astype(BF16), bit).astype(F32) for j in range(bit)]
            bit //= 2
        return parts[0]

    def gather_narrow(values):
        other = by_narrow(values, 2)
        return [values, by_narrow(values, 1), other, by_narrow(other, 1)]

    def reduce_narrow(keep_0, keep_2, send):
        got = by_narrow(send, 1)
        other = by_narrow((keep_2 + got[1].astype(F32)).astype(BF16), 2)
        return keep_0, got, other

    def finish_subs(keep, send):
        bit = len(keep)
        got = [by_sub(send[j], bit) for j in range(bit)]
        return reduce_subs([keep[j] + got[j].astype(F32) for j in range(bit)]), got

    def sum_narrow(values):
        values = values + by_narrow(values, 2)
        return values + by_narrow(values, 1)

    def sum_planes(values):
        values = values + by_plane(values, 1)
        return values + by_plane(values, 2)

    def sum_subs(values):
        bit = 1
        while bit < subs:
            values = values + by_sub(values, bit)
            bit *= 2
        return values

    turned_stream = swap(stream)

    size = max(shard_rows, TOK)

    def pad(rows, count):
        return jnp.pad(rows, ((0, count - rows.shape[0]), (0, size - rows.shape[1])))

    own_routes = jnp.concatenate([attn_routes.T, mlp_routes.T], axis=0).astype(BF16)
    own_rows = jnp.concatenate(
        [attn_gain[None, :], attn_router.T, mlp_gain[None, :], mlp_router.T], axis=0
    )
    parts = gather_subs(jnp.concatenate([pad(own_routes, 8), pad(own_rows, 16)], axis=0))
    parts = jnp.stack(parts)
    near = xor_shuffle(parts[:, 8:, :shard_rows], sub).swapaxes(0, 1).reshape(16, slice_width)
    gain_one_plane = near[0].astype(F32)
    router_one_plane = near[1:5].astype(F32)
    gain_two_plane = near[5].astype(F32)
    router_two_plane = near[6:10].astype(F32)

    route_parts = parts[:, :8, :TOK]
    at = jnp.stack([narrow ^ plane, sub, plane, narrow]).astype(jnp.int32)
    kv_parts = gather_subs(key_value)
    query_parts = gather_subs(query_proj, kv_parts[-1])
    out_parts = gather_subs(output_proj, query_parts[-1])
    home_stream = stream.astype(F32)

    rows_all = E * TOK
    sent = shape((2, TOK, local_width), BF16)
    kept_own = shape((2, TOK, local_width), F32)
    all_streams = gather_narrow(turned_stream)
    gained, own_stats, *kv_blocks = run(
        "key_value",
        key_value_body(subs),
        [shape((rows_all, slice_width), BF16), shape((8, TOK), F32), kept_own]
        + [shape((2 * TOK + 16, local_width), BF16)] * (E - 1),
        [
            at,
            *all_streams,
            gain_one_plane[None],
            jnp.pad(router_one_plane, ((0, 4), (0, 0))),
            route_parts,
            *kv_parts,
        ],
        [
            pltpu.VMEM((2, slice_width, local_width), BF16),
            pltpu.VMEM((2, rows_all, local_width), F32),
            pltpu.VMEM((E, 8, TOK), F32),
        ],
    )
    turned_grad = swap(after(out_grad, own_stats))
    kv_blocks = exchange_planes(kv_blocks)
    line_count = wide_count * 8
    hot_cols, home_hot, turned_hot, mlp_cols, expert_hot, select = run(
        "route",
        route_body(subs, capacity),
        [
            shape((E * TOK, 8), F32),
            shape((16, TOK), F32),
            shape((16, TOK), F32),
            shape((TOK, 8), F32),
            shape((8, TOK), F32),
            shape((E, SLOTS, TOK), BF16),
        ],
        [at, route_parts, *kv_blocks[1:]],
        [pltpu.VMEM((line_count, TOK), F32)] * 3 + [pltpu.VMEM((E, 8, TOK), F32)] * 2,
    )
    hot_one, keep_one = home_hot[0:8].reshape(TOPK, E, TOK), home_hot[8:10]
    hot_two, keep_two = turned_hot[0:8].reshape(TOPK, E, TOK), turned_hot[8:10]
    hot_two_k = expert_hot.reshape(E, TOPK, TOK)

    routed_scratch = [
        pltpu.VMEM((E, slice_width, local_width), BF16),
        pltpu.VMEM((TOPK, rows_all, local_width), F32),
    ]
    query_blocks = run(
        "query",
        routed_body(subs, True),
        [kept_own] + [sent] * (E - 1),
        [at, gained, hot_cols, *query_parts],
        routed_scratch,
    )
    query_blocks = exchange_planes(query_blocks)

    def gates(logits, hots):
        picked = jnp.sum(hots * logits[None], axis=1)
        gap = picked[0] - picked[1]
        return jnp.stack([jax.nn.sigmoid(gap), jax.nn.sigmoid(-gap)])

    def share(full):
        size = full.shape[-1]
        full = jnp.concatenate([full, by_side(full, 0)], axis=0)
        got = by_side(full, 1)
        full = jnp.concatenate([full, got], axis=0)
        bit = 2
        while bit < subs:
            full = jnp.concatenate([full, by_sub(full, bit)], axis=0)
            bit *= 2
        return jnp.concatenate([full, by_narrow(full, 1)], axis=0).reshape(-1, size), got

    picked = jnp.einsum("kst,td->ksd", select, turned_grad, preferred_element_type=F32).astype(BF16)
    token_rows, low, probs, context, gated = run(
        "attention",
        attention_body,
        [
            shape((16, TOK), F32),
            shape((4, TOK, local_width), BF16),
            shape((head_count, TOPK * TOK, TOK), F32),
            sent,
            sent,
        ],
        [doc_lengths[0], *kv_blocks, *query_blocks, own_stats, home_hot],
    )
    scale_one, prob_one, logits_one = token_rows[0], token_rows[3:5], token_rows[5:9]

    (full,) = run(
        "join",
        join_body,
        [shape((SLOTS, width), BF16)],
        [at, *after(exchange_planes([picked[k] for k in range(E)]), gated)],
    )
    grad_rows, grad_got = share(full)
    folded = [shape((TOK, slice_width), F32), shape((TOK, slice_width), F32), shape((2, TOK, slice_width), BF16)]
    mixed, *attention = run(
        "output",
        output_body(subs),
        [shape((E, rows_all, local_width), BF16)] + folded,
        [at, *gather_planes(gated), hot_cols, *out_parts],
        [pltpu.VMEM((E, slice_width, local_width), BF16)],
    )
    weight_in = expert_in[0]
    weight_down = expert_down[0]
    dact_raw = dot(grad_rows, weight_down, ((1,), (1,)))

    hidden, stats_two, *picked = run(
        "pick",
        pick_body,
        [shape((TOK, slice_width), F32), shape((8, TOK), F32)]
        + [shape((SLOTS, slice_width + 128), BF16)] * E,
        [
            at,
            turned_stream,
            *after(reduce_narrow(*attention), grad_got),
            gain_two_plane[None],
            jnp.pad(router_two_plane, ((0, 4), (0, 0))),
            mlp_cols,
            select,
        ],
    )
    (full,) = run(
        "join_rows",
        join_rows_body,
        [shape((SLOTS, width + 128), BF16)],
        [at, *exchange_planes(picked)],
    )
    stats_two = sum_planes(stats_two)
    full, _ = share(full)
    full = after(full, stats_two)
    expert_rows = full[:, :width]
    row_pairs = full[:, width : width + 4].astype(F32)
    row_scale = row_pairs[:, 0:1] + row_pairs[:, 1:2]
    row_gate = row_pairs[:, 2:3] + row_pairs[:, 3:4]
    scale_two = lax.rsqrt(stats_two[E] / width + EPSILON)
    logits_two = stats_two[:E] * scale_two
    prob_two = gates(logits_two, hot_two)

    gate_up = jnp.einsum("rd,dkf->krf", expert_rows, weight_in, preferred_element_type=F32)
    gate_pre = gate_up[0] * row_scale
    up_pre = gate_up[1] * row_scale
    gate_sig = jax.nn.sigmoid(gate_pre)
    silu_gate = gate_pre * gate_sig
    activation = (silu_gate * up_pre).astype(BF16)
    dactiv = dact_raw * row_gate
    dgate_pre = (dactiv * up_pre * gate_sig * (1.0 + gate_pre * (1.0 - gate_sig))).astype(BF16)
    dup_pre = (dactiv * silu_gate).astype(BF16)
    dprob_rows = jnp.sum(activation.astype(F32) * dact_raw, axis=-1)
    inner_rows = jnp.sum(dgate_pre.astype(F32) * gate_pre + dup_pre.astype(F32) * up_pre, axis=-1)
    drows = jnp.einsum(
        "krf,dkf->rd", jnp.stack([dgate_pre, dup_pre]), weight_in, preferred_element_type=F32
    )
    lanes = jnp.arange(128)
    row_stats = jnp.where(
        lanes[None, :] == 0, dprob_rows[:, None], jnp.where(lanes[None, :] == 1, inner_rows[:, None], 0.0)
    )

    def give_back(rows):
        half = rows.shape[0] // 2
        rows = rows[:half] + by_narrow(rows[half:].astype(BF16), 1).astype(F32)
        bit = subs // 2
        while bit > 1:
            half = rows.shape[0] // 2
            rows = rows[:half] + by_sub(rows[half:].astype(BF16), bit).astype(F32)
            bit //= 2
        half = rows.shape[0] // 2
        rows = rows[:half] + by_side(rows[half:].astype(BF16), 1).astype(F32)
        return rows[:SLOTS], by_side(rows[SLOTS:].astype(BF16), 0)

    def from_planes(own, got, extra, last=None):
        if last is not None:
            own = after(own, last)
        pieces = run(
            "split",
            split_body(extra),
            [shape((SLOTS, slice_width + extra), BF16)] * E,
            [at, own, got],
            [pltpu.VMEM(own.shape, BF16)],
        )
        return jnp.stack(exchange_planes(pieces))

    returned = give_back(jnp.concatenate([drows, row_stats], axis=1))
    returned = from_planes(*returned, row_stats.shape[1])
    combined = jnp.einsum("kst,ksd->ktd", select, returned, preferred_element_type=F32)
    per_expert = combined[:, :, slice_width : slice_width + 2]
    dprob_two = keep_two * jnp.sum(hot_two_k * per_expert[:, None, :, 0], axis=0)
    inner_two = jnp.sum(per_expert[:, :, 1], axis=0)
    dnormed_two = jnp.sum(combined[:, :, :slice_width], axis=0)

    def gate_back(prob, dprob, hots):
        dselect = prob * (dprob - jnp.sum(prob * dprob, axis=0, keepdims=True))
        return jnp.sum(hots * dselect[:, None, :], axis=0)

    dlogit_two = gate_back(prob_two, dprob_two, hot_two)
    dnormed_two = dnormed_two + dot(dlogit_two, router_two_plane, ((0,), (0,)), PRECISE)
    inner_two = inner_two + jnp.sum(dlogit_two * logits_two, axis=0)
    dhidden = (
        turned_grad.astype(F32)
        + scale_two[:, None] * (dnormed_two * gain_two_plane)
        - hidden * (scale_two * scale_two * inner_two / width)[:, None]
    )
    scaled_hidden = hidden * scale_two[:, None]
    mlp_terms = jnp.concatenate(
        [
            jnp.sum(dnormed_two * scaled_hidden, axis=0)[None],
            dot(dlogit_two, scaled_hidden * gain_two_plane, ((1,), (0,)), PRECISE),
        ],
        axis=0,
    )

    wide_grad, *dcontext_blocks = run(
        "dcontext",
        routed_body(subs, False),
        [shape((rows_all, slice_width), BF16), kept_own] + [sent] * (E - 1),
        [at, *gather_narrow(dhidden.astype(BF16)), hot_cols, *out_parts],
        routed_scratch,
    )
    dcontext_blocks = exchange_planes(dcontext_blocks)

    def weight_parts(count):
        return [
            shape((count, shard_rows, local_width), F32 if j < subs // 2 else BF16)
            for j in range(subs)
        ]

    def weight_sum(parts):
        return finish_subs(parts[: subs // 2], parts[subs // 2 :])

    weight_scratch = [pltpu.VMEM((slice_width, local_width), F32)]
    output_parts = run(
        "output_grad", weight_grad_body, weight_parts(E), [at, wide_grad, mixed], weight_scratch
    )
    expert_out = dot(activation, weight_down, ((1,), (0,))) * row_gate
    mixture = give_back(expert_out)
    output_grad, output_got = weight_sum(output_parts)
    gated_act = (activation.astype(F32) * row_gate).astype(BF16)
    down_grad = dot(after(gated_act, dcontext_blocks[0]), grad_rows, ((0,), (0,)))
    grads_low, home_sums = run(
        "attention_back",
        attention_back_body,
        [shape((4, TOK, local_width), BF16), shape((8, TOK), F32)],
        [
            at,
            *after(dcontext_blocks, output_parts[-1], down_grad),
            token_rows,
            low,
            probs,
            context,
        ],
    )
    grad_planes = gather_planes(grads_low)
    dboth = jnp.stack(
        [
            (dgate_pre.astype(F32) * row_scale).astype(BF16),
            (dup_pre.astype(F32) * row_scale).astype(BF16),
        ],
        axis=1,
    )
    up_grad = jnp.einsum(
        "rd,rkf->dkf", expert_rows, after(dboth, grad_planes[E - 1]), preferred_element_type=F32
    )
    dmixed, *query_grad_parts = run(
        "query_grad",
        query_grad_body,
        [shape((E, rows_all, local_width), BF16)] + weight_parts(E),
        [at, gained, hot_cols, *after(grad_planes, output_got, up_grad)],
        weight_scratch,
    )
    query_grad, query_got = weight_sum(query_grad_parts)
    dkv_all, gain_row, *dnormed_one = run(
        "input",
        input_body(subs),
        [shape((2, rows_all, local_width), BF16), shape((1, slice_width), F32)] + folded,
        [
            at,
            *after(grad_planes, query_grad_parts[-1]),
            dmixed,
            *kv_parts,
            *query_parts,
            *all_streams,
        ],
        [pltpu.VMEM((2 + E, slice_width, local_width), BF16)],
        flops=14 * rows_all * slice_width * local_width,
    )
    home_rows = swap(after(near, own_stats))
    gain_one_home = home_rows[0].astype(F32)
    router_one_home = home_rows[1:5].astype(F32)
    gained_home = home_stream * gain_one_home
    home_sums = sum_narrow(after(home_sums, gain_row))
    dprob_one = keep_one * home_sums[:2]
    dlogit_one = gate_back(prob_one, dprob_one, hot_one)
    inner_one = home_sums[2] + jnp.sum(dlogit_one * logits_one, axis=0)
    dlogit_scaled = dlogit_one * scale_one
    router_term = swap(dot(dlogit_scaled, gained_home, ((1,), (0,)), PRECISE))
    kv_grad_parts = run(
        "key_value_grad", weight_grad_body, weight_parts(2), [at, gained, dkv_all], weight_scratch, 14 * rows_all * slice_width * local_width
    )
    kv_grad, kv_got = weight_sum(after(kv_grad_parts, query_got))
    keep, got, other = after(reduce_narrow(*dnormed_one), kv_grad_parts[-1], query_got)
    dnormed_one = keep + got[0].astype(F32) + other.astype(F32)
    turned_out = dhidden + dnormed_one * gain_one_plane
    home_out = swap(turned_out.astype(BF16)).astype(F32)
    stream_grad = (
        home_out
        + gain_one_home * dot(dlogit_scaled, router_one_home, ((0,), (0,)), PRECISE)
        - home_stream * (scale_one * scale_one * inner_one / width)[:, None]
    )

    small = jnp.concatenate([mlp_terms, gain_row, router_term], axis=0)
    small = sum_subs(after(sum_narrow(small), kv_got))
    mine = lax.dynamic_slice_in_dim(small, sub * shard_rows, shard_rows, 1)
    router_one_grad = mine[6:10]
    gain_one_grad = mine[5] + jnp.sum(
        router_one_grad * attn_router.T.astype(F32), axis=0
    ) / attn_gain.astype(F32)

    mixture = from_planes(*mixture, 0, gain_row)
    mixture = jnp.einsum("kst,ksd->td", select, after(mixture, turned_out), preferred_element_type=F32)
    layer_out = swap((hidden + mixture).astype(BF16)).astype(F32)
    return (
        layer_out,
        stream_grad,
        gain_one_grad,
        router_one_grad.T,
        kv_grad,
        query_grad,
        output_grad,
        mine[0],
        mine[1:5].T,
        up_grad[None],
        down_grad[None],
    )


def solution(mesh):
    in_specs = (
        P("wide", "narrow"),
        P("wide", "narrow"),
        P("wide"),
        P("wide", None),
        P(None, "wide", "narrow"),
        P(None, "wide", "narrow"),
        P(None, "wide", "narrow"),
        P("wide"),
        P("wide", None),
        P("wide", None, None, "narrow"),
        P("wide", "narrow", None),
        P("wide", None),
        P("wide", None),
        P("wide", None),
    )
    out_specs = (
        P("wide", "narrow"),
        P("wide", "narrow"),
        P("wide"),
        P("wide", None),
        P(None, "wide", "narrow"),
        P(None, "wide", "narrow"),
        P(None, "wide", "narrow"),
        P("wide"),
        P("wide", None),
        P("wide", None, None, "narrow"),
        P("wide", "narrow", None),
    )
    return jax.shard_map(local, mesh=mesh, in_specs=in_specs, out_specs=out_specs, check_vma=False)
```
